32 devices in a mesh: group: 4 (over z_hi, core), blk: 4 (over y, x), head: 2 (over z_lo).
Axes of the slice: x: 2, y: 2, z: 4 (z_hi: 2, z_lo: 2; z = z_hi * 2 + z_lo), core: 2. Of those that a mesh axis runs over, the one named last changes fastest.
Arguments:
- tokens: bfloat16 [8, 1024, 1024], P('group', ('blk', 'head')), may hold values from -6 to 6
- segments: int32 [8, 1024], P('group'), may hold values from 0 to 7, never falling along the last dimension, each value on 1 to 512 neighbouring positions
- routes: int32 [8, 1024, 8], P('group', ('blk', 'head')), may hold values from 0 to 31, all different within a row; in each aligned block of 128 rows (0 to 127, 128 to 255, ..., all dimensions but the last counted through in order) at most 36 rows name the same one
- cotangent: bfloat16 [8, 1024, 1024], P('group', ('blk', 'head')), may hold values from -6 to 6
- attn_gain: bfloat16 [1024], P(('blk', 'head')), may hold values from 0.5 to 1.5
- moe_gain: bfloat16 [1024], P(('blk', 'head')), may hold values from 0.5 to 1.5
- query_weight: bfloat16 [1024, 1024], P(('blk', 'head')), may hold values from -0.1875 to 0.1875
- key_projection_matrix: bfloat16 [1024, 512], P(('blk', 'head')), may hold values from -0.1875 to 0.1875
- value_projection_matrix: bfloat16 [1024, 512], P(('blk', 'head')), may hold values from -0.1875 to 0.1875
- out_weight: bfloat16 [1024, 1024], P(('blk', 'head')), may hold values from -1.5 to 1.5
- router_weight: bfloat16 [1024, 32], P(('blk', 'head')), may hold values from -0.375 to 0.375
- gate_weight: bfloat16 [32, 1024, 512], P(('blk', 'head')), may hold values from -0.1875 to 0.1875
- up_weight: bfloat16 [32, 1024, 512], P(('blk', 'head')), may hold values from -0.1875 to 0.1875
- down_weight: bfloat16 [32, 512, 1024], P(('blk', 'head')), may hold values from -0.75 to 0.75
Outputs:
- mixed: bfloat16 [8, 1024, 1024], P('group', ('blk', 'head'))
- token_grad: float32 [8, 1024, 1024], P('group', ('blk', 'head'))
- attn_gain_grad: float32 [1024], P(('blk', 'head'))
- moe_gain_grad: float32 [1024], P(('blk', 'head'))
- query_weight_grad: float32 [1024, 1024], P(('blk', 'head'))
- key_weight_grad: float32 [1024, 512], P(('blk', 'head'))
- value_weight_grad: float32 [1024, 512], P(('blk', 'head'))
- out_weight_grad: float32 [1024, 1024], P(('blk', 'head'))
- router_weight_grad: float32 [1024, 32], P(('blk', 'head'))
- gate_weight_grad: float32 [32, 1024, 512], P(('blk', 'head'))
- up_weight_grad: float32 [32, 1024, 512], P(('blk', 'head'))
- down_weight_grad: float32 [32, 512, 1024], P(('blk', 'head'))
The draws below stay inside these ranges and needn't reach their ends.
Inputs may be any that keep to these rules, and one draw needn't show every extreme that they name: `routes`: each row names 8 distinct experts; in each aligned block of 128 positions of a sequence no expert is named by more than 36 rows, a bound that some block reaches. `segments`: within each sequence the numbers never fall; each document has at most 512 positions, and one has exactly 512.
All inputs are finite; a program needn't handle non-finite values.
Results may differ from the reference program's by a relative error of at most 0.03.
Values may be sent and summed in bfloat16 or wider, within the bound.
A program may use at most 192 MiB of HBM per device.

```python
import math
from functools import partial
import jax
import jax.numpy as jnp
import numpy as np
from jax import lax

MODEL_WIDTH = 1024
QUERY_HEADS = 16
KEY_VALUE_HEADS = 8
HEAD_SIZE = 64
FF = 512
EXPERTS = 32
TOP = 8
ROWS_DEV = 128
SEGS = 8
SEQUENCE_LENGTH = 1024
SEQUENCE_COUNT = 8
CAPH = 36
DOC_MAX = 512
N_HEAD = 2


def block_levels(stream_key, extent, split, smallest, high):
    def one(position, parts):
        draws = jax.random.uniform(jax.random.fold_in(jax.random.fold_in(stream_key, 6), position), (parts,), jnp.float32, smallest / len(split), high / len(split))
        return jnp.repeat(jnp.exp(draws), extent[position] // parts).reshape((-1,) + (1,) * (len(extent) - position - 1))

    level = one(*split[0])
    for cut in split[1:]:
        level = level * one(*cut)
    return level


def length_profile(number_of, total, most, lean):
    portions = [(1 << 20) // math.isqrt(standing ** lean) + 1 for standing in range(2, number_of + 1)]
    spare, given = total - most - (number_of - 1), [1] * (number_of - 1)
    while spare > 0:
        candidates = [i for i in range(number_of - 1) if given[i] < most]
        whole, left = sum([portions[i] for i in candidates]), spare
        for i in candidates:
            extra = min(most - given[i], max(1, left * portions[i] // whole), spare)
            given[i] = given[i] + extra
            spare = spare - extra
    return np.array([most] + given)


def ragged_sizes(own_key, count, total, reach, lean):
    if count == 2:
        one = jax.random.randint(own_key, (), max(1, total - reach), min(reach, total - 1) + 1)
        return jnp.stack([one, total - one])
    sizes = jnp.asarray(length_profile(count, total, reach, lean), jnp.int32)
    couples = (count - 1) // 2
    source_of, taker = sizes[1:1 + 2 * couples:2], sizes[2:2 + 2 * couples:2]
    room = jnp.minimum(source_of - 1, reach - taker)
    shifted = jax.random.randint(jax.random.fold_in(own_key, 1), (couples,), 0, 1 << 20) % (room + 1)
    sizes = sizes.at[1:1 + 2 * couples:2].set(source_of - shifted).at[2:2 + 2 * couples:2].set(taker + shifted)
    return sizes[jax.random.permutation(jax.random.fold_in(own_key, 2), count)]


def shared_out(stream_key, own, number, rows, count, top, reach, lean):
    ranking = jax.random.permutation(stream_key, count)
    crowded, usual = portions_of(count, rows * top, reach, lean, True), portions_of(count, rows * top, reach, lean, False)
    places = jnp.arange(count)

    def named(lengths, rotation):
        used = int((lengths > 0).sum())
        fixed = max(1, used // 4)
        moved = fixed + (places - fixed + rotation * (used - fixed)) % max(1, count - fixed)
        return jnp.zeros((count,), jnp.int32).at[ranking[jnp.where(places < fixed, places, moved)]].set(jnp.asarray(lengths, jnp.int32))

    lengths = jnp.where(number % 4 == 0, named(crowded, number // 4), named(usual, number - number // 4 - 1))
    mixed = jax.random.permutation(jax.random.fold_in(own, 3), count)
    source_of, sink = mixed[0:count // 2 * 2:2], mixed[1:count // 2 * 2:2]
    margin = jnp.minimum(lengths[source_of] - 1, reach - lengths[sink]) // 2
    margin = jnp.where((source_of == ranking[0]) | (sink == ranking[0]) | (lengths[sink] == 0), 0, jnp.maximum(margin, 0))
    moved = jax.random.randint(jax.random.fold_in(own, 4), (count // 2,), 0, 1 << 20) % (margin + 1)
    lengths = lengths.at[source_of].add(-moved).at[sink].add(moved)
    labels = jnp.searchsorted(jnp.cumsum(lengths), jnp.arange(rows * top), side="right").astype(jnp.int32)
    table = labels.reshape(top, rows).T
    table = table[jax.random.permutation(jax.random.fold_in(own, 1), rows)]
    rotation = jax.random.randint(jax.random.fold_in(own, 2), (rows, 1), 0, top)
    return jnp.take_along_axis(table, (jnp.arange(top)[None, :] + rotation) % top, axis=1)


def portions_of(number_of, total, bound, slope, full):
    weights = [(1 << 20) // math.isqrt(rank ** slope) + 1 for rank in range(1, number_of + 1)]
    largest = bound if full else min(bound, max(-(-total // number_of), total * weights[0] // sum(weights)))
    least = 1 if total - largest >= number_of - 1 else 0
    given, surplus = [largest] + [least] * (number_of - 1), total - largest - least * (number_of - 1)
    while surplus > 0:
        candidates = [i for i in range(1, number_of) if given[i] < largest] or [i for i in range(1, number_of) if given[i] < bound]
        pool, budget = sum([weights[i] for i in candidates]), surplus
        for i in candidates:
            extra = min(bound - given[i], max(1, budget * weights[i] // pool), surplus)
            given[i] = given[i] + extra
            surplus = surplus - extra
    return np.array(given)


def normal_values(key, extent, width, reach, cuts=(), kind=jnp.bfloat16):
    entries = width * jax.random.normal(key, extent, jnp.float32)
    if cuts:
        entries = entries * block_levels(key, extent, cuts, -0.22, 0.18)
    return jnp.clip(entries, -reach, reach).astype(kind)


def setup_inputs(seed: int = 0) -> dict:
    key_of = jax.random.split(jax.random.key(seed), 15)
    tokens = normal_values(key_of[0], (SEQUENCE_COUNT, SEQUENCE_LENGTH, MODEL_WIDTH), 1.0, 6.0, ((0, 4), (1, 8)))
    segments = jax.vmap(lambda own: jnp.searchsorted(jnp.cumsum(ragged_sizes(own, SEGS, SEQUENCE_LENGTH, DOC_MAX, 0)), jnp.arange(SEQUENCE_LENGTH), side="right"))(jax.random.split(key_of[1], SEQUENCE_COUNT)).reshape((SEQUENCE_COUNT, SEQUENCE_LENGTH)).astype(jnp.int32)
    routes_keys = jax.random.split(jax.random.fold_in(key_of[2], 1), SEQUENCE_COUNT * SEQUENCE_LENGTH // ROWS_DEV)
    routes_turns = jax.random.permutation(jax.random.fold_in(key_of[2], 3), SEQUENCE_COUNT * SEQUENCE_LENGTH // ROWS_DEV)
    routes = jax.vmap(lambda own, number: shared_out(jax.random.fold_in(key_of[2], 2), own, number, ROWS_DEV, EXPERTS, TOP, CAPH, 1))(routes_keys, routes_turns).reshape((SEQUENCE_COUNT, SEQUENCE_LENGTH, TOP))
    cotangent = normal_values(key_of[3], (SEQUENCE_COUNT, SEQUENCE_LENGTH, MODEL_WIDTH), 1.0, 6.0, ((0, 4), (1, 8)))
    attn_gain = jnp.clip(1.0 + 0.1 * jax.random.normal(key_of[4], (MODEL_WIDTH,), jnp.float32), 0.5, 1.5).astype(jnp.bfloat16)
    moe_gain = jnp.clip(1.0 + 0.1 * jax.random.normal(key_of[5], (MODEL_WIDTH,), jnp.float32), 0.5, 1.5).astype(jnp.bfloat16)
    query_weight = normal_values(key_of[6], (MODEL_WIDTH, QUERY_HEADS * HEAD_SIZE), MODEL_WIDTH ** -0.5, 0.1875, ((0, 8),))
    key_projection_matrix = normal_values(key_of[7], (MODEL_WIDTH, KEY_VALUE_HEADS * HEAD_SIZE), MODEL_WIDTH ** -0.5, 0.1875, ((0, 8),))
    value_projection_matrix = normal_values(key_of[8], (MODEL_WIDTH, KEY_VALUE_HEADS * HEAD_SIZE), MODEL_WIDTH ** -0.5, 0.1875, ((0, 8),))
    out_weight = normal_values(key_of[9], (QUERY_HEADS * HEAD_SIZE, MODEL_WIDTH), (QUERY_HEADS * HEAD_SIZE // 64) ** -0.5, 1.5, ((0, 8),))
    router_weight = normal_values(key_of[10], (MODEL_WIDTH, EXPERTS), (MODEL_WIDTH // 4) ** -0.5, 0.375, ((0, 8),))
    gate_weight = normal_values(key_of[11], (EXPERTS, MODEL_WIDTH, FF), MODEL_WIDTH ** -0.5, 0.1875, ((0, 8),))
    up_weight = normal_values(key_of[12], (EXPERTS, MODEL_WIDTH, FF), MODEL_WIDTH ** -0.5, 0.1875, ((0, 8),))
    down_weight = normal_values(key_of[13], (EXPERTS, FF, MODEL_WIDTH), (FF // 8) ** -0.5, 0.75, ((0, 8),))
    return dict(tokens=tokens, segments=segments, routes=routes, cotangent=cotangent, attn_gain=attn_gain, moe_gain=moe_gain, query_weight=query_weight, key_projection_matrix=key_projection_matrix, value_projection_matrix=value_projection_matrix, out_weight=out_weight, router_weight=router_weight, gate_weight=gate_weight, up_weight=up_weight, down_weight=down_weight)


epsilon = 1e-05
rope_base = 10000.0
masked_out = -1e+30
highest = lax.Precision.HIGHEST

@jax.custom_vjp
def reduced_precision(v):
    return lax.optimization_barrier(v.astype(jnp.bfloat16)).astype(jnp.float32)

@jax.custom_vjp
def low_back(v):
    return v

def low_keep(v):
    return (reduced_precision(v), None)

def low_pass(kept, grad):
    return (grad,)

def back_keep(v):
    return (v, None)

def back_low(kept, grad):
    return (reduced_precision(grad),)
reduced_precision.defvjp(low_keep, low_pass)
low_back.defvjp(back_keep, back_low)

def rms_norm(values, gain_vec):
    return values * lax.rsqrt(lax.optimization_barrier(jnp.mean(values * values, -1, keepdims=True)) + epsilon) * gain_vec

def rotary_embedding(field_vals, places, turn_sign):
    half_dim = field_vals.shape[-1] // 2
    frequency = rope_base ** (-jnp.arange(half_dim, dtype=jnp.float32) * 2.0 / field_vals.shape[-1])
    angles = places.astype(jnp.float32)[:, None] * frequency[None, :]
    cosine = jnp.cos(angles)[:, None, :]
    sine_vals = turn_sign * jnp.sin(angles)[:, None, :]
    first_half = field_vals[..., :half_dim]
    second = field_vals[..., half_dim:]
    return jnp.concatenate([first_half * cosine - second * sine_vals, second * cosine + first_half * sine_vals], -1)

def sequence_attention(packed):
    query_vectors, key_row_block, value_row_block, seg_row = packed
    query_per_key_head = QUERY_HEADS // KEY_VALUE_HEADS
    rows_per_block = ROWS_DEV * N_HEAD
    number_of_blocks = SEQUENCE_LENGTH // rows_per_block
    grouped_heads = query_vectors.reshape(number_of_blocks, rows_per_block, KEY_VALUE_HEADS, query_per_key_head, HEAD_SIZE)
    key_place = jnp.arange(SEQUENCE_LENGTH, dtype=jnp.int32)

    def one_block(packed_block):
        block_index, query_block = packed_block
        raw_scores = low_back(jnp.einsum('qgrd,kgd->qgrk', query_block, key_row_block, precision=highest))
        query_place = block_index * rows_per_block + jnp.arange(rows_per_block, dtype=jnp.int32)
        query_doc = lax.dynamic_slice_in_dim(seg_row, block_index * rows_per_block, rows_per_block)
        allowed = (query_place[:, None] >= key_place[None, :]) & (query_doc[:, None] == seg_row[None, :])
        scores = jnp.where(allowed[:, None, None, :], raw_scores * HEAD_SIZE ** (-0.5), masked_out)
        probability = jax.nn.softmax(scores, axis=-1)
        return jnp.einsum('qgrk,kgd->qgrd', reduced_precision(probability), value_row_block, precision=highest)
    blocks_out = lax.map(jax.checkpoint(one_block), (jnp.arange(number_of_blocks, dtype=jnp.int32), grouped_heads))
    return blocks_out.reshape(SEQUENCE_LENGTH, QUERY_HEADS * HEAD_SIZE)

def forward(tokens_f, attn_gain, moe_gain, query_weight, key_projection_matrix, value_projection_matrix, out_weight, router_weight, gate_weight, up_weight, down_weight, segments=None, routes=None):
    rows_all = SEQUENCE_COUNT * SEQUENCE_LENGTH
    flat_rows = tokens_f.reshape(rows_all, MODEL_WIDTH)
    attn_in = reduced_precision(rms_norm(flat_rows, attn_gain))
    token_positions = jnp.arange(SEQUENCE_LENGTH, dtype=jnp.int32)
    query_pre = low_back(jnp.dot(attn_in, query_weight, precision=highest))
    key_before_rotary = low_back(jnp.dot(attn_in, key_projection_matrix, precision=highest))
    value_row_block = low_back(reduced_precision(jnp.dot(attn_in, value_projection_matrix, precision=highest)))
    query_vectors = reduced_precision(rotary_embedding(query_pre.reshape(SEQUENCE_COUNT, SEQUENCE_LENGTH, QUERY_HEADS, HEAD_SIZE), token_positions, 1.0))
    key_row_block = reduced_precision(rotary_embedding(key_before_rotary.reshape(SEQUENCE_COUNT, SEQUENCE_LENGTH, KEY_VALUE_HEADS, HEAD_SIZE), token_positions, 1.0))
    combined_heads = lax.map(sequence_attention, (query_vectors, key_row_block, value_row_block.reshape(SEQUENCE_COUNT, SEQUENCE_LENGTH, KEY_VALUE_HEADS, HEAD_SIZE), segments))
    attn_mix = low_back(reduced_precision(combined_heads.reshape(rows_all, QUERY_HEADS * HEAD_SIZE)))
    residual = flat_rows + low_back(jnp.dot(attn_mix, out_weight, precision=highest))
    moe_in = reduced_precision(rms_norm(residual, moe_gain))
    logits = jnp.dot(moe_in, router_weight, precision=highest)
    route_flat = routes.reshape(rows_all, TOP)
    expert_ids = jnp.arange(EXPERTS, dtype=jnp.int32)
    choose = (route_flat[:, :, None] == expert_ids[None, None, :]).astype(jnp.float32)
    picked_logits = jnp.einsum('nke,ne->nk', choose, logits, precision=highest)
    route_weights = jax.nn.softmax(picked_logits, axis=-1)
    pair_expert = route_flat.reshape(-1)
    sorted_pairs = jnp.argsort(pair_expert, stable=True).astype(jnp.int32)
    counts = lax.optimization_barrier(jnp.sum((pair_expert[:, None] == expert_ids[None, :]).astype(jnp.int32), 0))
    starts = jnp.cumsum(counts).astype(jnp.int32) - counts
    slot_depth = SEQUENCE_COUNT * (SEQUENCE_LENGTH // ROWS_DEV) * CAPH
    slot_index = jnp.arange(slot_depth, dtype=jnp.int32)
    is_valid = slot_index[None, :] < counts[:, None]
    where_pos = jnp.minimum(starts[:, None] + slot_index[None, :], rows_all * TOP - 1).astype(jnp.int32)
    pair_pick = sorted_pairs[where_pos]
    token_rows = (pair_pick // TOP).astype(jnp.int32)
    pair_scale = jnp.where(is_valid, route_weights.reshape(-1)[pair_pick], 0.0)

    def run_expert(packed):
        gate_one, up_one, down_one, token_one, scale_one = packed
        rows_in = low_back(moe_in[token_one])
        gate_val = low_back(jnp.dot(rows_in, gate_one, precision=highest))
        up_val = low_back(jnp.dot(rows_in, up_one, precision=highest))
        hidden = reduced_precision(jax.nn.silu(gate_val) * up_val)
        expert_out = low_back(reduced_precision(jnp.dot(hidden, down_one, precision=highest)))
        return expert_out * scale_one[:, None]
    contributions = lax.map(jax.checkpoint(run_expert), (gate_weight, up_weight, down_weight, token_rows, pair_scale))
    moe_out = jnp.zeros((rows_all, MODEL_WIDTH), jnp.float32).at[token_rows.reshape(-1)].add(contributions.reshape(-1, MODEL_WIDTH))
    return (residual + moe_out).reshape(SEQUENCE_COUNT, SEQUENCE_LENGTH, MODEL_WIDTH)

def reference(tokens, segments, routes, cotangent, attn_gain, moe_gain, query_weight, key_projection_matrix, value_projection_matrix, out_weight, router_weight, gate_weight, up_weight, down_weight):
    floats = tuple((member.astype(jnp.float32) for member in (tokens, attn_gain, moe_gain, query_weight, key_projection_matrix, value_projection_matrix, out_weight, router_weight, gate_weight, up_weight, down_weight)))
    result, pullback = jax.vjp(partial(forward, segments=segments, routes=routes), *floats)
    grads = pullback(cotangent.astype(jnp.float32))
    return (result.astype(jnp.bfloat16), grads[0], grads[1], grads[2], grads[3], grads[4], grads[5], grads[6], grads[7], grads[8], grads[9], grads[10])
```

```python
import functools

import jax
import jax.numpy as jnp
from jax import lax
from jax.experimental import pallas as pl
from jax.experimental.pallas import tpu as pltpu
from jax.sharding import PartitionSpec as P

QUERY_HEADS = 16
KEY_VALUE_HEADS = 8
HEAD_SIZE = 64
TOP = 8
CAPH = 36


epsilon = 1e-05
rope_base = 10000.0
masked_out = -1e30
key_block = 512


def rms_norm(values, gain_vec):
    return values * lax.rsqrt(jnp.mean(values * values, -1, keepdims=True) + epsilon) * gain_vec


def rotary_embedding(field_vals, places, turn_sign):
    half_dim = field_vals.shape[-1] // 2
    frequency = rope_base ** (-jnp.arange(half_dim, dtype=jnp.float32) * 2.0 / field_vals.shape[-1])
    angles = places.astype(jnp.float32)[:, None] * frequency[None, :]
    cosine = jnp.cos(angles)[:, None, :]
    sine_vals = turn_sign * jnp.sin(angles)[:, None, :]
    first_half = field_vals[..., :half_dim]
    second = field_vals[..., half_dim:]
    return jnp.concatenate(
        [first_half * cosine - second * sine_vals, second * cosine + first_half * sine_vals], -1
    )


def add_rows(running, addend, row_start):
    current = lax.dynamic_slice_in_dim(running, row_start, addend.shape[1], 1)
    return lax.dynamic_update_slice_in_dim(running, current + addend, row_start, 1)


def on_device(
    tokens,
    segments,
    routes,
    cotangent,
    attn_gain,
    moe_gain,
    query_weight,
    key_projection_matrix,
    value_projection_matrix,
    out_weight,
    router_weight,
    gate_weight,
    up_weight,
    down_weight,
):
    head_groups, number_of_rows, width_dim = tokens.shape
    query_per_key_head = QUERY_HEADS // KEY_VALUE_HEADS
    shared_head_count = lax.axis_size("head")
    query_rows = number_of_rows * shared_head_count
    grouped_keys = KEY_VALUE_HEADS // shared_head_count
    scale_val = HEAD_SIZE ** (-0.5)
    number_of_tokens = head_groups * number_of_rows
    seq_length = lax.axis_size("blk") * query_rows
    cycle_index = lax.axis_index("blk")
    local_placement = (
        cycle_index * shared_head_count + lax.axis_index("head")
    ) * number_of_rows + jnp.arange(number_of_rows, dtype=jnp.int32)
    own_start = cycle_index * query_rows
    query_place = own_start + jnp.arange(query_rows, dtype=jnp.int32)
    query_doc = lax.dynamic_slice_in_dim(segments, own_start, query_rows, 1)
    query_full, key_full, value_full, out_full, router_full, gain_attn, gain_moe = (
        lax.all_gather(query_weight, ("blk", "head"), axis=0, tiled=True),
        lax.all_gather(key_projection_matrix, ("blk", "head"), axis=0, tiled=True),
        lax.all_gather(value_projection_matrix, ("blk", "head"), axis=0, tiled=True),
        lax.all_gather(out_weight, ("blk", "head"), axis=0, tiled=True),
        lax.all_gather(router_weight, ("blk", "head"), axis=0, tiled=True),
        lax.all_gather(attn_gain, ("blk", "head"), axis=0, tiled=True),
        lax.all_gather(moe_gain, ("blk", "head"), axis=0, tiled=True),
    )
    flat_rows = tokens.reshape(number_of_tokens, width_dim).astype(jnp.float32)
    attn_normed, attn_pull = jax.vjp(rms_norm, flat_rows, gain_attn.astype(jnp.float32))
    attn_in = attn_normed.astype(jnp.bfloat16)
    query_pre = jnp.dot(attn_in, query_full, preferred_element_type=jnp.float32)
    key_before_rotary = jnp.dot(attn_in, key_full, preferred_element_type=jnp.float32)
    value_low = (
        jnp.dot(attn_in, value_full, preferred_element_type=jnp.float32)
        .astype(jnp.bfloat16)
        .reshape(head_groups, number_of_rows, KEY_VALUE_HEADS * HEAD_SIZE)
    )
    query_low = (
        rotary_embedding(
            query_pre.reshape(head_groups, number_of_rows, QUERY_HEADS, HEAD_SIZE),
            local_placement,
            1.0,
        )
        .astype(jnp.bfloat16)
        .reshape(head_groups, number_of_rows, QUERY_HEADS * HEAD_SIZE)
    )
    key_low = (
        rotary_embedding(
            key_before_rotary.reshape(head_groups, number_of_rows, KEY_VALUE_HEADS, HEAD_SIZE),
            local_placement,
            1.0,
        )
        .astype(jnp.bfloat16)
        .reshape(head_groups, number_of_rows, KEY_VALUE_HEADS * HEAD_SIZE)
    )
    query_split, key_split, value_split = (
        lax.all_to_all(query_low, "head", split_axis=2, concat_axis=1, tiled=True),
        lax.all_to_all(key_low, "head", split_axis=2, concat_axis=1, tiled=True),
        lax.all_to_all(value_low, "head", split_axis=2, concat_axis=1, tiled=True),
    )
    query_vectors = query_split.reshape(
        head_groups, query_rows, grouped_keys, query_per_key_head, HEAD_SIZE
    )

    def key_view(source, offset, sub_rows):
        return lax.dynamic_slice_in_dim(source, offset, sub_rows, 1).reshape(
            head_groups, sub_rows, grouped_keys, HEAD_SIZE
        )

    def scored_at(query_part, key_row_block, q_place, q_doc, key_start, sub_rows):
        raw_scores = (
            jnp.einsum(
                "bqgrd,bkgd->bqgrk", query_part, key_row_block, preferred_element_type=jnp.float32
            )
            * scale_val
        )
        key_place = key_start + jnp.arange(sub_rows, dtype=jnp.int32)
        key_doc = lax.dynamic_slice_in_dim(segments, key_start, sub_rows, 1)
        allowed = (q_place[None, :, None] >= key_place[None, None, :]) & (
            q_doc[:, :, None] == key_doc[:, None, :]
        )
        return (raw_scores, allowed[:, :, None, None, :])

    def scored(key_row_block, key_start, sub_rows):
        return scored_at(query_vectors, key_row_block, query_place, query_doc, key_start, sub_rows)

    stats_shape = (head_groups, query_rows, grouped_keys, query_per_key_head)
    init_state = (
        jnp.full(stats_shape, masked_out, jnp.float32),
        jnp.zeros(stats_shape, jnp.float32),
        jnp.zeros(stats_shape + (HEAD_SIZE,), jnp.float32),
    )
    key_all, value_all = (
        lax.all_gather(key_split, "blk", axis=1, tiled=True),
        lax.all_gather(value_split, "blk", axis=1, tiled=True),
    )
    fold_state = init_state
    total_rows = key_all.shape[1]
    sub_rows = key_block

    def forward_one_block(block_state, block_index):
        offset = block_index * sub_rows
        key_row_block = key_view(key_all, offset, sub_rows)
        value_row_block = key_view(value_all, offset, sub_rows)
        raw_scores, allowed = scored(key_row_block, 0 + offset, sub_rows)
        running_max, running_sum, running_acc = block_state
        masked = jnp.where(allowed, raw_scores, masked_out)
        new_max = jnp.maximum(running_max, jnp.max(masked, -1))
        shrink = jnp.exp(running_max - new_max)
        weights_soft = jnp.where(allowed, jnp.exp(masked - new_max[..., None]), 0.0)
        new_sum = running_sum * shrink + jnp.sum(weights_soft, -1)
        new_acc = running_acc * shrink[..., None] + jnp.einsum(
            "bqgrk,bkgd->bqgrd",
            weights_soft.astype(jnp.bfloat16),
            value_row_block,
            preferred_element_type=jnp.float32,
        )
        return ((new_max, new_sum, new_acc), None)

    fold_state, unused = lax.scan(
        forward_one_block, fold_state, jnp.arange(total_rows // sub_rows, dtype=jnp.int32)
    )
    running_max, running_sum, running_acc = fold_state
    mix_heads = running_acc / running_sum[..., None]
    log_total = running_max + jnp.log(running_sum)
    mix_low = mix_heads.astype(jnp.bfloat16).reshape(
        head_groups, query_rows, grouped_keys * query_per_key_head * HEAD_SIZE
    )
    mix_tokens = lax.all_to_all(mix_low, "head", split_axis=1, concat_axis=2, tiled=True)
    attn_mix = mix_tokens.reshape(number_of_tokens, QUERY_HEADS * HEAD_SIZE)
    residual = flat_rows + jnp.dot(attn_mix, out_full, preferred_element_type=jnp.float32)
    moe_normed, moe_pull = jax.vjp(rms_norm, residual, gain_moe.astype(jnp.float32))
    moe_in = moe_normed.astype(jnp.bfloat16)
    logits = jnp.dot(moe_in, router_full, preferred_element_type=jnp.float32)
    route_flat = routes.reshape(number_of_tokens, TOP)
    experts_all = router_full.shape[1]
    choose = route_flat[:, :, None] == jnp.arange(experts_all, dtype=jnp.int32)[None, None, :]
    choose_float = choose.astype(jnp.float32)
    picked_logits = jnp.einsum("nke,ne->nk", choose_float, logits)
    route_weights = jax.nn.softmax(picked_logits, axis=-1)
    choose_whole = choose.astype(jnp.int32).reshape(head_groups, number_of_rows * TOP, experts_all)
    slot_rank = jnp.sum(jnp.cumsum(choose_whole, 1) * choose_whole, -1) - 1
    slot_index = (slot_rank + jnp.arange(head_groups, dtype=jnp.int32)[:, None] * CAPH).reshape(-1)
    targets = route_flat.reshape(-1)
    lane_count = head_groups * CAPH
    outgoing = (
        jnp.zeros((experts_all, lane_count, width_dim), jnp.bfloat16)
        .at[targets, slot_index]
        .set(jnp.repeat(moe_in, TOP, axis=0))
    )
    arrived = lax.all_to_all(outgoing, ("blk", "head"), split_axis=0, concat_axis=1, tiled=True)
    gate_val = jnp.einsum("end,edf->enf", arrived, gate_weight, preferred_element_type=jnp.float32)
    up_val = jnp.einsum("end,edf->enf", arrived, up_weight, preferred_element_type=jnp.float32)
    hidden_low = (jax.nn.silu(gate_val) * up_val).astype(jnp.bfloat16)
    expert_out = jnp.einsum(
        "enf,efd->end", hidden_low, down_weight, preferred_element_type=jnp.float32
    ).astype(jnp.bfloat16)
    returned = lax.all_to_all(expert_out, ("blk", "head"), split_axis=1, concat_axis=0, tiled=True)
    picked_rows = returned[targets, slot_index].reshape(number_of_tokens, TOP, width_dim)
    moe_out = jnp.einsum(
        "nk,nkd->nd", route_weights, picked_rows, preferred_element_type=jnp.float32
    )
    mixed = (
        (residual + moe_out).astype(jnp.bfloat16).reshape(head_groups, number_of_rows, width_dim)
    )
    grad_full = cotangent.reshape(number_of_tokens, width_dim).astype(jnp.float32)
    weight_grad = jnp.einsum(
        "nkd,nd->nk", picked_rows, grad_full, preferred_element_type=jnp.float32
    )
    pair_grad = (
        (route_weights[:, :, None] * grad_full[:, None, :])
        .astype(jnp.bfloat16)
        .reshape(number_of_tokens * TOP, width_dim)
    )
    grad_outgoing = jnp.zeros_like(outgoing).at[targets, slot_index].set(pair_grad)
    grad_arrived = lax.all_to_all(
        grad_outgoing, ("blk", "head"), split_axis=0, concat_axis=1, tiled=True
    )
    grad_hidden = jnp.einsum(
        "end,efd->enf", grad_arrived, down_weight, preferred_element_type=jnp.float32
    )
    sigmoid_val = jax.nn.sigmoid(gate_val)
    grad_gate = (
        grad_hidden * up_val * sigmoid_val * (1.0 + gate_val * (1.0 - sigmoid_val))
    ).astype(jnp.bfloat16)
    grad_up = (grad_hidden * gate_val * sigmoid_val).astype(jnp.bfloat16)
    down_weight_grad = jnp.einsum(
        "enf,end->efd", hidden_low, grad_arrived, preferred_element_type=jnp.float32
    )
    gate_weight_grad = jnp.einsum(
        "end,enf->edf", arrived, grad_gate, preferred_element_type=jnp.float32
    )
    up_weight_grad = jnp.einsum(
        "end,enf->edf", arrived, grad_up, preferred_element_type=jnp.float32
    )
    pair_back = (
        jnp.einsum("enf,edf->end", grad_gate, gate_weight, preferred_element_type=jnp.float32)
        + jnp.einsum("enf,edf->end", grad_up, up_weight, preferred_element_type=jnp.float32)
    ).astype(jnp.bfloat16)
    grad_returned = lax.all_to_all(
        pair_back, ("blk", "head"), split_axis=1, concat_axis=0, tiled=True
    )
    moe_in_grad = jnp.sum(
        grad_returned[targets, slot_index].reshape(number_of_tokens, TOP, width_dim),
        axis=1,
        dtype=jnp.float32,
    )
    mean_term = jnp.sum(route_weights * weight_grad, -1, keepdims=True)
    logit_grad = jnp.einsum("nk,nke->ne", route_weights * (weight_grad - mean_term), choose_float)
    router_grad = jnp.dot(moe_in.T, logit_grad, preferred_element_type=jnp.float32)
    moe_in_grad = moe_in_grad + jnp.dot(
        logit_grad, router_full.T, preferred_element_type=jnp.float32
    )
    residual_part, moe_gain_grad = moe_pull(moe_in_grad)
    residual_grad = grad_full + residual_part
    out_grad_low = residual_grad.astype(jnp.bfloat16)
    out_weight_grad = jnp.dot(attn_mix.T, out_grad_low, preferred_element_type=jnp.float32)
    mix_grad = (
        jnp.dot(out_grad_low, out_full.T, preferred_element_type=jnp.float32)
        .astype(jnp.bfloat16)
        .reshape(head_groups, number_of_rows, QUERY_HEADS * HEAD_SIZE)
    )
    mix_grad_heads = lax.all_to_all(
        mix_grad, "head", split_axis=2, concat_axis=1, tiled=True
    ).reshape(head_groups, query_rows, grouped_keys, query_per_key_head, HEAD_SIZE)
    delta_term = jnp.sum(mix_grad_heads.astype(jnp.float32) * mix_heads, -1)
    query_zero = jnp.zeros(stats_shape + (HEAD_SIZE,), jnp.float32)
    back_init = (
        query_zero,
        jnp.zeros((head_groups, seq_length, grouped_keys, HEAD_SIZE), jnp.float32),
        jnp.zeros((head_groups, seq_length, grouped_keys, HEAD_SIZE), jnp.float32),
    )
    fold_state = back_init
    total_rows = key_all.shape[1]

    def backward_one_block(block_state, block_index):
        offset = block_index * key_block
        key_start = 0 + offset
        key_row_block = key_view(key_all, offset, key_block)
        value_row_block = key_view(value_all, offset, key_block)
        raw_scores, allowed = scored(key_row_block, key_start, key_block)
        masked = jnp.where(allowed, raw_scores, masked_out)
        probability = jnp.where(allowed, jnp.exp(masked - log_total[..., None]), 0.0)
        prob_grad = jnp.einsum(
            "bqgrd,bkgd->bqgrk", mix_grad_heads, value_row_block, preferred_element_type=jnp.float32
        )
        score_grad = (probability * (prob_grad - delta_term[..., None]) * scale_val).astype(
            jnp.bfloat16
        )
        grad_query = block_state[0] + jnp.einsum(
            "bqgrk,bkgd->bqgrd", score_grad, key_row_block, preferred_element_type=jnp.float32
        )
        value_part_grad = jnp.einsum(
            "bqgrk,bqgrd->bkgd",
            probability.astype(jnp.bfloat16),
            mix_grad_heads,
            preferred_element_type=jnp.float32,
        )
        key_part_grad = jnp.einsum(
            "bqgrk,bqgrd->bkgd", score_grad, query_vectors, preferred_element_type=jnp.float32
        )
        grad_keys = add_rows(block_state[1], key_part_grad, key_start)
        grad_values = add_rows(block_state[2], value_part_grad, key_start)
        return ((grad_query, grad_keys, grad_values), None)

    fold_state, unused = lax.scan(
        backward_one_block, fold_state, jnp.arange(total_rows // key_block, dtype=jnp.int32)
    )
    grad_query, grad_keys, grad_values = fold_state
    key_own, value_own = (
        lax.psum_scatter(
            grad_keys.reshape(head_groups, seq_length, grouped_keys * HEAD_SIZE).astype(
                jnp.bfloat16
            ),
            "blk",
            scatter_dimension=1,
            tiled=True,
        ).astype(jnp.float32),
        lax.psum_scatter(
            grad_values.reshape(head_groups, seq_length, grouped_keys * HEAD_SIZE).astype(
                jnp.bfloat16
            ),
            "blk",
            scatter_dimension=1,
            tiled=True,
        ).astype(jnp.float32),
    )
    query_grad_low = (
        rotary_embedding(
            grad_query.reshape(
                head_groups, query_rows, grouped_keys * query_per_key_head, HEAD_SIZE
            ),
            query_place,
            -1.0,
        )
        .astype(jnp.bfloat16)
        .reshape(head_groups, query_rows, grouped_keys * query_per_key_head * HEAD_SIZE)
    )
    key_grad_low = (
        rotary_embedding(
            key_own.reshape(head_groups, query_rows, grouped_keys, HEAD_SIZE), query_place, -1.0
        )
        .astype(jnp.bfloat16)
        .reshape(head_groups, query_rows, grouped_keys * HEAD_SIZE)
    )
    value_grad_low = value_own.astype(jnp.bfloat16)
    query_back, key_pullback, value_pullback = (
        lax.all_to_all(query_grad_low, "head", split_axis=1, concat_axis=2, tiled=True),
        lax.all_to_all(key_grad_low, "head", split_axis=1, concat_axis=2, tiled=True),
        lax.all_to_all(value_grad_low, "head", split_axis=1, concat_axis=2, tiled=True),
    )
    query_flat = query_back.reshape(number_of_tokens, QUERY_HEADS * HEAD_SIZE)
    flattened_keys = key_pullback.reshape(number_of_tokens, KEY_VALUE_HEADS * HEAD_SIZE)
    flattened_values = value_pullback.reshape(number_of_tokens, KEY_VALUE_HEADS * HEAD_SIZE)
    query_weight_grad = jnp.dot(attn_in.T, query_flat, preferred_element_type=jnp.float32)
    key_weight_grad = jnp.dot(attn_in.T, flattened_keys, preferred_element_type=jnp.float32)
    value_weight_grad = jnp.dot(attn_in.T, flattened_values, preferred_element_type=jnp.float32)
    attn_in_grad = (
        jnp.dot(query_flat, query_full.T, preferred_element_type=jnp.float32)
        + jnp.dot(flattened_keys, key_full.T, preferred_element_type=jnp.float32)
        + jnp.dot(flattened_values, value_full.T, preferred_element_type=jnp.float32)
    )
    input_part, attn_gain_grad = attn_pull(attn_in_grad)
    token_grad = (residual_grad + input_part).reshape(head_groups, number_of_rows, width_dim)
    (
        query_shard,
        key_shard,
        value_shard,
        out_shard,
        router_shard,
        attn_gain_shard,
        moe_gain_shard,
    ) = (
        lax.psum_scatter(
            query_weight_grad.astype(jnp.bfloat16), ("blk", "head"), scatter_dimension=0, tiled=True
        ).astype(jnp.float32),
        lax.psum_scatter(
            key_weight_grad.astype(jnp.bfloat16), ("blk", "head"), scatter_dimension=0, tiled=True
        ).astype(jnp.float32),
        lax.psum_scatter(
            value_weight_grad.astype(jnp.bfloat16), ("blk", "head"), scatter_dimension=0, tiled=True
        ).astype(jnp.float32),
        lax.psum_scatter(
            out_weight_grad.astype(jnp.bfloat16), ("blk", "head"), scatter_dimension=0, tiled=True
        ).astype(jnp.float32),
        lax.psum_scatter(
            router_grad.astype(jnp.bfloat16), ("blk", "head"), scatter_dimension=0, tiled=True
        ).astype(jnp.float32),
        lax.psum_scatter(
            attn_gain_grad.astype(jnp.bfloat16), ("blk", "head"), scatter_dimension=0, tiled=True
        ).astype(jnp.float32),
        lax.psum_scatter(
            moe_gain_grad.astype(jnp.bfloat16), ("blk", "head"), scatter_dimension=0, tiled=True
        ).astype(jnp.float32),
    )
    summed = (
        lax.psum(query_shard.astype(jnp.bfloat16), "group").astype(jnp.float32),
        lax.psum(key_shard.astype(jnp.bfloat16), "group").astype(jnp.float32),
        lax.psum(value_shard.astype(jnp.bfloat16), "group").astype(jnp.float32),
        lax.psum(out_shard.astype(jnp.bfloat16), "group").astype(jnp.float32),
        lax.psum(router_shard.astype(jnp.bfloat16), "group").astype(jnp.float32),
        lax.psum(attn_gain_shard.astype(jnp.bfloat16), "group").astype(jnp.float32),
        lax.psum(moe_gain_shard.astype(jnp.bfloat16), "group").astype(jnp.float32),
        lax.psum(gate_weight_grad.astype(jnp.bfloat16), "group").astype(jnp.float32),
        lax.psum(up_weight_grad.astype(jnp.bfloat16), "group").astype(jnp.float32),
        lax.psum(down_weight_grad.astype(jnp.bfloat16), "group").astype(jnp.float32),
    )
    return (
        mixed,
        token_grad,
        summed[5],
        summed[6],
        summed[0],
        summed[1],
        summed[2],
        summed[3],
        summed[4],
        summed[7],
        summed[8],
        summed[9],
    )


bf16 = jnp.bfloat16
f32 = jnp.float32
MESH_ID = pl.DeviceIdType.MESH
VMEM_LIMIT = 66 * 1000 * 1000
COLOURS = ((0, 96), (96, 80), (176, 80))
LINKS = (("head", 1), ("blk", 1), ("blk", 2), ("group", 2), ("group", 1))
ORDERS = ((0, 1, 2), (1, 2, 0), (2, 0, 1))


def vmem():
    return pl.BlockSpec(memory_space=pltpu.VMEM)


def anywhere():
    return pl.BlockSpec(memory_space=pl.ANY)


def swap(value, link):
    axis, step = LINKS[link]
    count = lax.axis_size(axis)
    return lax.ppermute(value, axis, [(i, i ^ step) for i in range(count)])


def gather_swaps(value, order):
    held = value[None]
    for link in order:
        held = jnp.concatenate([held, swap(held, link)], 0)
    return held


def gather_rows(rows):
    return tuple(
        gather_swaps(rows[start : start + count], ORDERS[k])
        for k, (start, count) in enumerate(COLOURS)
    )


def dot_last(left, right):
    return lax.dot_general(left, right, (((1,), (1,)), ((), ())), preferred_element_type=f32)


def dot_first(left, right):
    return lax.dot_general(left, right, (((0,), (0,)), ((), ())), preferred_element_type=f32)


def dot(left, right):
    return jnp.dot(left, right, preferred_element_type=f32)


def my_place():
    return lax.axis_index("blk") * 2 + lax.axis_index("head")


def peer(step):
    place = lax.rem(my_place() + step, 8)
    return place, {"blk": place // 2, "head": lax.rem(place, 2)}


def neighbour(link):
    if link == 0:
        return {"head": 1 - lax.axis_index("head")}
    blk = lax.axis_index("blk")
    if link == 1:
        return {"blk": blk + 1 - 2 * lax.rem(blk, 2)}
    return {"blk": lax.rem(blk + 2, 4)}


def my_bits():
    blk = lax.axis_index("blk")
    return (lax.axis_index("head"), lax.rem(blk, 2), blk // 2)


def meet_all():
    barrier = pltpu.get_barrier_semaphore()
    for step in range(1, 8):
        pl.semaphore_signal(barrier, 1, device_id=peer(step)[1], device_id_type=MESH_ID)
    pl.semaphore_wait(barrier, 7)


def remote(src, dst, send, recv, target):
    return pltpu.make_async_remote_copy(
        src_ref=src, dst_ref=dst, send_sem=send, recv_sem=recv, device_id=target, device_id_type=MESH_ID
    )


def cube_index(bits, fixed, rows):
    entries = [pl.ds(fixed[link], 1) if link in fixed else pl.ds(0, 2) for link in (2, 1, 0)]
    return tuple(entries) + (pl.ds(*rows),)


def cube_gather(src, dst, send, recv, local_sem):
    bits = my_bits()
    own = pltpu.make_async_copy(src, dst.at[bits[2], bits[1], bits[0]], local_sem)
    own.start()
    started = []
    for step in range(3):
        now = []
        for k, order in enumerate(ORDERS):
            fixed = {link: bits[link] for link in order[step:]}
            where = dst.at[cube_index(bits, fixed, COLOURS[k])]
            if step == 0:
                start, count = COLOURS[k]
                here = src.at[pl.ds(start, count)]
                where = dst.at[bits[2], bits[1], bits[0], pl.ds(start, count)]
            else:
                here = where
            copy = remote(here, where, send.at[step, k], recv.at[step, k], neighbour(order[step]))
            copy.start()
            now.append(copy)
        if step == 0:
            own.wait()
        for copy in now:
            copy.wait_recv()
        started += now
    return started


def front_kernel(
    tok, wq, wkv, gains, router, routes, tok_all, w_all, gains_all, router_all, routes_all,
    send, recv, small_send, small_recv, local_sem, own_sem,
):
    me = my_place()
    meet_all()
    smalls = []
    for step in range(1, 8):
        place, target = peer(step)
        pairs = (
            (wq.at[:, pl.ds(place * 128, 128)], w_all.at[pl.ds(me * 128, 128), pl.ds(0, 128)]),
            (wkv.at[:, pl.ds(place * 128, 128)], w_all.at[pl.ds(me * 128, 128), pl.ds(128, 128)]),
            (gains, gains_all.at[:, pl.ds(me * 128, 128)]),
            (router, router_all.at[pl.ds(me * 128, 128)]),
            (routes, routes_all.at[:, pl.ds(me * 256, 256)]),
        )
        for kind, (src, dst) in enumerate(pairs):
            copy = remote(src, dst, small_send.at[kind, step], small_recv.at[kind, step], target)
            copy.start()
            smalls.append(copy)
    own = (
        (wq.at[:, pl.ds(me * 128, 128)], w_all.at[pl.ds(me * 128, 128), pl.ds(0, 128)]),
        (wkv.at[:, pl.ds(me * 128, 128)], w_all.at[pl.ds(me * 128, 128), pl.ds(128, 128)]),
        (gains, gains_all.at[:, pl.ds(me * 128, 128)]),
        (router, router_all.at[pl.ds(me * 128, 128)]),
        (routes, routes_all.at[:, pl.ds(me * 256, 256)]),
    )
    locals_ = []
    for kind, (src, dst) in enumerate(own):
        copy = pltpu.make_async_copy(src, dst, own_sem.at[kind])
        copy.start()
        locals_.append(copy)
    started = cube_gather(tok, tok_all, send, recv, local_sem)
    for copy in locals_:
        copy.wait()
    for copy in smalls:
        copy.wait()
    for copy in started:
        copy.wait_send()


def front(tok, wq, wkv, gains, router, routes):
    width = tok.shape[1]
    return pl.pallas_call(
        front_kernel,
        out_shape=(
            jax.ShapeDtypeStruct((2, 2, 2, 256, width), bf16),
            jax.ShapeDtypeStruct((width, 256), bf16),
            jax.ShapeDtypeStruct((16, width), bf16),
            jax.ShapeDtypeStruct((width, 32), bf16),
            jax.ShapeDtypeStruct((8, 2048), jnp.int32),
        ),
        in_specs=[vmem()] * 6,
        out_specs=(vmem(),) * 5,
        scratch_shapes=[
            pltpu.SemaphoreType.DMA((3, 3)),
            pltpu.SemaphoreType.DMA((3, 3)),
            pltpu.SemaphoreType.DMA((5, 8)),
            pltpu.SemaphoreType.DMA((5, 8)),
            pltpu.SemaphoreType.DMA,
            pltpu.SemaphoreType.DMA((5,)),
        ],
        compiler_params=pltpu.CompilerParams(
            collective_id=0, has_side_effects=True, vmem_limit_bytes=VMEM_LIMIT
        ),
        name="front",
    )(tok, wq, wkv, gains, router, routes)


def rows_gather_kernel(rows, small, rows_all, small_all, send, recv, small_send, small_recv, local_sem, own_sem):
    me = my_place()
    meet_all()
    smalls = []
    for step in range(1, 8):
        copy = remote(
            small, small_all.at[:, pl.ds(me * 256, 256)], small_send.at[step], small_recv.at[step], peer(step)[1]
        )
        copy.start()
        smalls.append(copy)
    own = pltpu.make_async_copy(small, small_all.at[:, pl.ds(me * 256, 256)], own_sem)
    own.start()
    started = cube_gather(rows, rows_all, send, recv, local_sem)
    own.wait()
    for copy in smalls:
        copy.wait()
    for copy in started:
        copy.wait_send()


def rows_gather(rows, small):
    return pl.pallas_call(
        rows_gather_kernel,
        out_shape=(
            jax.ShapeDtypeStruct((2, 2, 2) + rows.shape, bf16),
            jax.ShapeDtypeStruct((8, 2048), f32),
        ),
        in_specs=[vmem()] * 2,
        out_specs=(vmem(),) * 2,
        scratch_shapes=[
            pltpu.SemaphoreType.DMA((3, 3)),
            pltpu.SemaphoreType.DMA((3, 3)),
            pltpu.SemaphoreType.DMA((8,)),
            pltpu.SemaphoreType.DMA((8,)),
            pltpu.SemaphoreType.DMA,
            pltpu.SemaphoreType.DMA,
        ],
        compiler_params=pltpu.CompilerParams(
            collective_id=1, has_side_effects=True, vmem_limit_bytes=VMEM_LIMIT
        ),
        name="rows_gather",
    )(rows, small)


def exchange_kernel(count, *refs):
    ins, outs = refs[:count], refs[count : 2 * count]
    send, recv, own_sem = refs[2 * count :]
    me = my_place()
    meet_all()
    copies = []
    for k in range(count):
        for step in range(1, 8):
            place, target = peer(step)
            copy = remote(ins[k].at[place], outs[k].at[me], send.at[k, step], recv.at[k, step], target)
            copy.start()
            copies.append(copy)
        own = pltpu.make_async_copy(ins[k].at[me], outs[k].at[me], own_sem.at[k])
        own.start()
        copies.append(own)
    for copy in copies:
        copy.wait()


def exchange(values, identity):
    count = len(values)
    return pl.pallas_call(
        functools.partial(exchange_kernel, count),
        out_shape=tuple(jax.ShapeDtypeStruct(v.shape, v.dtype) for v in values),
        in_specs=[vmem()] * count,
        out_specs=(vmem(),) * count,
        scratch_shapes=[
            pltpu.SemaphoreType.DMA((count, 8)),
            pltpu.SemaphoreType.DMA((count, 8)),
            pltpu.SemaphoreType.DMA((count,)),
        ],
        compiler_params=pltpu.CompilerParams(
            collective_id=identity, has_side_effects=True, vmem_limit_bytes=VMEM_LIMIT
        ),
        name="exchange",
    )(*values)


def cube_sum_kernel(part, total, got0, got1, got2, held0, held1, send, recv):
    bits = my_bits()
    meet_all()
    started = []
    copies = []
    for k, order in enumerate(ORDERS):
        start, count = COLOURS[k]
        src = part.at[cube_index(bits, {order[0]: 1 - bits[order[0]]}, COLOURS[k])]
        dst = got0.at[cube_index(bits, {order[0]: 0}, COLOURS[k])]
        copy = remote(src, dst, send.at[0, k], recv.at[0, k], neighbour(order[0]))
        copy.start()
        copies.append(copy)
    started += copies
    later = []
    for k, order in enumerate(ORDERS):
        copies[k].wait_recv()
        rows = pl.ds(*COLOURS[k])
        for u in range(2):
            for v in range(2):
                coords = {order[0]: bits[order[0]], order[1]: u, order[2]: v}
                landed = {order[0]: 0, order[1]: u, order[2]: v}
                here = (coords[2], coords[1], coords[0], rows)
                there = (landed[2], landed[1], landed[0], rows)
                held0[u, v, rows] = (part[here].astype(f32) + got0[there].astype(f32)).astype(bf16)
        copy = remote(
            held0.at[1 - bits[order[1]], :, rows], got1.at[:, rows], send.at[1, k], recv.at[1, k], neighbour(order[1])
        )
        copy.start()
        later.append(copy)
    started += later
    last = []
    for k, order in enumerate(ORDERS):
        later[k].wait_recv()
        rows = pl.ds(*COLOURS[k])
        for v in range(2):
            held1[v, rows] = (held0[bits[order[1]], v, rows].astype(f32) + got1[v, rows].astype(f32)).astype(bf16)
        copy = remote(
            held1.at[1 - bits[order[2]], rows], got2.at[rows], send.at[2, k], recv.at[2, k], neighbour(order[2])
        )
        copy.start()
        last.append(copy)
    started += last
    for k, order in enumerate(ORDERS):
        last[k].wait_recv()
        rows = pl.ds(*COLOURS[k])
        total[rows] = held1[bits[order[2]], rows].astype(f32) + got2[rows].astype(f32)
    for copy in started:
        copy.wait_send()


def cube_sum(part, identity):
    width = part.shape[-1]
    return pl.pallas_call(
        cube_sum_kernel,
        out_shape=jax.ShapeDtypeStruct((256, width), f32),
        in_specs=[vmem()],
        out_specs=vmem(),
        scratch_shapes=[
            pltpu.VMEM((2, 2, 2, 256, width), bf16),
            pltpu.VMEM((2, 256, width), bf16),
            pltpu.VMEM((256, width), bf16),
            pltpu.VMEM((2, 2, 256, width), bf16),
            pltpu.VMEM((2, 256, width), bf16),
            pltpu.SemaphoreType.DMA((3, 3)),
            pltpu.SemaphoreType.DMA((3, 3)),
        ],
        compiler_params=pltpu.CompilerParams(
            collective_id=identity, has_side_effects=True, vmem_limit_bytes=VMEM_LIMIT
        ),
        name="cube_sum",
    )(part)


def lanes(shape):
    return lax.broadcasted_iota(jnp.int32, shape, len(shape) - 1)


def turned(u):
    low = lax.rem(lanes(u.shape), 64) < 32
    return jnp.where(low, -pltpu.roll(u, 96, 1), pltpu.roll(u, 32, 1))


def two_heads(q):
    low = lanes(q.shape) < 64
    return jnp.concatenate([jnp.where(low, q, 0.0), jnp.where(low, pltpu.roll(q, 64, 1), 0.0)], 0)


def two_heads_high(g):
    high = lanes(g.shape) >= 64
    return jnp.concatenate([jnp.where(high, pltpu.roll(g, 64, 1), 0.0), jnp.where(high, g, 0.0)], 0)


def block_probability(q_ref, kv_ref, seg_col, seg_row, s, i):
    first = max(0, i - 4) * 128
    count = (i + 1) * 128 - first
    q2 = two_heads(q_ref[s, pl.ds(i * 128, 128)].astype(f32))
    kv = kv_ref[s, pl.ds(first, count)]
    raw = dot_last((q2 * 0.125).astype(bf16), kv)
    q_place = i * 128 + lax.broadcasted_iota(jnp.int32, (128, count), 0)
    k_place = first + lanes((128, count))
    q_doc = seg_col[s, pl.ds(i * 128, 128)]
    k_doc = seg_row[s, :, pl.ds(first, count)]
    allowed = (q_place >= k_place) & (q_doc == k_doc)
    allowed = jnp.concatenate([allowed, allowed], 0)
    masked = jnp.where(allowed, raw, masked_out)
    top = jnp.max(masked, -1, keepdims=True)
    weight = jnp.exp(masked - top)
    probability = weight * (1.0 / jnp.sum(weight, -1, keepdims=True))
    return first, count, q2, kv, probability


def attention_kernel(tok, w, gain, seg_col, seg_row, cosine, sine, attn_out, q_out, kv_out, mix_out):
    gain_row = gain[...]

    def project(j, carry):
        rows = pl.ds(pl.multiple_of(j * 128, 128), 128)
        x = tok[j].astype(f32)
        scale = lax.rsqrt(jnp.mean(x * x, -1, keepdims=True) + epsilon)
        attn_in = (x * scale * gain_row).astype(bf16)
        attn_out[j] = attn_in
        both = dot(attn_in, w[...])
        c = cosine[rows]
        n = sine[rows]
        c2 = jnp.concatenate([c, c], 0)
        n2 = jnp.concatenate([n, n], 0)
        q = both[:, :128]
        kv = both[:, 128:]
        q = (q * c2 + turned(q) * n2).astype(bf16)
        kv = jnp.where(lanes(kv.shape) < 64, kv * c2 + turned(kv) * n2, kv).astype(bf16)
        for s in range(2):
            q_out[s, rows] = q[s * 128 : (s + 1) * 128]
            kv_out[s, rows] = kv[s * 128 : (s + 1) * 128]
        return carry

    lax.fori_loop(0, 8, project, 0)

    def attend(s, carry):
        for i in range(8):
            first, count, q2, kv, probability = block_probability(q_out, kv_out, seg_col, seg_row, s, i)
            mixed = dot(probability.astype(bf16), kv)
            low = lanes((128, 128)) < 64
            mix_out[i, s] = jnp.where(low, pltpu.roll(mixed[:128], 64, 1), mixed[128:]).astype(bf16)
        return carry

    lax.fori_loop(0, 2, attend, 0)


def attention(tok, w, gain, seg_col, seg_row, cosine, sine):
    width = tok.shape[-1]
    return pl.pallas_call(
        attention_kernel,
        out_shape=(
            jax.ShapeDtypeStruct((8, 256, width), bf16),
            jax.ShapeDtypeStruct((2, 1024, 128), bf16),
            jax.ShapeDtypeStruct((2, 1024, 128), bf16),
            jax.ShapeDtypeStruct((8, 2, 128, 128), bf16),
        ),
        in_specs=[vmem()] * 7,
        out_specs=(vmem(),) * 4,
        compiler_params=pltpu.CompilerParams(vmem_limit_bytes=VMEM_LIMIT),
        name="attention",
    )(tok, w, gain, seg_col, seg_row, cosine, sine)


def attention_back_kernel(
    mix_grad, attn_in, q_in, kv_in, seg_col, seg_row, cosine, sine, gq_out, gkv_out, w_grad, kv_sum, g_all
):
    def attend(s, carry):
        kv_sum[...] = jnp.zeros_like(kv_sum)
        for i in range(8):
            first, count, q2, kv, probability = block_probability(q_in, kv_in, seg_col, seg_row, s, i)
            g2 = two_heads_high(mix_grad[i, s].astype(f32)).astype(bf16)
            prob_grad = dot_last(g2, kv)
            delta = jnp.sum(probability * prob_grad, -1, keepdims=True)
            score_grad = (probability * (prob_grad - delta) * 0.125).astype(bf16)
            dq = dot(score_grad, kv)
            keys = pl.ds(first, count)
            kv_sum[keys] += dot_first(score_grad, q2.astype(bf16)) + dot_first(probability.astype(bf16), g2)
            low = lanes((128, 128)) < 64
            dq = jnp.where(low, dq[:128], pltpu.roll(dq[128:], 64, 1))
            rows = pl.ds(i * 128, 128)
            dq = (dq * cosine[rows] - turned(dq) * sine[rows]).astype(bf16)
            gq_out[i, s] = dq
            g_all[i, s, :, 0:128] = dq
        for i in range(8):
            rows = pl.ds(i * 128, 128)
            dkv = kv_sum[rows]
            low = lanes((128, 128)) < 64
            dkv = jnp.where(low, dkv * cosine[rows] - turned(dkv) * sine[rows], dkv).astype(bf16)
            gkv_out[i, s] = dkv
            g_all[i, s, :, 128:256] = dkv
        return carry

    lax.fori_loop(0, 2, attend, 0)
    w_grad[...] = dot_first(attn_in[...].reshape(2048, attn_in.shape[-1]), g_all[...].reshape(2048, 256)).astype(bf16)


def attention_back(mix_grad, attn_in, q, kv, seg_col, seg_row, cosine, sine):
    width = attn_in.shape[-1]
    return pl.pallas_call(
        attention_back_kernel,
        out_shape=(
            jax.ShapeDtypeStruct((8, 2, 128, 128), bf16),
            jax.ShapeDtypeStruct((8, 2, 128, 128), bf16),
            jax.ShapeDtypeStruct((width, 256), bf16),
        ),
        in_specs=[vmem()] * 8,
        out_specs=(vmem(),) * 3,
        scratch_shapes=[pltpu.VMEM((1024, 128), f32), pltpu.VMEM((8, 2, 128, 256), bf16)],
        compiler_params=pltpu.CompilerParams(vmem_limit_bytes=VMEM_LIMIT),
        name="attention_back",
    )(mix_grad, attn_in, q, kv, seg_col, seg_row, cosine, sine)


def turned_place(m, order):
    return sum(((m >> link) & 1) << s for s, link in enumerate(order))


def load_weight(dst, own_half, other_half, order, sem):
    me = my_place()
    core = lax.rem(lax.axis_index("group"), 2)
    copies = []
    for i in range(8):
        entry = turned_place(me ^ i, order)
        for half, src in ((core, own_half), (1 - core, other_half)):
            copy = pltpu.make_async_copy(src.at[entry], dst.at[pl.ds(i * 128 + half * 64, 64)], sem)
            copy.start()
            copies.append(copy)
    return copies


def route_kernel(mix, tok, wo_own, wo_other, gain, router, routes, residual_out, moe_in_out, weights_out, wo, sem):
    copies = load_weight(wo, wo_own, wo_other, ORDERS[0], sem)
    for copy in copies:
        copy.wait()
    residual = tok[...].astype(f32) + dot(mix[...], wo[...])
    residual_out[...] = residual
    scale = lax.rsqrt(jnp.mean(residual * residual, -1, keepdims=True) + epsilon)
    moe_in = (residual * scale * gain[...]).astype(bf16)
    moe_in_out[...] = moe_in
    logits = lax.dot_general(router[...], moe_in, (((0,), (1,)), ((), ())), preferred_element_type=f32)
    experts = lax.broadcasted_iota(jnp.int32, logits.shape, 0)
    picked = [
        jnp.sum(jnp.where(experts == routes[pl.ds(k, 1)], logits, 0.0), 0, keepdims=True) for k in range(TOP)
    ]
    picked = jnp.concatenate(picked, 0)
    weight = jnp.exp(picked - jnp.max(picked, 0, keepdims=True))
    weights_out[...] = weight / jnp.sum(weight, 0, keepdims=True)


def route(mix, tok, wo_own, wo_other, gain, router, routes):
    width = tok.shape[-1]
    return pl.pallas_call(
        route_kernel,
        out_shape=(
            jax.ShapeDtypeStruct((256, width), f32),
            jax.ShapeDtypeStruct((256, width), bf16),
            jax.ShapeDtypeStruct((8, 256), f32),
            jax.ShapeDtypeStruct((width, width), bf16),
        ),
        in_specs=[vmem(), vmem(), anywhere(), anywhere(), vmem(), vmem(), vmem()],
        out_specs=(vmem(),) * 4,
        scratch_shapes=[pltpu.SemaphoreType.DMA],
        compiler_params=pltpu.CompilerParams(vmem_limit_bytes=VMEM_LIMIT),
        name="route",
    )(mix, tok, wo_own, wo_other, gain, router, routes)


def load_rows(dst, pieces, sem):
    me = my_place()
    copies = []
    for i in range(8):
        for k, (start, count) in enumerate(COLOURS):
            entry = turned_place(me ^ i, ORDERS[k])
            copy = pltpu.make_async_copy(pieces[k].at[entry], dst.at[i, pl.ds(start, count)], sem)
            copy.start()
            copies.append(copy)
    return copies


SLOT = 4 * CAPH
SPAN = 512


def choose_rows(routes, weights, upper, plain, scaled, first_expert, block):
    columns = pl.ds(pl.multiple_of(block * SPAN, SPAN), SPAN)
    chosen = routes[:, columns]
    weight = weights[:, columns]
    masks = [jnp.max((chosen == first_expert + e).astype(f32), 0, keepdims=True) for e in range(4)]
    mask = jnp.concatenate(masks + [jnp.zeros((4, SPAN), f32)], 0)
    rank = dot(mask.astype(bf16), upper[...])
    slots = lax.broadcasted_iota(jnp.int32, (SLOT, SPAN), 0).astype(f32)
    for e in range(4):
        share = jnp.sum(jnp.where(chosen == first_expert + e, weight, 0.0), 0, keepdims=True)
        hit = (slots == rank[e : e + 1]) & (mask[e : e + 1] > 0.0)
        plain[block, e * SLOT : (e + 1) * SLOT] = jnp.where(hit, 1.0, 0.0).astype(bf16)
        scaled[block, e * SLOT : (e + 1) * SLOT] = jnp.where(hit, share, 0.0).astype(bf16)


def dispatch(x, c, plain, scaled, rows, pair_grad, block):
    pair = pl.ds(block * 2, 2)
    width = x.shape[-1]
    rows[block] = dot(plain[block], x[pair].reshape(SPAN, width)).astype(bf16)
    pair_grad[block] = dot(scaled[block], c[pair].reshape(SPAN, width)).astype(bf16)


def weight_copies(e, slot, gate_hbm, up_hbm, down_hbm, gate, up, down, sem):
    return [
        pltpu.make_async_copy(gate_hbm.at[e], gate.at[slot], sem.at[slot, 0]),
        pltpu.make_async_copy(up_hbm.at[e], up.at[slot], sem.at[slot, 1]),
        pltpu.make_async_copy(down_hbm.at[e], down.at[slot], sem.at[slot, 2]),
    ]


def expert_inner(rows_e, pair_e, gate_w, up_w, down_w):
    gate_val = dot(rows_e, gate_w)
    up_val = dot(rows_e, up_w)
    sig = 1.0 / (1.0 + jnp.exp(-gate_val))
    silu = gate_val * sig
    hidden = (silu * up_val).astype(bf16)
    hidden_grad = dot_last(pair_e, down_w)
    gate_grad = (hidden_grad * up_val * sig * (1.0 + gate_val * (1.0 - sig))).astype(bf16)
    up_grad = (hidden_grad * silu).astype(bf16)
    return hidden, gate_grad, up_grad


def experts_kernel(
    x_hbm, c0, c1, c2, routes, weights, upper, gate_hbm, up_hbm, down_hbm,
    out_part, in_part, p_out, rows_out, pair_out, hidden_out, gate_out, up_out,
    x, c, plain, scaled, rows, pair_grad, expert_out, pair_in, p_col,
    gate, up, down, hid_buf, gg_buf, ug_buf, part_buf,
    sem_x, sem_c, sem_w, sem_rows, sem_h, sem_part,
):
    first = my_place() * 4
    width = x.shape[-1]
    load_x = pltpu.make_async_copy(x_hbm, x, sem_x)
    load_x.start()
    load_c = load_rows(c, (c0, c1, c2), sem_c)
    for copy in weight_copies(0, 0, gate_hbm, up_hbm, down_hbm, gate, up, down, sem_w):
        copy.start()

    def build(block, carry):
        choose_rows(routes, weights, upper, plain, scaled, first, block)
        return carry

    lax.fori_loop(0, 4, build, 0)
    load_x.wait()
    for copy in load_c:
        copy.wait()

    def send(block, carry):
        dispatch(x, c, plain, scaled, rows, pair_grad, block)
        return carry

    lax.fori_loop(0, 4, send, 0)
    keep = [
        pltpu.make_async_copy(rows, rows_out, sem_rows.at[0]),
        pltpu.make_async_copy(pair_grad, pair_out, sem_rows.at[1]),
    ]
    for copy in keep:
        copy.start()
    keep_h = []
    for e in range(4):
        slot = e % 2
        for copy in weight_copies(e, slot, gate_hbm, up_hbm, down_hbm, gate, up, down, sem_w):
            copy.wait()
        if e < 3:
            for copy in weight_copies(e + 1, 1 - slot, gate_hbm, up_hbm, down_hbm, gate, up, down, sem_w):
                copy.start()
        mine = pl.ds(e * SLOT, SLOT)
        rows_e = rows[:, mine].reshape(4 * SLOT, width)
        pair_e = pair_grad[:, mine].reshape(4 * SLOT, width)
        hidden, gate_grad, up_grad = expert_inner(rows_e, pair_e, gate[slot], up[slot], down[slot])
        if e >= 2:
            for copy in keep_h[e - 2]:
                copy.wait()
        hid_buf[slot] = hidden
        gg_buf[slot] = gate_grad
        ug_buf[slot] = up_grad
        now = [
            pltpu.make_async_copy(hid_buf.at[slot], hidden_out.at[e], sem_h.at[slot, 0]),
            pltpu.make_async_copy(gg_buf.at[slot], gate_out.at[e], sem_h.at[slot, 1]),
            pltpu.make_async_copy(ug_buf.at[slot], up_out.at[e], sem_h.at[slot, 2]),
        ]
        for copy in now:
            copy.start()
        keep_h.append(now)
        out_e = dot(hidden, down[slot]).astype(bf16)
        p = jnp.sum(out_e.astype(f32) * pair_e.astype(f32), -1, keepdims=True)
        p_col[:, mine] = p.reshape(4, SLOT, 1)
        expert_out[:, mine] = out_e.reshape(4, SLOT, width)
        back = dot_last(gate_grad, gate[slot]) + dot_last(up_grad, up[slot])
        pair_in[:, mine] = back.astype(bf16).reshape(4, SLOT, width)
    for copies in keep_h[2:]:
        for copy in copies:
            copy.wait()

    def combine(block, carry):
        out = dot_first(scaled[block], expert_out[block]).astype(bf16)
        part_buf[0] = out.reshape(2, 256, width)
        first_copy = pltpu.make_async_copy(part_buf.at[0], out_part.at[pl.ds(block * 2, 2)], sem_part.at[0])
        first_copy.start()
        back = dot_first(plain[block], pair_in[block]).astype(bf16)
        part_buf[1] = back.reshape(2, 256, width)
        second_copy = pltpu.make_async_copy(part_buf.at[1], in_part.at[pl.ds(block * 2, 2)], sem_part.at[1])
        second_copy.start()
        for e in range(4):
            mine = pl.ds(e * SLOT, SLOT)
            p = jnp.sum(plain[block, mine].astype(f32) * p_col[block, mine], 0, keepdims=True)
            p_out[block * 2, pl.ds(e, 1)] = p[:, :256]
            p_out[block * 2 + 1, pl.ds(e, 1)] = p[:, 256:]
        first_copy.wait()
        second_copy.wait()
        return carry

    p_out[...] = jnp.zeros_like(p_out)
    lax.fori_loop(0, 4, combine, 0)
    for copy in keep:
        copy.wait()


def experts(x, c, routes, weights, upper, gate_w, up_w, down_w):
    width = x.shape[-1]
    ff = gate_w.shape[-1]
    taken = 4 * SLOT
    return pl.pallas_call(
        experts_kernel,
        out_shape=(
            jax.ShapeDtypeStruct((8, 256, width), bf16),
            jax.ShapeDtypeStruct((8, 256, width), bf16),
            jax.ShapeDtypeStruct((8, 8, 256), f32),
            jax.ShapeDtypeStruct((4, taken, width), bf16),
            jax.ShapeDtypeStruct((4, taken, width), bf16),
            jax.ShapeDtypeStruct((4, taken, ff), bf16),
            jax.ShapeDtypeStruct((4, taken, ff), bf16),
            jax.ShapeDtypeStruct((4, taken, ff), bf16),
        ),
        in_specs=[anywhere()] * 4 + [vmem()] * 3 + [anywhere()] * 3,
        out_specs=(anywhere(), anywhere(), vmem()) + (anywhere(),) * 5,
        scratch_shapes=[
            pltpu.VMEM((8, 256, width), bf16),
            pltpu.VMEM((8, 256, width), bf16),
            pltpu.VMEM((4, taken, SPAN), bf16),
            pltpu.VMEM((4, taken, SPAN), bf16),
            pltpu.VMEM((4, taken, width), bf16),
            pltpu.VMEM((4, taken, width), bf16),
            pltpu.VMEM((4, taken, width), bf16),
            pltpu.VMEM((4, taken, width), bf16),
            pltpu.VMEM((4, taken, 1), f32),
            pltpu.VMEM((2, width, ff), bf16),
            pltpu.VMEM((2, width, ff), bf16),
            pltpu.VMEM((2, ff, width), bf16),
            pltpu.VMEM((2, taken, ff), bf16),
            pltpu.VMEM((2, taken, ff), bf16),
            pltpu.VMEM((2, taken, ff), bf16),
            pltpu.VMEM((2, 2, 256, width), bf16),
            pltpu.SemaphoreType.DMA,
            pltpu.SemaphoreType.DMA,
            pltpu.SemaphoreType.DMA((2, 3)),
            pltpu.SemaphoreType.DMA((2,)),
            pltpu.SemaphoreType.DMA((2, 3)),
            pltpu.SemaphoreType.DMA((2,)),
        ],
        compiler_params=pltpu.CompilerParams(vmem_limit_bytes=VMEM_LIMIT),
        name="experts",
    )(x, *c, routes, weights, upper, gate_w, up_w, down_w)


def expert_weights_kernel(
    x0, x1, x2, c0, c1, c2, routes, weights, upper, gate_hbm, up_hbm, down_hbm,
    rows_hbm, pair_hbm, hidden_hbm, gg_hbm, ug_hbm,
    gate_grad_out, up_grad_out, down_grad_out,
    x, c, plain, scaled, rows, pair_grad, gate, up, down,
    both_rows, both_pair, both_hidden, both_gate, gate_buf, up_buf, down_buf,
    sem_x, sem_w, sem_own, sem_out,
):
    first = my_place() * 4
    side = lax.axis_index("group") // 2
    other = 1 - side
    width = x.shape[-1]
    ff = gate.shape[-1]
    load = load_rows(x, (x0, x1, x2), sem_x.at[0]) + load_rows(c, (c0, c1, c2), sem_x.at[1])
    for copy in weight_copies(0, 0, gate_hbm, up_hbm, down_hbm, gate, up, down, sem_w):
        copy.start()

    def build(block, carry):
        choose_rows(routes, weights, upper, plain, scaled, first, block)
        return carry

    lax.fori_loop(0, 4, build, 0)
    for copy in load:
        copy.wait()

    def send(block, carry):
        dispatch(x, c, plain, scaled, rows, pair_grad, block)
        return carry

    lax.fori_loop(0, 4, send, 0)
    taken = 4 * SLOT
    pending = []
    for e in range(4):
        slot = e % 2
        mine = pl.ds(e * SLOT, SLOT)
        own = [
            pltpu.make_async_copy(rows_hbm.at[:, mine], both_rows.at[side], sem_own.at[0]),
            pltpu.make_async_copy(pair_hbm.at[:, mine], both_pair.at[side], sem_own.at[1]),
            pltpu.make_async_copy(hidden_hbm.at[e], both_hidden.at[side], sem_own.at[2]),
            pltpu.make_async_copy(gg_hbm.at[e], both_gate.at[side, :, pl.ds(0, ff)], sem_own.at[3]),
            pltpu.make_async_copy(ug_hbm.at[e], both_gate.at[side, :, pl.ds(ff, ff)], sem_own.at[4]),
        ]
        for copy in own:
            copy.start()
        for copy in weight_copies(e, slot, gate_hbm, up_hbm, down_hbm, gate, up, down, sem_w):
            copy.wait()
        if e < 3:
            for copy in weight_copies(e + 1, 1 - slot, gate_hbm, up_hbm, down_hbm, gate, up, down, sem_w):
                copy.start()
        rows_e = rows[:, mine].reshape(taken, width)
        pair_e = pair_grad[:, mine].reshape(taken, width)
        hidden, gate_grad, up_grad = expert_inner(rows_e, pair_e, gate[slot], up[slot], down[slot])
        both_rows[other] = rows_e.reshape(4, SLOT, width)
        both_pair[other] = pair_e.reshape(4, SLOT, width)
        both_hidden[other] = hidden
        both_gate[other, :, 0:ff] = gate_grad
        both_gate[other, :, ff : 2 * ff] = up_grad
        for copy in own:
            copy.wait()
        if e >= 1:
            for copy in pending:
                copy.wait()
        sums = dot_first(both_rows[...].reshape(2 * taken, width), both_gate[...].reshape(2 * taken, 2 * ff))
        gate_buf[...] = sums[:, :ff].astype(bf16)
        up_buf[...] = sums[:, ff:].astype(bf16)
        down_buf[...] = dot_first(
            both_hidden[...].reshape(2 * taken, ff), both_pair[...].reshape(2 * taken, width)
        ).astype(bf16)
        pending = [
            pltpu.make_async_copy(gate_buf, gate_grad_out.at[e], sem_out.at[0]),
            pltpu.make_async_copy(up_buf, up_grad_out.at[e], sem_out.at[1]),
            pltpu.make_async_copy(down_buf, down_grad_out.at[e], sem_out.at[2]),
        ]
        for copy in pending:
            copy.start()
    for copy in pending:
        copy.wait()


def expert_weights(x, c, routes, weights, upper, gate_w, up_w, down_w, kept):
    width = gate_w.shape[1]
    ff = gate_w.shape[-1]
    taken = 4 * SLOT
    return pl.pallas_call(
        expert_weights_kernel,
        out_shape=(
            jax.ShapeDtypeStruct(gate_w.shape, bf16),
            jax.ShapeDtypeStruct(up_w.shape, bf16),
            jax.ShapeDtypeStruct(down_w.shape, bf16),
        ),
        in_specs=[anywhere()] * 6 + [vmem()] * 3 + [anywhere()] * 8,
        out_specs=(anywhere(),) * 3,
        scratch_shapes=[
            pltpu.VMEM((8, 256, width), bf16),
            pltpu.VMEM((8, 256, width), bf16),
            pltpu.VMEM((4, taken, SPAN), bf16),
            pltpu.VMEM((4, taken, SPAN), bf16),
            pltpu.VMEM((4, taken, width), bf16),
            pltpu.VMEM((4, taken, width), bf16),
            pltpu.VMEM((2, width, ff), bf16),
            pltpu.VMEM((2, width, ff), bf16),
            pltpu.VMEM((2, ff, width), bf16),
            pltpu.VMEM((2, 4, SLOT, width), bf16),
            pltpu.VMEM((2, 4, SLOT, width), bf16),
            pltpu.VMEM((2, taken, ff), bf16),
            pltpu.VMEM((2, taken, 2 * ff), bf16),
            pltpu.VMEM((width, ff), bf16),
            pltpu.VMEM((width, ff), bf16),
            pltpu.VMEM((ff, width), bf16),
            pltpu.SemaphoreType.DMA((2,)),
            pltpu.SemaphoreType.DMA((2, 3)),
            pltpu.SemaphoreType.DMA((5,)),
            pltpu.SemaphoreType.DMA((3,)),
        ],
        compiler_params=pltpu.CompilerParams(vmem_limit_bytes=VMEM_LIMIT),
        name="expert_weights",
    )(*x, *c, routes, weights, upper, gate_w, up_w, down_w, *kept)


def norm_back(values, gain, grad):
    scale = lax.rsqrt(jnp.mean(values * values, -1, keepdims=True) + epsilon)
    inner = grad * gain
    along = jnp.mean(values * inner, -1, keepdims=True)
    out = scale * inner - values * (scale * scale * scale * along)
    gain_grad = jnp.sum(grad * values * scale, 0, keepdims=True)
    return out, gain_grad


def route_back_kernel(
    cot, residual, moe_in_sum, p_all, routes, weights, router, moe_in, gain, wo, mix,
    residual_grad_out, mix_grad_out, router_grad, gain_grad_out, wo_grad,
):
    experts_ids = lax.broadcasted_iota(jnp.int32, (32, 256), 0)
    dense = jnp.zeros((32, 256), f32)
    for k in range(TOP):
        dense = dense + jnp.where(experts_ids == routes[pl.ds(k, 1)], weights[pl.ds(k, 1)], 0.0)
    p = p_all[...]
    logit_grad = (p - dense * jnp.sum(p, 0, keepdims=True)).astype(bf16)
    moe_in_grad = moe_in_sum[...] + lax.dot_general(
        logit_grad, router[...], (((0,), (1,)), ((), ())), preferred_element_type=f32
    )
    router_grad[...] = lax.dot_general(
        moe_in[...], logit_grad, (((0,), (1,)), ((), ())), preferred_element_type=f32
    ).astype(bf16)
    part, gain_grad = norm_back(residual[...], gain[...], moe_in_grad)
    gain_grad_out[...] = gain_grad
    residual_grad = cot[...].astype(f32) + part
    residual_grad_out[...] = residual_grad
    low = residual_grad.astype(bf16)
    mix_grad = dot_last(low, wo[...]).astype(bf16)
    for j in range(8):
        mix_grad_out[j] = mix_grad[:, j * 128 : (j + 1) * 128].reshape(2, 128, 128)
    wo_grad[...] = dot_first(mix[...], low).astype(bf16)


def route_back(cot, residual, moe_in_sum, p_all, routes, weights, router, moe_in, gain, wo, mix):
    width = cot.shape[-1]
    return pl.pallas_call(
        route_back_kernel,
        out_shape=(
            jax.ShapeDtypeStruct((256, width), f32),
            jax.ShapeDtypeStruct((8, 2, 128, 128), bf16),
            jax.ShapeDtypeStruct((width, 32), bf16),
            jax.ShapeDtypeStruct((1, width), f32),
            jax.ShapeDtypeStruct((width, width), bf16),
        ),
        in_specs=[vmem()] * 11,
        out_specs=(vmem(),) * 5,
        compiler_params=pltpu.CompilerParams(vmem_limit_bytes=VMEM_LIMIT),
        name="route_back",
    )(cot, residual, moe_in_sum, p_all, routes, weights, router, moe_in, gain, wo, mix)


def token_back_kernel(
    gq, gkv, wq_own, wq_other, wkv_own, wkv_other, tok, gain, residual_grad, token_grad, gain_grad_out, wq, wkv, sem
):
    copies = load_weight(wq, wq_own, wq_other, ORDERS[1], sem.at[0])
    copies += load_weight(wkv, wkv_own, wkv_other, ORDERS[2], sem.at[1])
    for copy in copies:
        copy.wait()
    grad = dot_last(gq[...], wq[...]) + dot_last(gkv[...], wkv[...])
    part, gain_grad = norm_back(tok[...].astype(f32), gain[...], grad)
    gain_grad_out[...] = gain_grad
    token_grad[...] = residual_grad[...] + part


def token_back(gq, gkv, wq, wkv, tok, gain, residual_grad):
    width = tok.shape[-1]
    return pl.pallas_call(
        token_back_kernel,
        out_shape=(jax.ShapeDtypeStruct((256, width), f32), jax.ShapeDtypeStruct((1, width), f32)),
        in_specs=[vmem()] * 2 + [anywhere()] * 4 + [vmem()] * 3,
        out_specs=(vmem(),) * 2,
        scratch_shapes=[
            pltpu.VMEM((width, width), bf16),
            pltpu.VMEM((width, width), bf16),
            pltpu.SemaphoreType.DMA((2,)),
        ],
        compiler_params=pltpu.CompilerParams(vmem_limit_bytes=VMEM_LIMIT),
        name="token_back",
    )(gq, gkv, *wq, *wkv, tok, gain, residual_grad)


def sum_halves(value, link, axis):
    own = jnp.asarray(axis)
    keep = lax.dynamic_index_in_dim(value, own, 0, keepdims=False)
    give = lax.dynamic_index_in_dim(value, 1 - own, 0, keepdims=False)
    return (keep.astype(f32) + swap(give, link).astype(f32)).astype(bf16)


def rows_sum_swaps(part):
    blk = lax.axis_index("blk")
    part = sum_halves(part, 2, blk // 2)
    part = sum_halves(part, 1, lax.rem(blk, 2))
    return sum_halves(part, 0, lax.axis_index("head"))


def rows_sum_colours(part):
    blk = lax.axis_index("blk")
    bits = (lax.axis_index("head"), lax.rem(blk, 2), blk // 2)
    shares = []
    for k, (start, count) in enumerate(COLOURS):
        piece = part[:, :, :, start : start + count]
        axes = {2: 0, 1: 1, 0: 2}
        order = ORDERS[k]
        piece = jnp.transpose(piece, tuple(axes[link] for link in order) + (3, 4))
        for link in order:
            piece = sum_halves(piece, link, bits[link])
        shares.append(piece)
    return jnp.concatenate(shares, 0)


def group_sum(value):
    value = (value.astype(f32) + swap(value, 4).astype(f32)).astype(bf16)
    return value.astype(f32) + swap(value, 3).astype(f32)


def fast_on_device(
    tokens, segments, routes, cotangent, attn_gain, moe_gain, query_weight, key_projection_matrix,
    value_projection_matrix, out_weight, router_weight, gate_weight, up_weight, down_weight,
):
    width = tokens.shape[-1]
    core = lax.rem(lax.axis_index("group"), 2)
    tok = tokens.reshape(256, width)
    cot = cotangent.reshape(256, width)
    wkv = jnp.concatenate(
        [key_projection_matrix.reshape(128, 8, 64), value_projection_matrix.reshape(128, 8, 64)], -1
    ).reshape(128, 1024)
    gains = jnp.concatenate([attn_gain[None], moe_gain[None], jnp.zeros((14, 128), bf16)], 0)
    my_routes = routes.reshape(256, TOP).T
    tok_all, w_slice, gains_all, router_all, routes_all = front(tok, query_weight, wkv, gains, router_weight, my_routes)
    attn_gain_row = gains_all[0:1].astype(f32)
    moe_gain_row = gains_all[1:2].astype(f32)
    frequency = rope_base ** (-(jnp.arange(128) % 32).astype(f32) * 2.0 / 64)
    angle = jnp.arange(1024, dtype=f32)[:, None] * frequency[None, :]
    cosine, sine = jnp.cos(angle), jnp.sin(angle)
    seg_col, seg_row = segments[:, :, None], segments[:, None, :]

    tok_done, cot_later, wo_later, wq_later, wkv_later = lax.optimization_barrier(
        (tok_all, cot, out_weight, query_weight, wkv)
    )

    def weight_halves(weight, order):
        mine = lax.dynamic_slice_in_dim(weight, core * 64, 64, 0)
        own = gather_swaps(mine, order)
        return own, swap(own, 4)

    wo_halves = weight_halves(wo_later, ORDERS[0])
    wq_halves = weight_halves(wq_later, ORDERS[1])
    wkv_halves = weight_halves(wkv_later, ORDERS[2])
    cot_all = gather_rows(cot_later)
    cot_mirror = gather_rows(swap(cot_later, 3))
    routes_mirror = swap(routes_all, 3)

    attn_in, q, kv, mix = attention(
        tok_done.reshape(8, 256, width), w_slice, attn_gain_row, seg_col, seg_row, cosine, sine
    )
    (mix_rows,) = exchange((mix,), 2)
    attn_mix = jnp.transpose(mix_rows, (1, 2, 0, 3)).reshape(256, 1024)
    residual, moe_in, weights, wo = route(attn_mix, tok, *wo_halves, moe_gain_row, router_all, my_routes)
    moe_all, weights_all = rows_gather(moe_in, weights)
    moe_mirror = gather_rows(swap(moe_in, 3))
    weights_mirror = swap(weights_all, 3)
    places = jnp.arange(SPAN)
    upper = (places[:, None] < places[None, :]).astype(bf16)
    out_part, in_part, p_part, *kept = experts(
        moe_all.reshape(8, 256, width), cot_all, routes_all, weights_all, upper, gate_weight, up_weight, down_weight
    )
    in_sum = cube_sum(in_part.reshape(2, 2, 2, 256, width), 3)
    (p_rows,) = exchange((p_part,), 4)
    p_all = p_rows[:, :4].reshape(32, 256)
    out_sum = rows_sum_colours(out_part.reshape(2, 2, 2, 256, width))
    mixed = (residual + out_sum.astype(f32)).astype(bf16).reshape(tokens.shape)
    residual_grad, mix_grad, router_grad, moe_gain_grad, wo_grad = route_back(
        cot, residual, in_sum, p_all, my_routes, weights, router_all, moe_in, moe_gain_row, wo, attn_mix
    )
    (mix_grad_rows,) = exchange((mix_grad,), 5)
    gq, gkv, w_grad = attention_back(mix_grad_rows_order(mix_grad_rows), attn_in, q, kv, seg_col, seg_row, cosine, sine)
    gq_rows, gkv_rows = exchange((gq, gkv), 6)
    gq_rows = jnp.transpose(gq_rows, (1, 2, 0, 3)).reshape(256, 1024)
    gkv_rows = jnp.transpose(gkv_rows, (1, 2, 0, 3)).reshape(256, 1024)
    token_grad, attn_gain_grad = token_back(
        gq_rows, gkv_rows, wq_halves, wkv_halves, tok, attn_gain_row, residual_grad
    )
    gate_part, up_part, down_part = expert_weights(
        moe_mirror, cot_mirror, routes_mirror, weights_mirror, upper, gate_weight, up_weight, down_weight, kept
    )
    expert_grads = tuple(part.astype(f32) + swap(part, 4).astype(f32) for part in (gate_part, up_part, down_part))
    (w_rows,) = exchange((w_grad.reshape(8, 128, 256),), 7)
    w_sum = group_sum(jnp.transpose(w_rows, (1, 0, 2)))
    query_grad = w_sum[:, :, :128].reshape(128, 1024)
    key_grad = w_sum[:, :, 128:192].reshape(128, 512)
    value_grad = w_sum[:, :, 192:].reshape(128, 512)
    wo_sum = group_sum(rows_sum_swaps(wo_grad.reshape(2, 2, 2, 128, 1024)))
    small = jnp.concatenate(
        [router_grad, moe_gain_grad.reshape(1024, 1).astype(bf16), attn_gain_grad.reshape(1024, 1).astype(bf16)], 1
    )
    small_sum = group_sum(rows_sum_swaps(small.reshape(2, 2, 2, 128, 34)))
    return (
        mixed, token_grad.reshape(tokens.shape), small_sum[:, 33], small_sum[:, 32], query_grad, key_grad, value_grad,
        wo_sum, small_sum[:, :32], *expert_grads,
    )


def mix_grad_rows_order(rows):
    return rows


def fits(mesh):
    return dict(mesh.shape) == {"group": 4, "blk": 4, "head": 2}


def solution(mesh):
    placed = (
        P("group", ("blk", "head"), None),
        P("group", None),
        P("group", ("blk", "head"), None),
        P("group", ("blk", "head"), None),
        P(("blk", "head")),
        P(("blk", "head")),
        P(("blk", "head"), None),
        P(("blk", "head"), None),
        P(("blk", "head"), None),
        P(("blk", "head"), None),
        P(("blk", "head"), None),
        P(("blk", "head"), None, None),
        P(("blk", "head"), None, None),
        P(("blk", "head"), None, None),
    )
    return jax.shard_map(
        fast_on_device if fits(mesh) else on_device,
        mesh=mesh,
        in_specs=placed,
        out_specs=(
            P("group", ("blk", "head"), None),
            P("group", ("blk", "head"), None),
            P(("blk", "head")),
            P(("blk", "head")),
            P(("blk", "head"), None),
            P(("blk", "head"), None),
            P(("blk", "head"), None),
            P(("blk", "head"), None),
            P(("blk", "head"), None),
            P(("blk", "head"), None, None),
            P(("blk", "head"), None, None),
            P(("blk", "head"), None, None),
        ),
        check_vma=False,
    )
```

```python
import functools

import jax
import jax.numpy as jnp
import numpy as np
from jax import lax
from jax.experimental import pallas as pl
from jax.experimental.pallas import tpu as pltpu
from jax.sharding import PartitionSpec as P

QUERY_HEADS = 16
KEY_VALUE_HEADS = 8
HEAD_SIZE = 64
TOP = 8
CAPH = 36


epsilon = 1e-05
rope_base = 10000.0
masked_out = -1e30
key_block = 512


def rms_norm(values, gain_vec):
    return values * lax.rsqrt(jnp.mean(values * values, -1, keepdims=True) + epsilon) * gain_vec


def rotary_embedding(field_vals, places, turn_sign):
    half_dim = field_vals.shape[-1] // 2
    frequency = rope_base ** (-jnp.arange(half_dim, dtype=jnp.float32) * 2.0 / field_vals.shape[-1])
    angles = places.astype(jnp.float32)[:, None] * frequency[None, :]
    cosine = jnp.cos(angles)[:, None, :]
    sine_vals = turn_sign * jnp.sin(angles)[:, None, :]
    first_half = field_vals[..., :half_dim]
    second = field_vals[..., half_dim:]
    return jnp.concatenate(
        [first_half * cosine - second * sine_vals, second * cosine + first_half * sine_vals], -1
    )


def add_rows(running, addend, row_start):
    current = lax.dynamic_slice_in_dim(running, row_start, addend.shape[1], 1)
    return lax.dynamic_update_slice_in_dim(running, current + addend, row_start, 1)


def on_device(
    tokens,
    segments,
    routes,
    cotangent,
    attn_gain,
    moe_gain,
    query_weight,
    key_projection_matrix,
    value_projection_matrix,
    out_weight,
    router_weight,
    gate_weight,
    up_weight,
    down_weight,
):
    head_groups, number_of_rows, width_dim = tokens.shape
    query_per_key_head = QUERY_HEADS // KEY_VALUE_HEADS
    shared_head_count = lax.axis_size("head")
    query_rows = number_of_rows * shared_head_count
    grouped_keys = KEY_VALUE_HEADS // shared_head_count
    scale_val = HEAD_SIZE ** (-0.5)
    number_of_tokens = head_groups * number_of_rows
    seq_length = lax.axis_size("blk") * query_rows
    cycle_index = lax.axis_index("blk")
    local_placement = (
        cycle_index * shared_head_count + lax.axis_index("head")
    ) * number_of_rows + jnp.arange(number_of_rows, dtype=jnp.int32)
    own_start = cycle_index * query_rows
    query_place = own_start + jnp.arange(query_rows, dtype=jnp.int32)
    query_doc = lax.dynamic_slice_in_dim(segments, own_start, query_rows, 1)
    query_full, key_full, value_full, out_full, router_full, gain_attn, gain_moe = (
        lax.all_gather(query_weight, ("blk", "head"), axis=0, tiled=True),
        lax.all_gather(key_projection_matrix, ("blk", "head"), axis=0, tiled=True),
        lax.all_gather(value_projection_matrix, ("blk", "head"), axis=0, tiled=True),
        lax.all_gather(out_weight, ("blk", "head"), axis=0, tiled=True),
        lax.all_gather(router_weight, ("blk", "head"), axis=0, tiled=True),
        lax.all_gather(attn_gain, ("blk", "head"), axis=0, tiled=True),
        lax.all_gather(moe_gain, ("blk", "head"), axis=0, tiled=True),
    )
    flat_rows = tokens.reshape(number_of_tokens, width_dim).astype(jnp.float32)
    attn_normed, attn_pull = jax.vjp(rms_norm, flat_rows, gain_attn.astype(jnp.float32))
    attn_in = attn_normed.astype(jnp.bfloat16)
    query_pre = jnp.dot(attn_in, query_full, preferred_element_type=jnp.float32)
    key_before_rotary = jnp.dot(attn_in, key_full, preferred_element_type=jnp.float32)
    value_low = (
        jnp.dot(attn_in, value_full, preferred_element_type=jnp.float32)
        .astype(jnp.bfloat16)
        .reshape(head_groups, number_of_rows, KEY_VALUE_HEADS * HEAD_SIZE)
    )
    query_low = (
        rotary_embedding(
            query_pre.reshape(head_groups, number_of_rows, QUERY_HEADS, HEAD_SIZE),
            local_placement,
            1.0,
        )
        .astype(jnp.bfloat16)
        .reshape(head_groups, number_of_rows, QUERY_HEADS * HEAD_SIZE)
    )
    key_low = (
        rotary_embedding(
            key_before_rotary.reshape(head_groups, number_of_rows, KEY_VALUE_HEADS, HEAD_SIZE),
            local_placement,
            1.0,
        )
        .astype(jnp.bfloat16)
        .reshape(head_groups, number_of_rows, KEY_VALUE_HEADS * HEAD_SIZE)
    )
    query_split, key_split, value_split = (
        lax.all_to_all(query_low, "head", split_axis=2, concat_axis=1, tiled=True),
        lax.all_to_all(key_low, "head", split_axis=2, concat_axis=1, tiled=True),
        lax.all_to_all(value_low, "head", split_axis=2, concat_axis=1, tiled=True),
    )
    query_vectors = query_split.reshape(
        head_groups, query_rows, grouped_keys, query_per_key_head, HEAD_SIZE
    )

    def key_view(source, offset, sub_rows):
        return lax.dynamic_slice_in_dim(source, offset, sub_rows, 1).reshape(
            head_groups, sub_rows, grouped_keys, HEAD_SIZE
        )

    def scored_at(query_part, key_row_block, q_place, q_doc, key_start, sub_rows):
        raw_scores = (
            jnp.einsum(
                "bqgrd,bkgd->bqgrk", query_part, key_row_block, preferred_element_type=jnp.float32
            )
            * scale_val
        )
        key_place = key_start + jnp.arange(sub_rows, dtype=jnp.int32)
        key_doc = lax.dynamic_slice_in_dim(segments, key_start, sub_rows, 1)
        allowed = (q_place[None, :, None] >= key_place[None, None, :]) & (
            q_doc[:, :, None] == key_doc[:, None, :]
        )
        return (raw_scores, allowed[:, :, None, None, :])

    def scored(key_row_block, key_start, sub_rows):
        return scored_at(query_vectors, key_row_block, query_place, query_doc, key_start, sub_rows)

    stats_shape = (head_groups, query_rows, grouped_keys, query_per_key_head)
    init_state = (
        jnp.full(stats_shape, masked_out, jnp.float32),
        jnp.zeros(stats_shape, jnp.float32),
        jnp.zeros(stats_shape + (HEAD_SIZE,), jnp.float32),
    )
    key_all, value_all = (
        lax.all_gather(key_split, "blk", axis=1, tiled=True),
        lax.all_gather(value_split, "blk", axis=1, tiled=True),
    )
    fold_state = init_state
    total_rows = key_all.shape[1]
    sub_rows = key_block

    def forward_one_block(block_state, block_index):
        offset = block_index * sub_rows
        key_row_block = key_view(key_all, offset, sub_rows)
        value_row_block = key_view(value_all, offset, sub_rows)
        raw_scores, allowed = scored(key_row_block, 0 + offset, sub_rows)
        running_max, running_sum, running_acc = block_state
        masked = jnp.where(allowed, raw_scores, masked_out)
        new_max = jnp.maximum(running_max, jnp.max(masked, -1))
        shrink = jnp.exp(running_max - new_max)
        weights_soft = jnp.where(allowed, jnp.exp(masked - new_max[..., None]), 0.0)
        new_sum = running_sum * shrink + jnp.sum(weights_soft, -1)
        new_acc = running_acc * shrink[..., None] + jnp.einsum(
            "bqgrk,bkgd->bqgrd",
            weights_soft.astype(jnp.bfloat16),
            value_row_block,
            preferred_element_type=jnp.float32,
        )
        return ((new_max, new_sum, new_acc), None)

    fold_state, unused = lax.scan(
        forward_one_block, fold_state, jnp.arange(total_rows // sub_rows, dtype=jnp.int32)
    )
    running_max, running_sum, running_acc = fold_state
    mix_heads = running_acc / running_sum[..., None]
    log_total = running_max + jnp.log(running_sum)
    mix_low = mix_heads.astype(jnp.bfloat16).reshape(
        head_groups, query_rows, grouped_keys * query_per_key_head * HEAD_SIZE
    )
    mix_tokens = lax.all_to_all(mix_low, "head", split_axis=1, concat_axis=2, tiled=True)
    attn_mix = mix_tokens.reshape(number_of_tokens, QUERY_HEADS * HEAD_SIZE)
    residual = flat_rows + jnp.dot(attn_mix, out_full, preferred_element_type=jnp.float32)
    moe_normed, moe_pull = jax.vjp(rms_norm, residual, gain_moe.astype(jnp.float32))
    moe_in = moe_normed.astype(jnp.bfloat16)
    logits = jnp.dot(moe_in, router_full, preferred_element_type=jnp.float32)
    route_flat = routes.reshape(number_of_tokens, TOP)
    experts_all = router_full.shape[1]
    choose = route_flat[:, :, None] == jnp.arange(experts_all, dtype=jnp.int32)[None, None, :]
    choose_float = choose.astype(jnp.float32)
    picked_logits = jnp.einsum("nke,ne->nk", choose_float, logits)
    route_weights = jax.nn.softmax(picked_logits, axis=-1)
    choose_whole = choose.astype(jnp.int32).reshape(head_groups, number_of_rows * TOP, experts_all)
    slot_rank = jnp.sum(jnp.cumsum(choose_whole, 1) * choose_whole, -1) - 1
    slot_index = (slot_rank + jnp.arange(head_groups, dtype=jnp.int32)[:, None] * CAPH).reshape(-1)
    targets = route_flat.reshape(-1)
    lane_count = head_groups * CAPH
    outgoing = (
        jnp.zeros((experts_all, lane_count, width_dim), jnp.bfloat16)
        .at[targets, slot_index]
        .set(jnp.repeat(moe_in, TOP, axis=0))
    )
    arrived = lax.all_to_all(outgoing, ("blk", "head"), split_axis=0, concat_axis=1, tiled=True)
    gate_val = jnp.einsum("end,edf->enf", arrived, gate_weight, preferred_element_type=jnp.float32)
    up_val = jnp.einsum("end,edf->enf", arrived, up_weight, preferred_element_type=jnp.float32)
    hidden_low = (jax.nn.silu(gate_val) * up_val).astype(jnp.bfloat16)
    expert_out = jnp.einsum(
        "enf,efd->end", hidden_low, down_weight, preferred_element_type=jnp.float32
    ).astype(jnp.bfloat16)
    returned = lax.all_to_all(expert_out, ("blk", "head"), split_axis=1, concat_axis=0, tiled=True)
    picked_rows = returned[targets, slot_index].reshape(number_of_tokens, TOP, width_dim)
    moe_out = jnp.einsum(
        "nk,nkd->nd", route_weights, picked_rows, preferred_element_type=jnp.float32
    )
    mixed = (
        (residual + moe_out).astype(jnp.bfloat16).reshape(head_groups, number_of_rows, width_dim)
    )
    grad_full = cotangent.reshape(number_of_tokens, width_dim).astype(jnp.float32)
    weight_grad = jnp.einsum(
        "nkd,nd->nk", picked_rows, grad_full, preferred_element_type=jnp.float32
    )
    pair_grad = (
        (route_weights[:, :, None] * grad_full[:, None, :])
        .astype(jnp.bfloat16)
        .reshape(number_of_tokens * TOP, width_dim)
    )
    grad_outgoing = jnp.zeros_like(outgoing).at[targets, slot_index].set(pair_grad)
    grad_arrived = lax.all_to_all(
        grad_outgoing, ("blk", "head"), split_axis=0, concat_axis=1, tiled=True
    )
    grad_hidden = jnp.einsum(
        "end,efd->enf", grad_arrived, down_weight, preferred_element_type=jnp.float32
    )
    sigmoid_val = jax.nn.sigmoid(gate_val)
    grad_gate = (
        grad_hidden * up_val * sigmoid_val * (1.0 + gate_val * (1.0 - sigmoid_val))
    ).astype(jnp.bfloat16)
    grad_up = (grad_hidden * gate_val * sigmoid_val).astype(jnp.bfloat16)
    down_weight_grad = jnp.einsum(
        "enf,end->efd", hidden_low, grad_arrived, preferred_element_type=jnp.float32
    )
    gate_weight_grad = jnp.einsum(
        "end,enf->edf", arrived, grad_gate, preferred_element_type=jnp.float32
    )
    up_weight_grad = jnp.einsum(
        "end,enf->edf", arrived, grad_up, preferred_element_type=jnp.float32
    )
    pair_back = (
        jnp.einsum("enf,edf->end", grad_gate, gate_weight, preferred_element_type=jnp.float32)
        + jnp.einsum("enf,edf->end", grad_up, up_weight, preferred_element_type=jnp.float32)
    ).astype(jnp.bfloat16)
    grad_returned = lax.all_to_all(
        pair_back, ("blk", "head"), split_axis=1, concat_axis=0, tiled=True
    )
    moe_in_grad = jnp.sum(
        grad_returned[targets, slot_index].reshape(number_of_tokens, TOP, width_dim),
        axis=1,
        dtype=jnp.float32,
    )
    mean_term = jnp.sum(route_weights * weight_grad, -1, keepdims=True)
    logit_grad = jnp.einsum("nk,nke->ne", route_weights * (weight_grad - mean_term), choose_float)
    router_grad = jnp.dot(moe_in.T, logit_grad, preferred_element_type=jnp.float32)
    moe_in_grad = moe_in_grad + jnp.dot(
        logit_grad, router_full.T, preferred_element_type=jnp.float32
    )
    residual_part, moe_gain_grad = moe_pull(moe_in_grad)
    residual_grad = grad_full + residual_part
    out_grad_low = residual_grad.astype(jnp.bfloat16)
    out_weight_grad = jnp.dot(attn_mix.T, out_grad_low, preferred_element_type=jnp.float32)
    mix_grad = (
        jnp.dot(out_grad_low, out_full.T, preferred_element_type=jnp.float32)
        .astype(jnp.bfloat16)
        .reshape(head_groups, number_of_rows, QUERY_HEADS * HEAD_SIZE)
    )
    mix_grad_heads = lax.all_to_all(
        mix_grad, "head", split_axis=2, concat_axis=1, tiled=True
    ).reshape(head_groups, query_rows, grouped_keys, query_per_key_head, HEAD_SIZE)
    delta_term = jnp.sum(mix_grad_heads.astype(jnp.float32) * mix_heads, -1)
    query_zero = jnp.zeros(stats_shape + (HEAD_SIZE,), jnp.float32)
    back_init = (
        query_zero,
        jnp.zeros((head_groups, seq_length, grouped_keys, HEAD_SIZE), jnp.float32),
        jnp.zeros((head_groups, seq_length, grouped_keys, HEAD_SIZE), jnp.float32),
    )
    fold_state = back_init
    total_rows = key_all.shape[1]

    def backward_one_block(block_state, block_index):
        offset = block_index * key_block
        key_start = 0 + offset
        key_row_block = key_view(key_all, offset, key_block)
        value_row_block = key_view(value_all, offset, key_block)
        raw_scores, allowed = scored(key_row_block, key_start, key_block)
        masked = jnp.where(allowed, raw_scores, masked_out)
        probability = jnp.where(allowed, jnp.exp(masked - log_total[..., None]), 0.0)
        prob_grad = jnp.einsum(
            "bqgrd,bkgd->bqgrk", mix_grad_heads, value_row_block, preferred_element_type=jnp.float32
        )
        score_grad = (probability * (prob_grad - delta_term[..., None]) * scale_val).astype(
            jnp.bfloat16
        )
        grad_query = block_state[0] + jnp.einsum(
            "bqgrk,bkgd->bqgrd", score_grad, key_row_block, preferred_element_type=jnp.float32
        )
        value_part_grad = jnp.einsum(
            "bqgrk,bqgrd->bkgd",
            probability.astype(jnp.bfloat16),
            mix_grad_heads,
            preferred_element_type=jnp.float32,
        )
        key_part_grad = jnp.einsum(
            "bqgrk,bqgrd->bkgd", score_grad, query_vectors, preferred_element_type=jnp.float32
        )
        grad_keys = add_rows(block_state[1], key_part_grad, key_start)
        grad_values = add_rows(block_state[2], value_part_grad, key_start)
        return ((grad_query, grad_keys, grad_values), None)

    fold_state, unused = lax.scan(
        backward_one_block, fold_state, jnp.arange(total_rows // key_block, dtype=jnp.int32)
    )
    grad_query, grad_keys, grad_values = fold_state
    key_own, value_own = (
        lax.psum_scatter(
            grad_keys.reshape(head_groups, seq_length, grouped_keys * HEAD_SIZE).astype(
                jnp.bfloat16
            ),
            "blk",
            scatter_dimension=1,
            tiled=True,
        ).astype(jnp.float32),
        lax.psum_scatter(
            grad_values.reshape(head_groups, seq_length, grouped_keys * HEAD_SIZE).astype(
                jnp.bfloat16
            ),
            "blk",
            scatter_dimension=1,
            tiled=True,
        ).astype(jnp.float32),
    )
    query_grad_low = (
        rotary_embedding(
            grad_query.reshape(
                head_groups, query_rows, grouped_keys * query_per_key_head, HEAD_SIZE
            ),
            query_place,
            -1.0,
        )
        .astype(jnp.bfloat16)
        .reshape(head_groups, query_rows, grouped_keys * query_per_key_head * HEAD_SIZE)
    )
    key_grad_low = (
        rotary_embedding(
            key_own.reshape(head_groups, query_rows, grouped_keys, HEAD_SIZE), query_place, -1.0
        )
        .astype(jnp.bfloat16)
        .reshape(head_groups, query_rows, grouped_keys * HEAD_SIZE)
    )
    value_grad_low = value_own.astype(jnp.bfloat16)
    query_back, key_pullback, value_pullback = (
        lax.all_to_all(query_grad_low, "head", split_axis=1, concat_axis=2, tiled=True),
        lax.all_to_all(key_grad_low, "head", split_axis=1, concat_axis=2, tiled=True),
        lax.all_to_all(value_grad_low, "head", split_axis=1, concat_axis=2, tiled=True),
    )
    query_flat = query_back.reshape(number_of_tokens, QUERY_HEADS * HEAD_SIZE)
    flattened_keys = key_pullback.reshape(number_of_tokens, KEY_VALUE_HEADS * HEAD_SIZE)
    flattened_values = value_pullback.reshape(number_of_tokens, KEY_VALUE_HEADS * HEAD_SIZE)
    query_weight_grad = jnp.dot(attn_in.T, query_flat, preferred_element_type=jnp.float32)
    key_weight_grad = jnp.dot(attn_in.T, flattened_keys, preferred_element_type=jnp.float32)
    value_weight_grad = jnp.dot(attn_in.T, flattened_values, preferred_element_type=jnp.float32)
    attn_in_grad = (
        jnp.dot(query_flat, query_full.T, preferred_element_type=jnp.float32)
        + jnp.dot(flattened_keys, key_full.T, preferred_element_type=jnp.float32)
        + jnp.dot(flattened_values, value_full.T, preferred_element_type=jnp.float32)
    )
    input_part, attn_gain_grad = attn_pull(attn_in_grad)
    token_grad = (residual_grad + input_part).reshape(head_groups, number_of_rows, width_dim)
    (
        query_shard,
        key_shard,
        value_shard,
        out_shard,
        router_shard,
        attn_gain_shard,
        moe_gain_shard,
    ) = (
        lax.psum_scatter(
            query_weight_grad.astype(jnp.bfloat16), ("blk", "head"), scatter_dimension=0, tiled=True
        ).astype(jnp.float32),
        lax.psum_scatter(
            key_weight_grad.astype(jnp.bfloat16), ("blk", "head"), scatter_dimension=0, tiled=True
        ).astype(jnp.float32),
        lax.psum_scatter(
            value_weight_grad.astype(jnp.bfloat16), ("blk", "head"), scatter_dimension=0, tiled=True
        ).astype(jnp.float32),
        lax.psum_scatter(
            out_weight_grad.astype(jnp.bfloat16), ("blk", "head"), scatter_dimension=0, tiled=True
        ).astype(jnp.float32),
        lax.psum_scatter(
            router_grad.astype(jnp.bfloat16), ("blk", "head"), scatter_dimension=0, tiled=True
        ).astype(jnp.float32),
        lax.psum_scatter(
            attn_gain_grad.astype(jnp.bfloat16), ("blk", "head"), scatter_dimension=0, tiled=True
        ).astype(jnp.float32),
        lax.psum_scatter(
            moe_gain_grad.astype(jnp.bfloat16), ("blk", "head"), scatter_dimension=0, tiled=True
        ).astype(jnp.float32),
    )
    summed = (
        lax.psum(query_shard.astype(jnp.bfloat16), "group").astype(jnp.float32),
        lax.psum(key_shard.astype(jnp.bfloat16), "group").astype(jnp.float32),
        lax.psum(value_shard.astype(jnp.bfloat16), "group").astype(jnp.float32),
        lax.psum(out_shard.astype(jnp.bfloat16), "group").astype(jnp.float32),
        lax.psum(router_shard.astype(jnp.bfloat16), "group").astype(jnp.float32),
        lax.psum(attn_gain_shard.astype(jnp.bfloat16), "group").astype(jnp.float32),
        lax.psum(moe_gain_shard.astype(jnp.bfloat16), "group").astype(jnp.float32),
        lax.psum(gate_weight_grad.astype(jnp.bfloat16), "group").astype(jnp.float32),
        lax.psum(up_weight_grad.astype(jnp.bfloat16), "group").astype(jnp.float32),
        lax.psum(down_weight_grad.astype(jnp.bfloat16), "group").astype(jnp.float32),
    )
    return (
        mixed,
        token_grad,
        summed[5],
        summed[6],
        summed[0],
        summed[1],
        summed[2],
        summed[3],
        summed[4],
        summed[7],
        summed[8],
        summed[9],
    )


bf16 = jnp.bfloat16
f32 = jnp.float32
MESH_ID = pl.DeviceIdType.MESH
VMEM_LIMIT = 66 * 1000 * 1000
COLOURS = ((0, 96), (96, 80), (176, 80))
LINKS = (("head", 1), ("blk", 1), ("blk", 2), ("group", 2), ("group", 1))
ORDERS = ((0, 1, 2), (1, 2, 0), (2, 0, 1))


def vmem():
    return pl.BlockSpec(memory_space=pltpu.VMEM)


def anywhere():
    return pl.BlockSpec(memory_space=pl.ANY)


def dot_last(left, right):
    return lax.dot_general(left, right, (((1,), (1,)), ((), ())), preferred_element_type=f32)


def dot_first(left, right):
    return lax.dot_general(left, right, (((0,), (0,)), ((), ())), preferred_element_type=f32)


def dot(left, right):
    return jnp.dot(left, right, preferred_element_type=f32)


def my_place():
    return lax.axis_index("blk") * 2 + lax.axis_index("head")


def peer(step):
    place = lax.rem(my_place() + step, 8)
    return place, {"blk": place // 2, "head": lax.rem(place, 2)}


def neighbour(link):
    if link == 0:
        return {"head": 1 - lax.axis_index("head")}
    blk = lax.axis_index("blk")
    if link == 1:
        return {"blk": blk + 1 - 2 * lax.rem(blk, 2)}
    return {"blk": lax.rem(blk + 2, 4)}


def my_bits():
    blk = lax.axis_index("blk")
    return (lax.axis_index("head"), lax.rem(blk, 2), blk // 2)


def meet_all():
    barrier = pltpu.get_barrier_semaphore()
    for step in range(1, 8):
        pl.semaphore_signal(barrier, 1, device_id=peer(step)[1], device_id_type=MESH_ID)
    pl.semaphore_wait(barrier, 7)


def remote(src, dst, send, recv, target):
    return pltpu.make_async_remote_copy(
        src_ref=src, dst_ref=dst, send_sem=send, recv_sem=recv, device_id=target, device_id_type=MESH_ID
    )


def cube_index(bits, fixed, rows):
    entries = [pl.ds(fixed[link], 1) if link in fixed else pl.ds(0, 2) for link in (2, 1, 0)]
    return tuple(entries) + (pl.ds(*rows),)


def lanes(shape):
    return lax.broadcasted_iota(jnp.int32, shape, len(shape) - 1)


def turned(u):
    low = lax.rem(lanes(u.shape), 64) < 32
    return jnp.where(low, -pltpu.roll(u, 96, 1), pltpu.roll(u, 32, 1))


def two_heads(q):
    low = lanes(q.shape) < 64
    return jnp.concatenate([jnp.where(low, q, 0.0), jnp.where(low, pltpu.roll(q, 64, 1), 0.0)], 0)


def two_heads_high(g):
    high = lanes(g.shape) >= 64
    return jnp.concatenate([jnp.where(high, pltpu.roll(g, 64, 1), 0.0), jnp.where(high, g, 0.0)], 0)


def block_probability(q_ref, kv_ref, seg_col, seg_row, s, i):
    first = max(0, i - 4) * 128
    count = (i + 1) * 128 - first
    q2 = two_heads(q_ref[s, pl.ds(i * 128, 128)].astype(f32))
    kv = kv_ref[s, pl.ds(first, count)]
    raw = dot_last((q2 * 0.125).astype(bf16), kv)
    q_place = i * 128 + lax.broadcasted_iota(jnp.int32, (128, count), 0)
    k_place = first + lanes((128, count))
    q_doc = seg_col[s, pl.ds(i * 128, 128)]
    k_doc = seg_row[s, :, pl.ds(first, count)]
    allowed = (q_place >= k_place) & (q_doc == k_doc)
    allowed = jnp.concatenate([allowed, allowed], 0)
    masked = jnp.where(allowed, raw, masked_out)
    top = jnp.max(masked, -1, keepdims=True)
    weight = jnp.exp(masked - top)
    probability = weight * (1.0 / jnp.sum(weight, -1, keepdims=True))
    return first, count, q2, kv, probability


def norm_back(values, gain, grad):
    scale = lax.rsqrt(jnp.mean(values * values, -1, keepdims=True) + epsilon)
    inner = grad * gain
    along = jnp.mean(values * inner, -1, keepdims=True)
    out = scale * inner - values * (scale * scale * scale * along)
    gain_grad = jnp.sum(grad * values * scale, 0, keepdims=True)
    return out, gain_grad


def expert_inner(rows_e, pair_e, gate_w, up_w, down_w):
    gate_val = dot(rows_e, gate_w)
    up_val = dot(rows_e, up_w)
    sig = 1.0 / (1.0 + jnp.exp(-gate_val))
    silu = gate_val * sig
    hidden = (silu * up_val).astype(bf16)
    hidden_grad = dot_last(pair_e, down_w)
    gate_grad = (hidden_grad * up_val * sig * (1.0 + gate_val * (1.0 - sig))).astype(bf16)
    up_grad = (hidden_grad * silu).astype(bf16)
    return hidden, gate_grad, up_grad


def sibling():
    group = lax.axis_index("group")
    return {"group": group + 1 - 2 * lax.rem(group, 2)}


def mirror():
    return {"group": lax.rem(lax.axis_index("group") + 2, 4)}


def my_core():
    return lax.rem(lax.axis_index("group"), 2)


def meet(targets):
    barrier = pltpu.get_barrier_semaphore()
    for target in targets:
        pl.semaphore_signal(barrier, 1, device_id=target, device_id_type=MESH_ID)
    pl.semaphore_wait(barrier, len(targets))


def peers():
    return [peer(step)[1] for step in range(1, 8)]


def cube_entry(fixed):
    return tuple(pl.ds(fixed[link], 1) if link in fixed else pl.ds(0, 2) for link in (2, 1, 0))


class Gather:
    def __init__(self, items, send, recv):
        self.items, self.send, self.recv, self.bits = items, send, recv, my_bits()

    def copies(self, step):
        made = []
        for k, (src, place, order) in enumerate(self.items):
            fixed = {link: self.bits[link] for link in order[step:]}
            where = place(cube_entry(fixed))
            here = where
            if step == 0:
                here = src
                where = place((self.bits[2], self.bits[1], self.bits[0]))
            made.append(remote(here, where, self.send.at[step, k], self.recv.at[step, k], neighbour(order[step])))
        return made

    def start(self, step):
        for copy in self.copies(step):
            copy.start()

    def wait(self, step):
        for copy in self.copies(step):
            copy.wait_recv()

    def sent(self):
        for step in range(3):
            for copy in self.copies(step):
                copy.wait_send()


def row_items(src, dst):
    def item(k):
        start, count = COLOURS[k]
        return (src.at[pl.ds(start, count)], lambda entry: dst.at[entry + (pl.ds(start, count),)], ORDERS[k])

    return [item(k) for k in range(3)]


class CubeSum:
    def __init__(self, part, got, held0, got1, held1, got2, send, recv):
        self.part, self.got, self.held0, self.got1, self.held1, self.got2 = part, got, held0, got1, held1, got2
        self.send, self.recv, self.bits = send, recv, my_bits()

    def copy(self, step, k):
        order, rows = ORDERS[k], pl.ds(*COLOURS[k])
        other = 1 - self.bits[order[step]]
        if step == 0:
            src = self.part.at[cube_entry({order[0]: other}) + (rows,)]
            dst = self.got[k]
        elif step == 1:
            src = self.held0.at[other, :, rows]
            dst = self.got1.at[:, rows]
        else:
            src = self.held1.at[other, rows]
            dst = self.got2.at[rows]
        return remote(src, dst, self.send.at[step, k], self.recv.at[step, k], neighbour(order[step]))

    def start(self):
        for k in range(3):
            self.copy(0, k).start()

    def middle(self):
        for k, order in enumerate(ORDERS):
            self.copy(0, k).wait_recv()
            rows = pl.ds(*COLOURS[k])
            for u in range(2):
                for v in range(2):
                    mine = {order[0]: self.bits[order[0]], order[1]: u, order[2]: v}
                    there = {order[0]: 0, order[1]: u, order[2]: v}
                    landed = self.got[k][there[2], there[1], there[0]].astype(f32)
                    here = self.part[mine[2], mine[1], mine[0], rows].astype(f32)
                    self.held0[u, v, rows] = (here + landed).astype(bf16)
            self.copy(1, k).start()

    def last(self):
        for k, order in enumerate(ORDERS):
            self.copy(1, k).wait_recv()
            rows = pl.ds(*COLOURS[k])
            for v in range(2):
                here = self.held0[self.bits[order[1]], v, rows].astype(f32)
                self.held1[v, rows] = (here + self.got1[v, rows].astype(f32)).astype(bf16)
            self.copy(2, k).start()

    def finish(self, store):
        for k, order in enumerate(ORDERS):
            self.copy(2, k).wait_recv()
            rows = pl.ds(*COLOURS[k])
            store(rows, self.held1[self.bits[order[2]], rows].astype(f32) + self.got2[rows].astype(f32))

    def sent(self):
        for step in range(3):
            for k in range(3):
                self.copy(step, k).wait_send()


def cube_sum_scratch(width):
    return [
        pltpu.VMEM((2, 2, 1, 96, width), bf16),
        pltpu.VMEM((2, 1, 2, 80, width), bf16),
        pltpu.VMEM((1, 2, 2, 80, width), bf16),
        pltpu.VMEM((2, 2, 256, width), bf16),
        pltpu.VMEM((2, 256, width), bf16),
        pltpu.VMEM((2, 256, width), bf16),
        pltpu.VMEM((256, width), bf16),
        pltpu.SemaphoreType.DMA((3, 3)),
        pltpu.SemaphoreType.DMA((3, 3)),
    ]


def make_cube_sum(part, scratch):
    g0, g1, g2, held0, got1, held1, got2, send, recv = scratch
    return CubeSum(part, (g0, g1, g2), held0, got1, held1, got2, send, recv)


class Spread:
    def __init__(self, src, dst, send, recv):
        self.src, self.dst, self.send, self.recv = src, dst, send, recv

    def copy(self, step):
        place, target = peer(step)
        return remote(self.src(place), self.dst(my_place()), self.send.at[step], self.recv.at[step], target)

    def start(self):
        for step in range(1, 8):
            self.copy(step).start()

    def wait(self):
        for step in range(1, 8):
            self.copy(step).wait()


def rope_tables():
    frequency = 10000.0 ** (-(np.arange(128) % 32) * 2.0 / 64)
    near = np.arange(128)[:, None] * frequency[None, :]
    far = np.arange(8)[:, None] * 128.0 * frequency[None, :]
    return tuple(np.asarray(t, np.float32) for t in (np.cos(near), np.sin(near), np.cos(far), np.sin(far)))


def fill_rope(near_cos, near_sin, far_cos, far_sin, cosine, sine):
    for j in range(8):
        rows = pl.ds(j * 128, 128)
        fc, fs = far_cos[pl.ds(j, 1)], far_sin[pl.ds(j, 1)]
        cosine[rows] = fc * near_cos[...] - fs * near_sin[...]
        sine[rows] = fs * near_cos[...] + fc * near_sin[...]


def forward_kernel(
    tok, cot, wq, wkv, wo, gains, router, routes, seg_col, seg_row, near_cos, near_sin, far_cos, far_sin,
    attn_hbm, q_out, kv_out, amix, residual_out, moe_in_out, weights_out, wo_hbm, gains_all, router_all, routes_all,
    cot_hbm, cot_mirror, routes_mirror,
    tok_all, attn_all, cot_all, wo_all, w_all, mix, cosine, sine,
    tok_send, tok_recv, cot_send, cot_recv, small_send, small_recv, mix_send, mix_recv, wo_send, wo_recv,
    pair_send, pair_recv, own_sem, out_sem,
):
    me, core = my_place(), my_core()
    meet(peers() + [sibling(), mirror()])
    pairs = (
        (lambda j: wq.at[:, pl.ds(j * 128, 128)], lambda i: w_all.at[pl.ds(i * 128, 128), pl.ds(0, 128)]),
        (lambda j: wkv.at[:, pl.ds(j * 128, 128)], lambda i: w_all.at[pl.ds(i * 128, 128), pl.ds(128, 128)]),
        (lambda j: gains, lambda i: gains_all.at[:, pl.ds(i * 128, 128)]),
        (lambda j: router, lambda i: router_all.at[pl.ds(i * 128, 128)]),
        (lambda j: routes, lambda i: routes_all.at[:, pl.ds(i * 256, 256)]),
    )
    smalls = [Spread(src, dst, small_send.at[k], small_recv.at[k]) for k, (src, dst) in enumerate(pairs)]
    own = [pltpu.make_async_copy(src(me), dst(me), own_sem.at[k]) for k, (src, dst) in enumerate(pairs)]
    own.append(pltpu.make_async_copy(tok, tok_all.at[me // 4, lax.rem(me // 2, 2), lax.rem(me, 2)], own_sem.at[5]))
    own.append(pltpu.make_async_copy(cot, cot_all.at[me // 4, lax.rem(me // 2, 2), lax.rem(me, 2)], own_sem.at[6]))
    half = pl.ds(pl.multiple_of(core * 64, 64), 64)
    own.append(
        pltpu.make_async_copy(
            wo.at[half], wo_all.at[me // 4, lax.rem(me // 2, 2), lax.rem(me, 2), half], own_sem.at[7]
        )
    )
    for copy in own:
        copy.start()
    tok_gather = Gather(row_items(tok, tok_all), tok_send, tok_recv)
    tok_gather.start(0)
    for small in smalls:
        small.start()
    fill_rope(near_cos, near_sin, far_cos, far_sin, cosine, sine)
    for copy in own:
        copy.wait()
    tok_gather.wait(0)
    tok_gather.start(1)
    tok_gather.wait(1)
    tok_gather.start(2)
    for small in smalls:
        small.wait()
    routes_copy = remote(routes_all, routes_mirror, pair_send.at[0], pair_recv.at[0], mirror())
    routes_copy.start()
    tok_gather.wait(2)
    wo_spread = Spread(
        lambda j: wo.at[half],
        lambda i: wo_all.at[i // 4, lax.rem(i // 2, 2), lax.rem(i, 2), half],
        wo_send,
        wo_recv,
    )
    wo_spread.start()
    cot_gather = Gather(row_items(cot, cot_all), cot_send, cot_recv)
    cot_gather.start(0)
    cot_copy = remote(cot, cot_mirror, pair_send.at[1], pair_recv.at[1], mirror())
    cot_copy.start()

    gain_row = gains_all[0:1].astype(f32)

    def project(j, carry):
        rows = pl.ds(pl.multiple_of(j * 128, 128), 128)
        x = tok_all[j // 4, lax.rem(j // 2, 2), lax.rem(j, 2)].astype(f32)
        scale = lax.rsqrt(jnp.mean(x * x, -1, keepdims=True) + epsilon)
        attn_in = (x * scale * gain_row).astype(bf16)
        attn_all[j] = attn_in
        both = dot(attn_in, w_all[...])
        c = cosine[rows]
        n = sine[rows]
        c2 = jnp.concatenate([c, c], 0)
        n2 = jnp.concatenate([n, n], 0)
        q = both[:, :128]
        kv = both[:, 128:]
        q = (q * c2 + turned(q) * n2).astype(bf16)
        kv = jnp.where(lanes(kv.shape) < 64, kv * c2 + turned(kv) * n2, kv).astype(bf16)
        for s in range(2):
            q_out[s, rows] = q[s * 128 : (s + 1) * 128]
            kv_out[s, rows] = kv[s * 128 : (s + 1) * 128]
        return carry

    lax.fori_loop(0, 8, project, 0)
    attn_copy = pltpu.make_async_copy(attn_all, attn_hbm, out_sem.at[0])
    attn_copy.start()
    wo_spread.wait()
    wo_pair = remote(
        wo_all.at[:, :, :, half], wo_all.at[:, :, :, half], pair_send.at[2], pair_recv.at[2], sibling()
    )
    wo_pair.start()
    cot_gather.wait(0)
    cot_gather.start(1)

    def mix_copy(i):
        return remote(
            mix.at[i],
            amix.at[:, :, pl.ds(pl.multiple_of(me * 128, 128), 128)],
            mix_send.at[i],
            mix_recv.at[me],
            {"blk": i // 2, "head": lax.rem(i, 2)},
        )

    def send_mix(i):
        @pl.when(me != i)
        def _():
            mix_copy(i).start()

    for i in range(8):

        def attend(s, carry, i=i):
            first, count, q2, kv, probability = block_probability(q_out, kv_out, seg_col, seg_row, s, i)
            mixed = dot(probability.astype(bf16), kv)
            low = lanes((128, 128)) < 64
            mix[i, s] = jnp.where(low, pltpu.roll(mixed[:128], 64, 1), mixed[128:]).astype(bf16)
            return carry

        lax.fori_loop(0, 2, attend, 0)
        if i > 0:
            send_mix(i - 1)
        if i == 4:
            cot_gather.wait(1)
            cot_gather.start(2)
    send_mix(7)
    mine = pltpu.make_async_copy(
        mix.at[me], amix.at[:, :, pl.ds(pl.multiple_of(me * 128, 128), 128)], own_sem.at[0]
    )
    mine.start()
    wo_pair.wait()
    wo_copy = pltpu.make_async_copy(wo_all, wo_hbm, out_sem.at[1])
    wo_copy.start()
    for step in range(1, 8):
        place, target = peer(step)
        remote(
            mix.at[place],
            amix.at[:, :, pl.ds(pl.multiple_of(place * 128, 128), 128)],
            mix_send.at[place],
            mix_recv.at[place],
            target,
        ).wait()
    mine.wait()
    width = tok.shape[-1]
    residual = tok[...].astype(f32) + dot(amix[...].reshape(256, width), wo_all[...].reshape(width, width))
    residual_out[...] = residual
    scale = lax.rsqrt(jnp.mean(residual * residual, -1, keepdims=True) + epsilon)
    moe_in = (residual * scale * gains_all[1:2].astype(f32)).astype(bf16)
    moe_in_out[...] = moe_in
    logits = lax.dot_general(router_all[...], moe_in, (((0,), (1,)), ((), ())), preferred_element_type=f32)
    experts = lax.broadcasted_iota(jnp.int32, logits.shape, 0)
    picked = [
        jnp.sum(jnp.where(experts == routes[pl.ds(k, 1)], logits, 0.0), 0, keepdims=True) for k in range(TOP)
    ]
    picked = jnp.concatenate(picked, 0)
    weight = jnp.exp(picked - jnp.max(picked, 0, keepdims=True))
    weights_out[...] = weight / jnp.sum(weight, 0, keepdims=True)
    cot_gather.wait(2)
    cot_out = pltpu.make_async_copy(cot_all, cot_hbm, out_sem.at[2])
    cot_out.start()
    routes_copy.wait()
    cot_copy.wait()
    tok_gather.sent()
    cot_gather.sent()
    attn_copy.wait()
    wo_copy.wait()
    cot_out.wait()


def forward(tok, cot, wq, wkv, wo, gains, router, routes, seg_col, seg_row):
    width = tok.shape[-1]
    tables = tuple(jnp.asarray(t) for t in rope_tables())
    return pl.pallas_call(
        forward_kernel,
        out_shape=(
            jax.ShapeDtypeStruct((8, 256, width), bf16),
            jax.ShapeDtypeStruct((2, 1024, 128), bf16),
            jax.ShapeDtypeStruct((2, 1024, 128), bf16),
            jax.ShapeDtypeStruct((2, 128, width), bf16),
            jax.ShapeDtypeStruct((256, width), f32),
            jax.ShapeDtypeStruct((256, width), bf16),
            jax.ShapeDtypeStruct((8, 256), f32),
            jax.ShapeDtypeStruct((2, 2, 2, 128, width), bf16),
            jax.ShapeDtypeStruct((16, width), bf16),
            jax.ShapeDtypeStruct((width, 32), bf16),
            jax.ShapeDtypeStruct((8, 2048), jnp.int32),
            jax.ShapeDtypeStruct((2, 2, 2, 256, width), bf16),
            jax.ShapeDtypeStruct((256, width), bf16),
            jax.ShapeDtypeStruct((8, 2048), jnp.int32),
        ),
        in_specs=[vmem()] * 14,
        out_specs=(
            anywhere(), vmem(), vmem(), vmem(), vmem(), vmem(), vmem(), anywhere(), vmem(), vmem(), vmem(),
            anywhere(), vmem(), vmem(),
        ),
        scratch_shapes=[
            pltpu.VMEM((2, 2, 2, 256, width), bf16),
            pltpu.VMEM((8, 256, width), bf16),
            pltpu.VMEM((2, 2, 2, 256, width), bf16),
            pltpu.VMEM((2, 2, 2, 128, width), bf16),
            pltpu.VMEM((width, 256), bf16),
            pltpu.VMEM((8, 2, 128, 128), bf16),
            pltpu.VMEM((1024, 128), f32),
            pltpu.VMEM((1024, 128), f32),
            pltpu.SemaphoreType.DMA((3, 3)),
            pltpu.SemaphoreType.DMA((3, 3)),
            pltpu.SemaphoreType.DMA((3, 3)),
            pltpu.SemaphoreType.DMA((3, 3)),
            pltpu.SemaphoreType.DMA((5, 8)),
            pltpu.SemaphoreType.DMA((5, 8)),
            pltpu.SemaphoreType.DMA((8,)),
            pltpu.SemaphoreType.DMA((8,)),
            pltpu.SemaphoreType.DMA((8,)),
            pltpu.SemaphoreType.DMA((8,)),
            pltpu.SemaphoreType.DMA((3,)),
            pltpu.SemaphoreType.DMA((3,)),
            pltpu.SemaphoreType.DMA((8,)),
            pltpu.SemaphoreType.DMA((3,)),
        ],
        compiler_params=pltpu.CompilerParams(
            collective_id=0, has_side_effects=True, vmem_limit_bytes=VMEM_LIMIT
        ),
        name="forward",
    )(tok, cot, wq, wkv, wo, gains, router, routes, seg_col, seg_row, *tables)


SLOT = 4 * CAPH
SPAN = 512
TAKEN = 4 * SLOT


def build_rows(routes, upper, plain, first_expert, block):
    columns = pl.ds(pl.multiple_of(block * SPAN, SPAN), SPAN)
    chosen = routes[:, columns]
    masks = [jnp.max((chosen == first_expert + e).astype(f32), 0, keepdims=True) for e in range(4)]
    mask = jnp.concatenate(masks + [jnp.zeros((4, SPAN), f32)], 0)
    rank = dot(mask.astype(bf16), upper[...])
    slots = lax.broadcasted_iota(jnp.int32, (SLOT, SPAN), 0).astype(f32)
    for e in range(4):
        hit = (slots == rank[e : e + 1]) & (mask[e : e + 1] > 0.0)
        plain[block, e * SLOT : (e + 1) * SLOT] = jnp.where(hit, 1.0, 0.0).astype(bf16)


def slot_weights(routes, weights, plain, column, first_expert, block):
    columns = pl.ds(pl.multiple_of(block * SPAN, SPAN), SPAN)
    chosen = routes[:, columns]
    weight = weights[:, columns]
    for e in range(4):
        share = jnp.sum(jnp.where(chosen == first_expert + e, weight, 0.0), 0, keepdims=True)
        mine = pl.ds(e * SLOT, SLOT)
        column[block, mine] = jnp.sum(plain[block, mine].astype(f32) * share, -1, keepdims=True)


def place_rows(source, block):
    width = source.shape[-1]
    return source[block // 2, lax.rem(block, 2)].reshape(SPAN, width)


def expert_rows(e):
    return pl.ds(pl.multiple_of(e * SLOT, 16), SLOT)


def experts_kernel(
    moe_in, my_weights, cot_mirror, cot_hbm, routes, upper, gate_hbm, up_hbm, down_hbm,
    out_part, in_sum, p_all, rows_out, pair_out, hidden_out, gate_out, up_out, cot_mirror_hbm, moe_mirror,
    weights_other,
    x, c, cm, plain, rows, pair_grad, pair_in, column, p_col, weights, p_part,
    gate, up, down, hid_buf, gg_buf, ug_buf, part_buf,
    g0, g1, g2, held0, got1, held1, got2, sum_send, sum_recv,
    row_send, row_recv, cm_send, cm_recv, w_send, w_recv, p_send, p_recv, pair_send, pair_recv,
    sem_c, sem_w, sem_rows, sem_h, sem_part, own_sem,
):
    me = my_place()
    first = me * 4
    width = x.shape[-1]
    meet(peers() + [mirror()])
    own = [
        pltpu.make_async_copy(moe_in, x.at[me // 4, lax.rem(me // 2, 2), lax.rem(me, 2)], own_sem.at[0]),
        pltpu.make_async_copy(
            my_weights, weights.at[:, pl.ds(pl.multiple_of(me * 256, 256), 256)], own_sem.at[1]
        ),
        pltpu.make_async_copy(cot_mirror, cm.at[me // 4, lax.rem(me // 2, 2), lax.rem(me, 2)], own_sem.at[2]),
    ]
    for copy in own:
        copy.start()
    row_gather = Gather(row_items(moe_in, x), row_send, row_recv)
    row_gather.start(0)
    weight_spread = Spread(
        lambda j: my_weights, lambda i: weights.at[:, pl.ds(pl.multiple_of(i * 256, 256), 256)], w_send, w_recv
    )
    weight_spread.start()
    load_c = pltpu.make_async_copy(cot_hbm, c, sem_c)
    load_c.start()

    def fetch(e, slot):
        return [
            pltpu.make_async_copy(gate_hbm.at[e], gate.at[slot], sem_w.at[slot, 0]),
            pltpu.make_async_copy(up_hbm.at[e], up.at[slot], sem_w.at[slot, 1]),
            pltpu.make_async_copy(down_hbm.at[e], down.at[slot], sem_w.at[slot, 2]),
        ]

    for copy in fetch(0, 0):
        copy.start()

    def build(block, carry):
        build_rows(routes, upper, plain, first, block)
        return carry

    lax.fori_loop(0, 4, build, 0)
    for copy in own:
        copy.wait()
    row_gather.wait(0)
    row_gather.start(1)
    load_c.wait()

    def take_c(block, carry):
        pair_grad[block] = dot(plain[block], place_rows(c, block)).astype(bf16)
        return carry

    lax.fori_loop(0, 2, take_c, 0)
    row_gather.wait(1)
    row_gather.start(2)
    lax.fori_loop(2, 4, take_c, 0)
    weight_spread.wait()
    weights_copy = remote(weights, weights_other, pair_send.at[0], pair_recv.at[0], mirror())
    weights_copy.start()

    def weigh(block, carry):
        slot_weights(routes, weights, plain, column, first, block)
        return carry

    lax.fori_loop(0, 4, weigh, 0)
    row_gather.wait(2)
    cm_gather = Gather(row_items(cot_mirror, cm), cm_send, cm_recv)
    cm_gather.start(0)
    moe_copy = remote(moe_in, moe_mirror, pair_send.at[1], pair_recv.at[1], mirror())
    moe_copy.start()

    def take_x(block, carry):
        rows[block] = dot(plain[block], place_rows(x, block)).astype(bf16)
        return carry

    lax.fori_loop(0, 4, take_x, 0)
    keep_rows = pltpu.make_async_copy(rows, rows_out, sem_rows.at[0])
    keep_rows.start()

    def keep(e, slot):
        return [
            pltpu.make_async_copy(hid_buf.at[slot], hidden_out.at[e], sem_h.at[slot, 0]),
            pltpu.make_async_copy(gg_buf.at[slot], gate_out.at[e], sem_h.at[slot, 1]),
            pltpu.make_async_copy(ug_buf.at[slot], up_out.at[e], sem_h.at[slot, 2]),
        ]

    def expert(e, carry):
        slot = lax.rem(e, 2)
        mine = expert_rows(e)
        for copy in fetch(e, slot):
            copy.wait()

        @pl.when(e < 3)
        def _():
            for copy in fetch(e + 1, 1 - slot):
                copy.start()

        rows_e = rows[:, mine].reshape(TAKEN, width)
        weight_e = column[:, mine].reshape(TAKEN, 1)
        pair_e = (pair_grad[:, mine].reshape(TAKEN, width).astype(f32) * weight_e).astype(bf16)
        pair_grad[:, mine] = pair_e.reshape(4, SLOT, width)
        hidden, gate_grad, up_grad = expert_inner(rows_e, pair_e, gate[slot], up[slot], down[slot])

        @pl.when(e >= 2)
        def _():
            for copy in keep(e - 2, slot):
                copy.wait()

        hid_buf[slot] = hidden
        gg_buf[slot] = gate_grad
        ug_buf[slot] = up_grad
        for copy in keep(e, slot):
            copy.start()

        @pl.when(e == 0)
        def _():
            keep_rows.wait()

        @pl.when(e == 1)
        def _():
            cm_gather.wait(0)
            cm_gather.start(1)

        @pl.when(e == 2)
        def _():
            cm_gather.wait(1)
            cm_gather.start(2)

        out_e = dot(hidden, down[slot]).astype(bf16).astype(f32)
        p = jnp.sum(out_e * pair_e.astype(f32), -1, keepdims=True)
        p_col[:, mine] = p.reshape(4, SLOT, 1)
        rows[:, mine] = (out_e * weight_e).astype(bf16).reshape(4, SLOT, width)
        back = dot_last(gate_grad, gate[slot]) + dot_last(up_grad, up[slot])
        pair_in[:, mine] = back.astype(bf16).reshape(4, SLOT, width)
        return carry

    lax.fori_loop(0, 4, expert, 0)
    keep_pair = pltpu.make_async_copy(pair_grad, pair_out, sem_rows.at[1])
    keep_pair.start()
    for copy in keep(2, 0) + keep(3, 1):
        copy.wait()
    row_gather.sent()
    p_part[...] = jnp.zeros_like(p_part)

    def combine_in(block, carry):
        back = dot_first(plain[block], pair_in[block]).astype(bf16)
        x[block // 2, lax.rem(block, 2)] = back.reshape(2, 256, width)
        for e in range(4):
            mine = pl.ds(e * SLOT, SLOT)
            p = jnp.sum(plain[block, mine].astype(f32) * p_col[block, mine], 0, keepdims=True)
            p_part[block * 2, pl.ds(e, 1)] = p[:, :256]
            p_part[block * 2 + 1, pl.ds(e, 1)] = p[:, 256:]
        return carry

    lax.fori_loop(0, 4, combine_in, 0)
    total = make_cube_sum(x, (g0, g1, g2, held0, got1, held1, got2, sum_send, sum_recv))
    total.start()
    p_spread = Spread(lambda j: p_part.at[j], lambda i: p_all.at[i], p_send, p_recv)
    p_spread.start()
    p_own = pltpu.make_async_copy(p_part.at[me], p_all.at[me], own_sem.at[3])
    p_own.start()

    def part_copy(block):
        slot = lax.rem(block, 2)
        return pltpu.make_async_copy(
            part_buf.at[slot], out_part.at[block // 2, lax.rem(block, 2)], sem_part.at[slot]
        )

    def combine_out(block, carry):
        slot = lax.rem(block, 2)

        @pl.when(block >= 2)
        def _():
            part_copy(block - 2).wait()

        out = dot_first(plain[block], rows[block]).astype(bf16)
        part_buf[slot] = out.reshape(2, 256, width)
        part_copy(block).start()
        return carry

    lax.fori_loop(0, 2, combine_out, 0)
    total.middle()
    lax.fori_loop(2, 4, combine_out, 0)
    cm_gather.wait(2)
    cm_out = pltpu.make_async_copy(cm, cot_mirror_hbm, sem_c)
    cm_out.start()
    total.last()
    p_spread.wait()
    p_own.wait()
    part_copy(2).wait()
    part_copy(3).wait()

    def store(where, value):
        in_sum[where] = value

    total.finish(store)
    total.sent()
    keep_pair.wait()
    cm_out.wait()
    cm_gather.sent()
    weights_copy.wait()
    moe_copy.wait()


def experts(moe_in, my_weights, cot_mirror, cot_all, routes, upper, gate_w, up_w, down_w):
    width = moe_in.shape[-1]
    ff = gate_w.shape[-1]
    return pl.pallas_call(
        experts_kernel,
        out_shape=(
            jax.ShapeDtypeStruct((2, 2, 2, 256, width), bf16),
            jax.ShapeDtypeStruct((256, width), f32),
            jax.ShapeDtypeStruct((8, 8, 256), f32),
            jax.ShapeDtypeStruct((4, TAKEN, width), bf16),
            jax.ShapeDtypeStruct((4, TAKEN, width), bf16),
            jax.ShapeDtypeStruct((4, TAKEN, ff), bf16),
            jax.ShapeDtypeStruct((4, TAKEN, ff), bf16),
            jax.ShapeDtypeStruct((4, TAKEN, ff), bf16),
            jax.ShapeDtypeStruct((2, 2, 2, 256, width), bf16),
            jax.ShapeDtypeStruct((256, width), bf16),
            jax.ShapeDtypeStruct((8, 2048), f32),
        ),
        in_specs=[vmem(), vmem(), vmem(), anywhere(), vmem(), vmem(), anywhere(), anywhere(), anywhere()],
        out_specs=(anywhere(), vmem(), vmem()) + (anywhere(),) * 6 + (vmem(), vmem()),
        scratch_shapes=[
            pltpu.VMEM((2, 2, 2, 256, width), bf16),
            pltpu.VMEM((2, 2, 2, 256, width), bf16),
            pltpu.VMEM((2, 2, 2, 256, width), bf16),
            pltpu.VMEM((4, TAKEN, SPAN), bf16),
            pltpu.VMEM((4, TAKEN, width), bf16),
            pltpu.VMEM((4, TAKEN, width), bf16),
            pltpu.VMEM((4, TAKEN, width), bf16),
            pltpu.VMEM((4, TAKEN, 1), f32),
            pltpu.VMEM((4, TAKEN, 1), f32),
            pltpu.VMEM((8, 2048), f32),
            pltpu.VMEM((8, 8, 256), f32),
            pltpu.VMEM((2, width, ff), bf16),
            pltpu.VMEM((2, width, ff), bf16),
            pltpu.VMEM((2, ff, width), bf16),
            pltpu.VMEM((2, TAKEN, ff), bf16),
            pltpu.VMEM((2, TAKEN, ff), bf16),
            pltpu.VMEM((2, TAKEN, ff), bf16),
            pltpu.VMEM((2, 2, 256, width), bf16),
        ]
        + cube_sum_scratch(width)
        + [
            pltpu.SemaphoreType.DMA((3, 3)),
            pltpu.SemaphoreType.DMA((3, 3)),
            pltpu.SemaphoreType.DMA((3, 3)),
            pltpu.SemaphoreType.DMA((3, 3)),
            pltpu.SemaphoreType.DMA((8,)),
            pltpu.SemaphoreType.DMA((8,)),
            pltpu.SemaphoreType.DMA((8,)),
            pltpu.SemaphoreType.DMA((8,)),
            pltpu.SemaphoreType.DMA((2,)),
            pltpu.SemaphoreType.DMA((2,)),
            pltpu.SemaphoreType.DMA,
            pltpu.SemaphoreType.DMA((2, 3)),
            pltpu.SemaphoreType.DMA((2,)),
            pltpu.SemaphoreType.DMA((2, 3)),
            pltpu.SemaphoreType.DMA((2,)),
            pltpu.SemaphoreType.DMA((4,)),
        ],
        compiler_params=pltpu.CompilerParams(
            collective_id=1, has_side_effects=True, vmem_limit_bytes=VMEM_LIMIT
        ),
        name="experts",
    )(moe_in, my_weights, cot_mirror, cot_all, routes, upper, gate_w, up_w, down_w)


LANE_SHARE = 128


def backward_kernel(
    cot, residual, in_sum, p_all, routes, weights, router, moe_in, gains_all, wo_hbm, amix, attn_hbm, q_in, kv_in,
    seg_col, seg_row, near_cos, near_sin, far_cos, far_sin, tok, wq, wkv, moe_mirror,
    token_grad, grads, mirror_hbm,
    wo_all, attn_all, wq_all, wkv_all, mm, mix_grad, mg, gq, gkv, gq_rows, gkv_rows, g_all, kv_sum, cosine, sine,
    residual_grad, small_grad,
    w_send, w_recv, mm_send, mm_recv, mg_send, mg_recv, g_send, g_recv, pair_send, pair_recv, own_sem, load_sem,
):
    me, core = my_place(), my_core()
    width = tok.shape[-1]
    meet(peers() + [sibling()])
    half = pl.ds(pl.multiple_of(core * 64, 64), 64)
    own_entry = (me // 4, lax.rem(me // 2, 2), lax.rem(me, 2))
    own = [
        pltpu.make_async_copy(wq.at[half], wq_all.at[own_entry + (half,)], own_sem.at[0]),
        pltpu.make_async_copy(wkv.at[half], wkv_all.at[own_entry + (half,)], own_sem.at[1]),
        pltpu.make_async_copy(moe_mirror, mm.at[own_entry], own_sem.at[2]),
    ]
    loads = [
        pltpu.make_async_copy(wo_hbm, wo_all, load_sem.at[0]),
        pltpu.make_async_copy(attn_hbm, attn_all, load_sem.at[1]),
    ]
    for copy in own + loads:
        copy.start()

    def weight_item(src, dst, start, count, order):
        rows = pl.ds(pl.multiple_of(core * 64 + start, 16), count)
        return (src.at[rows], lambda entry: dst.at[entry + (rows,)], order)

    w_gather = Gather(
        [
            weight_item(wq, wq_all, 0, 48, ORDERS[0]),
            weight_item(wq, wq_all, 48, 16, ORDERS[1]),
            weight_item(wkv, wkv_all, 0, 32, ORDERS[1]),
            weight_item(wkv, wkv_all, 32, 32, ORDERS[2]),
        ],
        w_send,
        w_recv,
    )
    w_gather.start(0)
    mm_gather = Gather(row_items(moe_mirror, mm), mm_send, mm_recv)
    fill_rope(near_cos, near_sin, far_cos, far_sin, cosine, sine)

    ids = lax.broadcasted_iota(jnp.int32, (32, 256), 0)
    dense = jnp.zeros((32, 256), f32)
    for k in range(TOP):
        dense = dense + jnp.where(ids == routes[pl.ds(k, 1)], weights[pl.ds(k, 1)], 0.0)
    p = jnp.concatenate([p_all[i, 0:4] for i in range(8)], 0)
    logit_grad = (p - dense * jnp.sum(p, 0, keepdims=True)).astype(bf16)
    moe_in_grad = in_sum[...] + lax.dot_general(
        logit_grad, router[...], (((0,), (1,)), ((), ())), preferred_element_type=f32
    )
    part, moe_gain_grad = norm_back(residual[...], gains_all[1:2].astype(f32), moe_in_grad)
    total = cot[...].astype(f32) + part
    residual_grad[...] = total
    low_grad = total.astype(bf16)
    for copy in loads[:1]:
        copy.wait()
    back = dot_last(low_grad, wo_all[...].reshape(width, width)).astype(bf16)
    for j in range(8):
        mix_grad[j] = back[:, j * 128 : (j + 1) * 128].reshape(2, 128, 128)
    mix_spread = Spread(lambda j: mix_grad.at[j], lambda i: mg.at[i], mg_send, mg_recv)
    mix_spread.start()
    mix_own = pltpu.make_async_copy(mix_grad.at[me], mg.at[me], own_sem.at[3])
    mix_own.start()
    mm_gather.start(0)
    for copy in own:
        copy.wait()
    w_gather.wait(0)
    w_gather.start(1)
    wo_grad = dot_first(amix[...].reshape(256, width), low_grad)
    grads[:, :, 0:width] = wo_grad.astype(bf16).reshape(8, 128, width)
    padded = jnp.concatenate([logit_grad, jnp.zeros((LANE_SHARE - 32, 256), bf16)], 0)
    small_grad[...] = lax.dot_general(moe_in[...], padded, (((0,), (1,)), ((), ())), preferred_element_type=f32)
    mix_spread.wait()
    mix_own.wait()

    def lane_block(i):
        return pl.ds(pl.multiple_of(i * 128, 128), 128)

    def spread_of(s):
        return [
            Spread(lambda j: gq.at[j, s], lambda i: gq_rows.at[s, :, lane_block(i)], g_send.at[2 * s], g_recv.at[2 * s]),
            Spread(
                lambda j: gkv.at[j, s],
                lambda i: gkv_rows.at[s, :, lane_block(i)],
                g_send.at[2 * s + 1],
                g_recv.at[2 * s + 1],
            ),
        ]

    keep_own = []
    for s in range(2):
        kv_sum[...] = jnp.zeros_like(kv_sum)
        for i in range(8):
            first, count, q2, kv, probability = block_probability(q_in, kv_in, seg_col, seg_row, s, i)
            g2 = two_heads_high(mg[i, s].astype(f32)).astype(bf16)
            prob_grad = dot_last(g2, kv)
            delta = jnp.sum(probability * prob_grad, -1, keepdims=True)
            score_grad = (probability * (prob_grad - delta) * 0.125).astype(bf16)
            dq = dot(score_grad, kv)
            keys = pl.ds(first, count)
            kv_sum[keys] += dot_first(score_grad, q2.astype(bf16)) + dot_first(probability.astype(bf16), g2)
            low = lanes((128, 128)) < 64
            dq = jnp.where(low, dq[:128], pltpu.roll(dq[128:], 64, 1))
            rows = pl.ds(i * 128, 128)
            dq = (dq * cosine[rows] - turned(dq) * sine[rows]).astype(bf16)
            gq[i, s] = dq
            g_all[i, s, :, 0:128] = dq
            if s == 0 and i == 3:
                w_gather.wait(1)
                w_gather.start(2)
        for i in range(8):
            rows = pl.ds(i * 128, 128)
            dkv = kv_sum[rows]
            low = lanes((128, 128)) < 64
            dkv = jnp.where(low, dkv * cosine[rows] - turned(dkv) * sine[rows], dkv).astype(bf16)
            gkv[i, s] = dkv
            g_all[i, s, :, 128:256] = dkv
        for spread in spread_of(s):
            spread.start()
        mine = [
            pltpu.make_async_copy(gq.at[me, s], gq_rows.at[s, :, lane_block(me)], own_sem.at[4 + 2 * s]),
            pltpu.make_async_copy(gkv.at[me, s], gkv_rows.at[s, :, lane_block(me)], own_sem.at[5 + 2 * s]),
        ]
        for copy in mine:
            copy.start()
        keep_own += mine
        if s == 0:
            mm_gather.wait(0)
            mm_gather.start(1)
    w_gather.wait(2)
    shared = [
        remote(w.at[:, :, :, half], w.at[:, :, :, half], pair_send.at[k], pair_recv.at[k], sibling())
        for k, w in enumerate((wq_all, wkv_all))
    ]
    for copy in shared:
        copy.start()
    mm_gather.wait(1)
    mm_gather.start(2)
    loads[1].wait()
    w_grad = dot_first(attn_all[...].reshape(2048, width), g_all[...].reshape(2048, 256))
    grads[:, :, width : width + 256] = w_grad.astype(bf16).reshape(8, 128, 256)
    for copy in shared + keep_own:
        copy.wait()
    for s in range(2):
        for spread in spread_of(s):
            spread.wait()
    back = dot_last(gq_rows[...].reshape(256, 1024), wq_all[...].reshape(width, 1024))
    back = back + dot_last(gkv_rows[...].reshape(256, 1024), wkv_all[...].reshape(width, 1024))
    part, attn_gain_grad = norm_back(tok[...].astype(f32), gains_all[0:1].astype(f32), back)
    token_grad[...] = residual_grad[...] + part
    row = lax.broadcasted_iota(jnp.int32, (LANE_SHARE, width), 0)
    gain_rows = jnp.where(row == 32, moe_gain_grad, jnp.where(row == 33, attn_gain_grad, 0.0))
    grads[:, :, width + 256 :] = (small_grad[...] + gain_rows.T).astype(bf16).reshape(8, 128, LANE_SHARE)
    mm_gather.wait(2)
    mm_out = pltpu.make_async_copy(mm, mirror_hbm, load_sem.at[0])
    mm_out.start()
    w_gather.sent()
    mm_gather.sent()
    mm_out.wait()


def backward(*values):
    tok = values[16]
    width = tok.shape[-1]
    tables = tuple(jnp.asarray(t) for t in rope_tables())
    values = values[:16] + tables + values[16:]
    specs = [vmem()] * 24
    specs[9] = specs[11] = anywhere()
    return pl.pallas_call(
        backward_kernel,
        out_shape=(
            jax.ShapeDtypeStruct((256, width), f32),
            jax.ShapeDtypeStruct((8, 128, width + 256 + LANE_SHARE), bf16),
            jax.ShapeDtypeStruct((2, 2, 2, 256, width), bf16),
        ),
        in_specs=specs,
        out_specs=(vmem(), vmem(), anywhere()),
        scratch_shapes=[
            pltpu.VMEM((2, 2, 2, 128, width), bf16),
            pltpu.VMEM((8, 256, width), bf16),
            pltpu.VMEM((2, 2, 2, 128, width), bf16),
            pltpu.VMEM((2, 2, 2, 128, width), bf16),
            pltpu.VMEM((2, 2, 2, 256, width), bf16),
            pltpu.VMEM((8, 2, 128, 128), bf16),
            pltpu.VMEM((8, 2, 128, 128), bf16),
            pltpu.VMEM((8, 2, 128, 128), bf16),
            pltpu.VMEM((8, 2, 128, 128), bf16),
            pltpu.VMEM((2, 128, 1024), bf16),
            pltpu.VMEM((2, 128, 1024), bf16),
            pltpu.VMEM((8, 2, 128, 256), bf16),
            pltpu.VMEM((1024, 128), f32),
            pltpu.VMEM((1024, 128), f32),
            pltpu.VMEM((1024, 128), f32),
            pltpu.VMEM((256, width), f32),
            pltpu.VMEM((width, LANE_SHARE), f32),
            pltpu.SemaphoreType.DMA((3, 4)),
            pltpu.SemaphoreType.DMA((3, 4)),
            pltpu.SemaphoreType.DMA((3, 3)),
            pltpu.SemaphoreType.DMA((3, 3)),
            pltpu.SemaphoreType.DMA((8,)),
            pltpu.SemaphoreType.DMA((8,)),
            pltpu.SemaphoreType.DMA((4, 8)),
            pltpu.SemaphoreType.DMA((4, 8)),
            pltpu.SemaphoreType.DMA((2,)),
            pltpu.SemaphoreType.DMA((2,)),
            pltpu.SemaphoreType.DMA((8,)),
            pltpu.SemaphoreType.DMA((2,)),
        ],
        compiler_params=pltpu.CompilerParams(
            collective_id=2, has_side_effects=True, vmem_limit_bytes=VMEM_LIMIT
        ),
        name="backward",
    )(*values)


def expert_weights_kernel(
    x_hbm, c_hbm, routes, weights, upper, gate_hbm, up_hbm, down_hbm, rows_hbm, pair_hbm, hidden_hbm, gg_hbm, ug_hbm,
    out_part, residual, grads,
    gate_own, up_own, down_own, gate_other, up_other, down_other, mixed, shares,
    x, c, plain, rows, pair_grad, column, gate, up, down,
    both_rows, both_pair, both_hidden, both_gate, gate_buf, up_buf, down_buf,
    g0, g1, g2, got1, got2, core_got, core_sum, all_got, side_sum, side_got,
    sum_send, sum_recv, grad_send, grad_recv, core_send, core_recv, part_send, part_recv,
    sem_x, sem_w, sem_own, sem_out, own_sem,
):
    me, core = my_place(), my_core()
    first = me * 4
    side = lax.axis_index("group") // 2
    other = 1 - side
    width = x.shape[-1]
    ff = gate.shape[-1]
    wide = width + 256 + LANE_SHARE
    half = pl.ds(pl.multiple_of(core * 64, 64), 64)
    other_half = pl.ds(pl.multiple_of((1 - core) * 64, 64), 64)
    meet(peers() + [sibling(), mirror()])
    core_copy = remote(grads.at[:, other_half], core_got, core_send.at[0], core_recv.at[0], sibling())
    core_copy.start()
    loads = [
        pltpu.make_async_copy(x_hbm, x, sem_x.at[0]),
        pltpu.make_async_copy(c_hbm, c, sem_x.at[1]),
    ]
    for copy in loads:
        copy.start()

    def fetch(e, slot):
        return [
            pltpu.make_async_copy(gate_hbm.at[e], gate.at[slot], sem_w.at[slot, 0]),
            pltpu.make_async_copy(up_hbm.at[e], up.at[slot], sem_w.at[slot, 1]),
            pltpu.make_async_copy(down_hbm.at[e], down.at[slot], sem_w.at[slot, 2]),
        ]

    for copy in fetch(0, 0):
        copy.start()

    def build(block, carry):
        build_rows(routes, upper, plain, first, block)
        slot_weights(routes, weights, plain, column, first, block)
        return carry

    lax.fori_loop(0, 4, build, 0)
    core_copy.wait()
    core_sum[...] = (grads[:, half].astype(f32) + core_got[...].astype(f32)).astype(bf16)
    spread = Spread(lambda j: core_sum.at[j], lambda i: all_got.at[i], grad_send, grad_recv)
    spread.start()
    spread_own = pltpu.make_async_copy(core_sum.at[me], all_got.at[me], own_sem)
    spread_own.start()
    for copy in loads:
        copy.wait()

    def take(block, carry):
        rows[block] = dot(plain[block], place_rows(x, block)).astype(bf16)
        taken = dot(plain[block], place_rows(c, block))
        pair_grad[block] = (taken * column[block]).astype(bf16)
        return carry

    lax.fori_loop(0, 4, take, 0)
    load_part = pltpu.make_async_copy(out_part, x, sem_x.at[0])
    load_part.start()
    total = CubeSum(x, (g0, g1, g2), c.at[0], got1, c.at[1, 0], got2, sum_send, sum_recv)
    side_copy = remote(side_sum, side_got, core_send.at[1], core_recv.at[1], mirror())
    last_copy = remote(shares.at[half], shares.at[half], core_send.at[2], core_recv.at[2], sibling())

    def part_copies(e):
        return [
            pltpu.make_async_copy(gate_buf, gate_own.at[e], sem_out.at[0]),
            pltpu.make_async_copy(up_buf, up_own.at[e], sem_out.at[1]),
            pltpu.make_async_copy(down_buf, down_own.at[e], sem_out.at[2]),
            remote(gate_buf, gate_other.at[e], part_send.at[0], part_recv.at[e, 0], sibling()),
            remote(up_buf, up_other.at[e], part_send.at[1], part_recv.at[e, 1], sibling()),
            remote(down_buf, down_other.at[e], part_send.at[2], part_recv.at[e, 2], sibling()),
        ]

    def sent(e):
        made = part_copies(e)
        for copy in made[:3]:
            copy.wait()
        for copy in made[3:]:
            copy.wait_send()

    def expert(e, carry):
        slot = lax.rem(e, 2)
        mine = expert_rows(e)
        own = [
            pltpu.make_async_copy(rows_hbm.at[:, mine], both_rows.at[side], sem_own.at[0]),
            pltpu.make_async_copy(pair_hbm.at[:, mine], both_pair.at[side], sem_own.at[1]),
            pltpu.make_async_copy(hidden_hbm.at[e], both_hidden.at[side], sem_own.at[2]),
            pltpu.make_async_copy(gg_hbm.at[e], both_gate.at[side, :, pl.ds(0, ff)], sem_own.at[3]),
            pltpu.make_async_copy(ug_hbm.at[e], both_gate.at[side, :, pl.ds(ff, ff)], sem_own.at[4]),
        ]
        for copy in own:
            copy.start()
        for copy in fetch(e, slot):
            copy.wait()

        @pl.when(e < 3)
        def _():
            for copy in fetch(e + 1, 1 - slot):
                copy.start()

        rows_e = rows[:, mine].reshape(TAKEN, width)
        pair_e = pair_grad[:, mine].reshape(TAKEN, width)
        hidden, gate_grad, up_grad = expert_inner(rows_e, pair_e, gate[slot], up[slot], down[slot])
        both_rows[other] = rows_e.reshape(4, SLOT, width)
        both_pair[other] = pair_e.reshape(4, SLOT, width)
        both_hidden[other] = hidden
        both_gate[other, :, 0:ff] = gate_grad
        both_gate[other, :, ff : 2 * ff] = up_grad

        @pl.when(e == 0)
        def _():
            load_part.wait()
            total.start()
            spread.wait()
            spread_own.wait()
            wo_sum = jnp.zeros((64, width), f32)
            small_sum = jnp.zeros((64, LANE_SHARE), f32)
            for i in range(8):
                wo_sum = wo_sum + all_got[i, :, 0:width].astype(f32)
                small_sum = small_sum + all_got[i, :, width + 256 : wide].astype(f32)
                side_sum[:, width + LANE_SHARE + i * 256 : width + LANE_SHARE + (i + 1) * 256] = all_got[
                    i, :, width : width + 256
                ]
            side_sum[:, 0:width] = wo_sum.astype(bf16)
            side_sum[:, width : width + LANE_SHARE] = small_sum.astype(bf16)
            side_copy.start()

        @pl.when(e == 1)
        def _():
            total.middle()

        @pl.when(e == 2)
        def _():
            total.last()
            side_copy.wait()
            shares[half] = (side_sum[...].astype(f32) + side_got[...].astype(f32)).astype(bf16)
            last_copy.start()

        for copy in own:
            copy.wait()

        @pl.when(e >= 1)
        def _():
            sent(e - 1)

        sums = dot_first(both_rows[...].reshape(2 * TAKEN, width), both_gate[...].reshape(2 * TAKEN, 2 * ff))
        gate_buf[...] = sums[:, :ff].astype(bf16)
        up_buf[...] = sums[:, ff:].astype(bf16)
        down_buf[...] = dot_first(
            both_hidden[...].reshape(2 * TAKEN, ff), both_pair[...].reshape(2 * TAKEN, width)
        ).astype(bf16)
        for copy in part_copies(e):
            copy.start()
        return carry

    lax.fori_loop(0, 4, expert, 0)

    def store(where, value):
        mixed[where] = (residual[where] + value).astype(bf16)

    total.finish(store)
    total.sent()
    last_copy.wait()
    sent(3)
    for e in range(4):
        for copy in part_copies(e)[3:]:
            copy.wait_recv()


def expert_weights(x, c, routes, weights, upper, gate_w, up_w, down_w, kept, out_part, residual, grads):
    width = gate_w.shape[1]
    ff = gate_w.shape[-1]
    wide = grads.shape[-1]
    out = [jax.ShapeDtypeStruct(w.shape, bf16) for w in (gate_w, up_w, down_w)]
    sums = cube_sum_scratch(width)
    return pl.pallas_call(
        expert_weights_kernel,
        out_shape=(
            *out,
            *out,
            jax.ShapeDtypeStruct((256, width), bf16),
            jax.ShapeDtypeStruct((128, width + LANE_SHARE + 2048), bf16),
        ),
        in_specs=[anywhere()] * 2 + [vmem()] * 3 + [anywhere()] * 9 + [vmem()] * 2,
        out_specs=(anywhere(),) * 6 + (vmem(),) * 2,
        scratch_shapes=[
            pltpu.VMEM((2, 2, 2, 256, width), bf16),
            pltpu.VMEM((2, 2, 2, 256, width), bf16),
            pltpu.VMEM((4, TAKEN, SPAN), bf16),
            pltpu.VMEM((4, TAKEN, width), bf16),
            pltpu.VMEM((4, TAKEN, width), bf16),
            pltpu.VMEM((4, TAKEN, 1), f32),
            pltpu.VMEM((2, width, ff), bf16),
            pltpu.VMEM((2, width, ff), bf16),
            pltpu.VMEM((2, ff, width), bf16),
            pltpu.VMEM((2, 4, SLOT, width), bf16),
            pltpu.VMEM((2, 4, SLOT, width), bf16),
            pltpu.VMEM((2, TAKEN, ff), bf16),
            pltpu.VMEM((2, TAKEN, 2 * ff), bf16),
            pltpu.VMEM((width, ff), bf16),
            pltpu.VMEM((width, ff), bf16),
            pltpu.VMEM((ff, width), bf16),
            *sums[:3],
            sums[4],
            sums[6],
            pltpu.VMEM((8, 64, wide), bf16),
            pltpu.VMEM((8, 64, wide), bf16),
            pltpu.VMEM((8, 64, wide), bf16),
            pltpu.VMEM((64, width + LANE_SHARE + 2048), bf16),
            pltpu.VMEM((64, width + LANE_SHARE + 2048), bf16),
            *sums[7:],
            pltpu.SemaphoreType.DMA((8,)),
            pltpu.SemaphoreType.DMA((8,)),
            pltpu.SemaphoreType.DMA((3,)),
            pltpu.SemaphoreType.DMA((3,)),
            pltpu.SemaphoreType.DMA((3,)),
            pltpu.SemaphoreType.DMA((4, 3)),
            pltpu.SemaphoreType.DMA((2,)),
            pltpu.SemaphoreType.DMA((2, 3)),
            pltpu.SemaphoreType.DMA((5,)),
            pltpu.SemaphoreType.DMA((3,)),
            pltpu.SemaphoreType.DMA,
        ],
        compiler_params=pltpu.CompilerParams(
            collective_id=3, has_side_effects=True, vmem_limit_bytes=VMEM_LIMIT
        ),
        name="expert_weights",
    )(x, c, routes, weights, upper, gate_w, up_w, down_w, *kept, out_part, residual, grads)


def finish_kernel(
    gate_own, up_own, down_own, gate_other, up_other, down_other, shares,
    gate_out, up_out, down_out, query_out, key_out, value_out, wo_out, small_out,
):
    for own, other, out in ((gate_own, gate_other, gate_out), (up_own, up_other, up_out), (down_own, down_other, down_out)):
        out[...] = own[...].astype(f32) + other[...].astype(f32)

    @pl.when(pl.program_id(0) == 0)
    def _():
        width = wo_out.shape[-1]
        wo_out[...] = shares[:, 0:width].astype(f32)
        small_out[...] = shares[:, width : width + LANE_SHARE].astype(f32)
        low = lanes((128, 128)) < 64
        base = width + LANE_SHARE
        for j in range(8):
            query_out[:, j * 128 : (j + 1) * 128] = shares[:, base + j * 256 : base + j * 256 + 128].astype(f32)
        for j in range(4):
            left = shares[:, base + j * 512 + 128 : base + j * 512 + 256].astype(f32)
            right = shares[:, base + j * 512 + 384 : base + j * 512 + 512].astype(f32)
            where = slice(j * 128, (j + 1) * 128)
            key_out[:, where] = jnp.where(low, left, pltpu.roll(right, 64, 1))
            value_out[:, where] = jnp.where(low, pltpu.roll(left, 64, 1), right)


def finish(parts, shares):
    width = parts[0].shape[1]

    def block(shape):
        return pl.BlockSpec((1,) + shape[1:], lambda e: (e, 0, 0))

    def whole(shape):
        return pl.BlockSpec(shape, lambda e: (0,) * len(shape))

    small = [(128, 1024), (128, 512), (128, 512), (128, width), (128, LANE_SHARE)]
    return pl.pallas_call(
        finish_kernel,
        grid=(parts[0].shape[0],),
        out_shape=tuple(jax.ShapeDtypeStruct(p.shape, f32) for p in parts[:3])
        + tuple(jax.ShapeDtypeStruct(shape, f32) for shape in small),
        in_specs=[block(p.shape) for p in parts] + [whole(shares.shape)],
        out_specs=tuple(block(p.shape) for p in parts[:3]) + tuple(whole(shape) for shape in small),
        compiler_params=pltpu.CompilerParams(vmem_limit_bytes=VMEM_LIMIT),
        name="finish",
    )(*parts, shares)


def fast_on_device(
    tokens, segments, routes, cotangent, attn_gain, moe_gain, query_weight, key_projection_matrix,
    value_projection_matrix, out_weight, router_weight, gate_weight, up_weight, down_weight,
):
    width = tokens.shape[-1]
    tok = tokens.reshape(256, width)
    cot = cotangent.reshape(256, width)
    wkv = jnp.concatenate(
        [key_projection_matrix.reshape(128, 8, 64), value_projection_matrix.reshape(128, 8, 64)], -1
    ).reshape(128, 1024)
    gains = jnp.concatenate([attn_gain[None], moe_gain[None], jnp.zeros((14, 128), bf16)], 0)
    my_routes = routes.reshape(256, TOP).T
    seg_col, seg_row = segments[:, :, None], segments[:, None, :]
    places = jnp.arange(SPAN)
    upper = (places[:, None] < places[None, :]).astype(bf16)
    (
        attn_in, q, kv, amix, residual, moe_in, weights, wo_all, gains_all, router_all, routes_all,
        cot_all, cot_mirror, routes_mirror,
    ) = forward(tok, cot, query_weight, wkv, out_weight, gains, router_weight, my_routes, seg_col, seg_row)
    out_part, in_sum, p_all, *kept, cot_mirror_all, moe_mirror, weights_mirror = experts(
        moe_in, weights, cot_mirror, cot_all, routes_all, upper, gate_weight, up_weight, down_weight
    )
    token_grad, grads, moe_mirror_all = backward(
        cot, residual, in_sum, p_all, my_routes, weights, router_all, moe_in, gains_all, wo_all, amix, attn_in,
        q, kv, seg_col, seg_row, tok, query_weight, wkv, moe_mirror,
    )
    *parts, mixed, shares = expert_weights(
        moe_mirror_all, cot_mirror_all, routes_mirror, weights_mirror, upper, gate_weight, up_weight, down_weight,
        kept, out_part, residual, grads,
    )
    gate_grad, up_grad, down_grad, query_grad, key_grad, value_grad, wo_grad, small = finish(parts, shares)
    return (
        mixed.reshape(tokens.shape), token_grad.reshape(tokens.shape), small[:, 33], small[:, 32],
        query_grad, key_grad, value_grad, wo_grad, small[:, :32], gate_grad, up_grad, down_grad,
    )


def fits(mesh):
    return dict(mesh.shape) == {"group": 4, "blk": 4, "head": 2}


def solution(mesh):
    placed = (
        P("group", ("blk", "head"), None),
        P("group", None),
        P("group", ("blk", "head"), None),
        P("group", ("blk", "head"), None),
        P(("blk", "head")),
        P(("blk", "head")),
        P(("blk", "head"), None),
        P(("blk", "head"), None),
        P(("blk", "head"), None),
        P(("blk", "head"), None),
        P(("blk", "head"), None),
        P(("blk", "head"), None, None),
        P(("blk", "head"), None, None),
        P(("blk", "head"), None, None),
    )
    return jax.shard_map(
        fast_on_device if fits(mesh) else on_device,
        mesh=mesh,
        in_specs=placed,
        out_specs=(
            P("group", ("blk", "head"), None),
            P("group", ("blk", "head"), None),
            P(("blk", "head")),
            P(("blk", "head")),
            P(("blk", "head"), None),
            P(("blk", "head"), None),
            P(("blk", "head"), None),
            P(("blk", "head"), None),
            P(("blk", "head"), None),
            P(("blk", "head"), None, None),
            P(("blk", "head"), None, None),
            P(("blk", "head"), None, None),
        ),
        check_vma=False,
    )
```

```python
import functools

import jax
import jax.numpy as jnp
import numpy as np
from jax import lax
from jax.experimental import pallas as pl
from jax.experimental.pallas import tpu as pltpu
from jax.sharding import PartitionSpec as P

QUERY_HEADS = 16
KEY_VALUE_HEADS = 8
HEAD_SIZE = 64
TOP = 8
CAPH = 36


epsilon = 1e-05
rope_base = 10000.0
masked_out = -1e30
key_block = 512


def rms_norm(values, gain_vec):
    return values * lax.rsqrt(jnp.mean(values * values, -1, keepdims=True) + epsilon) * gain_vec


def rotary_embedding(field_vals, places, turn_sign):
    half_dim = field_vals.shape[-1] // 2
    frequency = rope_base ** (-jnp.arange(half_dim, dtype=jnp.float32) * 2.0 / field_vals.shape[-1])
    angles = places.astype(jnp.float32)[:, None] * frequency[None, :]
    cosine = jnp.cos(angles)[:, None, :]
    sine_vals = turn_sign * jnp.sin(angles)[:, None, :]
    first_half = field_vals[..., :half_dim]
    second = field_vals[..., half_dim:]
    return jnp.concatenate(
        [first_half * cosine - second * sine_vals, second * cosine + first_half * sine_vals], -1
    )


def add_rows(running, addend, row_start):
    current = lax.dynamic_slice_in_dim(running, row_start, addend.shape[1], 1)
    return lax.dynamic_update_slice_in_dim(running, current + addend, row_start, 1)


def on_device(
    tokens,
    segments,
    routes,
    cotangent,
    attn_gain,
    moe_gain,
    query_weight,
    key_projection_matrix,
    value_projection_matrix,
    out_weight,
    router_weight,
    gate_weight,
    up_weight,
    down_weight,
):
    head_groups, number_of_rows, width_dim = tokens.shape
    query_per_key_head = QUERY_HEADS // KEY_VALUE_HEADS
    shared_head_count = lax.axis_size("head")
    query_rows = number_of_rows * shared_head_count
    grouped_keys = KEY_VALUE_HEADS // shared_head_count
    scale_val = HEAD_SIZE ** (-0.5)
    number_of_tokens = head_groups * number_of_rows
    seq_length = lax.axis_size("blk") * query_rows
    cycle_index = lax.axis_index("blk")
    local_placement = (
        cycle_index * shared_head_count + lax.axis_index("head")
    ) * number_of_rows + jnp.arange(number_of_rows, dtype=jnp.int32)
    own_start = cycle_index * query_rows
    query_place = own_start + jnp.arange(query_rows, dtype=jnp.int32)
    query_doc = lax.dynamic_slice_in_dim(segments, own_start, query_rows, 1)
    query_full, key_full, value_full, out_full, router_full, gain_attn, gain_moe = (
        lax.all_gather(query_weight, ("blk", "head"), axis=0, tiled=True),
        lax.all_gather(key_projection_matrix, ("blk", "head"), axis=0, tiled=True),
        lax.all_gather(value_projection_matrix, ("blk", "head"), axis=0, tiled=True),
        lax.all_gather(out_weight, ("blk", "head"), axis=0, tiled=True),
        lax.all_gather(router_weight, ("blk", "head"), axis=0, tiled=True),
        lax.all_gather(attn_gain, ("blk", "head"), axis=0, tiled=True),
        lax.all_gather(moe_gain, ("blk", "head"), axis=0, tiled=True),
    )
    flat_rows = tokens.reshape(number_of_tokens, width_dim).astype(jnp.float32)
    attn_normed, attn_pull = jax.vjp(rms_norm, flat_rows, gain_attn.astype(jnp.float32))
    attn_in = attn_normed.astype(jnp.bfloat16)
    query_pre = jnp.dot(attn_in, query_full, preferred_element_type=jnp.float32)
    key_before_rotary = jnp.dot(attn_in, key_full, preferred_element_type=jnp.float32)
    value_low = (
        jnp.dot(attn_in, value_full, preferred_element_type=jnp.float32)
        .astype(jnp.bfloat16)
        .reshape(head_groups, number_of_rows, KEY_VALUE_HEADS * HEAD_SIZE)
    )
    query_low = (
        rotary_embedding(
            query_pre.reshape(head_groups, number_of_rows, QUERY_HEADS, HEAD_SIZE),
            local_placement,
            1.0,
        )
        .astype(jnp.bfloat16)
        .reshape(head_groups, number_of_rows, QUERY_HEADS * HEAD_SIZE)
    )
    key_low = (
        rotary_embedding(
            key_before_rotary.reshape(head_groups, number_of_rows, KEY_VALUE_HEADS, HEAD_SIZE),
            local_placement,
            1.0,
        )
        .astype(jnp.bfloat16)
        .reshape(head_groups, number_of_rows, KEY_VALUE_HEADS * HEAD_SIZE)
    )
    query_split, key_split, value_split = (
        lax.all_to_all(query_low, "head", split_axis=2, concat_axis=1, tiled=True),
        lax.all_to_all(key_low, "head", split_axis=2, concat_axis=1, tiled=True),
        lax.all_to_all(value_low, "head", split_axis=2, concat_axis=1, tiled=True),
    )
    query_vectors = query_split.reshape(
        head_groups, query_rows, grouped_keys, query_per_key_head, HEAD_SIZE
    )

    def key_view(source, offset, sub_rows):
        return lax.dynamic_slice_in_dim(source, offset, sub_rows, 1).reshape(
            head_groups, sub_rows, grouped_keys, HEAD_SIZE
        )

    def scored_at(query_part, key_row_block, q_place, q_doc, key_start, sub_rows):
        raw_scores = (
            jnp.einsum(
                "bqgrd,bkgd->bqgrk", query_part, key_row_block, preferred_element_type=jnp.float32
            )
            * scale_val
        )
        key_place = key_start + jnp.arange(sub_rows, dtype=jnp.int32)
        key_doc = lax.dynamic_slice_in_dim(segments, key_start, sub_rows, 1)
        allowed = (q_place[None, :, None] >= key_place[None, None, :]) & (
            q_doc[:, :, None] == key_doc[:, None, :]
        )
        return (raw_scores, allowed[:, :, None, None, :])

    def scored(key_row_block, key_start, sub_rows):
        return scored_at(query_vectors, key_row_block, query_place, query_doc, key_start, sub_rows)

    stats_shape = (head_groups, query_rows, grouped_keys, query_per_key_head)
    init_state = (
        jnp.full(stats_shape, masked_out, jnp.float32),
        jnp.zeros(stats_shape, jnp.float32),
        jnp.zeros(stats_shape + (HEAD_SIZE,), jnp.float32),
    )
    key_all, value_all = (
        lax.all_gather(key_split, "blk", axis=1, tiled=True),
        lax.all_gather(value_split, "blk", axis=1, tiled=True),
    )
    fold_state = init_state
    total_rows = key_all.shape[1]
    sub_rows = key_block

    def forward_one_block(block_state, block_index):
        offset = block_index * sub_rows
        key_row_block = key_view(key_all, offset, sub_rows)
        value_row_block = key_view(value_all, offset, sub_rows)
        raw_scores, allowed = scored(key_row_block, 0 + offset, sub_rows)
        running_max, running_sum, running_acc = block_state
        masked = jnp.where(allowed, raw_scores, masked_out)
        new_max = jnp.maximum(running_max, jnp.max(masked, -1))
        shrink = jnp.exp(running_max - new_max)
        weights_soft = jnp.where(allowed, jnp.exp(masked - new_max[..., None]), 0.0)
        new_sum = running_sum * shrink + jnp.sum(weights_soft, -1)
        new_acc = running_acc * shrink[..., None] + jnp.einsum(
            "bqgrk,bkgd->bqgrd",
            weights_soft.astype(jnp.bfloat16),
            value_row_block,
            preferred_element_type=jnp.float32,
        )
        return ((new_max, new_sum, new_acc), None)

    fold_state, unused = lax.scan(
        forward_one_block, fold_state, jnp.arange(total_rows // sub_rows, dtype=jnp.int32)
    )
    running_max, running_sum, running_acc = fold_state
    mix_heads = running_acc / running_sum[..., None]
    log_total = running_max + jnp.log(running_sum)
    mix_low = mix_heads.astype(jnp.bfloat16).reshape(
        head_groups, query_rows, grouped_keys * query_per_key_head * HEAD_SIZE
    )
    mix_tokens = lax.all_to_all(mix_low, "head", split_axis=1, concat_axis=2, tiled=True)
    attn_mix = mix_tokens.reshape(number_of_tokens, QUERY_HEADS * HEAD_SIZE)
    residual = flat_rows + jnp.dot(attn_mix, out_full, preferred_element_type=jnp.float32)
    moe_normed, moe_pull = jax.vjp(rms_norm, residual, gain_moe.astype(jnp.float32))
    moe_in = moe_normed.astype(jnp.bfloat16)
    logits = jnp.dot(moe_in, router_full, preferred_element_type=jnp.float32)
    route_flat = routes.reshape(number_of_tokens, TOP)
    experts_all = router_full.shape[1]
    choose = route_flat[:, :, None] == jnp.arange(experts_all, dtype=jnp.int32)[None, None, :]
    choose_float = choose.astype(jnp.float32)
    picked_logits = jnp.einsum("nke,ne->nk", choose_float, logits)
    route_weights = jax.nn.softmax(picked_logits, axis=-1)
    choose_whole = choose.astype(jnp.int32).reshape(head_groups, number_of_rows * TOP, experts_all)
    slot_rank = jnp.sum(jnp.cumsum(choose_whole, 1) * choose_whole, -1) - 1
    slot_index = (slot_rank + jnp.arange(head_groups, dtype=jnp.int32)[:, None] * CAPH).reshape(-1)
    targets = route_flat.reshape(-1)
    lane_count = head_groups * CAPH
    outgoing = (
        jnp.zeros((experts_all, lane_count, width_dim), jnp.bfloat16)
        .at[targets, slot_index]
        .set(jnp.repeat(moe_in, TOP, axis=0))
    )
    arrived = lax.all_to_all(outgoing, ("blk", "head"), split_axis=0, concat_axis=1, tiled=True)
    gate_val = jnp.einsum("end,edf->enf", arrived, gate_weight, preferred_element_type=jnp.float32)
    up_val = jnp.einsum("end,edf->enf", arrived, up_weight, preferred_element_type=jnp.float32)
    hidden_low = (jax.nn.silu(gate_val) * up_val).astype(jnp.bfloat16)
    expert_out = jnp.einsum(
        "enf,efd->end", hidden_low, down_weight, preferred_element_type=jnp.float32
    ).astype(jnp.bfloat16)
    returned = lax.all_to_all(expert_out, ("blk", "head"), split_axis=1, concat_axis=0, tiled=True)
    picked_rows = returned[targets, slot_index].reshape(number_of_tokens, TOP, width_dim)
    moe_out = jnp.einsum(
        "nk,nkd->nd", route_weights, picked_rows, preferred_element_type=jnp.float32
    )
    mixed = (
        (residual + moe_out).astype(jnp.bfloat16).reshape(head_groups, number_of_rows, width_dim)
    )
    grad_full = cotangent.reshape(number_of_tokens, width_dim).astype(jnp.float32)
    weight_grad = jnp.einsum(
        "nkd,nd->nk", picked_rows, grad_full, preferred_element_type=jnp.float32
    )
    pair_grad = (
        (route_weights[:, :, None] * grad_full[:, None, :])
        .astype(jnp.bfloat16)
        .reshape(number_of_tokens * TOP, width_dim)
    )
    grad_outgoing = jnp.zeros_like(outgoing).at[targets, slot_index].set(pair_grad)
    grad_arrived = lax.all_to_all(
        grad_outgoing, ("blk", "head"), split_axis=0, concat_axis=1, tiled=True
    )
    grad_hidden = jnp.einsum(
        "end,efd->enf", grad_arrived, down_weight, preferred_element_type=jnp.float32
    )
    sigmoid_val = jax.nn.sigmoid(gate_val)
    grad_gate = (
        grad_hidden * up_val * sigmoid_val * (1.0 + gate_val * (1.0 - sigmoid_val))
    ).astype(jnp.bfloat16)
    grad_up = (grad_hidden * gate_val * sigmoid_val).astype(jnp.bfloat16)
    down_weight_grad = jnp.einsum(
        "enf,end->efd", hidden_low, grad_arrived, preferred_element_type=jnp.float32
    )
    gate_weight_grad = jnp.einsum(
        "end,enf->edf", arrived, grad_gate, preferred_element_type=jnp.float32
    )
    up_weight_grad = jnp.einsum(
        "end,enf->edf", arrived, grad_up, preferred_element_type=jnp.float32
    )
    pair_back = (
        jnp.einsum("enf,edf->end", grad_gate, gate_weight, preferred_element_type=jnp.float32)
        + jnp.einsum("enf,edf->end", grad_up, up_weight, preferred_element_type=jnp.float32)
    ).astype(jnp.bfloat16)
    grad_returned = lax.all_to_all(
        pair_back, ("blk", "head"), split_axis=1, concat_axis=0, tiled=True
    )
    moe_in_grad = jnp.sum(
        grad_returned[targets, slot_index].reshape(number_of_tokens, TOP, width_dim),
        axis=1,
        dtype=jnp.float32,
    )
    mean_term = jnp.sum(route_weights * weight_grad, -1, keepdims=True)
    logit_grad = jnp.einsum("nk,nke->ne", route_weights * (weight_grad - mean_term), choose_float)
    router_grad = jnp.dot(moe_in.T, logit_grad, preferred_element_type=jnp.float32)
    moe_in_grad = moe_in_grad + jnp.dot(
        logit_grad, router_full.T, preferred_element_type=jnp.float32
    )
    residual_part, moe_gain_grad = moe_pull(moe_in_grad)
    residual_grad = grad_full + residual_part
    out_grad_low = residual_grad.astype(jnp.bfloat16)
    out_weight_grad = jnp.dot(attn_mix.T, out_grad_low, preferred_element_type=jnp.float32)
    mix_grad = (
        jnp.dot(out_grad_low, out_full.T, preferred_element_type=jnp.float32)
        .astype(jnp.bfloat16)
        .reshape(head_groups, number_of_rows, QUERY_HEADS * HEAD_SIZE)
    )
    mix_grad_heads = lax.all_to_all(
        mix_grad, "head", split_axis=2, concat_axis=1, tiled=True
    ).reshape(head_groups, query_rows, grouped_keys, query_per_key_head, HEAD_SIZE)
    delta_term = jnp.sum(mix_grad_heads.astype(jnp.float32) * mix_heads, -1)
    query_zero = jnp.zeros(stats_shape + (HEAD_SIZE,), jnp.float32)
    back_init = (
        query_zero,
        jnp.zeros((head_groups, seq_length, grouped_keys, HEAD_SIZE), jnp.float32),
        jnp.zeros((head_groups, seq_length, grouped_keys, HEAD_SIZE), jnp.float32),
    )
    fold_state = back_init
    total_rows = key_all.shape[1]

    def backward_one_block(block_state, block_index):
        offset = block_index * key_block
        key_start = 0 + offset
        key_row_block = key_view(key_all, offset, key_block)
        value_row_block = key_view(value_all, offset, key_block)
        raw_scores, allowed = scored(key_row_block, key_start, key_block)
        masked = jnp.where(allowed, raw_scores, masked_out)
        probability = jnp.where(allowed, jnp.exp(masked - log_total[..., None]), 0.0)
        prob_grad = jnp.einsum(
            "bqgrd,bkgd->bqgrk", mix_grad_heads, value_row_block, preferred_element_type=jnp.float32
        )
        score_grad = (probability * (prob_grad - delta_term[..., None]) * scale_val).astype(
            jnp.bfloat16
        )
        grad_query = block_state[0] + jnp.einsum(
            "bqgrk,bkgd->bqgrd", score_grad, key_row_block, preferred_element_type=jnp.float32
        )
        value_part_grad = jnp.einsum(
            "bqgrk,bqgrd->bkgd",
            probability.astype(jnp.bfloat16),
            mix_grad_heads,
            preferred_element_type=jnp.float32,
        )
        key_part_grad = jnp.einsum(
            "bqgrk,bqgrd->bkgd", score_grad, query_vectors, preferred_element_type=jnp.float32
        )
        grad_keys = add_rows(block_state[1], key_part_grad, key_start)
        grad_values = add_rows(block_state[2], value_part_grad, key_start)
        return ((grad_query, grad_keys, grad_values), None)

    fold_state, unused = lax.scan(
        backward_one_block, fold_state, jnp.arange(total_rows // key_block, dtype=jnp.int32)
    )
    grad_query, grad_keys, grad_values = fold_state
    key_own, value_own = (
        lax.psum_scatter(
            grad_keys.reshape(head_groups, seq_length, grouped_keys * HEAD_SIZE).astype(
                jnp.bfloat16
            ),
            "blk",
            scatter_dimension=1,
            tiled=True,
        ).astype(jnp.float32),
        lax.psum_scatter(
            grad_values.reshape(head_groups, seq_length, grouped_keys * HEAD_SIZE).astype(
                jnp.bfloat16
            ),
            "blk",
            scatter_dimension=1,
            tiled=True,
        ).astype(jnp.float32),
    )
    query_grad_low = (
        rotary_embedding(
            grad_query.reshape(
                head_groups, query_rows, grouped_keys * query_per_key_head, HEAD_SIZE
            ),
            query_place,
            -1.0,
        )
        .astype(jnp.bfloat16)
        .reshape(head_groups, query_rows, grouped_keys * query_per_key_head * HEAD_SIZE)
    )
    key_grad_low = (
        rotary_embedding(
            key_own.reshape(head_groups, query_rows, grouped_keys, HEAD_SIZE), query_place, -1.0
        )
        .astype(jnp.bfloat16)
        .reshape(head_groups, query_rows, grouped_keys * HEAD_SIZE)
    )
    value_grad_low = value_own.astype(jnp.bfloat16)
    query_back, key_pullback, value_pullback = (
        lax.all_to_all(query_grad_low, "head", split_axis=1, concat_axis=2, tiled=True),
        lax.all_to_all(key_grad_low, "head", split_axis=1, concat_axis=2, tiled=True),
        lax.all_to_all(value_grad_low, "head", split_axis=1, concat_axis=2, tiled=True),
    )
    query_flat = query_back.reshape(number_of_tokens, QUERY_HEADS * HEAD_SIZE)
    flattened_keys = key_pullback.reshape(number_of_tokens, KEY_VALUE_HEADS * HEAD_SIZE)
    flattened_values = value_pullback.reshape(number_of_tokens, KEY_VALUE_HEADS * HEAD_SIZE)
    query_weight_grad = jnp.dot(attn_in.T, query_flat, preferred_element_type=jnp.float32)
    key_weight_grad = jnp.dot(attn_in.T, flattened_keys, preferred_element_type=jnp.float32)
    value_weight_grad = jnp.dot(attn_in.T, flattened_values, preferred_element_type=jnp.float32)
    attn_in_grad = (
        jnp.dot(query_flat, query_full.T, preferred_element_type=jnp.float32)
        + jnp.dot(flattened_keys, key_full.T, preferred_element_type=jnp.float32)
        + jnp.dot(flattened_values, value_full.T, preferred_element_type=jnp.float32)
    )
    input_part, attn_gain_grad = attn_pull(attn_in_grad)
    token_grad = (residual_grad + input_part).reshape(head_groups, number_of_rows, width_dim)
    (
        query_shard,
        key_shard,
        value_shard,
        out_shard,
        router_shard,
        attn_gain_shard,
        moe_gain_shard,
    ) = (
        lax.psum_scatter(
            query_weight_grad.astype(jnp.bfloat16), ("blk", "head"), scatter_dimension=0, tiled=True
        ).astype(jnp.float32),
        lax.psum_scatter(
            key_weight_grad.astype(jnp.bfloat16), ("blk", "head"), scatter_dimension=0, tiled=True
        ).astype(jnp.float32),
        lax.psum_scatter(
            value_weight_grad.astype(jnp.bfloat16), ("blk", "head"), scatter_dimension=0, tiled=True
        ).astype(jnp.float32),
        lax.psum_scatter(
            out_weight_grad.astype(jnp.bfloat16), ("blk", "head"), scatter_dimension=0, tiled=True
        ).astype(jnp.float32),
        lax.psum_scatter(
            router_grad.astype(jnp.bfloat16), ("blk", "head"), scatter_dimension=0, tiled=True
        ).astype(jnp.float32),
        lax.psum_scatter(
            attn_gain_grad.astype(jnp.bfloat16), ("blk", "head"), scatter_dimension=0, tiled=True
        ).astype(jnp.float32),
        lax.psum_scatter(
            moe_gain_grad.astype(jnp.bfloat16), ("blk", "head"), scatter_dimension=0, tiled=True
        ).astype(jnp.float32),
    )
    summed = (
        lax.psum(query_shard.astype(jnp.bfloat16), "group").astype(jnp.float32),
        lax.psum(key_shard.astype(jnp.bfloat16), "group").astype(jnp.float32),
        lax.psum(value_shard.astype(jnp.bfloat16), "group").astype(jnp.float32),
        lax.psum(out_shard.astype(jnp.bfloat16), "group").astype(jnp.float32),
        lax.psum(router_shard.astype(jnp.bfloat16), "group").astype(jnp.float32),
        lax.psum(attn_gain_shard.astype(jnp.bfloat16), "group").astype(jnp.float32),
        lax.psum(moe_gain_shard.astype(jnp.bfloat16), "group").astype(jnp.float32),
        lax.psum(gate_weight_grad.astype(jnp.bfloat16), "group").astype(jnp.float32),
        lax.psum(up_weight_grad.astype(jnp.bfloat16), "group").astype(jnp.float32),
        lax.psum(down_weight_grad.astype(jnp.bfloat16), "group").astype(jnp.float32),
    )
    return (
        mixed,
        token_grad,
        summed[5],
        summed[6],
        summed[0],
        summed[1],
        summed[2],
        summed[3],
        summed[4],
        summed[7],
        summed[8],
        summed[9],
    )


bf16 = jnp.bfloat16
f32 = jnp.float32
MESH_ID = pl.DeviceIdType.MESH
VMEM_LIMIT = 66 * 1000 * 1000
COLOURS = ((0, 96), (96, 80), (176, 80))
LINKS = (("head", 1), ("blk", 1), ("blk", 2), ("group", 2), ("group", 1))
ORDERS = ((0, 1, 2), (1, 2, 0), (2, 0, 1))


def vmem():
    return pl.BlockSpec(memory_space=pltpu.VMEM)


def anywhere():
    return pl.BlockSpec(memory_space=pl.ANY)


def dot_last(left, right):
    return lax.dot_general(left, right, (((1,), (1,)), ((), ())), preferred_element_type=f32)


def dot_first(left, right):
    return lax.dot_general(left, right, (((0,), (0,)), ((), ())), preferred_element_type=f32)


def dot(left, right):
    return jnp.dot(left, right, preferred_element_type=f32)


def my_place():
    return lax.axis_index("blk") * 2 + lax.axis_index("head")


def peer(step):
    place = lax.rem(my_place() + step, 8)
    return place, {"blk": place // 2, "head": lax.rem(place, 2)}


def neighbour(link):
    if link == 0:
        return {"head": 1 - lax.axis_index("head")}
    blk = lax.axis_index("blk")
    if link == 1:
        return {"blk": blk + 1 - 2 * lax.rem(blk, 2)}
    return {"blk": lax.rem(blk + 2, 4)}


def my_bits():
    blk = lax.axis_index("blk")
    return (lax.axis_index("head"), lax.rem(blk, 2), blk // 2)


def meet_all():
    barrier = pltpu.get_barrier_semaphore()
    for step in range(1, 8):
        pl.semaphore_signal(barrier, 1, device_id=peer(step)[1], device_id_type=MESH_ID)
    pl.semaphore_wait(barrier, 7)


def remote(src, dst, send, recv, target):
    return pltpu.make_async_remote_copy(
        src_ref=src, dst_ref=dst, send_sem=send, recv_sem=recv, device_id=target, device_id_type=MESH_ID
    )


def cube_index(bits, fixed, rows):
    entries = [pl.ds(fixed[link], 1) if link in fixed else pl.ds(0, 2) for link in (2, 1, 0)]
    return tuple(entries) + (pl.ds(*rows),)


def lanes(shape):
    return lax.broadcasted_iota(jnp.int32, shape, len(shape) - 1)


def turned(u):
    low = lax.rem(lanes(u.shape), 64) < 32
    return jnp.where(low, -pltpu.roll(u, 96, 1), pltpu.roll(u, 32, 1))


def two_heads(q):
    low = lanes(q.shape) < 64
    return jnp.concatenate([jnp.where(low, q, 0.0), jnp.where(low, pltpu.roll(q, 64, 1), 0.0)], 0)


def two_heads_high(g):
    high = lanes(g.shape) >= 64
    return jnp.concatenate([jnp.where(high, pltpu.roll(g, 64, 1), 0.0), jnp.where(high, g, 0.0)], 0)


def block_probability(q_ref, kv_ref, docs, segs, s, i):
    first = max(0, i - 4) * 128
    count = (i + 1) * 128 - first
    q2 = two_heads(q_ref[s, pl.ds(i * 128, 128)].astype(f32))
    kv = kv_ref[s, pl.ds(first, count)]
    raw = dot_last((q2 * 0.125).astype(bf16), kv)
    q_place = i * 128 + lax.broadcasted_iota(jnp.int32, (128, count), 0)
    k_place = first + lanes((128, count))
    q_doc = docs[s, pl.ds(i * 128, 128)]
    keys = pl.ds(first, count)
    k_doc = jnp.where(s == 0, segs[0:1, keys], segs[1:2, keys]).astype(f32)
    allowed = (q_place >= k_place) & (q_doc == k_doc)
    allowed = jnp.concatenate([allowed, allowed], 0)
    masked = jnp.where(allowed, raw, masked_out)
    top = jnp.max(masked, -1, keepdims=True)
    weight = jnp.exp(masked - top)
    probability = weight * (1.0 / jnp.sum(weight, -1, keepdims=True))
    return first, count, q2, kv, probability


def norm_back(values, gain, grad):
    scale = lax.rsqrt(jnp.mean(values * values, -1, keepdims=True) + epsilon)
    inner = grad * gain
    along = jnp.mean(values * inner, -1, keepdims=True)
    out = scale * inner - values * (scale * scale * scale * along)
    gain_grad = jnp.sum(grad * values * scale, 0, keepdims=True)
    return out, gain_grad


def expert_inner(rows_e, pair_e, gate_w, up_w, down_w):
    gate_val = dot(rows_e, gate_w)
    up_val = dot(rows_e, up_w)
    sig = 1.0 / (1.0 + jnp.exp(-gate_val))
    silu = gate_val * sig
    hidden = (silu * up_val).astype(bf16)
    hidden_grad = dot_last(pair_e, down_w)
    gate_grad = (hidden_grad * up_val * sig * (1.0 + gate_val * (1.0 - sig))).astype(bf16)
    up_grad = (hidden_grad * silu).astype(bf16)
    return hidden, gate_grad, up_grad


def sibling():
    group = lax.axis_index("group")
    return {"group": group + 1 - 2 * lax.rem(group, 2)}


def mirror():
    return {"group": lax.rem(lax.axis_index("group") + 2, 4)}


def my_core():
    return lax.rem(lax.axis_index("group"), 2)


def meet(targets):
    barrier = pltpu.get_barrier_semaphore()
    for target in targets:
        pl.semaphore_signal(barrier, 1, device_id=target, device_id_type=MESH_ID)
    pl.semaphore_wait(barrier, len(targets))


def peers():
    return [peer(step)[1] for step in range(1, 8)]


def cube_entry(fixed):
    return tuple(pl.ds(fixed[link], 1) if link in fixed else pl.ds(0, 2) for link in (2, 1, 0))


class Gather:
    def __init__(self, items, send, recv):
        self.items, self.send, self.recv, self.bits = items, send, recv, my_bits()

    def copies(self, step):
        made = []
        for k, (src, place, order) in enumerate(self.items):
            fixed = {link: self.bits[link] for link in order[step:]}
            where = place(cube_entry(fixed))
            here = where
            if step == 0:
                here = src
                where = place((self.bits[2], self.bits[1], self.bits[0]))
            made.append(remote(here, where, self.send.at[step, k], self.recv.at[step, k], neighbour(order[step])))
        return made

    def start(self, step):
        for copy in self.copies(step):
            copy.start()

    def wait(self, step):
        for copy in self.copies(step):
            copy.wait_recv()

    def advance(self, step):
        for before, after in zip(self.copies(step - 1), self.copies(step)):
            before.wait_recv()
            after.start()

    def sent(self):
        for step in range(3):
            for copy in self.copies(step):
                copy.wait_send()


def row_items(src, dst):
    def item(k):
        start, count = COLOURS[k]
        return (src.at[pl.ds(start, count)], lambda entry: dst.at[entry + (pl.ds(start, count),)], ORDERS[k])

    return [item(k) for k in range(3)]


ROW_CUTS = tuple((pl.ds(start, count), slice(None)) for start, count in COLOURS)


class CubeSum:
    def __init__(self, source, part, cuts, scratch):
        self.source, self.part, self.cuts = source, part, cuts
        *self.got, self.held0, self.got1, self.held1, self.got2, self.send, self.recv = scratch
        self.bits = my_bits()

    def copy(self, step, k):
        order, cut = ORDERS[k], self.cuts[k]
        other = 1 - self.bits[order[step]]
        if step == 0:
            src = self.source.at[cube_entry({order[0]: other}) + cut]
            dst = self.got[k]
        elif step == 1:
            src = self.held0.at[(other, slice(None)) + cut]
            dst = self.got1.at[(slice(None),) + cut]
        else:
            src = self.held1.at[(other,) + cut]
            dst = self.got2.at[cut]
        return remote(src, dst, self.send.at[step, k], self.recv.at[step, k], neighbour(order[step]))

    def start(self):
        for k in range(3):
            self.copy(0, k).start()

    def middle(self):
        for k, order in enumerate(ORDERS):
            self.copy(0, k).wait_recv()
            cut = self.cuts[k]
            for u in range(2):
                for v in range(2):
                    mine = {order[0]: self.bits[order[0]], order[1]: u, order[2]: v}
                    there = {order[0]: 0, order[1]: u, order[2]: v}
                    landed = self.got[k][there[2], there[1], there[0]].astype(f32)
                    here = self.part[(mine[2], mine[1], mine[0]) + cut].astype(f32)
                    self.held0[(u, v) + cut] = (here + landed).astype(bf16)
            self.copy(1, k).start()

    def last(self):
        for k, order in enumerate(ORDERS):
            self.copy(1, k).wait_recv()
            cut = self.cuts[k]
            for v in range(2):
                here = self.held0[(self.bits[order[1]], v) + cut].astype(f32)
                self.held1[(v,) + cut] = (here + self.got1[(v,) + cut].astype(f32)).astype(bf16)
            self.copy(2, k).start()

    def finish(self, store):
        for k, order in enumerate(ORDERS):
            self.copy(2, k).wait_recv()
            cut = self.cuts[k]
            store(cut, self.held1[(self.bits[order[2]],) + cut].astype(f32) + self.got2[cut].astype(f32))

    def sent(self):
        for step in range(3):
            for k in range(3):
                self.copy(step, k).wait_send()


def cube_sum_scratch(rows, width, cuts):
    def share(k):
        row, lane = cuts[k]
        shape = [2, 2, 2, rows if row == slice(None) else row.size, width if lane == slice(None) else lane.size]
        shape[2 - ORDERS[k][0]] = 1
        return pltpu.VMEM(tuple(shape), bf16)

    return [
        share(0),
        share(1),
        share(2),
        pltpu.VMEM((2, 2, rows, width), bf16),
        pltpu.VMEM((2, rows, width), bf16),
        pltpu.VMEM((2, rows, width), bf16),
        pltpu.VMEM((rows, width), bf16),
        pltpu.SemaphoreType.DMA((3, 3)),
        pltpu.SemaphoreType.DMA((3, 3)),
    ]


class Spread:
    def __init__(self, src, dst, send, recv):
        self.src, self.dst, self.send, self.recv = src, dst, send, recv

    def copy(self, step):
        place, target = peer(step)
        return remote(self.src(place), self.dst(my_place()), self.send.at[step], self.recv.at[step], target)

    def start(self):
        for step in range(1, 8):
            self.copy(step).start()

    def wait(self):
        for step in range(1, 8):
            self.copy(step).wait()


def rope_tables():
    frequency = 10000.0 ** (-(np.arange(128) % 32) * 2.0 / 64)
    near = np.arange(128)[:, None] * frequency[None, :]
    far = np.arange(8)[:, None] * 128.0 * frequency[None, :]
    return tuple(np.asarray(t, np.float32) for t in (np.cos(near), np.sin(near), np.cos(far), np.sin(far)))


def fill_rope(near_cos, near_sin, far_cos, far_sin, cosine, sine):
    for j in range(8):
        rows = pl.ds(j * 128, 128)
        fc, fs = far_cos[pl.ds(j, 1)], far_sin[pl.ds(j, 1)]
        cosine[rows] = fc * near_cos[...] - fs * near_sin[...]
        sine[rows] = fs * near_cos[...] + fc * near_sin[...]


THIRDS = ((0, 384), (384, 384), (768, 256))


def fill_docs(segs, docs):
    for s in range(2):
        for j in range(8):
            row = segs[pl.ds(s, 1), pl.ds(j * 128, 128)].astype(f32)
            docs[s, pl.ds(j * 128, 128)] = jnp.broadcast_to(row, (128, 128)).T[:, 0:1]


def fill_upper(upper):
    row = lax.broadcasted_iota(jnp.int32, upper.shape, 0)
    upper[...] = jnp.where(row < lanes(upper.shape), 1.0, 0.0).astype(bf16)


def forward_kernel(
    tok, cot, wq, wk, wv, wo, attn_gain, moe_gain, router, routes, segs, near_cos, near_sin, far_cos, far_sin,
    attn_hbm, q_out, kv_out, amix, residual_out, moe_in_out, weights_out, wo_hbm, gains_all, router_all, routes_all,
    cot_hbm, cot_mirror, routes_mirror, wkv,
    tok_all, attn_all, cot_all, wo_all, w_all, mix, cosine, sine, docs, gains,
    tok_send, tok_recv, cot_send, cot_recv, small_send, small_recv, mix_send, mix_recv, wo_send, wo_recv,
    pair_send, pair_recv, own_sem, out_sem,
):
    me, core = my_place(), my_core()
    half = pl.ds(pl.multiple_of(core * 64, 64), 64)
    own_entry = (me // 4, lax.rem(me // 2, 2), lax.rem(me, 2))
    first_row = lax.broadcasted_iota(jnp.int32, (16, 128), 0)
    both_gains = jnp.where(first_row == 1, moe_gain[...].astype(f32), 0.0)
    gains[...] = jnp.where(first_row == 0, attn_gain[...].astype(f32), both_gains).astype(bf16)
    for j in range(4):
        low = lanes((128, 128)) < 64
        k_two, v_two = (w[:, j * 128 : (j + 1) * 128].astype(f32) for w in (wk, wv))
        wkv[:, j * 256 : j * 256 + 128] = jnp.where(low, k_two, pltpu.roll(v_two, 64, 1)).astype(bf16)
        wkv[:, j * 256 + 128 : j * 256 + 256] = jnp.where(low, pltpu.roll(k_two, 64, 1), v_two).astype(bf16)
    meet(peers() + [sibling(), mirror()])
    tok_gather = Gather(row_items(tok, tok_all), tok_send, tok_recv)
    tok_gather.start(0)
    pairs = (
        (lambda j: wq.at[:, pl.ds(j * 128, 128)], lambda i: w_all.at[pl.ds(i * 128, 128), pl.ds(0, 128)]),
        (lambda j: wkv.at[:, pl.ds(j * 128, 128)], lambda i: w_all.at[pl.ds(i * 128, 128), pl.ds(128, 128)]),
        (lambda j: gains, lambda i: gains_all.at[:, pl.ds(i * 128, 128)]),
        (lambda j: router, lambda i: router_all.at[:, pl.ds(i * 128, 128)]),
        (lambda j: routes, lambda i: routes_all.at[:, pl.ds(i * 256, 256)]),
    )
    smalls = [Spread(src, dst, small_send.at[k], small_recv.at[k]) for k, (src, dst) in enumerate(pairs)]
    own = [pltpu.make_async_copy(src(me), dst(me), own_sem.at[k]) for k, (src, dst) in enumerate(pairs)]
    own += [
        pltpu.make_async_copy(tok, tok_all.at[own_entry], own_sem.at[5]),
        pltpu.make_async_copy(cot, cot_all.at[own_entry], own_sem.at[6]),
        pltpu.make_async_copy(wo.at[half], wo_all.at[own_entry + (half,)], own_sem.at[7]),
    ]
    for copy in own:
        copy.start()
    for small in smalls:
        small.start()
    fill_rope(near_cos, near_sin, far_cos, far_sin, cosine, sine)
    for copy in own:
        copy.wait()
    tok_gather.advance(1)
    fill_docs(segs, docs)
    tok_gather.advance(2)
    for small in smalls:
        small.wait()
    tok_gather.wait(2)

    def wo_item(k):
        where = (half, pl.ds(*THIRDS[k]))
        return (wo.at[where], lambda entry: wo_all.at[entry + where], ORDERS[k])

    wo_gather = Gather([wo_item(k) for k in range(3)], wo_send, wo_recv)
    wo_gather.start(0)
    cot_gather = Gather(row_items(cot, cot_all), cot_send, cot_recv)
    cot_gather.start(0)
    cot_copy = remote(cot, cot_mirror, pair_send.at[1], pair_recv.at[1], mirror())
    cot_copy.start()
    routes_copy = remote(routes_all, routes_mirror, pair_send.at[0], pair_recv.at[0], mirror())
    routes_copy.start()

    gain_row = gains_all[0:1].astype(f32)

    def project(j, carry):
        rows = pl.ds(pl.multiple_of(j * 128, 128), 128)
        x = tok_all[j // 4, lax.rem(j // 2, 2), lax.rem(j, 2)].astype(f32)
        scale = lax.rsqrt(jnp.mean(x * x, -1, keepdims=True) + epsilon)
        attn_in = (x * scale * gain_row).astype(bf16)
        attn_all[j] = attn_in
        both = dot(attn_in, w_all[...])
        c = cosine[rows]
        n = sine[rows]
        c2 = jnp.concatenate([c, c], 0)
        n2 = jnp.concatenate([n, n], 0)
        q = both[:, :128]
        kv = both[:, 128:]
        q = (q * c2 + turned(q) * n2).astype(bf16)
        kv = jnp.where(lanes(kv.shape) < 64, kv * c2 + turned(kv) * n2, kv).astype(bf16)
        for s in range(2):
            q_out[s, rows] = q[s * 128 : (s + 1) * 128]
            kv_out[s, rows] = kv[s * 128 : (s + 1) * 128]
        return carry

    lax.fori_loop(0, 8, project, 0)
    attn_copy = pltpu.make_async_copy(attn_all, attn_hbm, out_sem.at[0])
    attn_copy.start()
    wo_gather.advance(1)
    cot_gather.advance(1)
    wo_pair = remote(
        wo_all.at[:, :, :, half], wo_all.at[:, :, :, half], pair_send.at[2], pair_recv.at[2], sibling()
    )

    def mix_copy(i):
        return remote(
            mix.at[i],
            amix.at[:, :, pl.ds(pl.multiple_of(me * 128, 128), 128)],
            mix_send.at[i],
            mix_recv.at[me],
            {"blk": i // 2, "head": lax.rem(i, 2)},
        )

    def send_mix(i):
        @pl.when(me != i)
        def _():
            mix_copy(i).start()

    for i in range(8):

        def attend(s, carry, i=i):
            first, count, q2, kv, probability = block_probability(q_out, kv_out, docs, segs, s, i)
            mixed = dot(probability.astype(bf16), kv)
            low = lanes((128, 128)) < 64
            mix[i, s] = jnp.where(low, pltpu.roll(mixed[:128], 64, 1), mixed[128:]).astype(bf16)
            return carry

        lax.fori_loop(0, 2, attend, 0)
        if i > 0:
            send_mix(i - 1)
        if i == 2:
            wo_gather.advance(2)
        if i == 4:
            cot_gather.advance(2)
    send_mix(7)
    wo_gather.wait(2)
    wo_pair.start()
    mine = pltpu.make_async_copy(
        mix.at[me], amix.at[:, :, pl.ds(pl.multiple_of(me * 128, 128), 128)], own_sem.at[0]
    )
    mine.start()
    wo_pair.wait()
    wo_copy = pltpu.make_async_copy(wo_all, wo_hbm, out_sem.at[1])
    wo_copy.start()
    for step in range(1, 8):
        place, target = peer(step)
        remote(
            mix.at[place],
            amix.at[:, :, pl.ds(pl.multiple_of(place * 128, 128), 128)],
            mix_send.at[place],
            mix_recv.at[place],
            target,
        ).wait()
    mine.wait()
    width = tok.shape[-1]
    residual = tok[...].astype(f32) + dot(amix[...].reshape(256, width), wo_all[...].reshape(width, width))
    residual_out[...] = residual
    scale = lax.rsqrt(jnp.mean(residual * residual, -1, keepdims=True) + epsilon)
    moe_in = (residual * scale * gains_all[1:2].astype(f32)).astype(bf16)
    moe_in_out[...] = moe_in
    logits = dot_last(router_all[...], moe_in)
    experts = lax.broadcasted_iota(jnp.int32, logits.shape, 0)
    picked = [
        jnp.sum(jnp.where(experts == routes[pl.ds(k, 1)], logits, 0.0), 0, keepdims=True) for k in range(TOP)
    ]
    picked = jnp.concatenate(picked, 0)
    weight = jnp.exp(picked - jnp.max(picked, 0, keepdims=True))
    weights_out[...] = weight / jnp.sum(weight, 0, keepdims=True)
    cot_gather.wait(2)
    cot_out = pltpu.make_async_copy(cot_all, cot_hbm, out_sem.at[2])
    cot_out.start()
    routes_copy.wait()
    cot_copy.wait()
    tok_gather.sent()
    cot_gather.sent()
    wo_gather.sent()
    attn_copy.wait()
    wo_copy.wait()
    cot_out.wait()


def forward(*values):
    tok = values[0]
    width = tok.shape[-1]
    tables = tuple(jnp.asarray(t) for t in rope_tables())
    return pl.pallas_call(
        forward_kernel,
        out_shape=(
            jax.ShapeDtypeStruct((8, 256, width), bf16),
            jax.ShapeDtypeStruct((2, 1024, 128), bf16),
            jax.ShapeDtypeStruct((2, 1024, 128), bf16),
            jax.ShapeDtypeStruct((2, 128, width), bf16),
            jax.ShapeDtypeStruct((256, width), f32),
            jax.ShapeDtypeStruct((256, width), bf16),
            jax.ShapeDtypeStruct((8, 256), f32),
            jax.ShapeDtypeStruct((2, 2, 2, 128, width), bf16),
            jax.ShapeDtypeStruct((16, width), bf16),
            jax.ShapeDtypeStruct((32, width), bf16),
            jax.ShapeDtypeStruct((8, 2048), jnp.int32),
            jax.ShapeDtypeStruct((2, 2, 2, 256, width), bf16),
            jax.ShapeDtypeStruct((256, width), bf16),
            jax.ShapeDtypeStruct((8, 2048), jnp.int32),
            jax.ShapeDtypeStruct((128, 1024), bf16),
        ),
        in_specs=[vmem()] * 15,
        out_specs=(
            anywhere(), vmem(), vmem(), vmem(), vmem(), vmem(), vmem(), anywhere(), vmem(), vmem(), vmem(),
            anywhere(), vmem(), vmem(), vmem(),
        ),
        scratch_shapes=[
            pltpu.VMEM((2, 2, 2, 256, width), bf16),
            pltpu.VMEM((8, 256, width), bf16),
            pltpu.VMEM((2, 2, 2, 256, width), bf16),
            pltpu.VMEM((2, 2, 2, 128, width), bf16),
            pltpu.VMEM((width, 256), bf16),
            pltpu.VMEM((8, 2, 128, 128), bf16),
            pltpu.VMEM((1024, 128), f32),
            pltpu.VMEM((1024, 128), f32),
            pltpu.VMEM((2, 1024, 1), f32),
            pltpu.VMEM((16, 128), bf16),
            pltpu.SemaphoreType.DMA((3, 3)),
            pltpu.SemaphoreType.DMA((3, 3)),
            pltpu.SemaphoreType.DMA((3, 3)),
            pltpu.SemaphoreType.DMA((3, 3)),
            pltpu.SemaphoreType.DMA((5, 8)),
            pltpu.SemaphoreType.DMA((5, 8)),
            pltpu.SemaphoreType.DMA((8,)),
            pltpu.SemaphoreType.DMA((8,)),
            pltpu.SemaphoreType.DMA((3, 3)),
            pltpu.SemaphoreType.DMA((3, 3)),
            pltpu.SemaphoreType.DMA((3,)),
            pltpu.SemaphoreType.DMA((3,)),
            pltpu.SemaphoreType.DMA((8,)),
            pltpu.SemaphoreType.DMA((3,)),
        ],
        compiler_params=pltpu.CompilerParams(
            collective_id=0, has_side_effects=True, vmem_limit_bytes=VMEM_LIMIT
        ),
        name="forward",
    )(*values, *tables)


SLOT = 4 * CAPH
SPAN = 512
TAKEN = 4 * SLOT


def build_rows(routes, upper, plain, first_expert, block):
    columns = pl.ds(pl.multiple_of(block * SPAN, SPAN), SPAN)
    chosen = routes[:, columns]
    masks = [jnp.max((chosen == first_expert + e).astype(f32), 0, keepdims=True) for e in range(4)]
    mask = jnp.concatenate(masks + [jnp.zeros((4, SPAN), f32)], 0)
    rank = dot(mask.astype(bf16), upper[...])
    slots = lax.broadcasted_iota(jnp.int32, (SLOT, SPAN), 0).astype(f32)
    for e in range(4):
        hit = (slots == rank[e : e + 1]) & (mask[e : e + 1] > 0.0)
        plain[block, e * SLOT : (e + 1) * SLOT] = jnp.where(hit, 1.0, 0.0).astype(bf16)


def slot_weights(routes, weights, plain, column, first_expert, block):
    columns = pl.ds(pl.multiple_of(block * SPAN, SPAN), SPAN)
    chosen = routes[:, columns]
    weight = weights[:, columns]
    for e in range(4):
        share = jnp.sum(jnp.where(chosen == first_expert + e, weight, 0.0), 0, keepdims=True)
        mine = pl.ds(e * SLOT, SLOT)
        column[block, mine] = jnp.sum(plain[block, mine].astype(f32) * share, -1, keepdims=True)


def place_rows(source, block):
    width = source.shape[-1]
    return source[block // 2, lax.rem(block, 2)].reshape(SPAN, width)


def expert_rows(e):
    return pl.ds(pl.multiple_of(e * SLOT, 16), SLOT)


def experts_kernel(
    moe_in, my_weights, cot_mirror, cot_hbm, routes, gate_hbm, up_hbm, down_hbm,
    out_part, in_sum, p_all, rows_out, pair_out, hidden_out, gate_out, up_out, cot_mirror_hbm, moe_mirror,
    weights_other,
    x, c, cm, upper, plain, rows, pair_grad, pair_in, column, p_col, weights, p_part,
    gate, up, down, hid_buf, gg_buf, ug_buf, part_buf,
    g0, g1, g2, held0, got1, held1, got2, sum_send, sum_recv,
    row_send, row_recv, cm_send, cm_recv, w_send, w_recv, p_send, p_recv, pair_send, pair_recv,
    sem_c, sem_w, sem_rows, sem_h, sem_part, own_sem,
):
    me = my_place()
    first = me * 4
    width = x.shape[-1]
    meet(peers() + [mirror()])
    own = [
        pltpu.make_async_copy(moe_in, x.at[me // 4, lax.rem(me // 2, 2), lax.rem(me, 2)], own_sem.at[0]),
        pltpu.make_async_copy(
            my_weights, weights.at[:, pl.ds(pl.multiple_of(me * 256, 256), 256)], own_sem.at[1]
        ),
        pltpu.make_async_copy(cot_mirror, cm.at[me // 4, lax.rem(me // 2, 2), lax.rem(me, 2)], own_sem.at[2]),
    ]
    for copy in own:
        copy.start()
    row_gather = Gather(row_items(moe_in, x), row_send, row_recv)
    row_gather.start(0)
    weight_spread = Spread(
        lambda j: my_weights, lambda i: weights.at[:, pl.ds(pl.multiple_of(i * 256, 256), 256)], w_send, w_recv
    )
    weight_spread.start()
    load_c = pltpu.make_async_copy(cot_hbm, c, sem_c)
    load_c.start()

    def fetch(e, slot):
        return [
            pltpu.make_async_copy(gate_hbm.at[e], gate.at[slot], sem_w.at[slot, 0]),
            pltpu.make_async_copy(up_hbm.at[e], up.at[slot], sem_w.at[slot, 1]),
            pltpu.make_async_copy(down_hbm.at[e], down.at[slot], sem_w.at[slot, 2]),
        ]

    for copy in fetch(0, 0):
        copy.start()
    fill_upper(upper)

    def build(block, carry):
        build_rows(routes, upper, plain, first, block)
        return carry

    lax.fori_loop(0, 4, build, 0)
    for copy in own:
        copy.wait()
    row_gather.advance(1)
    load_c.wait()

    def take_c(block, carry):
        pair_grad[block] = dot(plain[block], place_rows(c, block)).astype(bf16)
        return carry

    lax.fori_loop(0, 2, take_c, 0)
    row_gather.advance(2)
    lax.fori_loop(2, 4, take_c, 0)
    weight_spread.wait()
    weights_copy = remote(weights, weights_other, pair_send.at[0], pair_recv.at[0], mirror())
    weights_copy.start()

    def weigh(block, carry):
        slot_weights(routes, weights, plain, column, first, block)
        return carry

    lax.fori_loop(0, 4, weigh, 0)
    row_gather.wait(2)
    cm_gather = Gather(row_items(cot_mirror, cm), cm_send, cm_recv)
    cm_gather.start(0)
    moe_copy = remote(moe_in, moe_mirror, pair_send.at[1], pair_recv.at[1], mirror())
    moe_copy.start()

    def take_x(block, carry):
        rows[block] = dot(plain[block], place_rows(x, block)).astype(bf16)
        return carry

    lax.fori_loop(0, 4, take_x, 0)
    keep_rows = pltpu.make_async_copy(rows, rows_out, sem_rows.at[0])
    keep_rows.start()

    def keep(e, slot):
        return [
            pltpu.make_async_copy(hid_buf.at[slot], hidden_out.at[e], sem_h.at[slot, 0]),
            pltpu.make_async_copy(gg_buf.at[slot], gate_out.at[e], sem_h.at[slot, 1]),
            pltpu.make_async_copy(ug_buf.at[slot], up_out.at[e], sem_h.at[slot, 2]),
        ]

    def expert(e, carry):
        slot = lax.rem(e, 2)
        mine = expert_rows(e)
        for copy in fetch(e, slot):
            copy.wait()

        @pl.when(e < 3)
        def _():
            for copy in fetch(e + 1, 1 - slot):
                copy.start()

        rows_e = rows[:, mine].reshape(TAKEN, width)
        weight_e = column[:, mine].reshape(TAKEN, 1)
        pair_e = (pair_grad[:, mine].reshape(TAKEN, width).astype(f32) * weight_e).astype(bf16)
        pair_grad[:, mine] = pair_e.reshape(4, SLOT, width)
        hidden, gate_grad, up_grad = expert_inner(rows_e, pair_e, gate[slot], up[slot], down[slot])

        @pl.when(e >= 2)
        def _():
            for copy in keep(e - 2, slot):
                copy.wait()

        hid_buf[slot] = hidden
        gg_buf[slot] = gate_grad
        ug_buf[slot] = up_grad
        for copy in keep(e, slot):
            copy.start()

        @pl.when(e == 0)
        def _():
            keep_rows.wait()

        @pl.when(e == 0)
        def _():
            cm_gather.advance(1)

        @pl.when(e == 1)
        def _():
            cm_gather.advance(2)

        out_e = dot(hidden, down[slot]).astype(bf16).astype(f32)
        p = jnp.sum(out_e * pair_e.astype(f32), -1, keepdims=True)
        p_col[:, mine] = p.reshape(4, SLOT, 1)
        rows[:, mine] = (out_e * weight_e).astype(bf16).reshape(4, SLOT, width)
        back = dot_last(gate_grad, gate[slot]) + dot_last(up_grad, up[slot])
        pair_in[:, mine] = back.astype(bf16).reshape(4, SLOT, width)
        return carry

    lax.fori_loop(0, 4, expert, 0)
    keep_pair = pltpu.make_async_copy(pair_grad, pair_out, sem_rows.at[1])
    keep_pair.start()
    for copy in keep(2, 0) + keep(3, 1):
        copy.wait()
    row_gather.sent()
    p_part[...] = jnp.zeros_like(p_part)

    def combine_in(block, carry):
        back = dot_first(plain[block], pair_in[block]).astype(bf16)
        x[block // 2, lax.rem(block, 2)] = back.reshape(2, 256, width)
        for e in range(4):
            mine = pl.ds(e * SLOT, SLOT)
            p = jnp.sum(plain[block, mine].astype(f32) * p_col[block, mine], 0, keepdims=True)
            p_part[block * 2, pl.ds(e, 1)] = p[:, :256]
            p_part[block * 2 + 1, pl.ds(e, 1)] = p[:, 256:]
        return carry

    lax.fori_loop(0, 4, combine_in, 0)
    total = CubeSum(x, x, ROW_CUTS, (g0, g1, g2, held0, got1, held1, got2, sum_send, sum_recv))
    total.start()
    p_spread = Spread(lambda j: p_part.at[j], lambda i: p_all.at[i], p_send, p_recv)
    p_spread.start()
    p_own = pltpu.make_async_copy(p_part.at[me], p_all.at[me], own_sem.at[3])
    p_own.start()

    def part_copy(block):
        slot = lax.rem(block, 2)
        return pltpu.make_async_copy(
            part_buf.at[slot], out_part.at[block // 2, lax.rem(block, 2)], sem_part.at[slot]
        )

    def combine_out(block, carry):
        slot = lax.rem(block, 2)

        @pl.when(block >= 2)
        def _():
            part_copy(block - 2).wait()

        out = dot_first(plain[block], rows[block]).astype(bf16)
        part_buf[slot] = out.reshape(2, 256, width)
        part_copy(block).start()
        return carry

    lax.fori_loop(0, 2, combine_out, 0)
    total.middle()
    lax.fori_loop(2, 4, combine_out, 0)
    cm_gather.wait(2)
    cm_out = pltpu.make_async_copy(cm, cot_mirror_hbm, sem_c)
    cm_out.start()
    total.last()
    p_spread.wait()
    p_own.wait()
    part_copy(2).wait()
    part_copy(3).wait()

    def store(where, value):
        in_sum[where] = value

    total.finish(store)
    total.sent()
    keep_pair.wait()
    cm_out.wait()
    cm_gather.sent()
    weights_copy.wait()
    moe_copy.wait()


def experts(moe_in, my_weights, cot_mirror, cot_all, routes, gate_w, up_w, down_w):
    width = moe_in.shape[-1]
    ff = gate_w.shape[-1]
    return pl.pallas_call(
        experts_kernel,
        out_shape=(
            jax.ShapeDtypeStruct((2, 2, 2, 256, width), bf16),
            jax.ShapeDtypeStruct((256, width), f32),
            jax.ShapeDtypeStruct((8, 8, 256), f32),
            jax.ShapeDtypeStruct((4, TAKEN, width), bf16),
            jax.ShapeDtypeStruct((4, TAKEN, width), bf16),
            jax.ShapeDtypeStruct((4, TAKEN, ff), bf16),
            jax.ShapeDtypeStruct((4, TAKEN, ff), bf16),
            jax.ShapeDtypeStruct((4, TAKEN, ff), bf16),
            jax.ShapeDtypeStruct((2, 2, 2, 256, width), bf16),
            jax.ShapeDtypeStruct((256, width), bf16),
            jax.ShapeDtypeStruct((8, 2048), f32),
        ),
        in_specs=[vmem(), vmem(), vmem(), anywhere(), vmem(), anywhere(), anywhere(), anywhere()],
        out_specs=(anywhere(), vmem(), vmem()) + (anywhere(),) * 6 + (vmem(), vmem()),
        scratch_shapes=[
            pltpu.VMEM((2, 2, 2, 256, width), bf16),
            pltpu.VMEM((2, 2, 2, 256, width), bf16),
            pltpu.VMEM((2, 2, 2, 256, width), bf16),
            pltpu.VMEM((SPAN, SPAN), bf16),
            pltpu.VMEM((4, TAKEN, SPAN), bf16),
            pltpu.VMEM((4, TAKEN, width), bf16),
            pltpu.VMEM((4, TAKEN, width), bf16),
            pltpu.VMEM((4, TAKEN, width), bf16),
            pltpu.VMEM((4, TAKEN, 1), f32),
            pltpu.VMEM((4, TAKEN, 1), f32),
            pltpu.VMEM((8, 2048), f32),
            pltpu.VMEM((8, 8, 256), f32),
            pltpu.VMEM((2, width, ff), bf16),
            pltpu.VMEM((2, width, ff), bf16),
            pltpu.VMEM((2, ff, width), bf16),
            pltpu.VMEM((2, TAKEN, ff), bf16),
            pltpu.VMEM((2, TAKEN, ff), bf16),
            pltpu.VMEM((2, TAKEN, ff), bf16),
            pltpu.VMEM((2, 2, 256, width), bf16),
        ]
        + cube_sum_scratch(256, width, ROW_CUTS)
        + [
            pltpu.SemaphoreType.DMA((3, 3)),
            pltpu.SemaphoreType.DMA((3, 3)),
            pltpu.SemaphoreType.DMA((3, 3)),
            pltpu.SemaphoreType.DMA((3, 3)),
            pltpu.SemaphoreType.DMA((8,)),
            pltpu.SemaphoreType.DMA((8,)),
            pltpu.SemaphoreType.DMA((8,)),
            pltpu.SemaphoreType.DMA((8,)),
            pltpu.SemaphoreType.DMA((2,)),
            pltpu.SemaphoreType.DMA((2,)),
            pltpu.SemaphoreType.DMA,
            pltpu.SemaphoreType.DMA((2, 3)),
            pltpu.SemaphoreType.DMA((2,)),
            pltpu.SemaphoreType.DMA((2, 3)),
            pltpu.SemaphoreType.DMA((2,)),
            pltpu.SemaphoreType.DMA((4,)),
        ],
        compiler_params=pltpu.CompilerParams(
            collective_id=1, has_side_effects=True, vmem_limit_bytes=VMEM_LIMIT
        ),
        name="experts",
    )(moe_in, my_weights, cot_mirror, cot_all, routes, gate_w, up_w, down_w)


LANE_SHARE = 128


def backward_kernel(
    cot, residual, in_sum, p_all, routes, weights, router, moe_in, gains_all, wo_hbm, amix, attn_hbm, q_in, kv_in,
    segs, near_cos, near_sin, far_cos, far_sin, tok, wq, wkv, moe_mirror,
    token_grad, grads, mirror_hbm,
    wo_all, attn_all, wq_all, wkv_all, mm, mix_grad, mg, gq, gkv, gq_rows, gkv_rows, g_all, kv_sum, cosine, sine, docs,
    residual_grad, small_grad,
    w_send, w_recv, mm_send, mm_recv, mg_send, mg_recv, g_send, g_recv, pair_send, pair_recv, own_sem, load_sem,
):
    me, core = my_place(), my_core()
    width = tok.shape[-1]
    meet(peers() + [sibling()])
    half = pl.ds(pl.multiple_of(core * 64, 64), 64)
    own_entry = (me // 4, lax.rem(me // 2, 2), lax.rem(me, 2))
    own = [
        pltpu.make_async_copy(wq.at[half], wq_all.at[own_entry + (half,)], own_sem.at[0]),
        pltpu.make_async_copy(wkv.at[half], wkv_all.at[own_entry + (half,)], own_sem.at[1]),
        pltpu.make_async_copy(moe_mirror, mm.at[own_entry], own_sem.at[2]),
    ]
    loads = [
        pltpu.make_async_copy(wo_hbm, wo_all, load_sem.at[0]),
        pltpu.make_async_copy(attn_hbm, attn_all, load_sem.at[1]),
    ]
    for copy in own + loads:
        copy.start()

    def weight_item(src, dst, start, count, order):
        rows = pl.ds(pl.multiple_of(core * 64 + start, 16), count)
        return (src.at[rows], lambda entry: dst.at[entry + (rows,)], order)

    w_gather = Gather(
        [
            weight_item(wq, wq_all, 0, 48, ORDERS[0]),
            weight_item(wq, wq_all, 48, 16, ORDERS[1]),
            weight_item(wkv, wkv_all, 0, 32, ORDERS[1]),
            weight_item(wkv, wkv_all, 32, 32, ORDERS[2]),
        ],
        w_send,
        w_recv,
    )
    w_gather.start(0)
    mm_gather = Gather(row_items(moe_mirror, mm), mm_send, mm_recv)
    mm_gather.start(0)
    ids = lax.broadcasted_iota(jnp.int32, (32, 256), 0)
    dense = jnp.zeros((32, 256), f32)
    for k in range(TOP):
        dense = dense + jnp.where(ids == routes[pl.ds(k, 1)], weights[pl.ds(k, 1)], 0.0)
    p = jnp.concatenate([p_all[i, 0:4] for i in range(8)], 0)
    logit_grad = (p - dense * jnp.sum(p, 0, keepdims=True)).astype(bf16)
    moe_in_grad = in_sum[...] + dot_first(logit_grad, router[...])
    part, moe_gain_grad = norm_back(residual[...], gains_all[1:2].astype(f32), moe_in_grad)
    total = cot[...].astype(f32) + part
    residual_grad[...] = total
    low_grad = total.astype(bf16)
    for copy in loads[:1]:
        copy.wait()
    back = dot_last(low_grad, wo_all[...].reshape(width, width)).astype(bf16)
    for j in range(8):
        mix_grad[j] = back[:, j * 128 : (j + 1) * 128].reshape(2, 128, 128)
    mix_spread = Spread(lambda j: mix_grad.at[j], lambda i: mg.at[i], mg_send, mg_recv)
    mix_spread.start()
    mix_own = pltpu.make_async_copy(mix_grad.at[me], mg.at[me], own_sem.at[3])
    mix_own.start()
    for copy in own:
        copy.wait()
    w_gather.advance(1)
    fill_rope(near_cos, near_sin, far_cos, far_sin, cosine, sine)
    fill_docs(segs, docs)
    wo_grad = dot_first(amix[...].reshape(256, width), low_grad)
    grads[:, :, 0:width] = wo_grad.astype(bf16).reshape(8, 128, width)
    padded = jnp.concatenate([logit_grad, jnp.zeros((LANE_SHARE - 32, 256), bf16)], 0)
    small_grad[...] = lax.dot_general(moe_in[...], padded, (((0,), (1,)), ((), ())), preferred_element_type=f32)
    mix_spread.wait()
    mix_own.wait()
    mm_gather.advance(1)

    def lane_block(i):
        return pl.ds(pl.multiple_of(i * 128, 128), 128)

    def spread_of(s):
        return [
            Spread(lambda j: gq.at[j, s], lambda i: gq_rows.at[s, :, lane_block(i)], g_send.at[2 * s], g_recv.at[2 * s]),
            Spread(
                lambda j: gkv.at[j, s],
                lambda i: gkv_rows.at[s, :, lane_block(i)],
                g_send.at[2 * s + 1],
                g_recv.at[2 * s + 1],
            ),
        ]

    keep_own = []
    for s in range(2):
        kv_sum[...] = jnp.zeros_like(kv_sum)
        for i in range(8):
            first, count, q2, kv, probability = block_probability(q_in, kv_in, docs, segs, s, i)
            g2 = two_heads_high(mg[i, s].astype(f32)).astype(bf16)
            prob_grad = dot_last(g2, kv)
            delta = jnp.sum(probability * prob_grad, -1, keepdims=True)
            score_grad = (probability * (prob_grad - delta) * 0.125).astype(bf16)
            dq = dot(score_grad, kv)
            keys = pl.ds(first, count)
            kv_sum[keys] += dot_first(score_grad, q2.astype(bf16)) + dot_first(probability.astype(bf16), g2)
            low = lanes((128, 128)) < 64
            dq = jnp.where(low, dq[:128], pltpu.roll(dq[128:], 64, 1))
            rows = pl.ds(i * 128, 128)
            dq = (dq * cosine[rows] - turned(dq) * sine[rows]).astype(bf16)
            gq[i, s] = dq
            g_all[i, s, :, 0:128] = dq
            if s == 0 and i == 2:
                w_gather.advance(2)
            if s == 0 and i == 6:
                mm_gather.advance(2)
        for i in range(8):
            rows = pl.ds(i * 128, 128)
            dkv = kv_sum[rows]
            low = lanes((128, 128)) < 64
            dkv = jnp.where(low, dkv * cosine[rows] - turned(dkv) * sine[rows], dkv).astype(bf16)
            gkv[i, s] = dkv
            g_all[i, s, :, 128:256] = dkv
        for spread in spread_of(s):
            spread.start()
        mine = [
            pltpu.make_async_copy(gq.at[me, s], gq_rows.at[s, :, lane_block(me)], own_sem.at[4 + 2 * s]),
            pltpu.make_async_copy(gkv.at[me, s], gkv_rows.at[s, :, lane_block(me)], own_sem.at[5 + 2 * s]),
        ]
        for copy in mine:
            copy.start()
        keep_own += mine
    w_gather.wait(2)
    shared = [
        remote(w.at[:, :, :, half], w.at[:, :, :, half], pair_send.at[k], pair_recv.at[k], sibling())
        for k, w in enumerate((wq_all, wkv_all))
    ]
    for copy in shared:
        copy.start()
    loads[1].wait()
    w_grad = dot_first(attn_all[...].reshape(2048, width), g_all[...].reshape(2048, 256))
    grads[:, :, width + LANE_SHARE :] = w_grad.astype(bf16).reshape(8, 128, 256)
    for copy in shared + keep_own:
        copy.wait()
    for s in range(2):
        for spread in spread_of(s):
            spread.wait()
    back = dot_last(gq_rows[...].reshape(256, 1024), wq_all[...].reshape(width, 1024))
    back = back + dot_last(gkv_rows[...].reshape(256, 1024), wkv_all[...].reshape(width, 1024))
    part, attn_gain_grad = norm_back(tok[...].astype(f32), gains_all[0:1].astype(f32), back)
    token_grad[...] = residual_grad[...] + part
    row = lax.broadcasted_iota(jnp.int32, (LANE_SHARE, width), 0)
    gain_rows = jnp.where(row == 32, moe_gain_grad, jnp.where(row == 33, attn_gain_grad, 0.0))
    grads[:, :, width : width + LANE_SHARE] = (small_grad[...] + gain_rows.T).astype(bf16).reshape(8, 128, LANE_SHARE)
    mm_gather.wait(2)
    mm_out = pltpu.make_async_copy(mm, mirror_hbm, load_sem.at[0])
    mm_out.start()
    w_gather.sent()
    mm_gather.sent()
    mm_out.wait()


def backward(*values):
    tok = values[15]
    width = tok.shape[-1]
    tables = tuple(jnp.asarray(t) for t in rope_tables())
    values = values[:15] + tables + values[15:]
    specs = [vmem()] * 23
    specs[9] = specs[11] = anywhere()
    return pl.pallas_call(
        backward_kernel,
        out_shape=(
            jax.ShapeDtypeStruct((256, width), f32),
            jax.ShapeDtypeStruct((8, 128, width + 256 + LANE_SHARE), bf16),
            jax.ShapeDtypeStruct((2, 2, 2, 256, width), bf16),
        ),
        in_specs=specs,
        out_specs=(vmem(), vmem(), anywhere()),
        scratch_shapes=[
            pltpu.VMEM((2, 2, 2, 128, width), bf16),
            pltpu.VMEM((8, 256, width), bf16),
            pltpu.VMEM((2, 2, 2, 128, width), bf16),
            pltpu.VMEM((2, 2, 2, 128, width), bf16),
            pltpu.VMEM((2, 2, 2, 256, width), bf16),
            pltpu.VMEM((8, 2, 128, 128), bf16),
            pltpu.VMEM((8, 2, 128, 128), bf16),
            pltpu.VMEM((8, 2, 128, 128), bf16),
            pltpu.VMEM((8, 2, 128, 128), bf16),
            pltpu.VMEM((2, 128, 1024), bf16),
            pltpu.VMEM((2, 128, 1024), bf16),
            pltpu.VMEM((8, 2, 128, 256), bf16),
            pltpu.VMEM((1024, 128), f32),
            pltpu.VMEM((1024, 128), f32),
            pltpu.VMEM((1024, 128), f32),
            pltpu.VMEM((2, 1024, 1), f32),
            pltpu.VMEM((256, width), f32),
            pltpu.VMEM((width, LANE_SHARE), f32),
            pltpu.SemaphoreType.DMA((3, 4)),
            pltpu.SemaphoreType.DMA((3, 4)),
            pltpu.SemaphoreType.DMA((3, 3)),
            pltpu.SemaphoreType.DMA((3, 3)),
            pltpu.SemaphoreType.DMA((8,)),
            pltpu.SemaphoreType.DMA((8,)),
            pltpu.SemaphoreType.DMA((4, 8)),
            pltpu.SemaphoreType.DMA((4, 8)),
            pltpu.SemaphoreType.DMA((2,)),
            pltpu.SemaphoreType.DMA((2,)),
            pltpu.SemaphoreType.DMA((8,)),
            pltpu.SemaphoreType.DMA((2,)),
        ],
        compiler_params=pltpu.CompilerParams(
            collective_id=2, has_side_effects=True, vmem_limit_bytes=VMEM_LIMIT
        ),
        name="backward",
    )(*values)


SUM_CUTS = tuple((slice(None), pl.ds(k * 384, 384)) for k in range(3))


def expert_weights_kernel(
    x_hbm, c_hbm, routes, weights, gate_hbm, up_hbm, down_hbm, rows_hbm, pair_hbm, hidden_hbm, gg_hbm, ug_hbm,
    out_part, residual, grads,
    gate_own, up_own, down_own, gate_other, up_other, down_other, mixed, shares,
    x, c, upper, plain, rows, pair_grad, column, gate, up, down,
    both_rows, both_pair, both_hidden, both_gate, gate_buf, up_buf, down_buf,
    g0, g1, g2, got1, got2, sum_send, sum_recv,
    s0, s1, s2, sheld0, sgot1, sheld1, sgot2, ssend, srecv,
    core_got, core_sum, core_qkv, all_got, side_sum, side_got,
    grad_send, grad_recv, core_send, core_recv, part_send, part_recv,
    sem_x, sem_w, sem_own, sem_out, own_sem,
):
    me, core = my_place(), my_core()
    first = me * 4
    side = lax.axis_index("group") // 2
    other = 1 - side
    width = x.shape[-1]
    ff = gate.shape[-1]
    half = pl.ds(pl.multiple_of(core * 64, 64), 64)
    other_half = pl.ds(pl.multiple_of((1 - core) * 64, 64), 64)
    meet(peers() + [sibling(), mirror()])
    core_copy = remote(grads.at[:, other_half], core_got, core_send.at[0], core_recv.at[0], sibling())
    core_copy.start()
    total = CubeSum(
        out_part, x, ROW_CUTS, (g0, g1, g2, c.at[0], got1, c.at[1, 0], got2, sum_send, sum_recv)
    )
    total.start()
    loads = [
        pltpu.make_async_copy(x_hbm, x, sem_x.at[0]),
        pltpu.make_async_copy(c_hbm, c, sem_x.at[1]),
    ]
    for copy in loads:
        copy.start()

    def fetch(e, slot):
        return [
            pltpu.make_async_copy(gate_hbm.at[e], gate.at[slot], sem_w.at[slot, 0]),
            pltpu.make_async_copy(up_hbm.at[e], up.at[slot], sem_w.at[slot, 1]),
            pltpu.make_async_copy(down_hbm.at[e], down.at[slot], sem_w.at[slot, 2]),
        ]

    for copy in fetch(0, 0):
        copy.start()
    fill_upper(upper)

    def build(block, carry):
        build_rows(routes, upper, plain, first, block)
        slot_weights(routes, weights, plain, column, first, block)
        return carry

    lax.fori_loop(0, 4, build, 0)
    core_copy.wait()
    summed = width + LANE_SHARE
    for j in range(8):
        both = (grads[j, half].astype(f32) + core_got[j].astype(f32)).astype(bf16)
        core_sum[j // 4, j // 2 % 2, j % 2] = both[:, :summed]
        core_qkv[j] = both[:, summed:]
    spread = Spread(lambda j: core_qkv.at[j], lambda i: all_got.at[i], grad_send, grad_recv)
    spread.start()
    spread_own = pltpu.make_async_copy(core_qkv.at[me], all_got.at[me], own_sem)
    spread_own.start()
    small_total = CubeSum(
        core_sum, core_sum, SUM_CUTS, (s0, s1, s2, sheld0, sgot1, sheld1, sgot2, ssend, srecv)
    )
    small_total.start()
    for copy in loads:
        copy.wait()

    def take(block, carry):
        rows[block] = dot(plain[block], place_rows(x, block)).astype(bf16)
        taken = dot(plain[block], place_rows(c, block))
        pair_grad[block] = (taken * column[block]).astype(bf16)
        return carry

    lax.fori_loop(0, 4, take, 0)
    load_part = pltpu.make_async_copy(out_part, x, sem_x.at[0])
    load_part.start()
    side_copy = remote(side_sum, side_got, core_send.at[1], core_recv.at[1], mirror())
    last_copy = remote(shares.at[half], shares.at[half], core_send.at[2], core_recv.at[2], sibling())

    def part_copies(e):
        return [
            pltpu.make_async_copy(gate_buf, gate_own.at[e], sem_out.at[0]),
            pltpu.make_async_copy(up_buf, up_own.at[e], sem_out.at[1]),
            pltpu.make_async_copy(down_buf, down_own.at[e], sem_out.at[2]),
            remote(gate_buf, gate_other.at[e], part_send.at[0], part_recv.at[e, 0], sibling()),
            remote(up_buf, up_other.at[e], part_send.at[1], part_recv.at[e, 1], sibling()),
            remote(down_buf, down_other.at[e], part_send.at[2], part_recv.at[e, 2], sibling()),
        ]

    def sent(e):
        made = part_copies(e)
        for copy in made[:3]:
            copy.wait()
        for copy in made[3:]:
            copy.wait_send()

    def expert(e, carry):
        slot = lax.rem(e, 2)
        mine = expert_rows(e)
        own = [
            pltpu.make_async_copy(rows_hbm.at[:, mine], both_rows.at[side], sem_own.at[0]),
            pltpu.make_async_copy(pair_hbm.at[:, mine], both_pair.at[side], sem_own.at[1]),
            pltpu.make_async_copy(hidden_hbm.at[e], both_hidden.at[side], sem_own.at[2]),
            pltpu.make_async_copy(gg_hbm.at[e], both_gate.at[side, :, pl.ds(0, ff)], sem_own.at[3]),
            pltpu.make_async_copy(ug_hbm.at[e], both_gate.at[side, :, pl.ds(ff, ff)], sem_own.at[4]),
        ]
        for copy in own:
            copy.start()
        for copy in fetch(e, slot):
            copy.wait()

        @pl.when(e < 3)
        def _():
            for copy in fetch(e + 1, 1 - slot):
                copy.start()

        rows_e = rows[:, mine].reshape(TAKEN, width)
        pair_e = pair_grad[:, mine].reshape(TAKEN, width)
        hidden, gate_grad, up_grad = expert_inner(rows_e, pair_e, gate[slot], up[slot], down[slot])
        both_rows[other] = rows_e.reshape(4, SLOT, width)
        both_pair[other] = pair_e.reshape(4, SLOT, width)
        both_hidden[other] = hidden
        both_gate[other, :, 0:ff] = gate_grad
        both_gate[other, :, ff : 2 * ff] = up_grad

        for copy in own:
            copy.wait()

        @pl.when(e >= 1)
        def _():
            sent(e - 1)

        sums = dot_first(both_rows[...].reshape(2 * TAKEN, width), both_gate[...].reshape(2 * TAKEN, 2 * ff))
        gate_buf[...] = sums[:, :ff].astype(bf16)
        up_buf[...] = sums[:, ff:].astype(bf16)
        down_buf[...] = dot_first(
            both_hidden[...].reshape(2 * TAKEN, ff), both_pair[...].reshape(2 * TAKEN, width)
        ).astype(bf16)
        for copy in part_copies(e):
            copy.start()

        @pl.when(e == 0)
        def _():
            small_total.middle()
            load_part.wait()
            total.middle()

        @pl.when(e == 1)
        def _():
            small_total.last()
            total.last()

            def keep_sum(cut, value):
                side_sum[cut] = value.astype(bf16)

            small_total.finish(keep_sum)
            spread.wait()
            spread_own.wait()
            for i in range(8):
                side_sum[:, summed + i * 256 : summed + (i + 1) * 256] = all_got[i]
            side_copy.start()

        @pl.when(e == 2)
        def _():
            def store(cut, value):
                mixed[cut] = (residual[cut] + value).astype(bf16)

            total.finish(store)

        return carry

    lax.fori_loop(0, 4, expert, 0)
    side_copy.wait()
    shares[half] = (side_sum[...].astype(f32) + side_got[...].astype(f32)).astype(bf16)
    last_copy.start()
    total.sent()
    small_total.sent()
    last_copy.wait()
    sent(3)
    for e in range(4):
        for copy in part_copies(e)[3:]:
            copy.wait_recv()


def expert_weights(x, c, routes, weights, gate_w, up_w, down_w, kept, out_part, residual, grads):
    width = gate_w.shape[1]
    ff = gate_w.shape[-1]
    wide = grads.shape[-1]
    out = [jax.ShapeDtypeStruct(w.shape, bf16) for w in (gate_w, up_w, down_w)]
    sums = cube_sum_scratch(256, width, ROW_CUTS)
    return pl.pallas_call(
        expert_weights_kernel,
        out_shape=(
            *out,
            *out,
            jax.ShapeDtypeStruct((256, width), bf16),
            jax.ShapeDtypeStruct((128, width + LANE_SHARE + 2048), bf16),
        ),
        in_specs=[anywhere()] * 2 + [vmem()] * 2 + [anywhere()] * 9 + [vmem()] * 2,
        out_specs=(anywhere(),) * 6 + (vmem(),) * 2,
        scratch_shapes=[
            pltpu.VMEM((2, 2, 2, 256, width), bf16),
            pltpu.VMEM((2, 2, 2, 256, width), bf16),
            pltpu.VMEM((SPAN, SPAN), bf16),
            pltpu.VMEM((4, TAKEN, SPAN), bf16),
            pltpu.VMEM((4, TAKEN, width), bf16),
            pltpu.VMEM((4, TAKEN, width), bf16),
            pltpu.VMEM((4, TAKEN, 1), f32),
            pltpu.VMEM((2, width, ff), bf16),
            pltpu.VMEM((2, width, ff), bf16),
            pltpu.VMEM((2, ff, width), bf16),
            pltpu.VMEM((2, 4, SLOT, width), bf16),
            pltpu.VMEM((2, 4, SLOT, width), bf16),
            pltpu.VMEM((2, TAKEN, ff), bf16),
            pltpu.VMEM((2, TAKEN, 2 * ff), bf16),
            pltpu.VMEM((width, ff), bf16),
            pltpu.VMEM((width, ff), bf16),
            pltpu.VMEM((ff, width), bf16),
            *sums[:3],
            sums[4],
            sums[6],
            *sums[7:],
            *cube_sum_scratch(64, width + LANE_SHARE, SUM_CUTS),
            pltpu.VMEM((8, 64, wide), bf16),
            pltpu.VMEM((2, 2, 2, 64, width + LANE_SHARE), bf16),
            pltpu.VMEM((8, 64, 256), bf16),
            pltpu.VMEM((8, 64, 256), bf16),
            pltpu.VMEM((64, width + LANE_SHARE + 2048), bf16),
            pltpu.VMEM((64, width + LANE_SHARE + 2048), bf16),
            pltpu.SemaphoreType.DMA((8,)),
            pltpu.SemaphoreType.DMA((8,)),
            pltpu.SemaphoreType.DMA((3,)),
            pltpu.SemaphoreType.DMA((3,)),
            pltpu.SemaphoreType.DMA((3,)),
            pltpu.SemaphoreType.DMA((4, 3)),
            pltpu.SemaphoreType.DMA((2,)),
            pltpu.SemaphoreType.DMA((2, 3)),
            pltpu.SemaphoreType.DMA((5,)),
            pltpu.SemaphoreType.DMA((3,)),
            pltpu.SemaphoreType.DMA,
        ],
        compiler_params=pltpu.CompilerParams(
            collective_id=3, has_side_effects=True, vmem_limit_bytes=VMEM_LIMIT
        ),
        name="expert_weights",
    )(x, c, routes, weights, gate_w, up_w, down_w, *kept, out_part, residual, grads)


def finish_kernel(
    gate_own, up_own, down_own, gate_other, up_other, down_other, shares, mixed, token_grad,
    gate_out, up_out, down_out, query_out, key_out, value_out, wo_out, router_out, moe_gain_out, attn_gain_out,
    mixed_out, token_out,
):
    for own, other, out in ((gate_own, gate_other, gate_out), (up_own, up_other, up_out), (down_own, down_other, down_out)):
        out[...] = own[...].astype(f32) + other[...].astype(f32)
    mixed_out[...] = mixed[...]
    token_out[...] = token_grad[...]

    @pl.when(pl.program_id(0) == 0)
    def _():
        width = wo_out.shape[-1]
        wo_out[...] = shares[:, 0:width].astype(f32)
        small = shares[:, width : width + LANE_SHARE].astype(f32).T
        router_out[...] = small[0:32]
        moe_gain_out[...] = small[32:33]
        attn_gain_out[...] = small[33:34]
        low = lanes((128, 128)) < 64
        base = width + LANE_SHARE
        for j in range(8):
            query_out[:, j * 128 : (j + 1) * 128] = shares[:, base + j * 256 : base + j * 256 + 128].astype(f32)
        for j in range(4):
            left = shares[:, base + j * 512 + 128 : base + j * 512 + 256].astype(f32)
            right = shares[:, base + j * 512 + 384 : base + j * 512 + 512].astype(f32)
            where = slice(j * 128, (j + 1) * 128)
            key_out[:, where] = jnp.where(low, left, pltpu.roll(right, 64, 1))
            value_out[:, where] = jnp.where(low, pltpu.roll(left, 64, 1), right)


def finish(parts, shares, mixed, token_grad):
    width = parts[0].shape[1]
    steps = parts[0].shape[0]

    def block(shape):
        return pl.BlockSpec((1,) + shape[1:], lambda e: (e, 0, 0))

    def rows(shape):
        return pl.BlockSpec((shape[0] // steps,) + shape[1:], lambda e: (e, 0))

    def whole(shape):
        return pl.BlockSpec(shape, lambda e: (0,) * len(shape))

    small = [(128, 1024), (128, 512), (128, 512), (128, width), (32, LANE_SHARE), (1, LANE_SHARE), (1, LANE_SHARE)]
    return pl.pallas_call(
        finish_kernel,
        grid=(steps,),
        out_shape=tuple(jax.ShapeDtypeStruct(p.shape, f32) for p in parts[:3])
        + tuple(jax.ShapeDtypeStruct(shape, f32) for shape in small)
        + (jax.ShapeDtypeStruct(mixed.shape, bf16), jax.ShapeDtypeStruct(token_grad.shape, f32)),
        in_specs=[block(p.shape) for p in parts] + [whole(shares.shape), rows(mixed.shape), rows(token_grad.shape)],
        out_specs=tuple(block(p.shape) for p in parts[:3])
        + tuple(whole(shape) for shape in small)
        + (rows(mixed.shape), rows(token_grad.shape)),
        compiler_params=pltpu.CompilerParams(vmem_limit_bytes=VMEM_LIMIT),
        name="finish",
    )(*parts, shares, mixed, token_grad)


def fast_on_device(
    tokens, segments, routes, cotangent, attn_gain, moe_gain, query_weight, key_projection_matrix,
    value_projection_matrix, out_weight, router_weight, gate_weight, up_weight, down_weight,
):
    width = tokens.shape[-1]
    tok = tokens.reshape(256, width)
    cot = cotangent.reshape(256, width)
    my_routes = routes.reshape(256, TOP).T
    (
        attn_in, q, kv, amix, residual, moe_in, weights, wo_all, gains_all, router_all, routes_all,
        cot_all, cot_mirror, routes_mirror, wkv,
    ) = forward(
        tok, cot, query_weight, key_projection_matrix, value_projection_matrix, out_weight,
        attn_gain.reshape(1, 128), moe_gain.reshape(1, 128), router_weight.T, my_routes, segments,
    )
    out_part, in_sum, p_all, *kept, cot_mirror_all, moe_mirror, weights_mirror = experts(
        moe_in, weights, cot_mirror, cot_all, routes_all, gate_weight, up_weight, down_weight
    )
    token_grad, grads, moe_mirror_all = backward(
        cot, residual, in_sum, p_all, my_routes, weights, router_all, moe_in, gains_all, wo_all, amix, attn_in,
        q, kv, segments, tok, query_weight, wkv, moe_mirror,
    )
    *parts, mixed, shares = expert_weights(
        moe_mirror_all, cot_mirror_all, routes_mirror, weights_mirror, gate_weight, up_weight, down_weight,
        kept, out_part, residual, grads,
    )
    (
        gate_grad, up_grad, down_grad, query_grad, key_grad, value_grad, wo_grad, router_grad, moe_gain_grad,
        attn_gain_grad, mixed, token_grad,
    ) = finish(parts, shares, mixed, token_grad)
    return (
        mixed.reshape(tokens.shape), token_grad.reshape(tokens.shape), attn_gain_grad.reshape(128),
        moe_gain_grad.reshape(128), query_grad, key_grad, value_grad, wo_grad, router_grad.T,
        gate_grad, up_grad, down_grad,
    )


def fits(mesh):
    return dict(mesh.shape) == {"group": 4, "blk": 4, "head": 2}


def solution(mesh):
    placed = (
        P("group", ("blk", "head"), None),
        P("group", None),
        P("group", ("blk", "head"), None),
        P("group", ("blk", "head"), None),
        P(("blk", "head")),
        P(("blk", "head")),
        P(("blk", "head"), None),
        P(("blk", "head"), None),
        P(("blk", "head"), None),
        P(("blk", "head"), None),
        P(("blk", "head"), None),
        P(("blk", "head"), None, None),
        P(("blk", "head"), None, None),
        P(("blk", "head"), None, None),
    )
    return jax.shard_map(
        fast_on_device if fits(mesh) else on_device,
        mesh=mesh,
        in_specs=placed,
        out_specs=(
            P("group", ("blk", "head"), None),
            P("group", ("blk", "head"), None),
            P(("blk", "head")),
            P(("blk", "head")),
            P(("blk", "head"), None),
            P(("blk", "head"), None),
            P(("blk", "head"), None),
            P(("blk", "head"), None),
            P(("blk", "head"), None),
            P(("blk", "head"), None, None),
            P(("blk", "head"), None, None),
            P(("blk", "head"), None, None),
        ),
        check_vma=False,
    )
```

```python
import functools

import jax
import jax.numpy as jnp
import numpy as np
from jax import lax
from jax.experimental import pallas as pl
from jax.experimental.pallas import tpu as pltpu
from jax.sharding import PartitionSpec as P

QUERY_HEADS = 16
KEY_VALUE_HEADS = 8
HEAD_SIZE = 64
TOP = 8
CAPH = 36


epsilon = 1e-05
rope_base = 10000.0
masked_out = -1e30
key_block = 512


def rms_norm(values, gain_vec):
    return values * lax.rsqrt(jnp.mean(values * values, -1, keepdims=True) + epsilon) * gain_vec


def rotary_embedding(field_vals, places, turn_sign):
    half_dim = field_vals.shape[-1] // 2
    frequency = rope_base ** (-jnp.arange(half_dim, dtype=jnp.float32) * 2.0 / field_vals.shape[-1])
    angles = places.astype(jnp.float32)[:, None] * frequency[None, :]
    cosine = jnp.cos(angles)[:, None, :]
    sine_vals = turn_sign * jnp.sin(angles)[:, None, :]
    first_half = field_vals[..., :half_dim]
    second = field_vals[..., half_dim:]
    return jnp.concatenate(
        [first_half * cosine - second * sine_vals, second * cosine + first_half * sine_vals], -1
    )


def add_rows(running, addend, row_start):
    current = lax.dynamic_slice_in_dim(running, row_start, addend.shape[1], 1)
    return lax.dynamic_update_slice_in_dim(running, current + addend, row_start, 1)


def on_device(
    tokens,
    segments,
    routes,
    cotangent,
    attn_gain,
    moe_gain,
    query_weight,
    key_projection_matrix,
    value_projection_matrix,
    out_weight,
    router_weight,
    gate_weight,
    up_weight,
    down_weight,
):
    head_groups, number_of_rows, width_dim = tokens.shape
    query_per_key_head = QUERY_HEADS // KEY_VALUE_HEADS
    shared_head_count = lax.axis_size("head")
    query_rows = number_of_rows * shared_head_count
    grouped_keys = KEY_VALUE_HEADS // shared_head_count
    scale_val = HEAD_SIZE ** (-0.5)
    number_of_tokens = head_groups * number_of_rows
    seq_length = lax.axis_size("blk") * query_rows
    cycle_index = lax.axis_index("blk")
    local_placement = (
        cycle_index * shared_head_count + lax.axis_index("head")
    ) * number_of_rows + jnp.arange(number_of_rows, dtype=jnp.int32)
    own_start = cycle_index * query_rows
    query_place = own_start + jnp.arange(query_rows, dtype=jnp.int32)
    query_doc = lax.dynamic_slice_in_dim(segments, own_start, query_rows, 1)
    query_full, key_full, value_full, out_full, router_full, gain_attn, gain_moe = (
        lax.all_gather(query_weight, ("blk", "head"), axis=0, tiled=True),
        lax.all_gather(key_projection_matrix, ("blk", "head"), axis=0, tiled=True),
        lax.all_gather(value_projection_matrix, ("blk", "head"), axis=0, tiled=True),
        lax.all_gather(out_weight, ("blk", "head"), axis=0, tiled=True),
        lax.all_gather(router_weight, ("blk", "head"), axis=0, tiled=True),
        lax.all_gather(attn_gain, ("blk", "head"), axis=0, tiled=True),
        lax.all_gather(moe_gain, ("blk", "head"), axis=0, tiled=True),
    )
    flat_rows = tokens.reshape(number_of_tokens, width_dim).astype(jnp.float32)
    attn_normed, attn_pull = jax.vjp(rms_norm, flat_rows, gain_attn.astype(jnp.float32))
    attn_in = attn_normed.astype(jnp.bfloat16)
    query_pre = jnp.dot(attn_in, query_full, preferred_element_type=jnp.float32)
    key_before_rotary = jnp.dot(attn_in, key_full, preferred_element_type=jnp.float32)
    value_low = (
        jnp.dot(attn_in, value_full, preferred_element_type=jnp.float32)
        .astype(jnp.bfloat16)
        .reshape(head_groups, number_of_rows, KEY_VALUE_HEADS * HEAD_SIZE)
    )
    query_low = (
        rotary_embedding(
            query_pre.reshape(head_groups, number_of_rows, QUERY_HEADS, HEAD_SIZE),
            local_placement,
            1.0,
        )
        .astype(jnp.bfloat16)
        .reshape(head_groups, number_of_rows, QUERY_HEADS * HEAD_SIZE)
    )
    key_low = (
        rotary_embedding(
            key_before_rotary.reshape(head_groups, number_of_rows, KEY_VALUE_HEADS, HEAD_SIZE),
            local_placement,
            1.0,
        )
        .astype(jnp.bfloat16)
        .reshape(head_groups, number_of_rows, KEY_VALUE_HEADS * HEAD_SIZE)
    )
    query_split, key_split, value_split = (
        lax.all_to_all(query_low, "head", split_axis=2, concat_axis=1, tiled=True),
        lax.all_to_all(key_low, "head", split_axis=2, concat_axis=1, tiled=True),
        lax.all_to_all(value_low, "head", split_axis=2, concat_axis=1, tiled=True),
    )
    query_vectors = query_split.reshape(
        head_groups, query_rows, grouped_keys, query_per_key_head, HEAD_SIZE
    )

    def key_view(source, offset, sub_rows):
        return lax.dynamic_slice_in_dim(source, offset, sub_rows, 1).reshape(
            head_groups, sub_rows, grouped_keys, HEAD_SIZE
        )

    def scored_at(query_part, key_row_block, q_place, q_doc, key_start, sub_rows):
        raw_scores = (
            jnp.einsum(
                "bqgrd,bkgd->bqgrk", query_part, key_row_block, preferred_element_type=jnp.float32
            )
            * scale_val
        )
        key_place = key_start + jnp.arange(sub_rows, dtype=jnp.int32)
        key_doc = lax.dynamic_slice_in_dim(segments, key_start, sub_rows, 1)
        allowed = (q_place[None, :, None] >= key_place[None, None, :]) & (
            q_doc[:, :, None] == key_doc[:, None, :]
        )
        return (raw_scores, allowed[:, :, None, None, :])

    def scored(key_row_block, key_start, sub_rows):
        return scored_at(query_vectors, key_row_block, query_place, query_doc, key_start, sub_rows)

    stats_shape = (head_groups, query_rows, grouped_keys, query_per_key_head)
    init_state = (
        jnp.full(stats_shape, masked_out, jnp.float32),
        jnp.zeros(stats_shape, jnp.float32),
        jnp.zeros(stats_shape + (HEAD_SIZE,), jnp.float32),
    )
    key_all, value_all = (
        lax.all_gather(key_split, "blk", axis=1, tiled=True),
        lax.all_gather(value_split, "blk", axis=1, tiled=True),
    )
    fold_state = init_state
    total_rows = key_all.shape[1]
    sub_rows = key_block

    def forward_one_block(block_state, block_index):
        offset = block_index * sub_rows
        key_row_block = key_view(key_all, offset, sub_rows)
        value_row_block = key_view(value_all, offset, sub_rows)
        raw_scores, allowed = scored(key_row_block, 0 + offset, sub_rows)
        running_max, running_sum, running_acc = block_state
        masked = jnp.where(allowed, raw_scores, masked_out)
        new_max = jnp.maximum(running_max, jnp.max(masked, -1))
        shrink = jnp.exp(running_max - new_max)
        weights_soft = jnp.where(allowed, jnp.exp(masked - new_max[..., None]), 0.0)
        new_sum = running_sum * shrink + jnp.sum(weights_soft, -1)
        new_acc = running_acc * shrink[..., None] + jnp.einsum(
            "bqgrk,bkgd->bqgrd",
            weights_soft.astype(jnp.bfloat16),
            value_row_block,
            preferred_element_type=jnp.float32,
        )
        return ((new_max, new_sum, new_acc), None)

    fold_state, unused = lax.scan(
        forward_one_block, fold_state, jnp.arange(total_rows // sub_rows, dtype=jnp.int32)
    )
    running_max, running_sum, running_acc = fold_state
    mix_heads = running_acc / running_sum[..., None]
    log_total = running_max + jnp.log(running_sum)
    mix_low = mix_heads.astype(jnp.bfloat16).reshape(
        head_groups, query_rows, grouped_keys * query_per_key_head * HEAD_SIZE
    )
    mix_tokens = lax.all_to_all(mix_low, "head", split_axis=1, concat_axis=2, tiled=True)
    attn_mix = mix_tokens.reshape(number_of_tokens, QUERY_HEADS * HEAD_SIZE)
    residual = flat_rows + jnp.dot(attn_mix, out_full, preferred_element_type=jnp.float32)
    moe_normed, moe_pull = jax.vjp(rms_norm, residual, gain_moe.astype(jnp.float32))
    moe_in = moe_normed.astype(jnp.bfloat16)
    logits = jnp.dot(moe_in, router_full, preferred_element_type=jnp.float32)
    route_flat = routes.reshape(number_of_tokens, TOP)
    experts_all = router_full.shape[1]
    choose = route_flat[:, :, None] == jnp.arange(experts_all, dtype=jnp.int32)[None, None, :]
    choose_float = choose.astype(jnp.float32)
    picked_logits = jnp.einsum("nke,ne->nk", choose_float, logits)
    route_weights = jax.nn.softmax(picked_logits, axis=-1)
    choose_whole = choose.astype(jnp.int32).reshape(head_groups, number_of_rows * TOP, experts_all)
    slot_rank = jnp.sum(jnp.cumsum(choose_whole, 1) * choose_whole, -1) - 1
    slot_index = (slot_rank + jnp.arange(head_groups, dtype=jnp.int32)[:, None] * CAPH).reshape(-1)
    targets = route_flat.reshape(-1)
    lane_count = head_groups * CAPH
    outgoing = (
        jnp.zeros((experts_all, lane_count, width_dim), jnp.bfloat16)
        .at[targets, slot_index]
        .set(jnp.repeat(moe_in, TOP, axis=0))
    )
    arrived = lax.all_to_all(outgoing, ("blk", "head"), split_axis=0, concat_axis=1, tiled=True)
    gate_val = jnp.einsum("end,edf->enf", arrived, gate_weight, preferred_element_type=jnp.float32)
    up_val = jnp.einsum("end,edf->enf", arrived, up_weight, preferred_element_type=jnp.float32)
    hidden_low = (jax.nn.silu(gate_val) * up_val).astype(jnp.bfloat16)
    expert_out = jnp.einsum(
        "enf,efd->end", hidden_low, down_weight, preferred_element_type=jnp.float32
    ).astype(jnp.bfloat16)
    returned = lax.all_to_all(expert_out, ("blk", "head"), split_axis=1, concat_axis=0, tiled=True)
    picked_rows = returned[targets, slot_index].reshape(number_of_tokens, TOP, width_dim)
    moe_out = jnp.einsum(
        "nk,nkd->nd", route_weights, picked_rows, preferred_element_type=jnp.float32
    )
    mixed = (
        (residual + moe_out).astype(jnp.bfloat16).reshape(head_groups, number_of_rows, width_dim)
    )
    grad_full = cotangent.reshape(number_of_tokens, width_dim).astype(jnp.float32)
    weight_grad = jnp.einsum(
        "nkd,nd->nk", picked_rows, grad_full, preferred_element_type=jnp.float32
    )
    pair_grad = (
        (route_weights[:, :, None] * grad_full[:, None, :])
        .astype(jnp.bfloat16)
        .reshape(number_of_tokens * TOP, width_dim)
    )
    grad_outgoing = jnp.zeros_like(outgoing).at[targets, slot_index].set(pair_grad)
    grad_arrived = lax.all_to_all(
        grad_outgoing, ("blk", "head"), split_axis=0, concat_axis=1, tiled=True
    )
    grad_hidden = jnp.einsum(
        "end,efd->enf", grad_arrived, down_weight, preferred_element_type=jnp.float32
    )
    sigmoid_val = jax.nn.sigmoid(gate_val)
    grad_gate = (
        grad_hidden * up_val * sigmoid_val * (1.0 + gate_val * (1.0 - sigmoid_val))
    ).astype(jnp.bfloat16)
    grad_up = (grad_hidden * gate_val * sigmoid_val).astype(jnp.bfloat16)
    down_weight_grad = jnp.einsum(
        "enf,end->efd", hidden_low, grad_arrived, preferred_element_type=jnp.float32
    )
    gate_weight_grad = jnp.einsum(
        "end,enf->edf", arrived, grad_gate, preferred_element_type=jnp.float32
    )
    up_weight_grad = jnp.einsum(
        "end,enf->edf", arrived, grad_up, preferred_element_type=jnp.float32
    )
    pair_back = (
        jnp.einsum("enf,edf->end", grad_gate, gate_weight, preferred_element_type=jnp.float32)
        + jnp.einsum("enf,edf->end", grad_up, up_weight, preferred_element_type=jnp.float32)
    ).astype(jnp.bfloat16)
    grad_returned = lax.all_to_all(
        pair_back, ("blk", "head"), split_axis=1, concat_axis=0, tiled=True
    )
    moe_in_grad = jnp.sum(
        grad_returned[targets, slot_index].reshape(number_of_tokens, TOP, width_dim),
        axis=1,
        dtype=jnp.float32,
    )
    mean_term = jnp.sum(route_weights * weight_grad, -1, keepdims=True)
    logit_grad = jnp.einsum("nk,nke->ne", route_weights * (weight_grad - mean_term), choose_float)
    router_grad = jnp.dot(moe_in.T, logit_grad, preferred_element_type=jnp.float32)
    moe_in_grad = moe_in_grad + jnp.dot(
        logit_grad, router_full.T, preferred_element_type=jnp.float32
    )
    residual_part, moe_gain_grad = moe_pull(moe_in_grad)
    residual_grad = grad_full + residual_part
    out_grad_low = residual_grad.astype(jnp.bfloat16)
    out_weight_grad = jnp.dot(attn_mix.T, out_grad_low, preferred_element_type=jnp.float32)
    mix_grad = (
        jnp.dot(out_grad_low, out_full.T, preferred_element_type=jnp.float32)
        .astype(jnp.bfloat16)
        .reshape(head_groups, number_of_rows, QUERY_HEADS * HEAD_SIZE)
    )
    mix_grad_heads = lax.all_to_all(
        mix_grad, "head", split_axis=2, concat_axis=1, tiled=True
    ).reshape(head_groups, query_rows, grouped_keys, query_per_key_head, HEAD_SIZE)
    delta_term = jnp.sum(mix_grad_heads.astype(jnp.float32) * mix_heads, -1)
    query_zero = jnp.zeros(stats_shape + (HEAD_SIZE,), jnp.float32)
    back_init = (
        query_zero,
        jnp.zeros((head_groups, seq_length, grouped_keys, HEAD_SIZE), jnp.float32),
        jnp.zeros((head_groups, seq_length, grouped_keys, HEAD_SIZE), jnp.float32),
    )
    fold_state = back_init
    total_rows = key_all.shape[1]

    def backward_one_block(block_state, block_index):
        offset = block_index * key_block
        key_start = 0 + offset
        key_row_block = key_view(key_all, offset, key_block)
        value_row_block = key_view(value_all, offset, key_block)
        raw_scores, allowed = scored(key_row_block, key_start, key_block)
        masked = jnp.where(allowed, raw_scores, masked_out)
        probability = jnp.where(allowed, jnp.exp(masked - log_total[..., None]), 0.0)
        prob_grad = jnp.einsum(
            "bqgrd,bkgd->bqgrk", mix_grad_heads, value_row_block, preferred_element_type=jnp.float32
        )
        score_grad = (probability * (prob_grad - delta_term[..., None]) * scale_val).astype(
            jnp.bfloat16
        )
        grad_query = block_state[0] + jnp.einsum(
            "bqgrk,bkgd->bqgrd", score_grad, key_row_block, preferred_element_type=jnp.float32
        )
        value_part_grad = jnp.einsum(
            "bqgrk,bqgrd->bkgd",
            probability.astype(jnp.bfloat16),
            mix_grad_heads,
            preferred_element_type=jnp.float32,
        )
        key_part_grad = jnp.einsum(
            "bqgrk,bqgrd->bkgd", score_grad, query_vectors, preferred_element_type=jnp.float32
        )
        grad_keys = add_rows(block_state[1], key_part_grad, key_start)
        grad_values = add_rows(block_state[2], value_part_grad, key_start)
        return ((grad_query, grad_keys, grad_values), None)

    fold_state, unused = lax.scan(
        backward_one_block, fold_state, jnp.arange(total_rows // key_block, dtype=jnp.int32)
    )
    grad_query, grad_keys, grad_values = fold_state
    key_own, value_own = (
        lax.psum_scatter(
            grad_keys.reshape(head_groups, seq_length, grouped_keys * HEAD_SIZE).astype(
                jnp.bfloat16
            ),
            "blk",
            scatter_dimension=1,
            tiled=True,
        ).astype(jnp.float32),
        lax.psum_scatter(
            grad_values.reshape(head_groups, seq_length, grouped_keys * HEAD_SIZE).astype(
                jnp.bfloat16
            ),
            "blk",
            scatter_dimension=1,
            tiled=True,
        ).astype(jnp.float32),
    )
    query_grad_low = (
        rotary_embedding(
            grad_query.reshape(
                head_groups, query_rows, grouped_keys * query_per_key_head, HEAD_SIZE
            ),
            query_place,
            -1.0,
        )
        .astype(jnp.bfloat16)
        .reshape(head_groups, query_rows, grouped_keys * query_per_key_head * HEAD_SIZE)
    )
    key_grad_low = (
        rotary_embedding(
            key_own.reshape(head_groups, query_rows, grouped_keys, HEAD_SIZE), query_place, -1.0
        )
        .astype(jnp.bfloat16)
        .reshape(head_groups, query_rows, grouped_keys * HEAD_SIZE)
    )
    value_grad_low = value_own.astype(jnp.bfloat16)
    query_back, key_pullback, value_pullback = (
        lax.all_to_all(query_grad_low, "head", split_axis=1, concat_axis=2, tiled=True),
        lax.all_to_all(key_grad_low, "head", split_axis=1, concat_axis=2, tiled=True),
        lax.all_to_all(value_grad_low, "head", split_axis=1, concat_axis=2, tiled=True),
    )
    query_flat = query_back.reshape(number_of_tokens, QUERY_HEADS * HEAD_SIZE)
    flattened_keys = key_pullback.reshape(number_of_tokens, KEY_VALUE_HEADS * HEAD_SIZE)
    flattened_values = value_pullback.reshape(number_of_tokens, KEY_VALUE_HEADS * HEAD_SIZE)
    query_weight_grad = jnp.dot(attn_in.T, query_flat, preferred_element_type=jnp.float32)
    key_weight_grad = jnp.dot(attn_in.T, flattened_keys, preferred_element_type=jnp.float32)
    value_weight_grad = jnp.dot(attn_in.T, flattened_values, preferred_element_type=jnp.float32)
    attn_in_grad = (
        jnp.dot(query_flat, query_full.T, preferred_element_type=jnp.float32)
        + jnp.dot(flattened_keys, key_full.T, preferred_element_type=jnp.float32)
        + jnp.dot(flattened_values, value_full.T, preferred_element_type=jnp.float32)
    )
    input_part, attn_gain_grad = attn_pull(attn_in_grad)
    token_grad = (residual_grad + input_part).reshape(head_groups, number_of_rows, width_dim)
    (
        query_shard,
        key_shard,
        value_shard,
        out_shard,
        router_shard,
        attn_gain_shard,
        moe_gain_shard,
    ) = (
        lax.psum_scatter(
            query_weight_grad.astype(jnp.bfloat16), ("blk", "head"), scatter_dimension=0, tiled=True
        ).astype(jnp.float32),
        lax.psum_scatter(
            key_weight_grad.astype(jnp.bfloat16), ("blk", "head"), scatter_dimension=0, tiled=True
        ).astype(jnp.float32),
        lax.psum_scatter(
            value_weight_grad.astype(jnp.bfloat16), ("blk", "head"), scatter_dimension=0, tiled=True
        ).astype(jnp.float32),
        lax.psum_scatter(
            out_weight_grad.astype(jnp.bfloat16), ("blk", "head"), scatter_dimension=0, tiled=True
        ).astype(jnp.float32),
        lax.psum_scatter(
            router_grad.astype(jnp.bfloat16), ("blk", "head"), scatter_dimension=0, tiled=True
        ).astype(jnp.float32),
        lax.psum_scatter(
            attn_gain_grad.astype(jnp.bfloat16), ("blk", "head"), scatter_dimension=0, tiled=True
        ).astype(jnp.float32),
        lax.psum_scatter(
            moe_gain_grad.astype(jnp.bfloat16), ("blk", "head"), scatter_dimension=0, tiled=True
        ).astype(jnp.float32),
    )
    summed = (
        lax.psum(query_shard.astype(jnp.bfloat16), "group").astype(jnp.float32),
        lax.psum(key_shard.astype(jnp.bfloat16), "group").astype(jnp.float32),
        lax.psum(value_shard.astype(jnp.bfloat16), "group").astype(jnp.float32),
        lax.psum(out_shard.astype(jnp.bfloat16), "group").astype(jnp.float32),
        lax.psum(router_shard.astype(jnp.bfloat16), "group").astype(jnp.float32),
        lax.psum(attn_gain_shard.astype(jnp.bfloat16), "group").astype(jnp.float32),
        lax.psum(moe_gain_shard.astype(jnp.bfloat16), "group").astype(jnp.float32),
        lax.psum(gate_weight_grad.astype(jnp.bfloat16), "group").astype(jnp.float32),
        lax.psum(up_weight_grad.astype(jnp.bfloat16), "group").astype(jnp.float32),
        lax.psum(down_weight_grad.astype(jnp.bfloat16), "group").astype(jnp.float32),
    )
    return (
        mixed,
        token_grad,
        summed[5],
        summed[6],
        summed[0],
        summed[1],
        summed[2],
        summed[3],
        summed[4],
        summed[7],
        summed[8],
        summed[9],
    )


bf16 = jnp.bfloat16
f32 = jnp.float32
MESH_ID = pl.DeviceIdType.MESH
VMEM_LIMIT = 67 * 1000 * 1000
COLOURS = ((0, 96), (96, 80), (176, 80))
LINKS = (("head", 1), ("blk", 1), ("blk", 2), ("group", 2), ("group", 1))
ORDERS = ((0, 1, 2), (1, 2, 0), (2, 0, 1))


def vmem():
    return pl.BlockSpec(memory_space=pltpu.VMEM)


def anywhere():
    return pl.BlockSpec(memory_space=pl.ANY)


def dot_last(left, right):
    return lax.dot_general(left, right, (((1,), (1,)), ((), ())), preferred_element_type=f32)


def dot_first(left, right):
    return lax.dot_general(left, right, (((0,), (0,)), ((), ())), preferred_element_type=f32)


def dot(left, right):
    return jnp.dot(left, right, preferred_element_type=f32)


def my_place():
    return lax.axis_index("blk") * 2 + lax.axis_index("head")


def peer(step):
    place = lax.rem(my_place() + step, 8)
    return place, {"blk": place // 2, "head": lax.rem(place, 2)}


def neighbour(link):
    if link == 0:
        return {"head": 1 - lax.axis_index("head")}
    blk = lax.axis_index("blk")
    if link == 1:
        return {"blk": blk + 1 - 2 * lax.rem(blk, 2)}
    return {"blk": lax.rem(blk + 2, 4)}


def my_bits():
    blk = lax.axis_index("blk")
    return (lax.axis_index("head"), lax.rem(blk, 2), blk // 2)


def meet_all():
    barrier = pltpu.get_barrier_semaphore()
    for step in range(1, 8):
        pl.semaphore_signal(barrier, 1, device_id=peer(step)[1], device_id_type=MESH_ID)
    pl.semaphore_wait(barrier, 7)


def remote(src, dst, send, recv, target):
    return pltpu.make_async_remote_copy(
        src_ref=src, dst_ref=dst, send_sem=send, recv_sem=recv, device_id=target, device_id_type=MESH_ID
    )


def cube_index(bits, fixed, rows):
    entries = [pl.ds(fixed[link], 1) if link in fixed else pl.ds(0, 2) for link in (2, 1, 0)]
    return tuple(entries) + (pl.ds(*rows),)


def lanes(shape):
    return lax.broadcasted_iota(jnp.int32, shape, len(shape) - 1)


def turned(u):
    low = lax.rem(lanes(u.shape), 64) < 32
    return jnp.where(low, -pltpu.roll(u, 96, 1), pltpu.roll(u, 32, 1))


def two_heads(q):
    low = lanes(q.shape) < 64
    return jnp.concatenate([jnp.where(low, q, 0.0), jnp.where(low, pltpu.roll(q, 64, 1), 0.0)], 0)


def two_heads_high(g):
    high = lanes(g.shape) >= 64
    return jnp.concatenate([jnp.where(high, pltpu.roll(g, 64, 1), 0.0), jnp.where(high, g, 0.0)], 0)


def block_probability(q_ref, kv_ref, docs, segs, s, i):
    first = max(0, i - 4) * 128
    count = (i + 1) * 128 - first
    q2 = two_heads(q_ref[s, pl.ds(i * 128, 128)].astype(f32))
    kv = kv_ref[s, pl.ds(first, count)]
    raw = dot_last((q2 * 0.125).astype(bf16), kv)
    q_place = i * 128 + lax.broadcasted_iota(jnp.int32, (128, count), 0)
    k_place = first + lanes((128, count))
    q_doc = docs[s, pl.ds(i * 128, 128)]
    keys = pl.ds(first, count)
    k_doc = jnp.where(s == 0, segs[0:1, keys], segs[1:2, keys]).astype(f32)
    allowed = (q_place >= k_place) & (q_doc == k_doc)
    allowed = jnp.concatenate([allowed, allowed], 0)
    masked = jnp.where(allowed, raw, masked_out)
    top = jnp.max(masked, -1, keepdims=True)
    weight = jnp.exp(masked - top)
    probability = weight * (1.0 / jnp.sum(weight, -1, keepdims=True))
    return first, count, q2, kv, probability


def norm_back(values, gain, grad):
    scale = lax.rsqrt(jnp.mean(values * values, -1, keepdims=True) + epsilon)
    inner = grad * gain
    along = jnp.mean(values * inner, -1, keepdims=True)
    out = scale * inner - values * (scale * scale * scale * along)
    gain_grad = jnp.sum(grad * values * scale, 0, keepdims=True)
    return out, gain_grad


def expert_inner(rows_e, pair_e, gate_w, up_w, down_w):
    gate_val = dot(rows_e, gate_w)
    up_val = dot(rows_e, up_w)
    sig = 1.0 / (1.0 + jnp.exp(-gate_val))
    silu = gate_val * sig
    hidden = (silu * up_val).astype(bf16)
    hidden_grad = dot_last(pair_e, down_w)
    gate_grad = (hidden_grad * up_val * sig * (1.0 + gate_val * (1.0 - sig))).astype(bf16)
    up_grad = (hidden_grad * silu).astype(bf16)
    return hidden, gate_grad, up_grad


def sibling():
    group = lax.axis_index("group")
    return {"group": group + 1 - 2 * lax.rem(group, 2)}


def mirror():
    return {"group": lax.rem(lax.axis_index("group") + 2, 4)}


def my_core():
    return lax.rem(lax.axis_index("group"), 2)


def meet(targets):
    barrier = pltpu.get_barrier_semaphore()
    for target in targets:
        pl.semaphore_signal(barrier, 1, device_id=target, device_id_type=MESH_ID)
    pl.semaphore_wait(barrier, len(targets))


def peers():
    return [peer(step)[1] for step in range(1, 8)]


def cube_entry(fixed):
    return tuple(pl.ds(fixed[link], 1) if link in fixed else pl.ds(0, 2) for link in (2, 1, 0))


class Gather:
    def __init__(self, items, send, recv):
        self.items, self.send, self.recv, self.bits = items, send, recv, my_bits()

    def copies(self, step):
        made = []
        for k, (src, place, order) in enumerate(self.items):
            fixed = {link: self.bits[link] for link in order[step:]}
            where = place(cube_entry(fixed))
            here = where
            if step == 0:
                here = src
                where = place((self.bits[2], self.bits[1], self.bits[0]))
            made.append(remote(here, where, self.send.at[step, k], self.recv.at[step, k], neighbour(order[step])))
        return made

    def start(self, step):
        for copy in self.copies(step):
            copy.start()

    def wait(self, step):
        for copy in self.copies(step):
            copy.wait_recv()

    def advance(self, step):
        for before, after in zip(self.copies(step - 1), self.copies(step)):
            before.wait_recv()
            after.start()

    def sent(self):
        for step in range(3):
            for copy in self.copies(step):
                copy.wait_send()


SHARES = ((0, 48), (96, 48), (176, 48), (48, 48), (144, 32), (224, 32))
HALF_SHARES = tuple(
    tuple((s * 128 + start, count) for start, count in ((0, 32), (32, 32), (64, 16), (80, 16), (96, 16), (112, 16)))
    for s in range(2)
)


def row_items(src, dst, shares=SHARES):
    def item(k):
        start, count = shares[k]
        return (src.at[pl.ds(start, count)], lambda entry: dst.at[entry + (pl.ds(start, count),)], ORDERS[k % 3])

    return [item(k) for k in range(len(shares))]


ROW_CUTS = tuple((pl.ds(start, count), slice(None)) for start, count in SHARES)


class CubeSum:
    def __init__(self, source, part, cuts, scratch, base=0):
        self.source, self.part, self.cuts = source, part, cuts
        self.kept = tuple((pl.ds(row.start - base, row.size) if base else row, lane) for row, lane in cuts)
        *self.got, self.held0, self.got1, self.held1, self.got2, self.send, self.recv = scratch
        self.bits = my_bits()
        self.orders = [ORDERS[k % 3] for k in range(len(cuts))]

    def copy(self, step, k):
        order, cut, kept = self.orders[k], self.cuts[k], self.kept[k]
        other = 1 - self.bits[order[step]]
        if step == 0:
            src = self.source.at[cube_entry({order[0]: other}) + cut]
            dst = self.got[k]
        elif step == 1:
            src = self.held0.at[(other, slice(None)) + kept]
            dst = self.got1.at[(slice(None),) + kept]
        else:
            src = self.held1.at[(other,) + kept]
            dst = self.got2.at[kept]
        return remote(src, dst, self.send.at[step, k], self.recv.at[step, k], neighbour(order[step]))

    def start(self):
        for k in range(len(self.cuts)):
            self.copy(0, k).start()

    def middle(self):
        for k, order in enumerate(self.orders):
            self.copy(0, k).wait_recv()
            cut, kept = self.cuts[k], self.kept[k]
            for u in range(2):
                for v in range(2):
                    mine = {order[0]: self.bits[order[0]], order[1]: u, order[2]: v}
                    there = {order[0]: 0, order[1]: u, order[2]: v}
                    landed = self.got[k][there[2], there[1], there[0]].astype(f32)
                    here = self.part[(mine[2], mine[1], mine[0]) + cut].astype(f32)
                    self.held0[(u, v) + kept] = (here + landed).astype(bf16)
            self.copy(1, k).start()

    def last(self):
        for k, order in enumerate(self.orders):
            self.copy(1, k).wait_recv()
            kept = self.kept[k]
            for v in range(2):
                here = self.held0[(self.bits[order[1]], v) + kept].astype(f32)
                self.held1[(v,) + kept] = (here + self.got1[(v,) + kept].astype(f32)).astype(bf16)
            self.copy(2, k).start()

    def finish(self, store):
        for k, order in enumerate(self.orders):
            self.copy(2, k).wait_recv()
            kept = self.kept[k]
            store(
                self.cuts[k], self.held1[(self.bits[order[2]],) + kept].astype(f32) + self.got2[kept].astype(f32)
            )

    def sent(self):
        for step in range(3):
            for k in range(len(self.cuts)):
                self.copy(step, k).wait_send()


def cube_sum_scratch(rows, width, cuts):
    def share(k):
        row, lane = cuts[k]
        shape = [2, 2, 2, rows if row == slice(None) else row.size, width if lane == slice(None) else lane.size]
        shape[2 - ORDERS[k % 3][0]] = 1
        return pltpu.VMEM(tuple(shape), bf16)

    return [
        *(share(k) for k in range(len(cuts))),
        pltpu.VMEM((2, 2, rows, width), bf16),
        pltpu.VMEM((2, rows, width), bf16),
        pltpu.VMEM((2, rows, width), bf16),
        pltpu.VMEM((rows, width), bf16),
        pltpu.SemaphoreType.DMA((3, len(cuts))),
        pltpu.SemaphoreType.DMA((3, len(cuts))),
    ]


class Spread:
    def __init__(self, src, dst, send, recv):
        self.src, self.dst, self.send, self.recv = src, dst, send, recv

    def copy(self, step):
        place, target = peer(step)
        return remote(self.src(place), self.dst(my_place()), self.send.at[step], self.recv.at[step], target)

    def start(self):
        for step in range(1, 8):
            self.copy(step).start()

    def wait(self):
        for step in range(1, 8):
            self.copy(step).wait()


def rope_tables():
    frequency = 10000.0 ** (-(np.arange(128) % 32) * 2.0 / 64)
    near = np.arange(128)[:, None] * frequency[None, :]
    far = np.arange(8)[:, None] * 128.0 * frequency[None, :]
    return tuple(np.asarray(t, np.float32) for t in (np.cos(near), np.sin(near), np.cos(far), np.sin(far)))


def fill_rope(near_cos, near_sin, far_cos, far_sin, cosine, sine):
    for j in range(8):
        rows = pl.ds(j * 128, 128)
        fc, fs = far_cos[pl.ds(j, 1)], far_sin[pl.ds(j, 1)]
        cosine[rows] = fc * near_cos[...] - fs * near_sin[...]
        sine[rows] = fs * near_cos[...] + fc * near_sin[...]


THIRDS = ((0, 384), (384, 384), (768, 256))


def fill_docs(segs, docs):
    for s in range(2):
        for j in range(8):
            row = segs[pl.ds(s, 1), pl.ds(j * 128, 128)].astype(f32)
            docs[s, pl.ds(j * 128, 128)] = jnp.broadcast_to(row, (128, 128)).T[:, 0:1]


def fill_upper(upper):
    row = lax.broadcasted_iota(jnp.int32, upper.shape, 0)
    upper[...] = jnp.where(row < lanes(upper.shape), 1.0, 0.0).astype(bf16)


def forward_kernel(
    tok, cot, wq, wk, wv, wo, attn_gain, moe_gain, router, routes, segs, near_cos, near_sin, far_cos, far_sin,
    attn_hbm, q_out, kv_out, amix, residual_out, moe_in_out, weights_out, wo_hbm, gains_all, router_all, routes_all,
    cot_hbm, cot_mirror, routes_mirror, wkv,
    tok_all, attn_all, cot_all, wo_all, w_all, mix, cosine, sine, docs, gains,
    tok_send, tok_recv, cot_send, cot_recv, small_send, small_recv, mix_send, mix_recv, wo_send, wo_recv,
    pair_send, pair_recv, own_sem, out_sem,
):
    me, core = my_place(), my_core()
    half = pl.ds(pl.multiple_of(core * 64, 64), 64)
    own_entry = (me // 4, lax.rem(me // 2, 2), lax.rem(me, 2))
    first_row = lax.broadcasted_iota(jnp.int32, (16, 128), 0)
    both_gains = jnp.where(first_row == 1, moe_gain[...].astype(f32), 0.0)
    gains[...] = jnp.where(first_row == 0, attn_gain[...].astype(f32), both_gains).astype(bf16)
    for j in range(4):
        low = lanes((128, 128)) < 64
        k_two, v_two = (w[:, j * 128 : (j + 1) * 128].astype(f32) for w in (wk, wv))
        wkv[:, j * 256 : j * 256 + 128] = jnp.where(low, k_two, pltpu.roll(v_two, 64, 1)).astype(bf16)
        wkv[:, j * 256 + 128 : j * 256 + 256] = jnp.where(low, pltpu.roll(k_two, 64, 1), v_two).astype(bf16)
    meet(peers() + [sibling(), mirror()])
    tok_gather = Gather(row_items(tok, tok_all), tok_send, tok_recv)
    tok_gather.start(0)
    pairs = (
        (lambda j: wq.at[:, pl.ds(j * 128, 128)], lambda i: w_all.at[pl.ds(i * 128, 128), pl.ds(0, 128)]),
        (lambda j: wkv.at[:, pl.ds(j * 128, 128)], lambda i: w_all.at[pl.ds(i * 128, 128), pl.ds(128, 128)]),
        (lambda j: gains, lambda i: gains_all.at[:, pl.ds(i * 128, 128)]),
        (lambda j: router, lambda i: router_all.at[:, pl.ds(i * 128, 128)]),
        (lambda j: routes.at[:, pl.ds(0, 128)], lambda i: routes_all.at[:, pl.ds(i * 128, 128)]),
        (lambda j: routes.at[:, pl.ds(128, 128)], lambda i: routes_all.at[:, pl.ds(1024 + i * 128, 128)]),
    )
    smalls = [Spread(src, dst, small_send.at[k], small_recv.at[k]) for k, (src, dst) in enumerate(pairs)]
    own = [pltpu.make_async_copy(src(me), dst(me), own_sem.at[k]) for k, (src, dst) in enumerate(pairs)]
    own += [
        pltpu.make_async_copy(tok, tok_all.at[own_entry], own_sem.at[6]),
        pltpu.make_async_copy(cot, cot_all.at[own_entry], own_sem.at[7]),
        pltpu.make_async_copy(wo.at[half], wo_all.at[own_entry + (half,)], own_sem.at[8]),
    ]
    for copy in own:
        copy.start()
    for small in smalls:
        small.start()
    fill_rope(near_cos, near_sin, far_cos, far_sin, cosine, sine)
    for copy in own:
        copy.wait()
    tok_gather.advance(1)
    fill_docs(segs, docs)
    tok_gather.advance(2)
    for small in smalls:
        small.wait()
    tok_gather.wait(2)

    def wo_item(k):
        where = (half, pl.ds(*THIRDS[k]))
        return (wo.at[where], lambda entry: wo_all.at[entry + where], ORDERS[k])

    wo_gather = Gather([wo_item(k) for k in range(3)], wo_send, wo_recv)
    wo_gather.start(0)
    cot_gather = Gather(row_items(cot, cot_all), cot_send, cot_recv)
    cot_gather.start(0)
    cot_copy = remote(cot, cot_mirror, pair_send.at[1], pair_recv.at[1], mirror())
    cot_copy.start()
    routes_copy = remote(routes_all, routes_mirror, pair_send.at[0], pair_recv.at[0], mirror())
    routes_copy.start()

    gain_row = gains_all[0:1].astype(f32)

    def project(j, carry):
        rows = pl.ds(pl.multiple_of(j * 128, 128), 128)
        x = tok_all[j // 4, lax.rem(j // 2, 2), lax.rem(j, 2)].astype(f32)
        scale = lax.rsqrt(jnp.mean(x * x, -1, keepdims=True) + epsilon)
        attn_in = (x * scale * gain_row).astype(bf16)
        attn_all[j] = attn_in
        both = dot(attn_in, w_all[...])
        c = cosine[rows]
        n = sine[rows]
        c2 = jnp.concatenate([c, c], 0)
        n2 = jnp.concatenate([n, n], 0)
        q = both[:, :128]
        kv = both[:, 128:]
        q = (q * c2 + turned(q) * n2).astype(bf16)
        kv = jnp.where(lanes(kv.shape) < 64, kv * c2 + turned(kv) * n2, kv).astype(bf16)
        for s in range(2):
            q_out[s, rows] = q[s * 128 : (s + 1) * 128]
            kv_out[s, rows] = kv[s * 128 : (s + 1) * 128]
        return carry

    lax.fori_loop(0, 8, project, 0)
    attn_copy = pltpu.make_async_copy(attn_all, attn_hbm, out_sem.at[0])
    attn_copy.start()
    wo_gather.advance(1)
    cot_gather.advance(1)
    wo_pair = remote(
        wo_all.at[:, :, :, half], wo_all.at[:, :, :, half], pair_send.at[2], pair_recv.at[2], sibling()
    )

    def mix_copy(i):
        return remote(
            mix.at[i],
            amix.at[:, :, pl.ds(pl.multiple_of(me * 128, 128), 128)],
            mix_send.at[i],
            mix_recv.at[me],
            {"blk": i // 2, "head": lax.rem(i, 2)},
        )

    def send_mix(i):
        @pl.when(me != i)
        def _():
            mix_copy(i).start()

    for i in range(8):

        def attend(s, carry, i=i):
            first, count, q2, kv, probability = block_probability(q_out, kv_out, docs, segs, s, i)
            mixed = dot(probability.astype(bf16), kv)
            low = lanes((128, 128)) < 64
            mix[i, s] = jnp.where(low, pltpu.roll(mixed[:128], 64, 1), mixed[128:]).astype(bf16)
            return carry

        lax.fori_loop(0, 2, attend, 0)
        if i > 0:
            send_mix(i - 1)
        if i == 2:
            wo_gather.advance(2)
        if i == 4:
            cot_gather.advance(2)
    send_mix(7)
    wo_gather.wait(2)
    wo_pair.start()
    mine = pltpu.make_async_copy(
        mix.at[me], amix.at[:, :, pl.ds(pl.multiple_of(me * 128, 128), 128)], own_sem.at[0]
    )
    mine.start()
    wo_pair.wait()
    wo_copy = pltpu.make_async_copy(wo_all, wo_hbm, out_sem.at[1])
    wo_copy.start()
    for step in range(1, 8):
        place, target = peer(step)
        remote(
            mix.at[place],
            amix.at[:, :, pl.ds(pl.multiple_of(place * 128, 128), 128)],
            mix_send.at[place],
            mix_recv.at[place],
            target,
        ).wait()
    mine.wait()
    width = tok.shape[-1]
    residual = tok[...].astype(f32) + dot(amix[...].reshape(256, width), wo_all[...].reshape(width, width))
    residual_out[...] = residual
    scale = lax.rsqrt(jnp.mean(residual * residual, -1, keepdims=True) + epsilon)
    moe_in = (residual * scale * gains_all[1:2].astype(f32)).astype(bf16)
    moe_in_out[...] = moe_in
    logits = dot_last(router_all[...], moe_in)
    experts = lax.broadcasted_iota(jnp.int32, logits.shape, 0)
    picked = [
        jnp.sum(jnp.where(experts == routes[pl.ds(k, 1)], logits, 0.0), 0, keepdims=True) for k in range(TOP)
    ]
    picked = jnp.concatenate(picked, 0)
    weight = jnp.exp(picked - jnp.max(picked, 0, keepdims=True))
    weights_out[...] = weight / jnp.sum(weight, 0, keepdims=True)
    cot_gather.wait(2)
    cot_out = pltpu.make_async_copy(cot_all, cot_hbm, out_sem.at[2])
    cot_out.start()
    routes_copy.wait()
    cot_copy.wait()
    tok_gather.sent()
    cot_gather.sent()
    wo_gather.sent()
    attn_copy.wait()
    wo_copy.wait()
    cot_out.wait()


def forward(*values):
    tok = values[0]
    width = tok.shape[-1]
    tables = tuple(jnp.asarray(t) for t in rope_tables())
    return pl.pallas_call(
        forward_kernel,
        out_shape=(
            jax.ShapeDtypeStruct((8, 256, width), bf16),
            jax.ShapeDtypeStruct((2, 1024, 128), bf16),
            jax.ShapeDtypeStruct((2, 1024, 128), bf16),
            jax.ShapeDtypeStruct((2, 128, width), bf16),
            jax.ShapeDtypeStruct((256, width), f32),
            jax.ShapeDtypeStruct((256, width), bf16),
            jax.ShapeDtypeStruct((8, 256), f32),
            jax.ShapeDtypeStruct((2, 2, 2, 128, width), bf16),
            jax.ShapeDtypeStruct((16, width), bf16),
            jax.ShapeDtypeStruct((32, width), bf16),
            jax.ShapeDtypeStruct((8, 2048), jnp.int32),
            jax.ShapeDtypeStruct((2, 2, 2, 256, width), bf16),
            jax.ShapeDtypeStruct((256, width), bf16),
            jax.ShapeDtypeStruct((8, 2048), jnp.int32),
            jax.ShapeDtypeStruct((128, 1024), bf16),
        ),
        in_specs=[vmem()] * 15,
        out_specs=(
            anywhere(), vmem(), vmem(), vmem(), vmem(), vmem(), vmem(), anywhere(), vmem(), vmem(), vmem(),
            anywhere(), vmem(), vmem(), vmem(),
        ),
        scratch_shapes=[
            pltpu.VMEM((2, 2, 2, 256, width), bf16),
            pltpu.VMEM((8, 256, width), bf16),
            pltpu.VMEM((2, 2, 2, 256, width), bf16),
            pltpu.VMEM((2, 2, 2, 128, width), bf16),
            pltpu.VMEM((width, 256), bf16),
            pltpu.VMEM((8, 2, 128, 128), bf16),
            pltpu.VMEM((1024, 128), f32),
            pltpu.VMEM((1024, 128), f32),
            pltpu.VMEM((2, 1024, 1), f32),
            pltpu.VMEM((16, 128), bf16),
            pltpu.SemaphoreType.DMA((3, 6)),
            pltpu.SemaphoreType.DMA((3, 6)),
            pltpu.SemaphoreType.DMA((3, 6)),
            pltpu.SemaphoreType.DMA((3, 6)),
            pltpu.SemaphoreType.DMA((6, 8)),
            pltpu.SemaphoreType.DMA((6, 8)),
            pltpu.SemaphoreType.DMA((8,)),
            pltpu.SemaphoreType.DMA((8,)),
            pltpu.SemaphoreType.DMA((3, 3)),
            pltpu.SemaphoreType.DMA((3, 3)),
            pltpu.SemaphoreType.DMA((3,)),
            pltpu.SemaphoreType.DMA((3,)),
            pltpu.SemaphoreType.DMA((9,)),
            pltpu.SemaphoreType.DMA((3,)),
        ],
        compiler_params=pltpu.CompilerParams(
            collective_id=0, has_side_effects=True, vmem_limit_bytes=VMEM_LIMIT
        ),
        name="forward",
    )(*values, *tables)


SLOT = 4 * CAPH
SPAN = 512
TAKEN = 4 * SLOT


def build_rows(routes, upper, plain, first_expert, block):
    columns = pl.ds(pl.multiple_of(block * SPAN, SPAN), SPAN)
    chosen = routes[:, columns]
    masks = [jnp.max((chosen == first_expert + e).astype(f32), 0, keepdims=True) for e in range(4)]
    mask = jnp.concatenate(masks + [jnp.zeros((4, SPAN), f32)], 0)
    rank = dot(mask.astype(bf16), upper[...])
    slots = lax.broadcasted_iota(jnp.int32, (SLOT, SPAN), 0).astype(f32)
    for e in range(4):
        hit = (slots == rank[e : e + 1]) & (mask[e : e + 1] > 0.0)
        plain[block, e * SLOT : (e + 1) * SLOT] = jnp.where(hit, 1.0, 0.0).astype(bf16)


def slot_weights(routes, weights, plain, column, first_expert, block):
    columns = pl.ds(pl.multiple_of(block * SPAN, SPAN), SPAN)
    chosen = routes[:, columns]
    weight = weights[:, columns]
    for e in range(4):
        share = jnp.sum(jnp.where(chosen == first_expert + e, weight, 0.0), 0, keepdims=True)
        mine = pl.ds(e * SLOT, SLOT)
        column[block, mine] = jnp.sum(plain[block, mine].astype(f32) * share, -1, keepdims=True)


def place_rows(source, block):
    width = source.shape[-1]
    rows = pl.ds(pl.multiple_of((block // 2) * 128, 128), 128)
    return source[lax.rem(block, 2), :, :, rows].reshape(SPAN, width)


def expert_rows(e):
    return pl.ds(pl.multiple_of(e * SLOT, 16), SLOT)


def experts_kernel(
    moe_in, my_weights, cot_mirror, cot_hbm, routes, routes_mirror, gate_hbm, up_hbm, down_hbm,
    out_part, in_sum, p_all, rows_out, pair_out, hidden_out, gate_out, up_out, plain_mirror, pair_mirror, moe_mirror,
    weights_other,
    x, c, cm, upper, plain, rows, pair_grad, pair_in, column, p_col, weights, p_part,
    gate, up, down, hid_buf, gg_buf, ug_buf, part_buf,
    row_send, row_recv, cm_send, cm_recv, w_send, w_recv, p_send, p_recv, pair_send, pair_recv,
    sem_c, sem_w, sem_rows, sem_h, sem_part, own_sem, *sums,
):
    me = my_place()
    first = me * 4
    width = x.shape[-1]
    count = 2 * SLOT
    own_entry = (me // 4, lax.rem(me // 2, 2), lax.rem(me, 2))
    meet(peers() + [mirror()])
    gathers = [
        Gather(row_items(moe_in, x, HALF_SHARES[s]), row_send.at[s], row_recv.at[s]) for s in range(2)
    ]
    gathers[0].start(0)

    def weight_lanes(s, i):
        return weights.at[:, pl.ds(pl.multiple_of(s * 1024 + i * 128, 128), 128)]

    own = [
        pltpu.make_async_copy(moe_in, x.at[own_entry], own_sem.at[0]),
        pltpu.make_async_copy(my_weights.at[:, pl.ds(0, 128)], weight_lanes(0, me), own_sem.at[1]),
        pltpu.make_async_copy(my_weights.at[:, pl.ds(128, 128)], weight_lanes(1, me), own_sem.at[2]),
        pltpu.make_async_copy(cot_mirror, cm.at[own_entry], own_sem.at[3]),
    ]
    for copy in own:
        copy.start()
    weight_spreads = [
        Spread(
            lambda j, s=s: my_weights.at[:, pl.ds(s * 128, 128)],
            lambda i, s=s: weight_lanes(s, i),
            w_send.at[s],
            w_recv.at[s],
        )
        for s in range(2)
    ]
    for spread in weight_spreads:
        spread.start()
    load_c = pltpu.make_async_copy(cot_hbm, c, sem_c)
    load_c.start()

    def fetch(e, slot):
        return [
            pltpu.make_async_copy(gate_hbm.at[e], gate.at[slot], sem_w.at[slot, 0]),
            pltpu.make_async_copy(up_hbm.at[e], up.at[slot], sem_w.at[slot, 1]),
            pltpu.make_async_copy(down_hbm.at[e], down.at[slot], sem_w.at[slot, 2]),
        ]

    for copy in fetch(0, 0):
        copy.start()
    fill_upper(upper)

    def build(block, carry):
        build_rows(routes, upper, plain, first, block)
        return carry

    lax.fori_loop(0, 2, build, 0)
    for copy in own:
        copy.wait()
    gathers[0].advance(1)
    lax.fori_loop(2, 4, build, 0)
    load_c.wait()

    def take_c(block, carry):
        pair_grad[block] = dot(plain[block], place_rows(c, block)).astype(bf16)
        return carry

    gathers[0].advance(2)
    gathers[1].start(0)
    lax.fori_loop(0, 4, take_c, 0)
    for spread in weight_spreads:
        spread.wait()
    weights_copy = remote(weights, weights_other, pair_send.at[0], pair_recv.at[0], mirror())
    weights_copy.start()

    def weigh(block, carry):
        slot_weights(routes, weights, plain, column, first, block)
        return carry

    lax.fori_loop(0, 4, weigh, 0)
    cm_gather = Gather(row_items(cot_mirror, cm), cm_send, cm_recv)
    moe_copy = remote(moe_in, moe_mirror, pair_send.at[1], pair_recv.at[1], mirror())
    p_part[...] = jnp.zeros_like(p_part)

    def take_x(block, carry):
        rows[block] = dot(plain[block], place_rows(x, block)).astype(bf16)
        return carry

    def keep_rows(s):
        pair = pl.ds(2 * s, 2)
        return pltpu.make_async_copy(rows.at[pair], rows_out.at[pair], sem_rows.at[s])

    def keep(s, e, slot):
        where = pl.ds(s * count, count)
        return [
            pltpu.make_async_copy(hid_buf.at[slot], hidden_out.at[e, where], sem_h.at[slot, 0]),
            pltpu.make_async_copy(gg_buf.at[slot], gate_out.at[e, where], sem_h.at[slot, 1]),
            pltpu.make_async_copy(ug_buf.at[slot], up_out.at[e, where], sem_h.at[slot, 2]),
        ]

    def total_of(s):
        cuts = tuple((pl.ds(*cut), slice(None)) for cut in HALF_SHARES[s])
        return CubeSum(x, x, cuts, sums[12 * s : 12 * s + 12], s * 128)

    totals = [total_of(s) for s in range(2)]

    def store(cut, value):
        in_sum[cut] = value

    for s in range(2):
        gathers[s].wait(2)
        if s == 0:
            gathers[1].advance(1)
        lax.fori_loop(2 * s, 2 * s + 2, take_x, 0)
        keep_rows(s).start()
        if s == 0:
            gathers[1].advance(2)
            cm_gather.start(0)
            moe_copy.start()

        def expert(e, carry, s=s):
            slot = lax.rem(e, 2)
            mine = expert_rows(e)
            pair = pl.ds(2 * s, 2)
            for copy in fetch(e, slot):
                copy.wait()
            if s == 0:
                for copy in fetch(lax.rem(e + 1, 4), 1 - slot):
                    copy.start()
            else:

                @pl.when(e < 3)
                def _():
                    for copy in fetch(e + 1, 1 - slot):
                        copy.start()

            rows_e = rows[pair, mine].reshape(count, width)
            weight_e = column[pair, mine].reshape(count, 1)
            pair_e = (pair_grad[pair, mine].reshape(count, width).astype(f32) * weight_e).astype(bf16)
            pair_grad[pair, mine] = pair_e.reshape(2, SLOT, width)
            hidden, gate_grad, up_grad = expert_inner(rows_e, pair_e, gate[slot], up[slot], down[slot])

            @pl.when(e >= 2)
            def _():
                for copy in keep(s, e - 2, slot):
                    copy.wait()

            hid_buf[slot] = hidden
            gg_buf[slot] = gate_grad
            ug_buf[slot] = up_grad
            for copy in keep(s, e, slot):
                copy.start()

            @pl.when(e == 0)
            def _():
                keep_rows(s).wait()

            out_e = dot(hidden, down[slot]).astype(bf16).astype(f32)
            p = jnp.sum(out_e * pair_e.astype(f32), -1, keepdims=True)
            p_col[pair, mine] = p.reshape(2, SLOT, 1)
            rows[pair, mine] = (out_e * weight_e).astype(bf16).reshape(2, SLOT, width)
            back = dot_last(gate_grad, gate[slot]) + dot_last(up_grad, up[slot])
            pair_in[pair, mine] = back.astype(bf16).reshape(2, SLOT, width)
            if s == 0:

                @pl.when(e == 3)
                def _():
                    cm_gather.advance(1)

            else:

                @pl.when(e == 1)
                def _():
                    cm_gather.advance(2)

                @pl.when(e == 2)
                def _():
                    totals[0].middle()

            return carry

        lax.fori_loop(0, 4, expert, 0)
        for copy in keep(s, 2, 0) + keep(s, 3, 1):
            copy.wait()
        gathers[s].sent()

        def combine_in(block, carry, s=s):
            y = lax.rem(block, 2)
            back = dot_first(plain[block], pair_in[block]).astype(bf16)
            x[y, :, :, s * 128 : (s + 1) * 128] = back.reshape(2, 2, 128, width)
            for e in range(4):
                mine = pl.ds(e * SLOT, SLOT)
                p = jnp.sum(plain[block, mine].astype(f32) * p_col[block, mine], 0, keepdims=True)
                for d in range(4):
                    p_part[y * 4 + d, pl.ds(e, 1), s * 128 : (s + 1) * 128] = p[:, d * 128 : (d + 1) * 128]
            return carry

        lax.fori_loop(2 * s, 2 * s + 2, combine_in, 0)
        totals[s].start()
        if s == 1:
            totals[0].last()

    keep_pair = pltpu.make_async_copy(pair_grad, pair_out, sem_rows.at[0])
    keep_pair.start()
    p_spread = Spread(lambda j: p_part.at[j], lambda i: p_all.at[i], p_send, p_recv)
    p_spread.start()
    p_own = pltpu.make_async_copy(p_part.at[me], p_all.at[me], own_sem.at[0])
    p_own.start()

    def part_copy(block):
        slot = lax.rem(block, 2)
        rows_of = pl.ds(pl.multiple_of((block // 2) * 128, 128), 128)
        return pltpu.make_async_copy(
            part_buf.at[slot], out_part.at[lax.rem(block, 2), :, :, rows_of], sem_part.at[slot]
        )

    def combine_out(block, carry):
        slot = lax.rem(block, 2)

        @pl.when(block >= 2)
        def _():
            part_copy(block - 2).wait()

        out = dot_first(plain[block], rows[block]).astype(bf16)
        part_buf[slot] = out.reshape(2, 2, 128, width)
        part_copy(block).start()
        return carry

    lax.fori_loop(0, 4, combine_out, 0)
    totals[0].finish(store)
    keep_pair.wait()

    def build_mirror(block, carry):
        build_rows(routes_mirror, upper, plain, first, block)
        return carry

    lax.fori_loop(0, 2, build_mirror, 0)
    totals[1].middle()
    lax.fori_loop(2, 4, build_mirror, 0)
    keep_plain = pltpu.make_async_copy(plain, plain_mirror, sem_rows.at[0])
    keep_plain.start()
    cm_gather.wait(2)

    def take_mirror(block, carry):
        pair_grad[block] = dot(plain[block], place_rows(cm, block)).astype(bf16)
        return carry

    lax.fori_loop(0, 2, take_mirror, 0)
    totals[1].last()
    lax.fori_loop(2, 4, take_mirror, 0)
    keep_mirror = pltpu.make_async_copy(pair_grad, pair_mirror, sem_rows.at[1])
    keep_mirror.start()
    p_spread.wait()
    p_own.wait()
    part_copy(2).wait()
    part_copy(3).wait()
    totals[1].finish(store)
    for total in totals:
        total.sent()
    keep_plain.wait()
    keep_mirror.wait()
    cm_gather.sent()
    weights_copy.wait()
    moe_copy.wait()


def half_cuts(s):
    return tuple((pl.ds(*cut), slice(None)) for cut in HALF_SHARES[s])


def experts(moe_in, my_weights, cot_mirror, cot_all, routes, routes_mirror, gate_w, up_w, down_w):
    width = moe_in.shape[-1]
    ff = gate_w.shape[-1]
    return pl.pallas_call(
        experts_kernel,
        out_shape=(
            jax.ShapeDtypeStruct((2, 2, 2, 256, width), bf16),
            jax.ShapeDtypeStruct((256, width), f32),
            jax.ShapeDtypeStruct((8, 8, 256), f32),
            jax.ShapeDtypeStruct((4, TAKEN, width), bf16),
            jax.ShapeDtypeStruct((4, TAKEN, width), bf16),
            jax.ShapeDtypeStruct((4, TAKEN, ff), bf16),
            jax.ShapeDtypeStruct((4, TAKEN, ff), bf16),
            jax.ShapeDtypeStruct((4, TAKEN, ff), bf16),
            jax.ShapeDtypeStruct((4, TAKEN, SPAN), bf16),
            jax.ShapeDtypeStruct((4, TAKEN, width), bf16),
            jax.ShapeDtypeStruct((256, width), bf16),
            jax.ShapeDtypeStruct((8, 2048), f32),
        ),
        in_specs=[vmem(), vmem(), vmem(), anywhere(), vmem(), vmem(), anywhere(), anywhere(), anywhere()],
        out_specs=(anywhere(), vmem(), vmem()) + (anywhere(),) * 7 + (vmem(), vmem()),
        scratch_shapes=[
            pltpu.VMEM((2, 2, 2, 256, width), bf16),
            pltpu.VMEM((2, 2, 2, 256, width), bf16),
            pltpu.VMEM((2, 2, 2, 256, width), bf16),
            pltpu.VMEM((SPAN, SPAN), bf16),
            pltpu.VMEM((4, TAKEN, SPAN), bf16),
            pltpu.VMEM((4, TAKEN, width), bf16),
            pltpu.VMEM((4, TAKEN, width), bf16),
            pltpu.VMEM((4, TAKEN, width), bf16),
            pltpu.VMEM((4, TAKEN, 1), f32),
            pltpu.VMEM((4, TAKEN, 1), f32),
            pltpu.VMEM((8, 2048), f32),
            pltpu.VMEM((8, 8, 256), f32),
            pltpu.VMEM((2, width, ff), bf16),
            pltpu.VMEM((2, width, ff), bf16),
            pltpu.VMEM((2, ff, width), bf16),
            pltpu.VMEM((2, 2 * SLOT, ff), bf16),
            pltpu.VMEM((2, 2 * SLOT, ff), bf16),
            pltpu.VMEM((2, 2 * SLOT, ff), bf16),
            pltpu.VMEM((2, 2, 2, 128, width), bf16),
            pltpu.SemaphoreType.DMA((2, 3, 6)),
            pltpu.SemaphoreType.DMA((2, 3, 6)),
            pltpu.SemaphoreType.DMA((3, 6)),
            pltpu.SemaphoreType.DMA((3, 6)),
            pltpu.SemaphoreType.DMA((2, 8)),
            pltpu.SemaphoreType.DMA((2, 8)),
            pltpu.SemaphoreType.DMA((8,)),
            pltpu.SemaphoreType.DMA((8,)),
            pltpu.SemaphoreType.DMA((2,)),
            pltpu.SemaphoreType.DMA((2,)),
            pltpu.SemaphoreType.DMA,
            pltpu.SemaphoreType.DMA((2, 3)),
            pltpu.SemaphoreType.DMA((2,)),
            pltpu.SemaphoreType.DMA((2, 3)),
            pltpu.SemaphoreType.DMA((2,)),
            pltpu.SemaphoreType.DMA((4,)),
            *cube_sum_scratch(128, width, half_cuts(0)),
            *cube_sum_scratch(128, width, half_cuts(1)),
        ],
        compiler_params=pltpu.CompilerParams(
            collective_id=1, has_side_effects=True, vmem_limit_bytes=VMEM_LIMIT
        ),
        name="experts",
    )(moe_in, my_weights, cot_mirror, cot_all, routes, routes_mirror, gate_w, up_w, down_w)


LANE_SHARE = 128


def backward_kernel(
    cot, residual, in_sum, p_all, routes, weights, router, moe_in, gains_all, wo_hbm, amix, attn_hbm, q_in, kv_in,
    segs, near_cos, near_sin, far_cos, far_sin, tok, wq, wkv, moe_mirror,
    token_grad, grads, mirror_hbm,
    wo_all, attn_all, wq_all, wkv_all, mm, mix_grad, mg, gq, gkv, gq_rows, gkv_rows, g_all, kv_sum, cosine, sine, docs,
    residual_grad, small_grad,
    w_send, w_recv, mm_send, mm_recv, mg_send, mg_recv, g_send, g_recv, pair_send, pair_recv, own_sem, load_sem,
):
    me, core = my_place(), my_core()
    width = tok.shape[-1]
    meet(peers() + [sibling()])
    half = pl.ds(pl.multiple_of(core * 64, 64), 64)
    own_entry = (me // 4, lax.rem(me // 2, 2), lax.rem(me, 2))
    own = [
        pltpu.make_async_copy(wq.at[half], wq_all.at[own_entry + (half,)], own_sem.at[0]),
        pltpu.make_async_copy(wkv.at[half], wkv_all.at[own_entry + (half,)], own_sem.at[1]),
        pltpu.make_async_copy(moe_mirror, mm.at[own_entry], own_sem.at[2]),
    ]
    loads = [
        pltpu.make_async_copy(wo_hbm, wo_all, load_sem.at[0]),
        pltpu.make_async_copy(attn_hbm, attn_all, load_sem.at[1]),
    ]
    for copy in own + loads:
        copy.start()

    def weight_item(src, dst, start, count, order):
        rows = pl.ds(pl.multiple_of(core * 64 + start, 16), count)
        return (src.at[rows], lambda entry: dst.at[entry + (rows,)], order)

    w_gather = Gather(
        [
            weight_item(wq, wq_all, 0, 48, ORDERS[0]),
            weight_item(wq, wq_all, 48, 16, ORDERS[1]),
            weight_item(wkv, wkv_all, 0, 32, ORDERS[1]),
            weight_item(wkv, wkv_all, 32, 32, ORDERS[2]),
        ],
        w_send,
        w_recv,
    )
    w_gather.start(0)
    mm_gather = Gather(row_items(moe_mirror, mm), mm_send, mm_recv)
    mm_gather.start(0)
    ids = lax.broadcasted_iota(jnp.int32, (32, 256), 0)
    dense = jnp.zeros((32, 256), f32)
    for k in range(TOP):
        dense = dense + jnp.where(ids == routes[pl.ds(k, 1)], weights[pl.ds(k, 1)], 0.0)
    p = jnp.concatenate([p_all[i, 0:4] for i in range(8)], 0)
    logit_grad = (p - dense * jnp.sum(p, 0, keepdims=True)).astype(bf16)
    moe_in_grad = in_sum[...] + dot_first(logit_grad, router[...])
    part, moe_gain_grad = norm_back(residual[...], gains_all[1:2].astype(f32), moe_in_grad)
    total = cot[...].astype(f32) + part
    residual_grad[...] = total
    low_grad = total.astype(bf16)
    for copy in loads[:1]:
        copy.wait()
    back = dot_last(low_grad, wo_all[...].reshape(width, width)).astype(bf16)
    for j in range(8):
        mix_grad[j] = back[:, j * 128 : (j + 1) * 128].reshape(2, 128, 128)
    mix_spread = Spread(lambda j: mix_grad.at[j], lambda i: mg.at[i], mg_send, mg_recv)
    mix_spread.start()
    mix_own = pltpu.make_async_copy(mix_grad.at[me], mg.at[me], own_sem.at[3])
    mix_own.start()
    for copy in own:
        copy.wait()
    w_gather.advance(1)
    fill_rope(near_cos, near_sin, far_cos, far_sin, cosine, sine)
    fill_docs(segs, docs)
    wo_grad = dot_first(amix[...].reshape(256, width), low_grad)
    grads[:, :, 0:width] = wo_grad.astype(bf16).reshape(8, 128, width)
    padded = jnp.concatenate([logit_grad, jnp.zeros((LANE_SHARE - 32, 256), bf16)], 0)
    small_grad[...] = lax.dot_general(moe_in[...], padded, (((0,), (1,)), ((), ())), preferred_element_type=f32)
    mix_spread.wait()
    mix_own.wait()
    mm_gather.advance(1)

    def lane_block(i):
        return pl.ds(pl.multiple_of(i * 128, 128), 128)

    def spread_of(s):
        return [
            Spread(lambda j: gq.at[j, s], lambda i: gq_rows.at[s, :, lane_block(i)], g_send.at[2 * s], g_recv.at[2 * s]),
            Spread(
                lambda j: gkv.at[j, s],
                lambda i: gkv_rows.at[s, :, lane_block(i)],
                g_send.at[2 * s + 1],
                g_recv.at[2 * s + 1],
            ),
        ]

    keep_own = []
    for s in range(2):
        kv_sum[...] = jnp.zeros_like(kv_sum)
        for i in range(8):
            first, count, q2, kv, probability = block_probability(q_in, kv_in, docs, segs, s, i)
            g2 = two_heads_high(mg[i, s].astype(f32)).astype(bf16)
            prob_grad = dot_last(g2, kv)
            delta = jnp.sum(probability * prob_grad, -1, keepdims=True)
            score_grad = (probability * (prob_grad - delta) * 0.125).astype(bf16)
            dq = dot(score_grad, kv)
            keys = pl.ds(first, count)
            kv_sum[keys] += dot_first(score_grad, q2.astype(bf16)) + dot_first(probability.astype(bf16), g2)
            low = lanes((128, 128)) < 64
            dq = jnp.where(low, dq[:128], pltpu.roll(dq[128:], 64, 1))
            rows = pl.ds(i * 128, 128)
            dq = (dq * cosine[rows] - turned(dq) * sine[rows]).astype(bf16)
            gq[i, s] = dq
            g_all[i, s, :, 0:128] = dq
            if s == 0 and i == 2:
                w_gather.advance(2)
            if s == 0 and i == 6:
                mm_gather.advance(2)
        for i in range(8):
            rows = pl.ds(i * 128, 128)
            dkv = kv_sum[rows]
            low = lanes((128, 128)) < 64
            dkv = jnp.where(low, dkv * cosine[rows] - turned(dkv) * sine[rows], dkv).astype(bf16)
            gkv[i, s] = dkv
            g_all[i, s, :, 128:256] = dkv
        for spread in spread_of(s):
            spread.start()
        mine = [
            pltpu.make_async_copy(gq.at[me, s], gq_rows.at[s, :, lane_block(me)], own_sem.at[4 + 2 * s]),
            pltpu.make_async_copy(gkv.at[me, s], gkv_rows.at[s, :, lane_block(me)], own_sem.at[5 + 2 * s]),
        ]
        for copy in mine:
            copy.start()
        keep_own += mine
    w_gather.wait(2)
    shared = [
        remote(w.at[:, :, :, half], w.at[:, :, :, half], pair_send.at[k], pair_recv.at[k], sibling())
        for k, w in enumerate((wq_all, wkv_all))
    ]
    for copy in shared:
        copy.start()
    loads[1].wait()
    w_grad = dot_first(attn_all[...].reshape(2048, width), g_all[...].reshape(2048, 256))
    grads[:, :, width + LANE_SHARE :] = w_grad.astype(bf16).reshape(8, 128, 256)
    for copy in shared + keep_own:
        copy.wait()
    for s in range(2):
        for spread in spread_of(s):
            spread.wait()
    back = dot_last(gq_rows[...].reshape(256, 1024), wq_all[...].reshape(width, 1024))
    back = back + dot_last(gkv_rows[...].reshape(256, 1024), wkv_all[...].reshape(width, 1024))
    part, attn_gain_grad = norm_back(tok[...].astype(f32), gains_all[0:1].astype(f32), back)
    token_grad[...] = residual_grad[...] + part
    row = lax.broadcasted_iota(jnp.int32, (LANE_SHARE, width), 0)
    gain_rows = jnp.where(row == 32, moe_gain_grad, jnp.where(row == 33, attn_gain_grad, 0.0))
    grads[:, :, width : width + LANE_SHARE] = (small_grad[...] + gain_rows.T).astype(bf16).reshape(8, 128, LANE_SHARE)
    mm_gather.wait(2)
    mm_out = pltpu.make_async_copy(mm, mirror_hbm, load_sem.at[0])
    mm_out.start()
    w_gather.sent()
    mm_gather.sent()
    mm_out.wait()


def backward(*values):
    tok = values[15]
    width = tok.shape[-1]
    tables = tuple(jnp.asarray(t) for t in rope_tables())
    values = values[:15] + tables + values[15:]
    specs = [vmem()] * 23
    specs[9] = specs[11] = anywhere()
    return pl.pallas_call(
        backward_kernel,
        out_shape=(
            jax.ShapeDtypeStruct((256, width), f32),
            jax.ShapeDtypeStruct((8, 128, width + 256 + LANE_SHARE), bf16),
            jax.ShapeDtypeStruct((2, 2, 2, 256, width), bf16),
        ),
        in_specs=specs,
        out_specs=(vmem(), vmem(), anywhere()),
        scratch_shapes=[
            pltpu.VMEM((2, 2, 2, 128, width), bf16),
            pltpu.VMEM((8, 256, width), bf16),
            pltpu.VMEM((2, 2, 2, 128, width), bf16),
            pltpu.VMEM((2, 2, 2, 128, width), bf16),
            pltpu.VMEM((2, 2, 2, 256, width), bf16),
            pltpu.VMEM((8, 2, 128, 128), bf16),
            pltpu.VMEM((8, 2, 128, 128), bf16),
            pltpu.VMEM((8, 2, 128, 128), bf16),
            pltpu.VMEM((8, 2, 128, 128), bf16),
            pltpu.VMEM((2, 128, 1024), bf16),
            pltpu.VMEM((2, 128, 1024), bf16),
            pltpu.VMEM((8, 2, 128, 256), bf16),
            pltpu.VMEM((1024, 128), f32),
            pltpu.VMEM((1024, 128), f32),
            pltpu.VMEM((1024, 128), f32),
            pltpu.VMEM((2, 1024, 1), f32),
            pltpu.VMEM((256, width), f32),
            pltpu.VMEM((width, LANE_SHARE), f32),
            pltpu.SemaphoreType.DMA((3, 4)),
            pltpu.SemaphoreType.DMA((3, 4)),
            pltpu.SemaphoreType.DMA((3, 6)),
            pltpu.SemaphoreType.DMA((3, 6)),
            pltpu.SemaphoreType.DMA((8,)),
            pltpu.SemaphoreType.DMA((8,)),
            pltpu.SemaphoreType.DMA((4, 8)),
            pltpu.SemaphoreType.DMA((4, 8)),
            pltpu.SemaphoreType.DMA((2,)),
            pltpu.SemaphoreType.DMA((2,)),
            pltpu.SemaphoreType.DMA((8,)),
            pltpu.SemaphoreType.DMA((2,)),
        ],
        compiler_params=pltpu.CompilerParams(
            collective_id=2, has_side_effects=True, vmem_limit_bytes=VMEM_LIMIT
        ),
        name="backward",
    )(*values)


SUM_CUTS = tuple((slice(None), pl.ds(k * 384, 384)) for k in range(3))


def expert_weights_kernel(
    x_hbm, plain_hbm, pair_raw, routes, weights, gate_hbm, up_hbm, down_hbm, rows_hbm, pair_hbm, hidden_hbm, gg_hbm, ug_hbm,
    out_part, residual, grads,
    gate_own, up_own, down_own, gate_other, up_other, down_other, mixed, shares,
    x, c, plain, rows, pair_grad, column, gate, up, down,
    both_rows, both_pair, both_hidden, both_gate, gate_buf, up_buf, down_buf,
    g0, g1, g2, g3, g4, g5, got1, got2, sum_send, sum_recv,
    s0, s1, s2, sheld0, sgot1, sheld1, sgot2, ssend, srecv,
    core_got, core_sum, core_qkv, all_got, side_sum, side_got,
    grad_send, grad_recv, core_send, core_recv, part_send, part_recv,
    sem_x, sem_w, sem_own, sem_out, own_sem,
):
    me, core = my_place(), my_core()
    first = me * 4
    side = lax.axis_index("group") // 2
    other = 1 - side
    width = x.shape[-1]
    ff = gate.shape[-1]
    half = pl.ds(pl.multiple_of(core * 64, 64), 64)
    other_half = pl.ds(pl.multiple_of((1 - core) * 64, 64), 64)
    meet(peers() + [sibling(), mirror()])
    core_copy = remote(grads.at[:, other_half], core_got, core_send.at[0], core_recv.at[0], sibling())
    core_copy.start()
    total = CubeSum(
        out_part, x, ROW_CUTS, (g0, g1, g2, g3, g4, g5, c.at[pl.ds(0, 2)], got1, c.at[2], got2, sum_send, sum_recv)
    )
    total.start()
    loads = [
        pltpu.make_async_copy(plain_hbm, plain, sem_x.at[1]),
        pltpu.make_async_copy(pair_raw, pair_grad, sem_x.at[2]),
        pltpu.make_async_copy(x_hbm, x, sem_x.at[0]),
    ]
    for copy in loads:
        copy.start()

    def fetch(e, slot):
        return [
            pltpu.make_async_copy(gate_hbm.at[e], gate.at[slot], sem_w.at[slot, 0]),
            pltpu.make_async_copy(up_hbm.at[e], up.at[slot], sem_w.at[slot, 1]),
            pltpu.make_async_copy(down_hbm.at[e], down.at[slot], sem_w.at[slot, 2]),
        ]

    for copy in fetch(0, 0):
        copy.start()
    loads[0].wait()

    def weigh(block, carry):
        slot_weights(routes, weights, plain, column, first, block)
        return carry

    lax.fori_loop(0, 4, weigh, 0)
    core_copy.wait()
    summed = width + LANE_SHARE
    for j in range(8):
        both = (grads[j, half].astype(f32) + core_got[j].astype(f32)).astype(bf16)
        core_sum[j // 4, j // 2 % 2, j % 2] = both[:, :summed]
        core_qkv[j] = both[:, summed:]
    spread = Spread(lambda j: core_qkv.at[j], lambda i: all_got.at[i], grad_send, grad_recv)
    spread.start()
    spread_own = pltpu.make_async_copy(core_qkv.at[me], all_got.at[me], own_sem)
    spread_own.start()
    small_total = CubeSum(
        core_sum, core_sum, SUM_CUTS, (s0, s1, s2, sheld0, sgot1, sheld1, sgot2, ssend, srecv)
    )
    small_total.start()
    for copy in loads[1:]:
        copy.wait()

    def take(block, carry):
        rows[block] = dot(plain[block], place_rows(x, block)).astype(bf16)
        pair_grad[block] = (pair_grad[block].astype(f32) * column[block]).astype(bf16)
        return carry

    lax.fori_loop(0, 4, take, 0)
    load_part = pltpu.make_async_copy(out_part, x, sem_x.at[0])
    load_part.start()
    side_copy = remote(side_sum, side_got, core_send.at[1], core_recv.at[1], mirror())
    last_copy = remote(shares.at[half], shares.at[half], core_send.at[2], core_recv.at[2], sibling())

    def part_copies(e):
        return [
            pltpu.make_async_copy(gate_buf, gate_own.at[e], sem_out.at[0]),
            pltpu.make_async_copy(up_buf, up_own.at[e], sem_out.at[1]),
            pltpu.make_async_copy(down_buf, down_own.at[e], sem_out.at[2]),
            remote(gate_buf, gate_other.at[e], part_send.at[0], part_recv.at[e, 0], sibling()),
            remote(up_buf, up_other.at[e], part_send.at[1], part_recv.at[e, 1], sibling()),
            remote(down_buf, down_other.at[e], part_send.at[2], part_recv.at[e, 2], sibling()),
        ]

    def sent(e):
        made = part_copies(e)
        for copy in made[:3]:
            copy.wait()
        for copy in made[3:]:
            copy.wait_send()

    def expert(e, carry):
        slot = lax.rem(e, 2)
        mine = expert_rows(e)
        own = [
            pltpu.make_async_copy(rows_hbm.at[:, mine], both_rows.at[side], sem_own.at[0]),
            pltpu.make_async_copy(pair_hbm.at[:, mine], both_pair.at[side], sem_own.at[1]),
            pltpu.make_async_copy(hidden_hbm.at[e], both_hidden.at[side], sem_own.at[2]),
            pltpu.make_async_copy(gg_hbm.at[e], both_gate.at[side, :, pl.ds(0, ff)], sem_own.at[3]),
            pltpu.make_async_copy(ug_hbm.at[e], both_gate.at[side, :, pl.ds(ff, ff)], sem_own.at[4]),
        ]
        for copy in own:
            copy.start()
        for copy in fetch(e, slot):
            copy.wait()

        @pl.when(e < 3)
        def _():
            for copy in fetch(e + 1, 1 - slot):
                copy.start()

        rows_e = rows[:, mine].reshape(TAKEN, width)
        pair_e = pair_grad[:, mine].reshape(TAKEN, width)
        hidden, gate_grad, up_grad = expert_inner(rows_e, pair_e, gate[slot], up[slot], down[slot])
        both_rows[other] = rows_e.reshape(4, SLOT, width)
        both_pair[other] = pair_e.reshape(4, SLOT, width)
        both_hidden[other] = hidden
        both_gate[other, :, 0:ff] = gate_grad
        both_gate[other, :, ff : 2 * ff] = up_grad

        for copy in own:
            copy.wait()

        @pl.when(e >= 1)
        def _():
            sent(e - 1)

        sums = dot_first(both_rows[...].reshape(2 * TAKEN, width), both_gate[...].reshape(2 * TAKEN, 2 * ff))
        gate_buf[...] = sums[:, :ff].astype(bf16)
        up_buf[...] = sums[:, ff:].astype(bf16)
        down_buf[...] = dot_first(
            both_hidden[...].reshape(2 * TAKEN, ff), both_pair[...].reshape(2 * TAKEN, width)
        ).astype(bf16)
        for copy in part_copies(e):
            copy.start()

        @pl.when(e == 0)
        def _():
            small_total.middle()
            load_part.wait()
            total.middle()

        @pl.when(e == 1)
        def _():
            small_total.last()
            total.last()

            def keep_sum(cut, value):
                side_sum[cut] = value.astype(bf16)

            small_total.finish(keep_sum)
            spread.wait()
            spread_own.wait()
            for i in range(8):
                side_sum[:, summed + i * 256 : summed + (i + 1) * 256] = all_got[i]
            side_copy.start()

        @pl.when(e == 2)
        def _():
            def store(cut, value):
                mixed[cut] = (residual[cut] + value).astype(bf16)

            total.finish(store)

        return carry

    lax.fori_loop(0, 4, expert, 0)
    side_copy.wait()
    shares[half] = (side_sum[...].astype(f32) + side_got[...].astype(f32)).astype(bf16)
    last_copy.start()
    total.sent()
    small_total.sent()
    last_copy.wait()
    sent(3)
    for e in range(4):
        for copy in part_copies(e)[3:]:
            copy.wait_recv()


def expert_weights(x, plain, pair, routes, weights, gate_w, up_w, down_w, kept, out_part, residual, grads):
    width = gate_w.shape[1]
    ff = gate_w.shape[-1]
    wide = grads.shape[-1]
    out = [jax.ShapeDtypeStruct(w.shape, bf16) for w in (gate_w, up_w, down_w)]
    sums = cube_sum_scratch(256, width, ROW_CUTS)
    return pl.pallas_call(
        expert_weights_kernel,
        out_shape=(
            *out,
            *out,
            jax.ShapeDtypeStruct((256, width), bf16),
            jax.ShapeDtypeStruct((128, width + LANE_SHARE + 2048), bf16),
        ),
        in_specs=[anywhere()] * 3 + [vmem()] * 2 + [anywhere()] * 9 + [vmem()] * 2,
        out_specs=(anywhere(),) * 6 + (vmem(),) * 2,
        scratch_shapes=[
            pltpu.VMEM((2, 2, 2, 256, width), bf16),
            pltpu.VMEM((3, 2, 256, width), bf16),
            pltpu.VMEM((4, TAKEN, SPAN), bf16),
            pltpu.VMEM((4, TAKEN, width), bf16),
            pltpu.VMEM((4, TAKEN, width), bf16),
            pltpu.VMEM((4, TAKEN, 1), f32),
            pltpu.VMEM((2, width, ff), bf16),
            pltpu.VMEM((2, width, ff), bf16),
            pltpu.VMEM((2, ff, width), bf16),
            pltpu.VMEM((2, 4, SLOT, width), bf16),
            pltpu.VMEM((2, 4, SLOT, width), bf16),
            pltpu.VMEM((2, TAKEN, ff), bf16),
            pltpu.VMEM((2, TAKEN, 2 * ff), bf16),
            pltpu.VMEM((width, ff), bf16),
            pltpu.VMEM((width, ff), bf16),
            pltpu.VMEM((ff, width), bf16),
            *sums[:6],
            sums[7],
            sums[9],
            *sums[10:],
            *cube_sum_scratch(64, width + LANE_SHARE, SUM_CUTS),
            pltpu.VMEM((8, 64, wide), bf16),
            pltpu.VMEM((2, 2, 2, 64, width + LANE_SHARE), bf16),
            pltpu.VMEM((8, 64, 256), bf16),
            pltpu.VMEM((8, 64, 256), bf16),
            pltpu.VMEM((64, width + LANE_SHARE + 2048), bf16),
            pltpu.VMEM((64, width + LANE_SHARE + 2048), bf16),
            pltpu.SemaphoreType.DMA((8,)),
            pltpu.SemaphoreType.DMA((8,)),
            pltpu.SemaphoreType.DMA((3,)),
            pltpu.SemaphoreType.DMA((3,)),
            pltpu.SemaphoreType.DMA((3,)),
            pltpu.SemaphoreType.DMA((4, 3)),
            pltpu.SemaphoreType.DMA((3,)),
            pltpu.SemaphoreType.DMA((2, 3)),
            pltpu.SemaphoreType.DMA((5,)),
            pltpu.SemaphoreType.DMA((3,)),
            pltpu.SemaphoreType.DMA,
        ],
        compiler_params=pltpu.CompilerParams(
            collective_id=3, has_side_effects=True, vmem_limit_bytes=VMEM_LIMIT
        ),
        name="expert_weights",
    )(x, plain, pair, routes, weights, gate_w, up_w, down_w, *kept, out_part, residual, grads)


def finish_kernel(
    gate_own, up_own, down_own, gate_other, up_other, down_other, shares, mixed, token_grad,
    gate_out, up_out, down_out, query_out, key_out, value_out, wo_out, router_out, moe_gain_out, attn_gain_out,
    mixed_out, token_out,
):
    for own, other, out in ((gate_own, gate_other, gate_out), (up_own, up_other, up_out), (down_own, down_other, down_out)):
        out[...] = own[...].astype(f32) + other[...].astype(f32)
    mixed_out[...] = mixed[...]
    token_out[...] = token_grad[...]

    @pl.when(pl.program_id(0) == 0)
    def _():
        width = wo_out.shape[-1]
        wo_out[...] = shares[:, 0:width].astype(f32)
        small = shares[:, width : width + LANE_SHARE].astype(f32).T
        router_out[...] = small[0:32]
        moe_gain_out[...] = small[32:33]
        attn_gain_out[...] = small[33:34]
        low = lanes((128, 128)) < 64
        base = width + LANE_SHARE
        for j in range(8):
            query_out[:, j * 128 : (j + 1) * 128] = shares[:, base + j * 256 : base + j * 256 + 128].astype(f32)
        for j in range(4):
            left = shares[:, base + j * 512 + 128 : base + j * 512 + 256].astype(f32)
            right = shares[:, base + j * 512 + 384 : base + j * 512 + 512].astype(f32)
            where = slice(j * 128, (j + 1) * 128)
            key_out[:, where] = jnp.where(low, left, pltpu.roll(right, 64, 1))
            value_out[:, where] = jnp.where(low, pltpu.roll(left, 64, 1), right)


def finish(parts, shares, mixed, token_grad):
    width = parts[0].shape[1]
    steps = parts[0].shape[0]

    def block(shape):
        return pl.BlockSpec((1,) + shape[1:], lambda e: (e, 0, 0))

    def rows(shape):
        return pl.BlockSpec((shape[0] // steps,) + shape[1:], lambda e: (e, 0))

    def whole(shape):
        return pl.BlockSpec(shape, lambda e: (0,) * len(shape))

    small = [(128, 1024), (128, 512), (128, 512), (128, width), (32, LANE_SHARE), (1, LANE_SHARE), (1, LANE_SHARE)]
    return pl.pallas_call(
        finish_kernel,
        grid=(steps,),
        out_shape=tuple(jax.ShapeDtypeStruct(p.shape, f32) for p in parts[:3])
        + tuple(jax.ShapeDtypeStruct(shape, f32) for shape in small)
        + (jax.ShapeDtypeStruct(mixed.shape, bf16), jax.ShapeDtypeStruct(token_grad.shape, f32)),
        in_specs=[block(p.shape) for p in parts] + [whole(shares.shape), rows(mixed.shape), rows(token_grad.shape)],
        out_specs=tuple(block(p.shape) for p in parts[:3])
        + tuple(whole(shape) for shape in small)
        + (rows(mixed.shape), rows(token_grad.shape)),
        compiler_params=pltpu.CompilerParams(vmem_limit_bytes=VMEM_LIMIT),
        name="finish",
    )(*parts, shares, mixed, token_grad)


def fast_on_device(
    tokens, segments, routes, cotangent, attn_gain, moe_gain, query_weight, key_projection_matrix,
    value_projection_matrix, out_weight, router_weight, gate_weight, up_weight, down_weight,
):
    width = tokens.shape[-1]
    tok = tokens.reshape(256, width)
    cot = cotangent.reshape(256, width)
    my_routes = routes.reshape(256, TOP).T
    (
        attn_in, q, kv, amix, residual, moe_in, weights, wo_all, gains_all, router_all, routes_all,
        cot_all, cot_mirror, routes_mirror, wkv,
    ) = forward(
        tok, cot, query_weight, key_projection_matrix, value_projection_matrix, out_weight,
        attn_gain.reshape(1, 128), moe_gain.reshape(1, 128), router_weight.T, my_routes, segments,
    )
    out_part, in_sum, p_all, *kept, plain_mirror, pair_mirror, moe_mirror, weights_mirror = experts(
        moe_in, weights, cot_mirror, cot_all, routes_all, routes_mirror, gate_weight, up_weight, down_weight
    )
    token_grad, grads, moe_mirror_all = backward(
        cot, residual, in_sum, p_all, my_routes, weights, router_all, moe_in, gains_all, wo_all, amix, attn_in,
        q, kv, segments, tok, query_weight, wkv, moe_mirror,
    )
    *parts, mixed, shares = expert_weights(
        moe_mirror_all, plain_mirror, pair_mirror, routes_mirror, weights_mirror, gate_weight, up_weight, down_weight,
        kept, out_part, residual, grads,
    )
    (
        gate_grad, up_grad, down_grad, query_grad, key_grad, value_grad, wo_grad, router_grad, moe_gain_grad,
        attn_gain_grad, mixed, token_grad,
    ) = finish(parts, shares, mixed, token_grad)
    return (
        mixed.reshape(tokens.shape), token_grad.reshape(tokens.shape), attn_gain_grad.reshape(128),
        moe_gain_grad.reshape(128), query_grad, key_grad, value_grad, wo_grad, router_grad.T,
        gate_grad, up_grad, down_grad,
    )


def fits(mesh):
    return dict(mesh.shape) == {"group": 4, "blk": 4, "head": 2}


def solution(mesh):
    placed = (
        P("group", ("blk", "head"), None),
        P("group", None),
        P("group", ("blk", "head"), None),
        P("group", ("blk", "head"), None),
        P(("blk", "head")),
        P(("blk", "head")),
        P(("blk", "head"), None),
        P(("blk", "head"), None),
        P(("blk", "head"), None),
        P(("blk", "head"), None),
        P(("blk", "head"), None),
        P(("blk", "head"), None, None),
        P(("blk", "head"), None, None),
        P(("blk", "head"), None, None),
    )
    return jax.shard_map(
        fast_on_device if fits(mesh) else on_device,
        mesh=mesh,
        in_specs=placed,
        out_specs=(
            P("group", ("blk", "head"), None),
            P("group", ("blk", "head"), None),
            P(("blk", "head")),
            P(("blk", "head")),
            P(("blk", "head"), None),
            P(("blk", "head"), None),
            P(("blk", "head"), None),
            P(("blk", "head"), None),
            P(("blk", "head"), None),
            P(("blk", "head"), None, None),
            P(("blk", "head"), None, None),
            P(("blk", "head"), None, None),
        ),
        check_vma=False,
    )
```

```python
import functools

import jax
import jax.numpy as jnp
import numpy as np
from jax import lax
from jax.experimental import pallas as pl
from jax.experimental.pallas import tpu as pltpu
from jax.sharding import PartitionSpec as P

QUERY_HEADS = 16
KEY_VALUE_HEADS = 8
HEAD_SIZE = 64
TOP = 8
CAPH = 36


epsilon = 1e-05
rope_base = 10000.0
masked_out = -1e30
key_block = 512


def rms_norm(values, gain_vec):
    return values * lax.rsqrt(jnp.mean(values * values, -1, keepdims=True) + epsilon) * gain_vec


def rotary_embedding(field_vals, places, turn_sign):
    half_dim = field_vals.shape[-1] // 2
    frequency = rope_base ** (-jnp.arange(half_dim, dtype=jnp.float32) * 2.0 / field_vals.shape[-1])
    angles = places.astype(jnp.float32)[:, None] * frequency[None, :]
    cosine = jnp.cos(angles)[:, None, :]
    sine_vals = turn_sign * jnp.sin(angles)[:, None, :]
    first_half = field_vals[..., :half_dim]
    second = field_vals[..., half_dim:]
    return jnp.concatenate(
        [first_half * cosine - second * sine_vals, second * cosine + first_half * sine_vals], -1
    )


def add_rows(running, addend, row_start):
    current = lax.dynamic_slice_in_dim(running, row_start, addend.shape[1], 1)
    return lax.dynamic_update_slice_in_dim(running, current + addend, row_start, 1)


def on_device(
    tokens,
    segments,
    routes,
    cotangent,
    attn_gain,
    moe_gain,
    query_weight,
    key_projection_matrix,
    value_projection_matrix,
    out_weight,
    router_weight,
    gate_weight,
    up_weight,
    down_weight,
):
    head_groups, number_of_rows, width_dim = tokens.shape
    query_per_key_head = QUERY_HEADS // KEY_VALUE_HEADS
    shared_head_count = lax.axis_size("head")
    query_rows = number_of_rows * shared_head_count
    grouped_keys = KEY_VALUE_HEADS // shared_head_count
    scale_val = HEAD_SIZE ** (-0.5)
    number_of_tokens = head_groups * number_of_rows
    seq_length = lax.axis_size("blk") * query_rows
    cycle_index = lax.axis_index("blk")
    local_placement = (
        cycle_index * shared_head_count + lax.axis_index("head")
    ) * number_of_rows + jnp.arange(number_of_rows, dtype=jnp.int32)
    own_start = cycle_index * query_rows
    query_place = own_start + jnp.arange(query_rows, dtype=jnp.int32)
    query_doc = lax.dynamic_slice_in_dim(segments, own_start, query_rows, 1)
    query_full, key_full, value_full, out_full, router_full, gain_attn, gain_moe = (
        lax.all_gather(query_weight, ("blk", "head"), axis=0, tiled=True),
        lax.all_gather(key_projection_matrix, ("blk", "head"), axis=0, tiled=True),
        lax.all_gather(value_projection_matrix, ("blk", "head"), axis=0, tiled=True),
        lax.all_gather(out_weight, ("blk", "head"), axis=0, tiled=True),
        lax.all_gather(router_weight, ("blk", "head"), axis=0, tiled=True),
        lax.all_gather(attn_gain, ("blk", "head"), axis=0, tiled=True),
        lax.all_gather(moe_gain, ("blk", "head"), axis=0, tiled=True),
    )
    flat_rows = tokens.reshape(number_of_tokens, width_dim).astype(jnp.float32)
    attn_normed, attn_pull = jax.vjp(rms_norm, flat_rows, gain_attn.astype(jnp.float32))
    attn_in = attn_normed.astype(jnp.bfloat16)
    query_pre = jnp.dot(attn_in, query_full, preferred_element_type=jnp.float32)
    key_before_rotary = jnp.dot(attn_in, key_full, preferred_element_type=jnp.float32)
    value_low = (
        jnp.dot(attn_in, value_full, preferred_element_type=jnp.float32)
        .astype(jnp.bfloat16)
        .reshape(head_groups, number_of_rows, KEY_VALUE_HEADS * HEAD_SIZE)
    )
    query_low = (
        rotary_embedding(
            query_pre.reshape(head_groups, number_of_rows, QUERY_HEADS, HEAD_SIZE),
            local_placement,
            1.0,
        )
        .astype(jnp.bfloat16)
        .reshape(head_groups, number_of_rows, QUERY_HEADS * HEAD_SIZE)
    )
    key_low = (
        rotary_embedding(
            key_before_rotary.reshape(head_groups, number_of_rows, KEY_VALUE_HEADS, HEAD_SIZE),
            local_placement,
            1.0,
        )
        .astype(jnp.bfloat16)
        .reshape(head_groups, number_of_rows, KEY_VALUE_HEADS * HEAD_SIZE)
    )
    query_split, key_split, value_split = (
        lax.all_to_all(query_low, "head", split_axis=2, concat_axis=1, tiled=True),
        lax.all_to_all(key_low, "head", split_axis=2, concat_axis=1, tiled=True),
        lax.all_to_all(value_low, "head", split_axis=2, concat_axis=1, tiled=True),
    )
    query_vectors = query_split.reshape(
        head_groups, query_rows, grouped_keys, query_per_key_head, HEAD_SIZE
    )

    def key_view(source, offset, sub_rows):
        return lax.dynamic_slice_in_dim(source, offset, sub_rows, 1).reshape(
            head_groups, sub_rows, grouped_keys, HEAD_SIZE
        )

    def scored_at(query_part, key_row_block, q_place, q_doc, key_start, sub_rows):
        raw_scores = (
            jnp.einsum(
                "bqgrd,bkgd->bqgrk", query_part, key_row_block, preferred_element_type=jnp.float32
            )
            * scale_val
        )
        key_place = key_start + jnp.arange(sub_rows, dtype=jnp.int32)
        key_doc = lax.dynamic_slice_in_dim(segments, key_start, sub_rows, 1)
        allowed = (q_place[None, :, None] >= key_place[None, None, :]) & (
            q_doc[:, :, None] == key_doc[:, None, :]
        )
        return (raw_scores, allowed[:, :, None, None, :])

    def scored(key_row_block, key_start, sub_rows):
        return scored_at(query_vectors, key_row_block, query_place, query_doc, key_start, sub_rows)

    stats_shape = (head_groups, query_rows, grouped_keys, query_per_key_head)
    init_state = (
        jnp.full(stats_shape, masked_out, jnp.float32),
        jnp.zeros(stats_shape, jnp.float32),
        jnp.zeros(stats_shape + (HEAD_SIZE,), jnp.float32),
    )
    key_all, value_all = (
        lax.all_gather(key_split, "blk", axis=1, tiled=True),
        lax.all_gather(value_split, "blk", axis=1, tiled=True),
    )
    fold_state = init_state
    total_rows = key_all.shape[1]
    sub_rows = key_block

    def forward_one_block(block_state, block_index):
        offset = block_index * sub_rows
        key_row_block = key_view(key_all, offset, sub_rows)
        value_row_block = key_view(value_all, offset, sub_rows)
        raw_scores, allowed = scored(key_row_block, 0 + offset, sub_rows)
        running_max, running_sum, running_acc = block_state
        masked = jnp.where(allowed, raw_scores, masked_out)
        new_max = jnp.maximum(running_max, jnp.max(masked, -1))
        shrink = jnp.exp(running_max - new_max)
        weights_soft = jnp.where(allowed, jnp.exp(masked - new_max[..., None]), 0.0)
        new_sum = running_sum * shrink + jnp.sum(weights_soft, -1)
        new_acc = running_acc * shrink[..., None] + jnp.einsum(
            "bqgrk,bkgd->bqgrd",
            weights_soft.astype(jnp.bfloat16),
            value_row_block,
            preferred_element_type=jnp.float32,
        )
        return ((new_max, new_sum, new_acc), None)

    fold_state, unused = lax.scan(
        forward_one_block, fold_state, jnp.arange(total_rows // sub_rows, dtype=jnp.int32)
    )
    running_max, running_sum, running_acc = fold_state
    mix_heads = running_acc / running_sum[..., None]
    log_total = running_max + jnp.log(running_sum)
    mix_low = mix_heads.astype(jnp.bfloat16).reshape(
        head_groups, query_rows, grouped_keys * query_per_key_head * HEAD_SIZE
    )
    mix_tokens = lax.all_to_all(mix_low, "head", split_axis=1, concat_axis=2, tiled=True)
    attn_mix = mix_tokens.reshape(number_of_tokens, QUERY_HEADS * HEAD_SIZE)
    residual = flat_rows + jnp.dot(attn_mix, out_full, preferred_element_type=jnp.float32)
    moe_normed, moe_pull = jax.vjp(rms_norm, residual, gain_moe.astype(jnp.float32))
    moe_in = moe_normed.astype(jnp.bfloat16)
    logits = jnp.dot(moe_in, router_full, preferred_element_type=jnp.float32)
    route_flat = routes.reshape(number_of_tokens, TOP)
    experts_all = router_full.shape[1]
    choose = route_flat[:, :, None] == jnp.arange(experts_all, dtype=jnp.int32)[None, None, :]
    choose_float = choose.astype(jnp.float32)
    picked_logits = jnp.einsum("nke,ne->nk", choose_float, logits)
    route_weights = jax.nn.softmax(picked_logits, axis=-1)
    choose_whole = choose.astype(jnp.int32).reshape(head_groups, number_of_rows * TOP, experts_all)
    slot_rank = jnp.sum(jnp.cumsum(choose_whole, 1) * choose_whole, -1) - 1
    slot_index = (slot_rank + jnp.arange(head_groups, dtype=jnp.int32)[:, None] * CAPH).reshape(-1)
    targets = route_flat.reshape(-1)
    lane_count = head_groups * CAPH
    outgoing = (
        jnp.zeros((experts_all, lane_count, width_dim), jnp.bfloat16)
        .at[targets, slot_index]
        .set(jnp.repeat(moe_in, TOP, axis=0))
    )
    arrived = lax.all_to_all(outgoing, ("blk", "head"), split_axis=0, concat_axis=1, tiled=True)
    gate_val = jnp.einsum("end,edf->enf", arrived, gate_weight, preferred_element_type=jnp.float32)
    up_val = jnp.einsum("end,edf->enf", arrived, up_weight, preferred_element_type=jnp.float32)
    hidden_low = (jax.nn.silu(gate_val) * up_val).astype(jnp.bfloat16)
    expert_out = jnp.einsum(
        "enf,efd->end", hidden_low, down_weight, preferred_element_type=jnp.float32
    ).astype(jnp.bfloat16)
    returned = lax.all_to_all(expert_out, ("blk", "head"), split_axis=1, concat_axis=0, tiled=True)
    picked_rows = returned[targets, slot_index].reshape(number_of_tokens, TOP, width_dim)
    moe_out = jnp.einsum(
        "nk,nkd->nd", route_weights, picked_rows, preferred_element_type=jnp.float32
    )
    mixed = (
        (residual + moe_out).astype(jnp.bfloat16).reshape(head_groups, number_of_rows, width_dim)
    )
    grad_full = cotangent.reshape(number_of_tokens, width_dim).astype(jnp.float32)
    weight_grad = jnp.einsum(
        "nkd,nd->nk", picked_rows, grad_full, preferred_element_type=jnp.float32
    )
    pair_grad = (
        (route_weights[:, :, None] * grad_full[:, None, :])
        .astype(jnp.bfloat16)
        .reshape(number_of_tokens * TOP, width_dim)
    )
    grad_outgoing = jnp.zeros_like(outgoing).at[targets, slot_index].set(pair_grad)
    grad_arrived = lax.all_to_all(
        grad_outgoing, ("blk", "head"), split_axis=0, concat_axis=1, tiled=True
    )
    grad_hidden = jnp.einsum(
        "end,efd->enf", grad_arrived, down_weight, preferred_element_type=jnp.float32
    )
    sigmoid_val = jax.nn.sigmoid(gate_val)
    grad_gate = (
        grad_hidden * up_val * sigmoid_val * (1.0 + gate_val * (1.0 - sigmoid_val))
    ).astype(jnp.bfloat16)
    grad_up = (grad_hidden * gate_val * sigmoid_val).astype(jnp.bfloat16)
    down_weight_grad = jnp.einsum(
        "enf,end->efd", hidden_low, grad_arrived, preferred_element_type=jnp.float32
    )
    gate_weight_grad = jnp.einsum(
        "end,enf->edf", arrived, grad_gate, preferred_element_type=jnp.float32
    )
    up_weight_grad = jnp.einsum(
        "end,enf->edf", arrived, grad_up, preferred_element_type=jnp.float32
    )
    pair_back = (
        jnp.einsum("enf,edf->end", grad_gate, gate_weight, preferred_element_type=jnp.float32)
        + jnp.einsum("enf,edf->end", grad_up, up_weight, preferred_element_type=jnp.float32)
    ).astype(jnp.bfloat16)
    grad_returned = lax.all_to_all(
        pair_back, ("blk", "head"), split_axis=1, concat_axis=0, tiled=True
    )
    moe_in_grad = jnp.sum(
        grad_returned[targets, slot_index].reshape(number_of_tokens, TOP, width_dim),
        axis=1,
        dtype=jnp.float32,
    )
    mean_term = jnp.sum(route_weights * weight_grad, -1, keepdims=True)
    logit_grad = jnp.einsum("nk,nke->ne", route_weights * (weight_grad - mean_term), choose_float)
    router_grad = jnp.dot(moe_in.T, logit_grad, preferred_element_type=jnp.float32)
    moe_in_grad = moe_in_grad + jnp.dot(
        logit_grad, router_full.T, preferred_element_type=jnp.float32
    )
    residual_part, moe_gain_grad = moe_pull(moe_in_grad)
    residual_grad = grad_full + residual_part
    out_grad_low = residual_grad.astype(jnp.bfloat16)
    out_weight_grad = jnp.dot(attn_mix.T, out_grad_low, preferred_element_type=jnp.float32)
    mix_grad = (
        jnp.dot(out_grad_low, out_full.T, preferred_element_type=jnp.float32)
        .astype(jnp.bfloat16)
        .reshape(head_groups, number_of_rows, QUERY_HEADS * HEAD_SIZE)
    )
    mix_grad_heads = lax.all_to_all(
        mix_grad, "head", split_axis=2, concat_axis=1, tiled=True
    ).reshape(head_groups, query_rows, grouped_keys, query_per_key_head, HEAD_SIZE)
    delta_term = jnp.sum(mix_grad_heads.astype(jnp.float32) * mix_heads, -1)
    query_zero = jnp.zeros(stats_shape + (HEAD_SIZE,), jnp.float32)
    back_init = (
        query_zero,
        jnp.zeros((head_groups, seq_length, grouped_keys, HEAD_SIZE), jnp.float32),
        jnp.zeros((head_groups, seq_length, grouped_keys, HEAD_SIZE), jnp.float32),
    )
    fold_state = back_init
    total_rows = key_all.shape[1]

    def backward_one_block(block_state, block_index):
        offset = block_index * key_block
        key_start = 0 + offset
        key_row_block = key_view(key_all, offset, key_block)
        value_row_block = key_view(value_all, offset, key_block)
        raw_scores, allowed = scored(key_row_block, key_start, key_block)
        masked = jnp.where(allowed, raw_scores, masked_out)
        probability = jnp.where(allowed, jnp.exp(masked - log_total[..., None]), 0.0)
        prob_grad = jnp.einsum(
            "bqgrd,bkgd->bqgrk", mix_grad_heads, value_row_block, preferred_element_type=jnp.float32
        )
        score_grad = (probability * (prob_grad - delta_term[..., None]) * scale_val).astype(
            jnp.bfloat16
        )
        grad_query = block_state[0] + jnp.einsum(
            "bqgrk,bkgd->bqgrd", score_grad, key_row_block, preferred_element_type=jnp.float32
        )
        value_part_grad = jnp.einsum(
            "bqgrk,bqgrd->bkgd",
            probability.astype(jnp.bfloat16),
            mix_grad_heads,
            preferred_element_type=jnp.float32,
        )
        key_part_grad = jnp.einsum(
            "bqgrk,bqgrd->bkgd", score_grad, query_vectors, preferred_element_type=jnp.float32
        )
        grad_keys = add_rows(block_state[1], key_part_grad, key_start)
        grad_values = add_rows(block_state[2], value_part_grad, key_start)
        return ((grad_query, grad_keys, grad_values), None)

    fold_state, unused = lax.scan(
        backward_one_block, fold_state, jnp.arange(total_rows // key_block, dtype=jnp.int32)
    )
    grad_query, grad_keys, grad_values = fold_state
    key_own, value_own = (
        lax.psum_scatter(
            grad_keys.reshape(head_groups, seq_length, grouped_keys * HEAD_SIZE).astype(
                jnp.bfloat16
            ),
            "blk",
            scatter_dimension=1,
            tiled=True,
        ).astype(jnp.float32),
        lax.psum_scatter(
            grad_values.reshape(head_groups, seq_length, grouped_keys * HEAD_SIZE).astype(
                jnp.bfloat16
            ),
            "blk",
            scatter_dimension=1,
            tiled=True,
        ).astype(jnp.float32),
    )
    query_grad_low = (
        rotary_embedding(
            grad_query.reshape(
                head_groups, query_rows, grouped_keys * query_per_key_head, HEAD_SIZE
            ),
            query_place,
            -1.0,
        )
        .astype(jnp.bfloat16)
        .reshape(head_groups, query_rows, grouped_keys * query_per_key_head * HEAD_SIZE)
    )
    key_grad_low = (
        rotary_embedding(
            key_own.reshape(head_groups, query_rows, grouped_keys, HEAD_SIZE), query_place, -1.0
        )
        .astype(jnp.bfloat16)
        .reshape(head_groups, query_rows, grouped_keys * HEAD_SIZE)
    )
    value_grad_low = value_own.astype(jnp.bfloat16)
    query_back, key_pullback, value_pullback = (
        lax.all_to_all(query_grad_low, "head", split_axis=1, concat_axis=2, tiled=True),
        lax.all_to_all(key_grad_low, "head", split_axis=1, concat_axis=2, tiled=True),
        lax.all_to_all(value_grad_low, "head", split_axis=1, concat_axis=2, tiled=True),
    )
    query_flat = query_back.reshape(number_of_tokens, QUERY_HEADS * HEAD_SIZE)
    flattened_keys = key_pullback.reshape(number_of_tokens, KEY_VALUE_HEADS * HEAD_SIZE)
    flattened_values = value_pullback.reshape(number_of_tokens, KEY_VALUE_HEADS * HEAD_SIZE)
    query_weight_grad = jnp.dot(attn_in.T, query_flat, preferred_element_type=jnp.float32)
    key_weight_grad = jnp.dot(attn_in.T, flattened_keys, preferred_element_type=jnp.float32)
    value_weight_grad = jnp.dot(attn_in.T, flattened_values, preferred_element_type=jnp.float32)
    attn_in_grad = (
        jnp.dot(query_flat, query_full.T, preferred_element_type=jnp.float32)
        + jnp.dot(flattened_keys, key_full.T, preferred_element_type=jnp.float32)
        + jnp.dot(flattened_values, value_full.T, preferred_element_type=jnp.float32)
    )
    input_part, attn_gain_grad = attn_pull(attn_in_grad)
    token_grad = (residual_grad + input_part).reshape(head_groups, number_of_rows, width_dim)
    (
        query_shard,
        key_shard,
        value_shard,
        out_shard,
        router_shard,
        attn_gain_shard,
        moe_gain_shard,
    ) = (
        lax.psum_scatter(
            query_weight_grad.astype(jnp.bfloat16), ("blk", "head"), scatter_dimension=0, tiled=True
        ).astype(jnp.float32),
        lax.psum_scatter(
            key_weight_grad.astype(jnp.bfloat16), ("blk", "head"), scatter_dimension=0, tiled=True
        ).astype(jnp.float32),
        lax.psum_scatter(
            value_weight_grad.astype(jnp.bfloat16), ("blk", "head"), scatter_dimension=0, tiled=True
        ).astype(jnp.float32),
        lax.psum_scatter(
            out_weight_grad.astype(jnp.bfloat16), ("blk", "head"), scatter_dimension=0, tiled=True
        ).astype(jnp.float32),
        lax.psum_scatter(
            router_grad.astype(jnp.bfloat16), ("blk", "head"), scatter_dimension=0, tiled=True
        ).astype(jnp.float32),
        lax.psum_scatter(
            attn_gain_grad.astype(jnp.bfloat16), ("blk", "head"), scatter_dimension=0, tiled=True
        ).astype(jnp.float32),
        lax.psum_scatter(
            moe_gain_grad.astype(jnp.bfloat16), ("blk", "head"), scatter_dimension=0, tiled=True
        ).astype(jnp.float32),
    )
    summed = (
        lax.psum(query_shard.astype(jnp.bfloat16), "group").astype(jnp.float32),
        lax.psum(key_shard.astype(jnp.bfloat16), "group").astype(jnp.float32),
        lax.psum(value_shard.astype(jnp.bfloat16), "group").astype(jnp.float32),
        lax.psum(out_shard.astype(jnp.bfloat16), "group").astype(jnp.float32),
        lax.psum(router_shard.astype(jnp.bfloat16), "group").astype(jnp.float32),
        lax.psum(attn_gain_shard.astype(jnp.bfloat16), "group").astype(jnp.float32),
        lax.psum(moe_gain_shard.astype(jnp.bfloat16), "group").astype(jnp.float32),
        lax.psum(gate_weight_grad.astype(jnp.bfloat16), "group").astype(jnp.float32),
        lax.psum(up_weight_grad.astype(jnp.bfloat16), "group").astype(jnp.float32),
        lax.psum(down_weight_grad.astype(jnp.bfloat16), "group").astype(jnp.float32),
    )
    return (
        mixed,
        token_grad,
        summed[5],
        summed[6],
        summed[0],
        summed[1],
        summed[2],
        summed[3],
        summed[4],
        summed[7],
        summed[8],
        summed[9],
    )


bf16 = jnp.bfloat16
f32 = jnp.float32
MESH_ID = pl.DeviceIdType.MESH
VMEM_LIMIT = 67 * 1000 * 1000
COLOURS = ((0, 96), (96, 80), (176, 80))
LINKS = (("head", 1), ("blk", 1), ("blk", 2), ("group", 2), ("group", 1))
ORDERS = ((0, 1, 2), (1, 2, 0), (2, 0, 1))


def vmem():
    return pl.BlockSpec(memory_space=pltpu.VMEM)


def anywhere():
    return pl.BlockSpec(memory_space=pl.ANY)


def dot_last(left, right):
    return lax.dot_general(left, right, (((1,), (1,)), ((), ())), preferred_element_type=f32)


def dot_first(left, right):
    return lax.dot_general(left, right, (((0,), (0,)), ((), ())), preferred_element_type=f32)


def dot(left, right):
    return jnp.dot(left, right, preferred_element_type=f32)


def my_place():
    return lax.axis_index("blk") * 2 + lax.axis_index("head")


def peer(step):
    place = lax.rem(my_place() + step, 8)
    return place, {"blk": place // 2, "head": lax.rem(place, 2)}


def neighbour(link):
    if link == 0:
        return {"head": 1 - lax.axis_index("head")}
    blk = lax.axis_index("blk")
    if link == 1:
        return {"blk": blk + 1 - 2 * lax.rem(blk, 2)}
    return {"blk": lax.rem(blk + 2, 4)}


def my_bits():
    blk = lax.axis_index("blk")
    return (lax.axis_index("head"), lax.rem(blk, 2), blk // 2)


def meet_all():
    barrier = pltpu.get_barrier_semaphore()
    for step in range(1, 8):
        pl.semaphore_signal(barrier, 1, device_id=peer(step)[1], device_id_type=MESH_ID)
    pl.semaphore_wait(barrier, 7)


def remote(src, dst, send, recv, target):
    return pltpu.make_async_remote_copy(
        src_ref=src, dst_ref=dst, send_sem=send, recv_sem=recv, device_id=target, device_id_type=MESH_ID
    )


def cube_index(bits, fixed, rows):
    entries = [pl.ds(fixed[link], 1) if link in fixed else pl.ds(0, 2) for link in (2, 1, 0)]
    return tuple(entries) + (pl.ds(*rows),)


def lanes(shape):
    return lax.broadcasted_iota(jnp.int32, shape, len(shape) - 1)


def turned(u):
    low = lax.rem(lanes(u.shape), 64) < 32
    return jnp.where(low, -pltpu.roll(u, 96, 1), pltpu.roll(u, 32, 1))


def two_heads(q):
    low = lanes(q.shape) < 64
    return jnp.concatenate([jnp.where(low, q, 0.0), jnp.where(low, pltpu.roll(q, 64, 1), 0.0)], 0)


def two_heads_high(g):
    high = lanes(g.shape) >= 64
    return jnp.concatenate([jnp.where(high, pltpu.roll(g, 64, 1), 0.0), jnp.where(high, g, 0.0)], 0)


def block_probability(q_ref, kv_ref, docs, segs, s, i):
    first = max(0, i - 4) * 128
    count = (i + 1) * 128 - first
    q2 = two_heads(q_ref[s, pl.ds(i * 128, 128)].astype(f32))
    kv = kv_ref[s, pl.ds(first, count)]
    raw = dot_last((q2 * 0.125).astype(bf16), kv)
    q_place = i * 128 + lax.broadcasted_iota(jnp.int32, (128, count), 0)
    k_place = first + lanes((128, count))
    q_doc = docs[s, pl.ds(i * 128, 128)]
    keys = pl.ds(first, count)
    k_doc = jnp.where(s == 0, segs[0:1, keys], segs[1:2, keys]).astype(f32)
    allowed = (q_place >= k_place) & (q_doc == k_doc)
    allowed = jnp.concatenate([allowed, allowed], 0)
    masked = jnp.where(allowed, raw, masked_out)
    top = jnp.max(masked, -1, keepdims=True)
    weight = jnp.exp(masked - top)
    probability = weight * (1.0 / jnp.sum(weight, -1, keepdims=True))
    return first, count, q2, kv, probability


def norm_back(values, gain, grad):
    scale = lax.rsqrt(jnp.mean(values * values, -1, keepdims=True) + epsilon)
    inner = grad * gain
    along = jnp.mean(values * inner, -1, keepdims=True)
    out = scale * inner - values * (scale * scale * scale * along)
    gain_grad = jnp.sum(grad * values * scale, 0, keepdims=True)
    return out, gain_grad


def expert_inner(rows_e, pair_e, gate_w, up_w, down_w):
    gate_val = dot(rows_e, gate_w)
    up_val = dot(rows_e, up_w)
    sig = 1.0 / (1.0 + jnp.exp(-gate_val))
    silu = gate_val * sig
    hidden = (silu * up_val).astype(bf16)
    hidden_grad = dot_last(pair_e, down_w)
    gate_grad = (hidden_grad * up_val * sig * (1.0 + gate_val * (1.0 - sig))).astype(bf16)
    up_grad = (hidden_grad * silu).astype(bf16)
    return hidden, gate_grad, up_grad


def sibling():
    group = lax.axis_index("group")
    return {"group": group + 1 - 2 * lax.rem(group, 2)}


def mirror():
    return {"group": lax.rem(lax.axis_index("group") + 2, 4)}


def my_core():
    return lax.rem(lax.axis_index("group"), 2)


def meet(targets):
    barrier = pltpu.get_barrier_semaphore()
    for target in targets:
        pl.semaphore_signal(barrier, 1, device_id=target, device_id_type=MESH_ID)
    pl.semaphore_wait(barrier, len(targets))


def peers():
    return [peer(step)[1] for step in range(1, 8)]


def cube_entry(fixed):
    return tuple(pl.ds(fixed[link], 1) if link in fixed else pl.ds(0, 2) for link in (2, 1, 0))


class Gather:
    def __init__(self, items, send, recv):
        self.items, self.send, self.recv, self.bits = items, send, recv, my_bits()

    def copies(self, step):
        made = []
        for k, (src, place, order) in enumerate(self.items):
            fixed = {link: self.bits[link] for link in order[step:]}
            where = place(cube_entry(fixed))
            here = where
            if step == 0:
                here = src
                where = place((self.bits[2], self.bits[1], self.bits[0]))
            made.append(remote(here, where, self.send.at[step, k], self.recv.at[step, k], neighbour(order[step])))
        return made

    def start(self, step):
        for copy in self.copies(step):
            copy.start()

    def wait(self, step):
        for copy in self.copies(step):
            copy.wait_recv()

    def advance(self, step):
        for before, after in zip(self.copies(step - 1), self.copies(step)):
            before.wait_recv()
            after.start()

    def sent(self):
        for step in range(3):
            for copy in self.copies(step):
                copy.wait_send()


SHARES = ((0, 48), (96, 48), (176, 48), (48, 48), (144, 32), (224, 32))
HALF_SHARES = tuple(
    tuple((s * 128 + start, count) for start, count in ((0, 32), (32, 32), (64, 16), (80, 16), (96, 16), (112, 16)))
    for s in range(2)
)


def row_items(src, dst, shares=SHARES):
    def item(k):
        start, count = shares[k]
        return (src.at[pl.ds(start, count)], lambda entry: dst.at[entry + (pl.ds(start, count),)], ORDERS[k % 3])

    return [item(k) for k in range(len(shares))]


ROW_CUTS = tuple((pl.ds(start, count), slice(None)) for start, count in SHARES)


class CubeSum:
    def __init__(self, source, part, cuts, scratch, base=0):
        self.source, self.part, self.cuts = source, part, cuts
        self.kept = tuple((pl.ds(row.start - base, row.size) if base else row, lane) for row, lane in cuts)
        *self.got, self.held0, self.got1, self.held1, self.got2, self.send, self.recv = scratch
        self.bits = my_bits()
        self.orders = [ORDERS[k % 3] for k in range(len(cuts))]

    def copy(self, step, k):
        order, cut, kept = self.orders[k], self.cuts[k], self.kept[k]
        other = 1 - self.bits[order[step]]
        if step == 0:
            src = self.source.at[cube_entry({order[0]: other}) + cut]
            dst = self.got[k]
        elif step == 1:
            src = self.held0.at[(other, slice(None)) + kept]
            dst = self.got1.at[(slice(None),) + kept]
        else:
            src = self.held1.at[(other,) + kept]
            dst = self.got2.at[kept]
        return remote(src, dst, self.send.at[step, k], self.recv.at[step, k], neighbour(order[step]))

    def start(self):
        for k in range(len(self.cuts)):
            self.copy(0, k).start()

    def middle(self):
        for k, order in enumerate(self.orders):
            self.copy(0, k).wait_recv()
            cut, kept = self.cuts[k], self.kept[k]

            def add(w, carry, k=k, order=order, cut=cut, kept=kept):
                u, v = w // 2, lax.rem(w, 2)
                mine = {order[0]: self.bits[order[0]], order[1]: u, order[2]: v}
                there = {order[0]: 0, order[1]: u, order[2]: v}
                landed = self.got[k][there[2], there[1], there[0]].astype(f32)
                here = self.part[(mine[2], mine[1], mine[0]) + cut].astype(f32)
                self.held0[(u, v) + kept] = (here + landed).astype(bf16)
                return carry

            lax.fori_loop(0, 4, add, 0)
            self.copy(1, k).start()

    def last(self):
        for k, order in enumerate(self.orders):
            self.copy(1, k).wait_recv()
            kept = self.kept[k]

            def add(v, carry, order=order, kept=kept):
                here = self.held0[(self.bits[order[1]], v) + kept].astype(f32)
                self.held1[(v,) + kept] = (here + self.got1[(v,) + kept].astype(f32)).astype(bf16)
                return carry

            lax.fori_loop(0, 2, add, 0)
            self.copy(2, k).start()

    def finish(self, store):
        for k, order in enumerate(self.orders):
            self.copy(2, k).wait_recv()
            kept = self.kept[k]
            store(
                self.cuts[k], self.held1[(self.bits[order[2]],) + kept].astype(f32) + self.got2[kept].astype(f32)
            )

    def sent(self):
        for step in range(3):
            for k in range(len(self.cuts)):
                self.copy(step, k).wait_send()


def cube_sum_scratch(rows, width, cuts):
    def share(k):
        row, lane = cuts[k]
        shape = [2, 2, 2, rows if row == slice(None) else row.size, width if lane == slice(None) else lane.size]
        shape[2 - ORDERS[k % 3][0]] = 1
        return pltpu.VMEM(tuple(shape), bf16)

    return [
        *(share(k) for k in range(len(cuts))),
        pltpu.VMEM((2, 2, rows, width), bf16),
        pltpu.VMEM((2, rows, width), bf16),
        pltpu.VMEM((2, rows, width), bf16),
        pltpu.VMEM((rows, width), bf16),
        pltpu.SemaphoreType.DMA((3, len(cuts))),
        pltpu.SemaphoreType.DMA((3, len(cuts))),
    ]


class Spread:
    def __init__(self, src, dst, send, recv):
        self.src, self.dst, self.send, self.recv = src, dst, send, recv

    def copy(self, step):
        place, target = peer(step)
        return remote(self.src(place), self.dst(my_place()), self.send.at[step], self.recv.at[step], target)

    def start(self):
        for step in range(1, 8):
            self.copy(step).start()

    def wait(self):
        for step in range(1, 8):
            self.copy(step).wait()


def rope_tables():
    frequency = 10000.0 ** (-(np.arange(128) % 32) * 2.0 / 64)
    near = np.arange(128)[:, None] * frequency[None, :]
    far = np.arange(8)[:, None] * 128.0 * frequency[None, :]
    return tuple(np.asarray(t, np.float32) for t in (np.cos(near), np.sin(near), np.cos(far), np.sin(far)))


def fill_rope(near_cos, near_sin, far_cos, far_sin, cosine, sine):
    for j in range(8):
        rows = pl.ds(j * 128, 128)
        fc, fs = far_cos[pl.ds(j, 1)], far_sin[pl.ds(j, 1)]
        cosine[rows] = fc * near_cos[...] - fs * near_sin[...]
        sine[rows] = fs * near_cos[...] + fc * near_sin[...]


THIRDS = ((0, 384), (384, 384), (768, 256))


def fill_docs(segs, docs):
    for s in range(2):
        for j in range(8):
            row = segs[pl.ds(s, 1), pl.ds(j * 128, 128)].astype(f32)
            docs[s, pl.ds(j * 128, 128)] = jnp.broadcast_to(row, (128, 128)).T[:, 0:1]


def fill_upper(upper):
    row = lax.broadcasted_iota(jnp.int32, upper.shape, 0)
    upper[...] = jnp.where(row < lanes(upper.shape), 1.0, 0.0).astype(bf16)


def forward_kernel(
    tok, cot, wq, wk, wv, wo, attn_gain, moe_gain, router, routes, segs, near_cos, near_sin, far_cos, far_sin,
    attn_hbm, q_out, kv_out, amix, residual_out, moe_in_out, weights_out, wo_hbm, gains_all, router_all, routes_all,
    cot_hbm, cot_mirror, routes_mirror, wkv,
    tok_all, attn_all, cot_all, wo_all, w_all, mix, cosine, sine, docs, gains,
    tok_send, tok_recv, cot_send, cot_recv, small_send, small_recv, mix_send, mix_recv, wo_send, wo_recv,
    pair_send, pair_recv, own_sem, out_sem,
):
    me, core = my_place(), my_core()
    half = pl.ds(pl.multiple_of(core * 64, 64), 64)
    own_entry = (me // 4, lax.rem(me // 2, 2), lax.rem(me, 2))
    first_row = lax.broadcasted_iota(jnp.int32, (16, 128), 0)
    both_gains = jnp.where(first_row == 1, moe_gain[...].astype(f32), 0.0)
    gains[...] = jnp.where(first_row == 0, attn_gain[...].astype(f32), both_gains).astype(bf16)
    for j in range(4):
        low = lanes((128, 128)) < 64
        k_two, v_two = (w[:, j * 128 : (j + 1) * 128].astype(f32) for w in (wk, wv))
        wkv[:, j * 256 : j * 256 + 128] = jnp.where(low, k_two, pltpu.roll(v_two, 64, 1)).astype(bf16)
        wkv[:, j * 256 + 128 : j * 256 + 256] = jnp.where(low, pltpu.roll(k_two, 64, 1), v_two).astype(bf16)
    meet(peers() + [sibling(), mirror()])
    tok_gather = Gather(row_items(tok, tok_all), tok_send, tok_recv)
    tok_gather.start(0)
    pairs = (
        (lambda j: wq.at[half, pl.ds(j * 128, 128)], lambda i: w_all.at[i, half, pl.ds(0, 128)]),
        (lambda j: wkv.at[half, pl.ds(j * 128, 128)], lambda i: w_all.at[i, half, pl.ds(128, 128)]),
        (lambda j: gains, lambda i: gains_all.at[:, pl.ds(i * 128, 128)]),
        (lambda j: router, lambda i: router_all.at[:, pl.ds(i * 128, 128)]),
        (lambda j: routes.at[:, pl.ds(0, 128)], lambda i: routes_all.at[:, pl.ds(i * 128, 128)]),
        (lambda j: routes.at[:, pl.ds(128, 128)], lambda i: routes_all.at[:, pl.ds(1024 + i * 128, 128)]),
    )
    smalls = [Spread(src, dst, small_send.at[k], small_recv.at[k]) for k, (src, dst) in enumerate(pairs)]
    own = [pltpu.make_async_copy(src(me), dst(me), own_sem.at[k]) for k, (src, dst) in enumerate(pairs)]
    own += [
        pltpu.make_async_copy(tok, tok_all.at[own_entry], own_sem.at[6]),
        pltpu.make_async_copy(cot, cot_all.at[own_entry], own_sem.at[7]),
        pltpu.make_async_copy(wo.at[half], wo_all.at[own_entry + (half,)], own_sem.at[8]),
    ]
    for copy in own:
        copy.start()
    for small in smalls:
        small.start()
    fill_rope(near_cos, near_sin, far_cos, far_sin, cosine, sine)
    for copy in own:
        copy.wait()
    tok_gather.advance(1)
    fill_docs(segs, docs)
    tok_gather.advance(2)
    for small in smalls:
        small.wait()
    w_pair = remote(w_all.at[:, half], w_all.at[:, half], pair_send.at[3], pair_recv.at[3], sibling())
    w_pair.start()
    tok_gather.wait(2)
    w_pair.wait()

    def wo_item(k):
        where = (half, pl.ds(*THIRDS[k]))
        return (wo.at[where], lambda entry: wo_all.at[entry + where], ORDERS[k])

    wo_gather = Gather([wo_item(k) for k in range(3)], wo_send, wo_recv)
    wo_gather.start(0)
    cot_gather = Gather(row_items(cot, cot_all), cot_send, cot_recv)
    cot_gather.start(0)
    cot_copy = remote(cot, cot_mirror, pair_send.at[1], pair_recv.at[1], mirror())
    cot_copy.start()
    routes_copy = remote(routes_all, routes_mirror, pair_send.at[0], pair_recv.at[0], mirror())
    routes_copy.start()

    gain_row = gains_all[0:1].astype(f32)

    def project(j, carry):
        rows = pl.ds(pl.multiple_of(j * 128, 128), 128)
        x = tok_all[j // 4, lax.rem(j // 2, 2), lax.rem(j, 2)].astype(f32)
        scale = lax.rsqrt(jnp.mean(x * x, -1, keepdims=True) + epsilon)
        attn_in = (x * scale * gain_row).astype(bf16)
        attn_all[j] = attn_in
        both = dot(attn_in, w_all[...].reshape(1024, 256))
        c = cosine[rows]
        n = sine[rows]
        c2 = jnp.concatenate([c, c], 0)
        n2 = jnp.concatenate([n, n], 0)
        q = both[:, :128]
        kv = both[:, 128:]
        q = (q * c2 + turned(q) * n2).astype(bf16)
        kv = jnp.where(lanes(kv.shape) < 64, kv * c2 + turned(kv) * n2, kv).astype(bf16)
        for s in range(2):
            q_out[s, rows] = q[s * 128 : (s + 1) * 128]
            kv_out[s, rows] = kv[s * 128 : (s + 1) * 128]
        return carry

    lax.fori_loop(0, 8, project, 0)
    attn_copy = pltpu.make_async_copy(attn_all, attn_hbm, out_sem.at[0])
    attn_copy.start()
    wo_gather.advance(1)
    cot_gather.advance(1)
    wo_pair = remote(
        wo_all.at[:, :, :, half], wo_all.at[:, :, :, half], pair_send.at[2], pair_recv.at[2], sibling()
    )

    def mix_copy(i):
        return remote(
            mix.at[i],
            amix.at[:, :, pl.ds(pl.multiple_of(me * 128, 128), 128)],
            mix_send.at[i],
            mix_recv.at[me],
            {"blk": i // 2, "head": lax.rem(i, 2)},
        )

    def send_mix(i):
        @pl.when(me != i)
        def _():
            mix_copy(i).start()

    for i in range(8):

        def attend(s, carry, i=i):
            first, count, q2, kv, probability = block_probability(q_out, kv_out, docs, segs, s, i)
            mixed = dot(probability.astype(bf16), kv)
            low = lanes((128, 128)) < 64
            mix[i, s] = jnp.where(low, pltpu.roll(mixed[:128], 64, 1), mixed[128:]).astype(bf16)
            return carry

        lax.fori_loop(0, 2, attend, 0)
        if i > 0:
            send_mix(i - 1)
        if i == 2:
            wo_gather.advance(2)
        if i == 4:
            cot_gather.advance(2)
    send_mix(7)
    wo_gather.wait(2)
    wo_pair.start()
    mine = pltpu.make_async_copy(
        mix.at[me], amix.at[:, :, pl.ds(pl.multiple_of(me * 128, 128), 128)], own_sem.at[0]
    )
    mine.start()
    wo_pair.wait()
    wo_copy = pltpu.make_async_copy(wo_all, wo_hbm, out_sem.at[1])
    wo_copy.start()
    for step in range(1, 8):
        place, target = peer(step)
        remote(
            mix.at[place],
            amix.at[:, :, pl.ds(pl.multiple_of(place * 128, 128), 128)],
            mix_send.at[place],
            mix_recv.at[place],
            target,
        ).wait()
    mine.wait()
    width = tok.shape[-1]
    residual = tok[...].astype(f32) + dot(amix[...].reshape(256, width), wo_all[...].reshape(width, width))
    residual_out[...] = residual
    scale = lax.rsqrt(jnp.mean(residual * residual, -1, keepdims=True) + epsilon)
    moe_in = (residual * scale * gains_all[1:2].astype(f32)).astype(bf16)
    moe_in_out[...] = moe_in
    logits = dot_last(router_all[...], moe_in)
    experts = lax.broadcasted_iota(jnp.int32, logits.shape, 0)
    picked = [
        jnp.sum(jnp.where(experts == routes[pl.ds(k, 1)], logits, 0.0), 0, keepdims=True) for k in range(TOP)
    ]
    picked = jnp.concatenate(picked, 0)
    weight = jnp.exp(picked - jnp.max(picked, 0, keepdims=True))
    weights_out[...] = weight / jnp.sum(weight, 0, keepdims=True)
    cot_gather.wait(2)
    cot_out = pltpu.make_async_copy(cot_all, cot_hbm, out_sem.at[2])
    cot_out.start()
    routes_copy.wait()
    cot_copy.wait()
    tok_gather.sent()
    cot_gather.sent()
    wo_gather.sent()
    attn_copy.wait()
    wo_copy.wait()
    cot_out.wait()


def forward(*values):
    tok = values[0]
    width = tok.shape[-1]
    tables = tuple(jnp.asarray(t) for t in rope_tables())
    return pl.pallas_call(
        forward_kernel,
        out_shape=(
            jax.ShapeDtypeStruct((8, 256, width), bf16),
            jax.ShapeDtypeStruct((2, 1024, 128), bf16),
            jax.ShapeDtypeStruct((2, 1024, 128), bf16),
            jax.ShapeDtypeStruct((2, 128, width), bf16),
            jax.ShapeDtypeStruct((256, width), f32),
            jax.ShapeDtypeStruct((256, width), bf16),
            jax.ShapeDtypeStruct((8, 256), f32),
            jax.ShapeDtypeStruct((2, 2, 2, 128, width), bf16),
            jax.ShapeDtypeStruct((16, width), bf16),
            jax.ShapeDtypeStruct((32, width), bf16),
            jax.ShapeDtypeStruct((8, 2048), jnp.int32),
            jax.ShapeDtypeStruct((2, 2, 2, 256, width), bf16),
            jax.ShapeDtypeStruct((256, width), bf16),
            jax.ShapeDtypeStruct((8, 2048), jnp.int32),
            jax.ShapeDtypeStruct((128, 1024), bf16),
        ),
        in_specs=[vmem()] * 15,
        out_specs=(
            anywhere(), vmem(), vmem(), vmem(), vmem(), vmem(), vmem(), anywhere(), vmem(), vmem(), vmem(),
            anywhere(), vmem(), vmem(), vmem(),
        ),
        scratch_shapes=[
            pltpu.VMEM((2, 2, 2, 256, width), bf16),
            pltpu.VMEM((8, 256, width), bf16),
            pltpu.VMEM((2, 2, 2, 256, width), bf16),
            pltpu.VMEM((2, 2, 2, 128, width), bf16),
            pltpu.VMEM((8, 128, 256), bf16),
            pltpu.VMEM((8, 2, 128, 128), bf16),
            pltpu.VMEM((1024, 128), f32),
            pltpu.VMEM((1024, 128), f32),
            pltpu.VMEM((2, 1024, 1), f32),
            pltpu.VMEM((16, 128), bf16),
            pltpu.SemaphoreType.DMA((3, 6)),
            pltpu.SemaphoreType.DMA((3, 6)),
            pltpu.SemaphoreType.DMA((3, 6)),
            pltpu.SemaphoreType.DMA((3, 6)),
            pltpu.SemaphoreType.DMA((6, 8)),
            pltpu.SemaphoreType.DMA((6, 8)),
            pltpu.SemaphoreType.DMA((8,)),
            pltpu.SemaphoreType.DMA((8,)),
            pltpu.SemaphoreType.DMA((3, 3)),
            pltpu.SemaphoreType.DMA((3, 3)),
            pltpu.SemaphoreType.DMA((4,)),
            pltpu.SemaphoreType.DMA((4,)),
            pltpu.SemaphoreType.DMA((9,)),
            pltpu.SemaphoreType.DMA((3,)),
        ],
        compiler_params=pltpu.CompilerParams(
            collective_id=0, has_side_effects=True, vmem_limit_bytes=VMEM_LIMIT
        ),
        name="forward",
    )(*values, *tables)


SLOT = 4 * CAPH
SPAN = 512
TAKEN = 4 * SLOT


def build_rows(routes, upper, plain, first_expert, block):
    columns = pl.ds(pl.multiple_of(block * SPAN, SPAN), SPAN)
    chosen = routes[:, columns]
    masks = [jnp.max((chosen == first_expert + e).astype(f32), 0, keepdims=True) for e in range(4)]
    mask = jnp.concatenate(masks + [jnp.zeros((4, SPAN), f32)], 0)
    rank = dot(mask.astype(bf16), upper[...])
    slots = lax.broadcasted_iota(jnp.int32, (SLOT, SPAN), 0).astype(f32)
    for e in range(4):
        hit = (slots == rank[e : e + 1]) & (mask[e : e + 1] > 0.0)
        plain[block, e * SLOT : (e + 1) * SLOT] = jnp.where(hit, 1.0, 0.0).astype(bf16)


def slot_weights(routes, weights, plain, column, first_expert, block):
    columns = pl.ds(pl.multiple_of(block * SPAN, SPAN), SPAN)
    chosen = routes[:, columns]
    weight = weights[:, columns]
    for e in range(4):
        share = jnp.sum(jnp.where(chosen == first_expert + e, weight, 0.0), 0, keepdims=True)
        mine = pl.ds(e * SLOT, SLOT)
        column[block, mine] = jnp.sum(plain[block, mine].astype(f32) * share, -1, keepdims=True)


def place_rows(source, block):
    width = source.shape[-1]
    rows = pl.ds(pl.multiple_of((block // 2) * 128, 128), 128)
    return source[lax.rem(block, 2), :, :, rows].reshape(SPAN, width)


def expert_rows(e):
    return pl.ds(pl.multiple_of(e * SLOT, 16), SLOT)


def experts_kernel(
    moe_in, my_weights, cot_mirror, cot_hbm, routes, routes_mirror, gate_hbm, up_hbm, down_hbm,
    out_part, in_sum, p_all, rows_out, pair_out, hidden_out, gate_out, up_out, plain_mirror, pair_mirror, moe_mirror,
    weights_other,
    x, c, cm, upper, plain, rows, pair_grad, pair_in, column, p_col, weights, p_part,
    gate, up, down, hid_buf, gg_buf, ug_buf, part_buf,
    row_send, row_recv, cm_send, cm_recv, w_send, w_recv, p_send, p_recv, pair_send, pair_recv,
    sem_c, sem_w, sem_rows, sem_h, sem_part, own_sem, *sums,
):
    me = my_place()
    first = me * 4
    width = x.shape[-1]
    count = 2 * SLOT
    own_entry = (me // 4, lax.rem(me // 2, 2), lax.rem(me, 2))
    meet(peers() + [mirror()])
    gathers = [
        Gather(row_items(moe_in, x, HALF_SHARES[s]), row_send.at[s], row_recv.at[s]) for s in range(2)
    ]
    gathers[0].start(0)

    def weight_lanes(s, i):
        return weights.at[:, pl.ds(pl.multiple_of(s * 1024 + i * 128, 128), 128)]

    own = [
        pltpu.make_async_copy(moe_in, x.at[own_entry], own_sem.at[0]),
        pltpu.make_async_copy(my_weights.at[:, pl.ds(0, 128)], weight_lanes(0, me), own_sem.at[1]),
        pltpu.make_async_copy(my_weights.at[:, pl.ds(128, 128)], weight_lanes(1, me), own_sem.at[2]),
        pltpu.make_async_copy(cot_mirror, cm.at[own_entry], own_sem.at[3]),
    ]
    for copy in own:
        copy.start()
    weight_spreads = [
        Spread(
            lambda j, s=s: my_weights.at[:, pl.ds(s * 128, 128)],
            lambda i, s=s: weight_lanes(s, i),
            w_send.at[s],
            w_recv.at[s],
        )
        for s in range(2)
    ]
    for spread in weight_spreads:
        spread.start()
    load_c = pltpu.make_async_copy(cot_hbm, c, sem_c)
    load_c.start()

    def fetch(e, slot):
        return [
            pltpu.make_async_copy(gate_hbm.at[e], gate.at[slot], sem_w.at[slot, 0]),
            pltpu.make_async_copy(up_hbm.at[e], up.at[slot], sem_w.at[slot, 1]),
            pltpu.make_async_copy(down_hbm.at[e], down.at[slot], sem_w.at[slot, 2]),
        ]

    for copy in fetch(0, 0):
        copy.start()
    fill_upper(upper)

    def build(block, carry):
        build_rows(routes, upper, plain, first, block)
        return carry

    lax.fori_loop(0, 2, build, 0)
    for copy in own:
        copy.wait()
    gathers[0].advance(1)
    lax.fori_loop(2, 4, build, 0)
    load_c.wait()

    def take_c(block, carry):
        pair_grad[block] = dot(plain[block], place_rows(c, block)).astype(bf16)
        return carry

    gathers[0].advance(2)
    gathers[1].start(0)
    lax.fori_loop(0, 4, take_c, 0)
    for spread in weight_spreads:
        spread.wait()
    weights_copy = remote(weights, weights_other, pair_send.at[0], pair_recv.at[0], mirror())
    weights_copy.start()

    def weigh(block, carry):
        slot_weights(routes, weights, plain, column, first, block)
        return carry

    lax.fori_loop(0, 4, weigh, 0)
    cm_gather = Gather(row_items(cot_mirror, cm), cm_send, cm_recv)
    moe_copy = remote(moe_in, moe_mirror, pair_send.at[1], pair_recv.at[1], mirror())
    p_part[...] = jnp.zeros_like(p_part)

    def take_x(block, carry):
        rows[block] = dot(plain[block], place_rows(x, block)).astype(bf16)
        return carry

    def keep_rows(s):
        pair = pl.ds(2 * s, 2)
        return pltpu.make_async_copy(rows.at[pair], rows_out.at[pair], sem_rows.at[s])

    def keep(s, e, slot):
        where = pl.ds(pl.multiple_of(s * count, 16), count)
        return [
            pltpu.make_async_copy(hid_buf.at[slot], hidden_out.at[e, where], sem_h.at[slot, 0]),
            pltpu.make_async_copy(gg_buf.at[slot], gate_out.at[e, where], sem_h.at[slot, 1]),
            pltpu.make_async_copy(ug_buf.at[slot], up_out.at[e, where], sem_h.at[slot, 2]),
        ]

    def total_of(s):
        cuts = tuple((pl.ds(*cut), slice(None)) for cut in HALF_SHARES[s])
        return CubeSum(x, x, cuts, sums[12 * s : 12 * s + 12], s * 128)

    totals = [total_of(s) for s in range(2)]

    def store(cut, value):
        in_sum[cut] = value

    def one_half(s, carry):
        for t in range(2):

            @pl.when(s == t)
            def _(t=t):
                gathers[t].wait(2)
                if t == 0:
                    gathers[1].advance(1)

        lax.fori_loop(2 * s, 2 * s + 2, take_x, 0)
        keep_rows(s).start()

        @pl.when(s == 0)
        def _():
            gathers[1].advance(2)
            cm_gather.start(0)
            moe_copy.start()

        def expert(e, inner):
            slot = lax.rem(e, 2)
            mine = expert_rows(e)
            pair = pl.ds(2 * s, 2)
            for copy in fetch(e, slot):
                copy.wait()

            @pl.when(4 * s + e < 7)
            def _():
                for copy in fetch(lax.rem(e + 1, 4), 1 - slot):
                    copy.start()

            rows_e = rows[pair, mine].reshape(count, width)
            weight_e = column[pair, mine].reshape(count, 1)
            pair_e = (pair_grad[pair, mine].reshape(count, width).astype(f32) * weight_e).astype(bf16)
            pair_grad[pair, mine] = pair_e.reshape(2, SLOT, width)
            hidden, gate_grad, up_grad = expert_inner(rows_e, pair_e, gate[slot], up[slot], down[slot])

            @pl.when(e >= 2)
            def _():
                for copy in keep(s, e - 2, slot):
                    copy.wait()

            hid_buf[slot] = hidden
            gg_buf[slot] = gate_grad
            ug_buf[slot] = up_grad
            for copy in keep(s, e, slot):
                copy.start()

            @pl.when(e == 0)
            def _():
                keep_rows(s).wait()

            out_e = dot(hidden, down[slot]).astype(bf16).astype(f32)
            p = jnp.sum(out_e * pair_e.astype(f32), -1, keepdims=True)
            p_col[pair, mine] = p.reshape(2, SLOT, 1)
            rows[pair, mine] = (out_e * weight_e).astype(bf16).reshape(2, SLOT, width)
            back = dot_last(gate_grad, gate[slot]) + dot_last(up_grad, up[slot])
            pair_in[pair, mine] = back.astype(bf16).reshape(2, SLOT, width)

            @pl.when(4 * s + e == 3)
            def _():
                cm_gather.advance(1)

            @pl.when(4 * s + e == 5)
            def _():
                cm_gather.advance(2)

            @pl.when(4 * s + e == 6)
            def _():
                totals[0].middle()

            return inner

        lax.fori_loop(0, 4, expert, 0)
        for copy in keep(s, 2, 0) + keep(s, 3, 1):
            copy.wait()
        for t in range(2):

            @pl.when(s == t)
            def _(t=t):
                gathers[t].sent()

        def combine_in(block, inner):
            y = lax.rem(block, 2)
            back = dot_first(plain[block], pair_in[block]).astype(bf16)
            mine = pl.ds(pl.multiple_of(s * 128, 128), 128)
            x[y, :, :, mine] = back.reshape(2, 2, 128, width)
            for e in range(4):
                slots = pl.ds(e * SLOT, SLOT)
                p = jnp.sum(plain[block, slots].astype(f32) * p_col[block, slots], 0, keepdims=True)
                for d in range(4):
                    p_part[y * 4 + d, pl.ds(e, 1), mine] = p[:, d * 128 : (d + 1) * 128]
            return inner

        lax.fori_loop(2 * s, 2 * s + 2, combine_in, 0)
        for t in range(2):

            @pl.when(s == t)
            def _(t=t):
                totals[t].start()
                if t == 1:
                    totals[0].last()

        return carry

    lax.fori_loop(0, 2, one_half, 0)
    keep_pair = pltpu.make_async_copy(pair_grad, pair_out, sem_rows.at[0])
    keep_pair.start()
    p_spread = Spread(lambda j: p_part.at[j], lambda i: p_all.at[i], p_send, p_recv)
    p_spread.start()
    p_own = pltpu.make_async_copy(p_part.at[me], p_all.at[me], own_sem.at[0])
    p_own.start()

    def part_copy(block):
        slot = lax.rem(block, 2)
        rows_of = pl.ds(pl.multiple_of((block // 2) * 128, 128), 128)
        return pltpu.make_async_copy(
            part_buf.at[slot], out_part.at[lax.rem(block, 2), :, :, rows_of], sem_part.at[slot]
        )

    def combine_out(block, carry):
        slot = lax.rem(block, 2)

        @pl.when(block >= 2)
        def _():
            part_copy(block - 2).wait()

        out = dot_first(plain[block], rows[block]).astype(bf16)
        part_buf[slot] = out.reshape(2, 2, 128, width)
        part_copy(block).start()
        return carry

    lax.fori_loop(0, 4, combine_out, 0)
    totals[0].finish(store)
    keep_pair.wait()

    def build_mirror(block, carry):
        build_rows(routes_mirror, upper, plain, first, block)
        return carry

    lax.fori_loop(0, 2, build_mirror, 0)
    totals[1].middle()
    lax.fori_loop(2, 4, build_mirror, 0)
    keep_plain = pltpu.make_async_copy(plain, plain_mirror, sem_rows.at[0])
    keep_plain.start()
    cm_gather.wait(2)

    def take_mirror(block, carry):
        pair_grad[block] = dot(plain[block], place_rows(cm, block)).astype(bf16)
        return carry

    lax.fori_loop(0, 2, take_mirror, 0)
    totals[1].last()
    lax.fori_loop(2, 4, take_mirror, 0)
    keep_mirror = pltpu.make_async_copy(pair_grad, pair_mirror, sem_rows.at[1])
    keep_mirror.start()
    p_spread.wait()
    p_own.wait()
    part_copy(2).wait()
    part_copy(3).wait()
    totals[1].finish(store)
    for total in totals:
        total.sent()
    keep_plain.wait()
    keep_mirror.wait()
    cm_gather.sent()
    weights_copy.wait()
    moe_copy.wait()


def half_cuts(s):
    return tuple((pl.ds(*cut), slice(None)) for cut in HALF_SHARES[s])


def experts(moe_in, my_weights, cot_mirror, cot_all, routes, routes_mirror, gate_w, up_w, down_w):
    width = moe_in.shape[-1]
    ff = gate_w.shape[-1]
    return pl.pallas_call(
        experts_kernel,
        out_shape=(
            jax.ShapeDtypeStruct((2, 2, 2, 256, width), bf16),
            jax.ShapeDtypeStruct((256, width), f32),
            jax.ShapeDtypeStruct((8, 8, 256), f32),
            jax.ShapeDtypeStruct((4, TAKEN, width), bf16),
            jax.ShapeDtypeStruct((4, TAKEN, width), bf16),
            jax.ShapeDtypeStruct((4, TAKEN, ff), bf16),
            jax.ShapeDtypeStruct((4, TAKEN, ff), bf16),
            jax.ShapeDtypeStruct((4, TAKEN, ff), bf16),
            jax.ShapeDtypeStruct((4, TAKEN, SPAN), bf16),
            jax.ShapeDtypeStruct((4, TAKEN, width), bf16),
            jax.ShapeDtypeStruct((256, width), bf16),
            jax.ShapeDtypeStruct((8, 2048), f32),
        ),
        in_specs=[vmem(), vmem(), vmem(), anywhere(), vmem(), vmem(), anywhere(), anywhere(), anywhere()],
        out_specs=(anywhere(), vmem(), vmem()) + (anywhere(),) * 7 + (vmem(), vmem()),
        scratch_shapes=[
            pltpu.VMEM((2, 2, 2, 256, width), bf16),
            pltpu.VMEM((2, 2, 2, 256, width), bf16),
            pltpu.VMEM((2, 2, 2, 256, width), bf16),
            pltpu.VMEM((SPAN, SPAN), bf16),
            pltpu.VMEM((4, TAKEN, SPAN), bf16),
            pltpu.VMEM((4, TAKEN, width), bf16),
            pltpu.VMEM((4, TAKEN, width), bf16),
            pltpu.VMEM((4, TAKEN, width), bf16),
            pltpu.VMEM((4, TAKEN, 1), f32),
            pltpu.VMEM((4, TAKEN, 1), f32),
            pltpu.VMEM((8, 2048), f32),
            pltpu.VMEM((8, 8, 256), f32),
            pltpu.VMEM((2, width, ff), bf16),
            pltpu.VMEM((2, width, ff), bf16),
            pltpu.VMEM((2, ff, width), bf16),
            pltpu.VMEM((2, 2 * SLOT, ff), bf16),
            pltpu.VMEM((2, 2 * SLOT, ff), bf16),
            pltpu.VMEM((2, 2 * SLOT, ff), bf16),
            pltpu.VMEM((2, 2, 2, 128, width), bf16),
            pltpu.SemaphoreType.DMA((2, 3, 6)),
            pltpu.SemaphoreType.DMA((2, 3, 6)),
            pltpu.SemaphoreType.DMA((3, 6)),
            pltpu.SemaphoreType.DMA((3, 6)),
            pltpu.SemaphoreType.DMA((2, 8)),
            pltpu.SemaphoreType.DMA((2, 8)),
            pltpu.SemaphoreType.DMA((8,)),
            pltpu.SemaphoreType.DMA((8,)),
            pltpu.SemaphoreType.DMA((2,)),
            pltpu.SemaphoreType.DMA((2,)),
            pltpu.SemaphoreType.DMA,
            pltpu.SemaphoreType.DMA((2, 3)),
            pltpu.SemaphoreType.DMA((2,)),
            pltpu.SemaphoreType.DMA((2, 3)),
            pltpu.SemaphoreType.DMA((2,)),
            pltpu.SemaphoreType.DMA((4,)),
            *cube_sum_scratch(128, width, half_cuts(0)),
            *cube_sum_scratch(128, width, half_cuts(1)),
        ],
        compiler_params=pltpu.CompilerParams(
            collective_id=1, has_side_effects=True, vmem_limit_bytes=VMEM_LIMIT
        ),
        name="experts",
    )(moe_in, my_weights, cot_mirror, cot_all, routes, routes_mirror, gate_w, up_w, down_w)


LANE_SHARE = 128


def backward_kernel(
    cot, residual, in_sum, p_all, routes, weights, router, moe_in, gains_all, wo_hbm, amix, attn_hbm, q_in, kv_in,
    segs, near_cos, near_sin, far_cos, far_sin, tok, wq, wkv, moe_mirror,
    token_grad, grads, mirror_hbm,
    wo_all, attn_all, wq_all, wkv_all, mm, mix_grad, mg, gq, gkv, gq_rows, gkv_rows, g_all, kv_sum, cosine, sine, docs,
    residual_grad, small_grad,
    w_send, w_recv, mm_send, mm_recv, mg_send, mg_recv, g_send, g_recv, pair_send, pair_recv, own_sem, load_sem,
):
    me, core = my_place(), my_core()
    width = tok.shape[-1]
    meet(peers() + [sibling()])
    half = pl.ds(pl.multiple_of(core * 64, 64), 64)
    own_entry = (me // 4, lax.rem(me // 2, 2), lax.rem(me, 2))
    own = [
        pltpu.make_async_copy(wq.at[half], wq_all.at[own_entry + (half,)], own_sem.at[0]),
        pltpu.make_async_copy(wkv.at[half], wkv_all.at[own_entry + (half,)], own_sem.at[1]),
        pltpu.make_async_copy(moe_mirror, mm.at[own_entry], own_sem.at[2]),
    ]
    loads = [
        pltpu.make_async_copy(wo_hbm, wo_all, load_sem.at[0]),
        pltpu.make_async_copy(attn_hbm, attn_all, load_sem.at[1]),
    ]
    for copy in own + loads:
        copy.start()

    def weight_item(src, dst, start, count, order):
        rows = pl.ds(pl.multiple_of(core * 64 + start, 16), count)
        return (src.at[rows], lambda entry: dst.at[entry + (rows,)], order)

    w_gather = Gather(
        [
            weight_item(wq, wq_all, 0, 48, ORDERS[0]),
            weight_item(wq, wq_all, 48, 16, ORDERS[1]),
            weight_item(wkv, wkv_all, 0, 32, ORDERS[1]),
            weight_item(wkv, wkv_all, 32, 32, ORDERS[2]),
        ],
        w_send,
        w_recv,
    )
    w_gather.start(0)
    mm_gather = Gather(row_items(moe_mirror, mm), mm_send, mm_recv)
    mm_gather.start(0)
    ids = lax.broadcasted_iota(jnp.int32, (32, 256), 0)
    dense = jnp.zeros((32, 256), f32)
    for k in range(TOP):
        dense = dense + jnp.where(ids == routes[pl.ds(k, 1)], weights[pl.ds(k, 1)], 0.0)
    p = jnp.concatenate([p_all[i, 0:4] for i in range(8)], 0)
    logit_grad = (p - dense * jnp.sum(p, 0, keepdims=True)).astype(bf16)
    moe_in_grad = in_sum[...] + dot_first(logit_grad, router[...])
    part, moe_gain_grad = norm_back(residual[...], gains_all[1:2].astype(f32), moe_in_grad)
    total = cot[...].astype(f32) + part
    residual_grad[...] = total
    low_grad = total.astype(bf16)
    for copy in loads[:1]:
        copy.wait()
    back = dot_last(low_grad, wo_all[...].reshape(width, width)).astype(bf16)
    for j in range(8):
        mix_grad[j] = back[:, j * 128 : (j + 1) * 128].reshape(2, 128, 128)
    mix_spread = Spread(lambda j: mix_grad.at[j], lambda i: mg.at[i], mg_send, mg_recv)
    mix_spread.start()
    mix_own = pltpu.make_async_copy(mix_grad.at[me], mg.at[me], own_sem.at[3])
    mix_own.start()
    for copy in own:
        copy.wait()
    w_gather.advance(1)
    fill_rope(near_cos, near_sin, far_cos, far_sin, cosine, sine)
    fill_docs(segs, docs)
    wo_grad = dot_first(amix[...].reshape(256, width), low_grad)
    grads[:, :, 0:width] = wo_grad.astype(bf16).reshape(8, 128, width)
    padded = jnp.concatenate([logit_grad, jnp.zeros((LANE_SHARE - 32, 256), bf16)], 0)
    small_grad[...] = lax.dot_general(moe_in[...], padded, (((0,), (1,)), ((), ())), preferred_element_type=f32)
    mix_spread.wait()
    mix_own.wait()
    mm_gather.advance(1)

    def lane_block(i):
        return pl.ds(pl.multiple_of(i * 128, 128), 128)

    def spread_of(s):
        return [
            Spread(lambda j: gq.at[j, s], lambda i: gq_rows.at[s, :, lane_block(i)], g_send.at[2 * s], g_recv.at[2 * s]),
            Spread(
                lambda j: gkv.at[j, s],
                lambda i: gkv_rows.at[s, :, lane_block(i)],
                g_send.at[2 * s + 1],
                g_recv.at[2 * s + 1],
            ),
        ]

    def own_blocks(s):
        return [
            pltpu.make_async_copy(gq.at[me, s], gq_rows.at[s, :, lane_block(me)], own_sem.at[4 + 2 * s]),
            pltpu.make_async_copy(gkv.at[me, s], gkv_rows.at[s, :, lane_block(me)], own_sem.at[5 + 2 * s]),
        ]

    def attend(s, carry):
        kv_sum[...] = jnp.zeros_like(kv_sum)
        for i in range(8):
            first, count, q2, kv, probability = block_probability(q_in, kv_in, docs, segs, s, i)
            g2 = two_heads_high(mg[i, s].astype(f32)).astype(bf16)
            prob_grad = dot_last(g2, kv)
            delta = jnp.sum(probability * prob_grad, -1, keepdims=True)
            score_grad = (probability * (prob_grad - delta) * 0.125).astype(bf16)
            dq = dot(score_grad, kv)
            keys = pl.ds(first, count)
            kv_sum[keys] += dot_first(score_grad, q2.astype(bf16)) + dot_first(probability.astype(bf16), g2)
            low = lanes((128, 128)) < 64
            dq = jnp.where(low, dq[:128], pltpu.roll(dq[128:], 64, 1))
            rows = pl.ds(i * 128, 128)
            dq = (dq * cosine[rows] - turned(dq) * sine[rows]).astype(bf16)
            gq[i, s] = dq
            g_all[i, s, :, 0:128] = dq
            if i == 2:

                @pl.when(s == 0)
                def _():
                    w_gather.advance(2)

            if i == 6:

                @pl.when(s == 0)
                def _():
                    mm_gather.advance(2)

        def keys_back(i, inner):
            rows = pl.ds(pl.multiple_of(i * 128, 128), 128)
            dkv = kv_sum[rows]
            low = lanes((128, 128)) < 64
            dkv = jnp.where(low, dkv * cosine[rows] - turned(dkv) * sine[rows], dkv).astype(bf16)
            gkv[i, s] = dkv
            g_all[i, s, :, 128:256] = dkv
            return inner

        lax.fori_loop(0, 8, keys_back, 0)
        for spread in spread_of(s):
            spread.start()
        for copy in own_blocks(s):
            copy.start()
        return carry

    lax.fori_loop(0, 2, attend, 0)
    keep_own = own_blocks(0) + own_blocks(1)
    w_gather.wait(2)
    shared = [
        remote(w.at[:, :, :, half], w.at[:, :, :, half], pair_send.at[k], pair_recv.at[k], sibling())
        for k, w in enumerate((wq_all, wkv_all))
    ]
    for copy in shared:
        copy.start()
    loads[1].wait()
    w_grad = dot_first(attn_all[...].reshape(2048, width), g_all[...].reshape(2048, 256))
    grads[:, :, width + LANE_SHARE :] = w_grad.astype(bf16).reshape(8, 128, 256)
    for copy in shared + keep_own:
        copy.wait()
    for s in range(2):
        for spread in spread_of(s):
            spread.wait()
    back = dot_last(gq_rows[...].reshape(256, 1024), wq_all[...].reshape(width, 1024))
    back = back + dot_last(gkv_rows[...].reshape(256, 1024), wkv_all[...].reshape(width, 1024))
    part, attn_gain_grad = norm_back(tok[...].astype(f32), gains_all[0:1].astype(f32), back)
    token_grad[...] = residual_grad[...] + part
    row = lax.broadcasted_iota(jnp.int32, (LANE_SHARE, width), 0)
    gain_rows = jnp.where(row == 32, moe_gain_grad, jnp.where(row == 33, attn_gain_grad, 0.0))
    grads[:, :, width : width + LANE_SHARE] = (small_grad[...] + gain_rows.T).astype(bf16).reshape(8, 128, LANE_SHARE)
    mm_gather.wait(2)
    mm_out = pltpu.make_async_copy(mm, mirror_hbm, load_sem.at[0])
    mm_out.start()
    w_gather.sent()
    mm_gather.sent()
    mm_out.wait()


def backward(*values):
    tok = values[15]
    width = tok.shape[-1]
    tables = tuple(jnp.asarray(t) for t in rope_tables())
    values = values[:15] + tables + values[15:]
    specs = [vmem()] * 23
    specs[9] = specs[11] = anywhere()
    return pl.pallas_call(
        backward_kernel,
        out_shape=(
            jax.ShapeDtypeStruct((256, width), f32),
            jax.ShapeDtypeStruct((8, 128, width + 256 + LANE_SHARE), bf16),
            jax.ShapeDtypeStruct((2, 2, 2, 256, width), bf16),
        ),
        in_specs=specs,
        out_specs=(vmem(), vmem(), anywhere()),
        scratch_shapes=[
            pltpu.VMEM((2, 2, 2, 128, width), bf16),
            pltpu.VMEM((8, 256, width), bf16),
            pltpu.VMEM((2, 2, 2, 128, width), bf16),
            pltpu.VMEM((2, 2, 2, 128, width), bf16),
            pltpu.VMEM((2, 2, 2, 256, width), bf16),
            pltpu.VMEM((8, 2, 128, 128), bf16),
            pltpu.VMEM((8, 2, 128, 128), bf16),
            pltpu.VMEM((8, 2, 128, 128), bf16),
            pltpu.VMEM((8, 2, 128, 128), bf16),
            pltpu.VMEM((2, 128, 1024), bf16),
            pltpu.VMEM((2, 128, 1024), bf16),
            pltpu.VMEM((8, 2, 128, 256), bf16),
            pltpu.VMEM((1024, 128), f32),
            pltpu.VMEM((1024, 128), f32),
            pltpu.VMEM((1024, 128), f32),
            pltpu.VMEM((2, 1024, 1), f32),
            pltpu.VMEM((256, width), f32),
            pltpu.VMEM((width, LANE_SHARE), f32),
            pltpu.SemaphoreType.DMA((3, 4)),
            pltpu.SemaphoreType.DMA((3, 4)),
            pltpu.SemaphoreType.DMA((3, 6)),
            pltpu.SemaphoreType.DMA((3, 6)),
            pltpu.SemaphoreType.DMA((8,)),
            pltpu.SemaphoreType.DMA((8,)),
            pltpu.SemaphoreType.DMA((4, 8)),
            pltpu.SemaphoreType.DMA((4, 8)),
            pltpu.SemaphoreType.DMA((2,)),
            pltpu.SemaphoreType.DMA((2,)),
            pltpu.SemaphoreType.DMA((8,)),
            pltpu.SemaphoreType.DMA((2,)),
        ],
        compiler_params=pltpu.CompilerParams(
            collective_id=2, has_side_effects=True, vmem_limit_bytes=VMEM_LIMIT
        ),
        name="backward",
    )(*values)


SUM_CUTS = tuple((slice(None), pl.ds(k * 384, 384)) for k in range(3))


def expert_weights_kernel(
    x_hbm, plain_hbm, pair_raw, routes, weights, gate_hbm, up_hbm, down_hbm, rows_hbm, pair_hbm, hidden_hbm, gg_hbm, ug_hbm,
    out_part, residual, grads,
    gate_own, up_own, down_own, gate_other, up_other, down_other, mixed, shares,
    x, c, plain, rows, pair_grad, column, gate, up, down,
    both_rows, both_pair, both_hidden, both_gate, gate_buf, up_buf, down_buf,
    g0, g1, g2, g3, g4, g5, got1, got2, sum_send, sum_recv,
    s0, s1, s2, sheld0, sgot1, sheld1, sgot2, ssend, srecv,
    core_got, core_sum, core_qkv, all_got, side_sum, side_got,
    grad_send, grad_recv, core_send, core_recv, part_send, part_recv,
    sem_x, sem_w, sem_own, sem_out, own_sem,
):
    me, core = my_place(), my_core()
    first = me * 4
    side = lax.axis_index("group") // 2
    other = 1 - side
    width = x.shape[-1]
    ff = gate.shape[-1]
    half = pl.ds(pl.multiple_of(core * 64, 64), 64)
    other_half = pl.ds(pl.multiple_of((1 - core) * 64, 64), 64)
    meet(peers() + [sibling(), mirror()])
    core_copy = remote(grads.at[:, other_half], core_got, core_send.at[0], core_recv.at[0], sibling())
    core_copy.start()
    total = CubeSum(
        out_part, x, ROW_CUTS, (g0, g1, g2, g3, g4, g5, c.at[pl.ds(0, 2)], got1, c.at[2], got2, sum_send, sum_recv)
    )
    total.start()
    loads = [
        pltpu.make_async_copy(plain_hbm, plain, sem_x.at[1]),
        pltpu.make_async_copy(pair_raw, pair_grad, sem_x.at[2]),
        pltpu.make_async_copy(x_hbm, x, sem_x.at[0]),
    ]
    for copy in loads:
        copy.start()

    def fetch(e, slot):
        return [
            pltpu.make_async_copy(gate_hbm.at[e], gate.at[slot], sem_w.at[slot, 0]),
            pltpu.make_async_copy(up_hbm.at[e], up.at[slot], sem_w.at[slot, 1]),
            pltpu.make_async_copy(down_hbm.at[e], down.at[slot], sem_w.at[slot, 2]),
        ]

    for copy in fetch(0, 0):
        copy.start()
    loads[0].wait()

    def weigh(block, carry):
        slot_weights(routes, weights, plain, column, first, block)
        return carry

    lax.fori_loop(0, 4, weigh, 0)
    core_copy.wait()
    summed = width + LANE_SHARE
    for j in range(8):
        both = (grads[j, half].astype(f32) + core_got[j].astype(f32)).astype(bf16)
        core_sum[j // 4, j // 2 % 2, j % 2] = both[:, :summed]
        core_qkv[j] = both[:, summed:]
    spread = Spread(lambda j: core_qkv.at[j], lambda i: all_got.at[i], grad_send, grad_recv)
    spread.start()
    spread_own = pltpu.make_async_copy(core_qkv.at[me], all_got.at[me], own_sem)
    spread_own.start()
    small_total = CubeSum(
        core_sum, core_sum, SUM_CUTS, (s0, s1, s2, sheld0, sgot1, sheld1, sgot2, ssend, srecv)
    )
    small_total.start()
    for copy in loads[1:]:
        copy.wait()

    def take(block, carry):
        rows[block] = dot(plain[block], place_rows(x, block)).astype(bf16)
        pair_grad[block] = (pair_grad[block].astype(f32) * column[block]).astype(bf16)
        return carry

    lax.fori_loop(0, 4, take, 0)
    load_part = pltpu.make_async_copy(out_part, x, sem_x.at[0])
    load_part.start()
    side_copy = remote(side_sum, side_got, core_send.at[1], core_recv.at[1], mirror())
    last_copy = remote(shares.at[half], shares.at[half], core_send.at[2], core_recv.at[2], sibling())

    def part_copies(e):
        return [
            pltpu.make_async_copy(gate_buf, gate_own.at[e], sem_out.at[0]),
            pltpu.make_async_copy(up_buf, up_own.at[e], sem_out.at[1]),
            pltpu.make_async_copy(down_buf, down_own.at[e], sem_out.at[2]),
            remote(gate_buf, gate_other.at[e], part_send.at[0], part_recv.at[e, 0], sibling()),
            remote(up_buf, up_other.at[e], part_send.at[1], part_recv.at[e, 1], sibling()),
            remote(down_buf, down_other.at[e], part_send.at[2], part_recv.at[e, 2], sibling()),
        ]

    def sent(e):
        made = part_copies(e)
        for copy in made[:3]:
            copy.wait()
        for copy in made[3:]:
            copy.wait_send()

    def expert(e, carry):
        slot = lax.rem(e, 2)
        mine = expert_rows(e)
        own = [
            pltpu.make_async_copy(rows_hbm.at[:, mine], both_rows.at[side], sem_own.at[0]),
            pltpu.make_async_copy(pair_hbm.at[:, mine], both_pair.at[side], sem_own.at[1]),
            pltpu.make_async_copy(hidden_hbm.at[e], both_hidden.at[side], sem_own.at[2]),
            pltpu.make_async_copy(gg_hbm.at[e], both_gate.at[side, :, pl.ds(0, ff)], sem_own.at[3]),
            pltpu.make_async_copy(ug_hbm.at[e], both_gate.at[side, :, pl.ds(ff, ff)], sem_own.at[4]),
        ]
        for copy in own:
            copy.start()
        for copy in fetch(e, slot):
            copy.wait()

        @pl.when(e < 3)
        def _():
            for copy in fetch(e + 1, 1 - slot):
                copy.start()

        rows_e = rows[:, mine].reshape(TAKEN, width)
        pair_e = pair_grad[:, mine].reshape(TAKEN, width)
        hidden, gate_grad, up_grad = expert_inner(rows_e, pair_e, gate[slot], up[slot], down[slot])
        both_rows[other] = rows_e.reshape(4, SLOT, width)
        both_pair[other] = pair_e.reshape(4, SLOT, width)
        both_hidden[other] = hidden
        both_gate[other, :, 0:ff] = gate_grad
        both_gate[other, :, ff : 2 * ff] = up_grad

        for copy in own:
            copy.wait()

        @pl.when(e >= 1)
        def _():
            sent(e - 1)

        sums = dot_first(both_rows[...].reshape(2 * TAKEN, width), both_gate[...].reshape(2 * TAKEN, 2 * ff))
        gate_buf[...] = sums[:, :ff].astype(bf16)
        up_buf[...] = sums[:, ff:].astype(bf16)
        down_buf[...] = dot_first(
            both_hidden[...].reshape(2 * TAKEN, ff), both_pair[...].reshape(2 * TAKEN, width)
        ).astype(bf16)
        for copy in part_copies(e):
            copy.start()

        @pl.when(e == 0)
        def _():
            small_total.middle()
            load_part.wait()
            total.middle()

        @pl.when(e == 1)
        def _():
            small_total.last()
            total.last()

            def keep_sum(cut, value):
                side_sum[cut] = value.astype(bf16)

            small_total.finish(keep_sum)
            spread.wait()
            spread_own.wait()
            for i in range(8):
                side_sum[:, summed + i * 256 : summed + (i + 1) * 256] = all_got[i]
            side_copy.start()

        @pl.when(e == 2)
        def _():
            def store(cut, value):
                mixed[cut] = (residual[cut] + value).astype(bf16)

            total.finish(store)

        return carry

    lax.fori_loop(0, 4, expert, 0)
    side_copy.wait()
    shares[half] = (side_sum[...].astype(f32) + side_got[...].astype(f32)).astype(bf16)
    last_copy.start()
    total.sent()
    small_total.sent()
    last_copy.wait()
    sent(3)
    for e in range(4):
        for copy in part_copies(e)[3:]:
            copy.wait_recv()


def expert_weights(x, plain, pair, routes, weights, gate_w, up_w, down_w, kept, out_part, residual, grads):
    width = gate_w.shape[1]
    ff = gate_w.shape[-1]
    wide = grads.shape[-1]
    out = [jax.ShapeDtypeStruct(w.shape, bf16) for w in (gate_w, up_w, down_w)]
    sums = cube_sum_scratch(256, width, ROW_CUTS)
    return pl.pallas_call(
        expert_weights_kernel,
        out_shape=(
            *out,
            *out,
            jax.ShapeDtypeStruct((256, width), bf16),
            jax.ShapeDtypeStruct((128, width + LANE_SHARE + 2048), bf16),
        ),
        in_specs=[anywhere()] * 3 + [vmem()] * 2 + [anywhere()] * 9 + [vmem()] * 2,
        out_specs=(anywhere(),) * 6 + (vmem(),) * 2,
        scratch_shapes=[
            pltpu.VMEM((2, 2, 2, 256, width), bf16),
            pltpu.VMEM((3, 2, 256, width), bf16),
            pltpu.VMEM((4, TAKEN, SPAN), bf16),
            pltpu.VMEM((4, TAKEN, width), bf16),
            pltpu.VMEM((4, TAKEN, width), bf16),
            pltpu.VMEM((4, TAKEN, 1), f32),
            pltpu.VMEM((2, width, ff), bf16),
            pltpu.VMEM((2, width, ff), bf16),
            pltpu.VMEM((2, ff, width), bf16),
            pltpu.VMEM((2, 4, SLOT, width), bf16),
            pltpu.VMEM((2, 4, SLOT, width), bf16),
            pltpu.VMEM((2, TAKEN, ff), bf16),
            pltpu.VMEM((2, TAKEN, 2 * ff), bf16),
            pltpu.VMEM((width, ff), bf16),
            pltpu.VMEM((width, ff), bf16),
            pltpu.VMEM((ff, width), bf16),
            *sums[:6],
            sums[7],
            sums[9],
            *sums[10:],
            *cube_sum_scratch(64, width + LANE_SHARE, SUM_CUTS),
            pltpu.VMEM((8, 64, wide), bf16),
            pltpu.VMEM((2, 2, 2, 64, width + LANE_SHARE), bf16),
            pltpu.VMEM((8, 64, 256), bf16),
            pltpu.VMEM((8, 64, 256), bf16),
            pltpu.VMEM((64, width + LANE_SHARE + 2048), bf16),
            pltpu.VMEM((64, width + LANE_SHARE + 2048), bf16),
            pltpu.SemaphoreType.DMA((8,)),
            pltpu.SemaphoreType.DMA((8,)),
            pltpu.SemaphoreType.DMA((3,)),
            pltpu.SemaphoreType.DMA((3,)),
            pltpu.SemaphoreType.DMA((3,)),
            pltpu.SemaphoreType.DMA((4, 3)),
            pltpu.SemaphoreType.DMA((3,)),
            pltpu.SemaphoreType.DMA((2, 3)),
            pltpu.SemaphoreType.DMA((5,)),
            pltpu.SemaphoreType.DMA((3,)),
            pltpu.SemaphoreType.DMA,
        ],
        compiler_params=pltpu.CompilerParams(
            collective_id=3, has_side_effects=True, vmem_limit_bytes=VMEM_LIMIT
        ),
        name="expert_weights",
    )(x, plain, pair, routes, weights, gate_w, up_w, down_w, *kept, out_part, residual, grads)


def finish_kernel(
    gate_own, up_own, down_own, gate_other, up_other, down_other, shares, mixed, token_grad,
    gate_out, up_out, down_out, query_out, key_out, value_out, wo_out, router_out, moe_gain_out, attn_gain_out,
    mixed_out, token_out,
):
    for own, other, out in ((gate_own, gate_other, gate_out), (up_own, up_other, up_out), (down_own, down_other, down_out)):
        out[...] = own[...].astype(f32) + other[...].astype(f32)
    mixed_out[...] = mixed[...]
    token_out[...] = token_grad[...]

    @pl.when(pl.program_id(0) == 0)
    def _():
        width = wo_out.shape[-1]
        wo_out[...] = shares[:, 0:width].astype(f32)
        small = shares[:, width : width + LANE_SHARE].astype(f32).T
        router_out[...] = small[0:32]
        moe_gain_out[...] = small[32:33]
        attn_gain_out[...] = small[33:34]
        low = lanes((128, 128)) < 64
        base = width + LANE_SHARE
        for j in range(8):
            query_out[:, j * 128 : (j + 1) * 128] = shares[:, base + j * 256 : base + j * 256 + 128].astype(f32)
        for j in range(4):
            left = shares[:, base + j * 512 + 128 : base + j * 512 + 256].astype(f32)
            right = shares[:, base + j * 512 + 384 : base + j * 512 + 512].astype(f32)
            where = slice(j * 128, (j + 1) * 128)
            key_out[:, where] = jnp.where(low, left, pltpu.roll(right, 64, 1))
            value_out[:, where] = jnp.where(low, pltpu.roll(left, 64, 1), right)


def finish(parts, shares, mixed, token_grad):
    width = parts[0].shape[1]
    steps = parts[0].shape[0]

    def block(shape):
        return pl.BlockSpec((1,) + shape[1:], lambda e: (e, 0, 0))

    def rows(shape):
        return pl.BlockSpec((shape[0] // steps,) + shape[1:], lambda e: (e, 0))

    def whole(shape):
        return pl.BlockSpec(shape, lambda e: (0,) * len(shape))

    small = [(128, 1024), (128, 512), (128, 512), (128, width), (32, LANE_SHARE), (1, LANE_SHARE), (1, LANE_SHARE)]
    return pl.pallas_call(
        finish_kernel,
        grid=(steps,),
        out_shape=tuple(jax.ShapeDtypeStruct(p.shape, f32) for p in parts[:3])
        + tuple(jax.ShapeDtypeStruct(shape, f32) for shape in small)
        + (jax.ShapeDtypeStruct(mixed.shape, bf16), jax.ShapeDtypeStruct(token_grad.shape, f32)),
        in_specs=[block(p.shape) for p in parts] + [whole(shares.shape), rows(mixed.shape), rows(token_grad.shape)],
        out_specs=tuple(block(p.shape) for p in parts[:3])
        + tuple(whole(shape) for shape in small)
        + (rows(mixed.shape), rows(token_grad.shape)),
        compiler_params=pltpu.CompilerParams(vmem_limit_bytes=VMEM_LIMIT),
        name="finish",
    )(*parts, shares, mixed, token_grad)


def fast_on_device(
    tokens, segments, routes, cotangent, attn_gain, moe_gain, query_weight, key_projection_matrix,
    value_projection_matrix, out_weight, router_weight, gate_weight, up_weight, down_weight,
):
    width = tokens.shape[-1]
    tok = tokens.reshape(256, width)
    cot = cotangent.reshape(256, width)
    my_routes = routes.reshape(256, TOP).T
    (
        attn_in, q, kv, amix, residual, moe_in, weights, wo_all, gains_all, router_all, routes_all,
        cot_all, cot_mirror, routes_mirror, wkv,
    ) = forward(
        tok, cot, query_weight, key_projection_matrix, value_projection_matrix, out_weight,
        attn_gain.reshape(1, 128), moe_gain.reshape(1, 128), router_weight.T, my_routes, segments,
    )
    out_part, in_sum, p_all, *kept, plain_mirror, pair_mirror, moe_mirror, weights_mirror = experts(
        moe_in, weights, cot_mirror, cot_all, routes_all, routes_mirror, gate_weight, up_weight, down_weight
    )
    token_grad, grads, moe_mirror_all = backward(
        cot, residual, in_sum, p_all, my_routes, weights, router_all, moe_in, gains_all, wo_all, amix, attn_in,
        q, kv, segments, tok, query_weight, wkv, moe_mirror,
    )
    *parts, mixed, shares = expert_weights(
        moe_mirror_all, plain_mirror, pair_mirror, routes_mirror, weights_mirror, gate_weight, up_weight, down_weight,
        kept, out_part, residual, grads,
    )
    (
        gate_grad, up_grad, down_grad, query_grad, key_grad, value_grad, wo_grad, router_grad, moe_gain_grad,
        attn_gain_grad, mixed, token_grad,
    ) = finish(parts, shares, mixed, token_grad)
    return (
        mixed.reshape(tokens.shape), token_grad.reshape(tokens.shape), attn_gain_grad.reshape(128),
        moe_gain_grad.reshape(128), query_grad, key_grad, value_grad, wo_grad, router_grad.T,
        gate_grad, up_grad, down_grad,
    )


def fits(mesh):
    return dict(mesh.shape) == {"group": 4, "blk": 4, "head": 2}


def solution(mesh):
    placed = (
        P("group", ("blk", "head"), None),
        P("group", None),
        P("group", ("blk", "head"), None),
        P("group", ("blk", "head"), None),
        P(("blk", "head")),
        P(("blk", "head")),
        P(("blk", "head"), None),
        P(("blk", "head"), None),
        P(("blk", "head"), None),
        P(("blk", "head"), None),
        P(("blk", "head"), None),
        P(("blk", "head"), None, None),
        P(("blk", "head"), None, None),
        P(("blk", "head"), None, None),
    )
    return jax.shard_map(
        fast_on_device if fits(mesh) else on_device,
        mesh=mesh,
        in_specs=placed,
        out_specs=(
            P("group", ("blk", "head"), None),
            P("group", ("blk", "head"), None),
            P(("blk", "head")),
            P(("blk", "head")),
            P(("blk", "head"), None),
            P(("blk", "head"), None),
            P(("blk", "head"), None),
            P(("blk", "head"), None),
            P(("blk", "head"), None),
            P(("blk", "head"), None, None),
            P(("blk", "head"), None, None),
            P(("blk", "head"), None, None),
        ),
        check_vma=False,
    )
```

```python
import functools

import jax
import jax.numpy as jnp
import numpy as np
from jax import lax
from jax.experimental import pallas as pl
from jax.experimental.pallas import tpu as pltpu
from jax.sharding import PartitionSpec as P

QUERY_HEADS = 16
KEY_VALUE_HEADS = 8
HEAD_SIZE = 64
TOP = 8
CAPH = 36


epsilon = 1e-05
rope_base = 10000.0
masked_out = -1e30
key_block = 512


def rms_norm(values, gain_vec):
    return values * lax.rsqrt(jnp.mean(values * values, -1, keepdims=True) + epsilon) * gain_vec


def rotary_embedding(field_vals, places, turn_sign):
    half_dim = field_vals.shape[-1] // 2
    frequency = rope_base ** (-jnp.arange(half_dim, dtype=jnp.float32) * 2.0 / field_vals.shape[-1])
    angles = places.astype(jnp.float32)[:, None] * frequency[None, :]
    cosine = jnp.cos(angles)[:, None, :]
    sine_vals = turn_sign * jnp.sin(angles)[:, None, :]
    first_half = field_vals[..., :half_dim]
    second = field_vals[..., half_dim:]
    return jnp.concatenate(
        [first_half * cosine - second * sine_vals, second * cosine + first_half * sine_vals], -1
    )


def add_rows(running, addend, row_start):
    current = lax.dynamic_slice_in_dim(running, row_start, addend.shape[1], 1)
    return lax.dynamic_update_slice_in_dim(running, current + addend, row_start, 1)


def on_device(
    tokens,
    segments,
    routes,
    cotangent,
    attn_gain,
    moe_gain,
    query_weight,
    key_projection_matrix,
    value_projection_matrix,
    out_weight,
    router_weight,
    gate_weight,
    up_weight,
    down_weight,
):
    head_groups, number_of_rows, width_dim = tokens.shape
    query_per_key_head = QUERY_HEADS // KEY_VALUE_HEADS
    shared_head_count = lax.axis_size("head")
    query_rows = number_of_rows * shared_head_count
    grouped_keys = KEY_VALUE_HEADS // shared_head_count
    scale_val = HEAD_SIZE ** (-0.5)
    number_of_tokens = head_groups * number_of_rows
    seq_length = lax.axis_size("blk") * query_rows
    cycle_index = lax.axis_index("blk")
    local_placement = (
        cycle_index * shared_head_count + lax.axis_index("head")
    ) * number_of_rows + jnp.arange(number_of_rows, dtype=jnp.int32)
    own_start = cycle_index * query_rows
    query_place = own_start + jnp.arange(query_rows, dtype=jnp.int32)
    query_doc = lax.dynamic_slice_in_dim(segments, own_start, query_rows, 1)
    query_full, key_full, value_full, out_full, router_full, gain_attn, gain_moe = (
        lax.all_gather(query_weight, ("blk", "head"), axis=0, tiled=True),
        lax.all_gather(key_projection_matrix, ("blk", "head"), axis=0, tiled=True),
        lax.all_gather(value_projection_matrix, ("blk", "head"), axis=0, tiled=True),
        lax.all_gather(out_weight, ("blk", "head"), axis=0, tiled=True),
        lax.all_gather(router_weight, ("blk", "head"), axis=0, tiled=True),
        lax.all_gather(attn_gain, ("blk", "head"), axis=0, tiled=True),
        lax.all_gather(moe_gain, ("blk", "head"), axis=0, tiled=True),
    )
    flat_rows = tokens.reshape(number_of_tokens, width_dim).astype(jnp.float32)
    attn_normed, attn_pull = jax.vjp(rms_norm, flat_rows, gain_attn.astype(jnp.float32))
    attn_in = attn_normed.astype(jnp.bfloat16)
    query_pre = jnp.dot(attn_in, query_full, preferred_element_type=jnp.float32)
    key_before_rotary = jnp.dot(attn_in, key_full, preferred_element_type=jnp.float32)
    value_low = (
        jnp.dot(attn_in, value_full, preferred_element_type=jnp.float32)
        .astype(jnp.bfloat16)
        .reshape(head_groups, number_of_rows, KEY_VALUE_HEADS * HEAD_SIZE)
    )
    query_low = (
        rotary_embedding(
            query_pre.reshape(head_groups, number_of_rows, QUERY_HEADS, HEAD_SIZE),
            local_placement,
            1.0,
        )
        .astype(jnp.bfloat16)
        .reshape(head_groups, number_of_rows, QUERY_HEADS * HEAD_SIZE)
    )
    key_low = (
        rotary_embedding(
            key_before_rotary.reshape(head_groups, number_of_rows, KEY_VALUE_HEADS, HEAD_SIZE),
            local_placement,
            1.0,
        )
        .astype(jnp.bfloat16)
        .reshape(head_groups, number_of_rows, KEY_VALUE_HEADS * HEAD_SIZE)
    )
    query_split, key_split, value_split = (
        lax.all_to_all(query_low, "head", split_axis=2, concat_axis=1, tiled=True),
        lax.all_to_all(key_low, "head", split_axis=2, concat_axis=1, tiled=True),
        lax.all_to_all(value_low, "head", split_axis=2, concat_axis=1, tiled=True),
    )
    query_vectors = query_split.reshape(
        head_groups, query_rows, grouped_keys, query_per_key_head, HEAD_SIZE
    )

    def key_view(source, offset, sub_rows):
        return lax.dynamic_slice_in_dim(source, offset, sub_rows, 1).reshape(
            head_groups, sub_rows, grouped_keys, HEAD_SIZE
        )

    def scored_at(query_part, key_row_block, q_place, q_doc, key_start, sub_rows):
        raw_scores = (
            jnp.einsum(
                "bqgrd,bkgd->bqgrk", query_part, key_row_block, preferred_element_type=jnp.float32
            )
            * scale_val
        )
        key_place = key_start + jnp.arange(sub_rows, dtype=jnp.int32)
        key_doc = lax.dynamic_slice_in_dim(segments, key_start, sub_rows, 1)
        allowed = (q_place[None, :, None] >= key_place[None, None, :]) & (
            q_doc[:, :, None] == key_doc[:, None, :]
        )
        return (raw_scores, allowed[:, :, None, None, :])

    def scored(key_row_block, key_start, sub_rows):
        return scored_at(query_vectors, key_row_block, query_place, query_doc, key_start, sub_rows)

    stats_shape = (head_groups, query_rows, grouped_keys, query_per_key_head)
    init_state = (
        jnp.full(stats_shape, masked_out, jnp.float32),
        jnp.zeros(stats_shape, jnp.float32),
        jnp.zeros(stats_shape + (HEAD_SIZE,), jnp.float32),
    )
    key_all, value_all = (
        lax.all_gather(key_split, "blk", axis=1, tiled=True),
        lax.all_gather(value_split, "blk", axis=1, tiled=True),
    )
    fold_state = init_state
    total_rows = key_all.shape[1]
    sub_rows = key_block

    def forward_one_block(block_state, block_index):
        offset = block_index * sub_rows
        key_row_block = key_view(key_all, offset, sub_rows)
        value_row_block = key_view(value_all, offset, sub_rows)
        raw_scores, allowed = scored(key_row_block, 0 + offset, sub_rows)
        running_max, running_sum, running_acc = block_state
        masked = jnp.where(allowed, raw_scores, masked_out)
        new_max = jnp.maximum(running_max, jnp.max(masked, -1))
        shrink = jnp.exp(running_max - new_max)
        weights_soft = jnp.where(allowed, jnp.exp(masked - new_max[..., None]), 0.0)
        new_sum = running_sum * shrink + jnp.sum(weights_soft, -1)
        new_acc = running_acc * shrink[..., None] + jnp.einsum(
            "bqgrk,bkgd->bqgrd",
            weights_soft.astype(jnp.bfloat16),
            value_row_block,
            preferred_element_type=jnp.float32,
        )
        return ((new_max, new_sum, new_acc), None)

    fold_state, unused = lax.scan(
        forward_one_block, fold_state, jnp.arange(total_rows // sub_rows, dtype=jnp.int32)
    )
    running_max, running_sum, running_acc = fold_state
    mix_heads = running_acc / running_sum[..., None]
    log_total = running_max + jnp.log(running_sum)
    mix_low = mix_heads.astype(jnp.bfloat16).reshape(
        head_groups, query_rows, grouped_keys * query_per_key_head * HEAD_SIZE
    )
    mix_tokens = lax.all_to_all(mix_low, "head", split_axis=1, concat_axis=2, tiled=True)
    attn_mix = mix_tokens.reshape(number_of_tokens, QUERY_HEADS * HEAD_SIZE)
    residual = flat_rows + jnp.dot(attn_mix, out_full, preferred_element_type=jnp.float32)
    moe_normed, moe_pull = jax.vjp(rms_norm, residual, gain_moe.astype(jnp.float32))
    moe_in = moe_normed.astype(jnp.bfloat16)
    logits = jnp.dot(moe_in, router_full, preferred_element_type=jnp.float32)
    route_flat = routes.reshape(number_of_tokens, TOP)
    experts_all = router_full.shape[1]
    choose = route_flat[:, :, None] == jnp.arange(experts_all, dtype=jnp.int32)[None, None, :]
    choose_float = choose.astype(jnp.float32)
    picked_logits = jnp.einsum("nke,ne->nk", choose_float, logits)
    route_weights = jax.nn.softmax(picked_logits, axis=-1)
    choose_whole = choose.astype(jnp.int32).reshape(head_groups, number_of_rows * TOP, experts_all)
    slot_rank = jnp.sum(jnp.cumsum(choose_whole, 1) * choose_whole, -1) - 1
    slot_index = (slot_rank + jnp.arange(head_groups, dtype=jnp.int32)[:, None] * CAPH).reshape(-1)
    targets = route_flat.reshape(-1)
    lane_count = head_groups * CAPH
    outgoing = (
        jnp.zeros((experts_all, lane_count, width_dim), jnp.bfloat16)
        .at[targets, slot_index]
        .set(jnp.repeat(moe_in, TOP, axis=0))
    )
    arrived = lax.all_to_all(outgoing, ("blk", "head"), split_axis=0, concat_axis=1, tiled=True)
    gate_val = jnp.einsum("end,edf->enf", arrived, gate_weight, preferred_element_type=jnp.float32)
    up_val = jnp.einsum("end,edf->enf", arrived, up_weight, preferred_element_type=jnp.float32)
    hidden_low = (jax.nn.silu(gate_val) * up_val).astype(jnp.bfloat16)
    expert_out = jnp.einsum(
        "enf,efd->end", hidden_low, down_weight, preferred_element_type=jnp.float32
    ).astype(jnp.bfloat16)
    returned = lax.all_to_all(expert_out, ("blk", "head"), split_axis=1, concat_axis=0, tiled=True)
    picked_rows = returned[targets, slot_index].reshape(number_of_tokens, TOP, width_dim)
    moe_out = jnp.einsum(
        "nk,nkd->nd", route_weights, picked_rows, preferred_element_type=jnp.float32
    )
    mixed = (
        (residual + moe_out).astype(jnp.bfloat16).reshape(head_groups, number_of_rows, width_dim)
    )
    grad_full = cotangent.reshape(number_of_tokens, width_dim).astype(jnp.float32)
    weight_grad = jnp.einsum(
        "nkd,nd->nk", picked_rows, grad_full, preferred_element_type=jnp.float32
    )
    pair_grad = (
        (route_weights[:, :, None] * grad_full[:, None, :])
        .astype(jnp.bfloat16)
        .reshape(number_of_tokens * TOP, width_dim)
    )
    grad_outgoing = jnp.zeros_like(outgoing).at[targets, slot_index].set(pair_grad)
    grad_arrived = lax.all_to_all(
        grad_outgoing, ("blk", "head"), split_axis=0, concat_axis=1, tiled=True
    )
    grad_hidden = jnp.einsum(
        "end,efd->enf", grad_arrived, down_weight, preferred_element_type=jnp.float32
    )
    sigmoid_val = jax.nn.sigmoid(gate_val)
    grad_gate = (
        grad_hidden * up_val * sigmoid_val * (1.0 + gate_val * (1.0 - sigmoid_val))
    ).astype(jnp.bfloat16)
    grad_up = (grad_hidden * gate_val * sigmoid_val).astype(jnp.bfloat16)
    down_weight_grad = jnp.einsum(
        "enf,end->efd", hidden_low, grad_arrived, preferred_element_type=jnp.float32
    )
    gate_weight_grad = jnp.einsum(
        "end,enf->edf", arrived, grad_gate, preferred_element_type=jnp.float32
    )
    up_weight_grad = jnp.einsum(
        "end,enf->edf", arrived, grad_up, preferred_element_type=jnp.float32
    )
    pair_back = (
        jnp.einsum("enf,edf->end", grad_gate, gate_weight, preferred_element_type=jnp.float32)
        + jnp.einsum("enf,edf->end", grad_up, up_weight, preferred_element_type=jnp.float32)
    ).astype(jnp.bfloat16)
    grad_returned = lax.all_to_all(
        pair_back, ("blk", "head"), split_axis=1, concat_axis=0, tiled=True
    )
    moe_in_grad = jnp.sum(
        grad_returned[targets, slot_index].reshape(number_of_tokens, TOP, width_dim),
        axis=1,
        dtype=jnp.float32,
    )
    mean_term = jnp.sum(route_weights * weight_grad, -1, keepdims=True)
    logit_grad = jnp.einsum("nk,nke->ne", route_weights * (weight_grad - mean_term), choose_float)
    router_grad = jnp.dot(moe_in.T, logit_grad, preferred_element_type=jnp.float32)
    moe_in_grad = moe_in_grad + jnp.dot(
        logit_grad, router_full.T, preferred_element_type=jnp.float32
    )
    residual_part, moe_gain_grad = moe_pull(moe_in_grad)
    residual_grad = grad_full + residual_part
    out_grad_low = residual_grad.astype(jnp.bfloat16)
    out_weight_grad = jnp.dot(attn_mix.T, out_grad_low, preferred_element_type=jnp.float32)
    mix_grad = (
        jnp.dot(out_grad_low, out_full.T, preferred_element_type=jnp.float32)
        .astype(jnp.bfloat16)
        .reshape(head_groups, number_of_rows, QUERY_HEADS * HEAD_SIZE)
    )
    mix_grad_heads = lax.all_to_all(
        mix_grad, "head", split_axis=2, concat_axis=1, tiled=True
    ).reshape(head_groups, query_rows, grouped_keys, query_per_key_head, HEAD_SIZE)
    delta_term = jnp.sum(mix_grad_heads.astype(jnp.float32) * mix_heads, -1)
    query_zero = jnp.zeros(stats_shape + (HEAD_SIZE,), jnp.float32)
    back_init = (
        query_zero,
        jnp.zeros((head_groups, seq_length, grouped_keys, HEAD_SIZE), jnp.float32),
        jnp.zeros((head_groups, seq_length, grouped_keys, HEAD_SIZE), jnp.float32),
    )
    fold_state = back_init
    total_rows = key_all.shape[1]

    def backward_one_block(block_state, block_index):
        offset = block_index * key_block
        key_start = 0 + offset
        key_row_block = key_view(key_all, offset, key_block)
        value_row_block = key_view(value_all, offset, key_block)
        raw_scores, allowed = scored(key_row_block, key_start, key_block)
        masked = jnp.where(allowed, raw_scores, masked_out)
        probability = jnp.where(allowed, jnp.exp(masked - log_total[..., None]), 0.0)
        prob_grad = jnp.einsum(
            "bqgrd,bkgd->bqgrk", mix_grad_heads, value_row_block, preferred_element_type=jnp.float32
        )
        score_grad = (probability * (prob_grad - delta_term[..., None]) * scale_val).astype(
            jnp.bfloat16
        )
        grad_query = block_state[0] + jnp.einsum(
            "bqgrk,bkgd->bqgrd", score_grad, key_row_block, preferred_element_type=jnp.float32
        )
        value_part_grad = jnp.einsum(
            "bqgrk,bqgrd->bkgd",
            probability.astype(jnp.bfloat16),
            mix_grad_heads,
            preferred_element_type=jnp.float32,
        )
        key_part_grad = jnp.einsum(
            "bqgrk,bqgrd->bkgd", score_grad, query_vectors, preferred_element_type=jnp.float32
        )
        grad_keys = add_rows(block_state[1], key_part_grad, key_start)
        grad_values = add_rows(block_state[2], value_part_grad, key_start)
        return ((grad_query, grad_keys, grad_values), None)

    fold_state, unused = lax.scan(
        backward_one_block, fold_state, jnp.arange(total_rows // key_block, dtype=jnp.int32)
    )
    grad_query, grad_keys, grad_values = fold_state
    key_own, value_own = (
        lax.psum_scatter(
            grad_keys.reshape(head_groups, seq_length, grouped_keys * HEAD_SIZE).astype(
                jnp.bfloat16
            ),
            "blk",
            scatter_dimension=1,
            tiled=True,
        ).astype(jnp.float32),
        lax.psum_scatter(
            grad_values.reshape(head_groups, seq_length, grouped_keys * HEAD_SIZE).astype(
                jnp.bfloat16
            ),
            "blk",
            scatter_dimension=1,
            tiled=True,
        ).astype(jnp.float32),
    )
    query_grad_low = (
        rotary_embedding(
            grad_query.reshape(
                head_groups, query_rows, grouped_keys * query_per_key_head, HEAD_SIZE
            ),
            query_place,
            -1.0,
        )
        .astype(jnp.bfloat16)
        .reshape(head_groups, query_rows, grouped_keys * query_per_key_head * HEAD_SIZE)
    )
    key_grad_low = (
        rotary_embedding(
            key_own.reshape(head_groups, query_rows, grouped_keys, HEAD_SIZE), query_place, -1.0
        )
        .astype(jnp.bfloat16)
        .reshape(head_groups, query_rows, grouped_keys * HEAD_SIZE)
    )
    value_grad_low = value_own.astype(jnp.bfloat16)
    query_back, key_pullback, value_pullback = (
        lax.all_to_all(query_grad_low, "head", split_axis=1, concat_axis=2, tiled=True),
        lax.all_to_all(key_grad_low, "head", split_axis=1, concat_axis=2, tiled=True),
        lax.all_to_all(value_grad_low, "head", split_axis=1, concat_axis=2, tiled=True),
    )
    query_flat = query_back.reshape(number_of_tokens, QUERY_HEADS * HEAD_SIZE)
    flattened_keys = key_pullback.reshape(number_of_tokens, KEY_VALUE_HEADS * HEAD_SIZE)
    flattened_values = value_pullback.reshape(number_of_tokens, KEY_VALUE_HEADS * HEAD_SIZE)
    query_weight_grad = jnp.dot(attn_in.T, query_flat, preferred_element_type=jnp.float32)
    key_weight_grad = jnp.dot(attn_in.T, flattened_keys, preferred_element_type=jnp.float32)
    value_weight_grad = jnp.dot(attn_in.T, flattened_values, preferred_element_type=jnp.float32)
    attn_in_grad = (
        jnp.dot(query_flat, query_full.T, preferred_element_type=jnp.float32)
        + jnp.dot(flattened_keys, key_full.T, preferred_element_type=jnp.float32)
        + jnp.dot(flattened_values, value_full.T, preferred_element_type=jnp.float32)
    )
    input_part, attn_gain_grad = attn_pull(attn_in_grad)
    token_grad = (residual_grad + input_part).reshape(head_groups, number_of_rows, width_dim)
    (
        query_shard,
        key_shard,
        value_shard,
        out_shard,
        router_shard,
        attn_gain_shard,
        moe_gain_shard,
    ) = (
        lax.psum_scatter(
            query_weight_grad.astype(jnp.bfloat16), ("blk", "head"), scatter_dimension=0, tiled=True
        ).astype(jnp.float32),
        lax.psum_scatter(
            key_weight_grad.astype(jnp.bfloat16), ("blk", "head"), scatter_dimension=0, tiled=True
        ).astype(jnp.float32),
        lax.psum_scatter(
            value_weight_grad.astype(jnp.bfloat16), ("blk", "head"), scatter_dimension=0, tiled=True
        ).astype(jnp.float32),
        lax.psum_scatter(
            out_weight_grad.astype(jnp.bfloat16), ("blk", "head"), scatter_dimension=0, tiled=True
        ).astype(jnp.float32),
        lax.psum_scatter(
            router_grad.astype(jnp.bfloat16), ("blk", "head"), scatter_dimension=0, tiled=True
        ).astype(jnp.float32),
        lax.psum_scatter(
            attn_gain_grad.astype(jnp.bfloat16), ("blk", "head"), scatter_dimension=0, tiled=True
        ).astype(jnp.float32),
        lax.psum_scatter(
            moe_gain_grad.astype(jnp.bfloat16), ("blk", "head"), scatter_dimension=0, tiled=True
        ).astype(jnp.float32),
    )
    summed = (
        lax.psum(query_shard.astype(jnp.bfloat16), "group").astype(jnp.float32),
        lax.psum(key_shard.astype(jnp.bfloat16), "group").astype(jnp.float32),
        lax.psum(value_shard.astype(jnp.bfloat16), "group").astype(jnp.float32),
        lax.psum(out_shard.astype(jnp.bfloat16), "group").astype(jnp.float32),
        lax.psum(router_shard.astype(jnp.bfloat16), "group").astype(jnp.float32),
        lax.psum(attn_gain_shard.astype(jnp.bfloat16), "group").astype(jnp.float32),
        lax.psum(moe_gain_shard.astype(jnp.bfloat16), "group").astype(jnp.float32),
        lax.psum(gate_weight_grad.astype(jnp.bfloat16), "group").astype(jnp.float32),
        lax.psum(up_weight_grad.astype(jnp.bfloat16), "group").astype(jnp.float32),
        lax.psum(down_weight_grad.astype(jnp.bfloat16), "group").astype(jnp.float32),
    )
    return (
        mixed,
        token_grad,
        summed[5],
        summed[6],
        summed[0],
        summed[1],
        summed[2],
        summed[3],
        summed[4],
        summed[7],
        summed[8],
        summed[9],
    )


bf16 = jnp.bfloat16
f32 = jnp.float32
MESH_ID = pl.DeviceIdType.MESH
VMEM_LIMIT = 67 * 1000 * 1000
COLOURS = ((0, 96), (96, 80), (176, 80))
LINKS = (("head", 1), ("blk", 1), ("blk", 2), ("group", 2), ("group", 1))
ORDERS = ((0, 1, 2), (1, 2, 0), (2, 0, 1))


def vmem():
    return pl.BlockSpec(memory_space=pltpu.VMEM)


def anywhere():
    return pl.BlockSpec(memory_space=pl.ANY)


def dot_last(left, right):
    return lax.dot_general(left, right, (((1,), (1,)), ((), ())), preferred_element_type=f32)


def dot_first(left, right):
    return lax.dot_general(left, right, (((0,), (0,)), ((), ())), preferred_element_type=f32)


def dot(left, right):
    return jnp.dot(left, right, preferred_element_type=f32)


def my_place():
    return lax.axis_index("blk") * 2 + lax.axis_index("head")


def peer(step):
    place = lax.rem(my_place() + step, 8)
    return place, {"blk": place // 2, "head": lax.rem(place, 2)}


def neighbour(link):
    if link == 0:
        return {"head": 1 - lax.axis_index("head")}
    blk = lax.axis_index("blk")
    if link == 1:
        return {"blk": blk + 1 - 2 * lax.rem(blk, 2)}
    return {"blk": lax.rem(blk + 2, 4)}


def my_bits():
    blk = lax.axis_index("blk")
    return (lax.axis_index("head"), lax.rem(blk, 2), blk // 2)


def meet_all():
    barrier = pltpu.get_barrier_semaphore()
    for step in range(1, 8):
        pl.semaphore_signal(barrier, 1, device_id=peer(step)[1], device_id_type=MESH_ID)
    pl.semaphore_wait(barrier, 7)


def remote(src, dst, send, recv, target):
    return pltpu.make_async_remote_copy(
        src_ref=src, dst_ref=dst, send_sem=send, recv_sem=recv, device_id=target, device_id_type=MESH_ID
    )


def cube_index(bits, fixed, rows):
    entries = [pl.ds(fixed[link], 1) if link in fixed else pl.ds(0, 2) for link in (2, 1, 0)]
    return tuple(entries) + (pl.ds(*rows),)


def lanes(shape):
    return lax.broadcasted_iota(jnp.int32, shape, len(shape) - 1)


def turned(u):
    low = lax.rem(lanes(u.shape), 64) < 32
    return jnp.where(low, -pltpu.roll(u, 96, 1), pltpu.roll(u, 32, 1))


def two_heads(q):
    low = lanes(q.shape) < 64
    return jnp.concatenate([jnp.where(low, q, 0.0), jnp.where(low, pltpu.roll(q, 64, 1), 0.0)], 0)


def two_heads_high(g):
    high = lanes(g.shape) >= 64
    return jnp.concatenate([jnp.where(high, pltpu.roll(g, 64, 1), 0.0), jnp.where(high, g, 0.0)], 0)


def block_probability(q_ref, kv_ref, docs, segs, s, i):
    short = isinstance(i, int)
    first = 0 if short else pl.multiple_of((i - 4) * 128, 128)
    count = (i + 1) * 128 if short else 640
    mine = pl.ds(i * 128 if short else pl.multiple_of(i * 128, 128), 128)
    q2 = two_heads(q_ref[s, mine].astype(f32))
    kv = kv_ref[s, pl.ds(first, count)]
    raw = dot_last((q2 * 0.125).astype(bf16), kv)
    q_place = i * 128 + lax.broadcasted_iota(jnp.int32, (128, count), 0)
    k_place = first + lanes((128, count))
    q_doc = docs[s, mine]
    keys = pl.ds(first, count)
    k_doc = jnp.where(s == 0, segs[0:1, keys], segs[1:2, keys]).astype(f32)
    allowed = (q_place >= k_place) & (q_doc == k_doc)
    allowed = jnp.concatenate([allowed, allowed], 0)
    masked = jnp.where(allowed, raw, masked_out)
    top = jnp.max(masked, -1, keepdims=True)
    weight = jnp.exp(masked - top)
    probability = weight * (1.0 / jnp.sum(weight, -1, keepdims=True))
    return first, count, q2, kv, probability


def norm_back(values, gain, grad):
    scale = lax.rsqrt(jnp.mean(values * values, -1, keepdims=True) + epsilon)
    inner = grad * gain
    along = jnp.mean(values * inner, -1, keepdims=True)
    out = scale * inner - values * (scale * scale * scale * along)
    gain_grad = jnp.sum(grad * values * scale, 0, keepdims=True)
    return out, gain_grad


def expert_inner(rows_e, pair_e, gate_w, up_w, down_w):
    gate_val = dot(rows_e, gate_w)
    up_val = dot(rows_e, up_w)
    sig = 1.0 / (1.0 + jnp.exp(-gate_val))
    silu = gate_val * sig
    hidden = (silu * up_val).astype(bf16)
    hidden_grad = dot_last(pair_e, down_w)
    gate_grad = (hidden_grad * up_val * sig * (1.0 + gate_val * (1.0 - sig))).astype(bf16)
    up_grad = (hidden_grad * silu).astype(bf16)
    return hidden, gate_grad, up_grad


def sibling():
    group = lax.axis_index("group")
    return {"group": group + 1 - 2 * lax.rem(group, 2)}


def mirror():
    return {"group": lax.rem(lax.axis_index("group") + 2, 4)}


def my_core():
    return lax.rem(lax.axis_index("group"), 2)


def meet(targets):
    barrier = pltpu.get_barrier_semaphore()
    for target in targets:
        pl.semaphore_signal(barrier, 1, device_id=target, device_id_type=MESH_ID)
    pl.semaphore_wait(barrier, len(targets))


def peers():
    return [peer(step)[1] for step in range(1, 8)]


def cube_entry(fixed):
    return tuple(pl.ds(fixed[link], 1) if link in fixed else pl.ds(0, 2) for link in (2, 1, 0))


class Gather:
    def __init__(self, items, send, recv):
        self.items, self.send, self.recv, self.bits = items, send, recv, my_bits()

    def copies(self, step):
        made = []
        for k, (src, place, order) in enumerate(self.items):
            fixed = {link: self.bits[link] for link in order[step:]}
            where = place(cube_entry(fixed))
            here = where
            if step == 0:
                here = src
                where = place((self.bits[2], self.bits[1], self.bits[0]))
            made.append(remote(here, where, self.send.at[step, k], self.recv.at[step, k], neighbour(order[step])))
        return made

    def start(self, step):
        for copy in self.copies(step):
            copy.start()

    def wait(self, step):
        for copy in self.copies(step):
            copy.wait_recv()

    def advance(self, step):
        for before, after in zip(self.copies(step - 1), self.copies(step)):
            before.wait_recv()
            after.start()

    def sent(self):
        for step in range(3):
            for copy in self.copies(step):
                copy.wait_send()


SHARES = ((0, 48), (96, 48), (176, 48), (48, 48), (144, 32), (224, 32))
HALF_SHARES = tuple(
    tuple((s * 128 + start, count) for start, count in ((0, 32), (32, 32), (64, 16), (80, 16), (96, 16), (112, 16)))
    for s in range(2)
)


def row_items(src, dst, shares=SHARES):
    def item(k):
        start, count = shares[k]
        return (src.at[pl.ds(start, count)], lambda entry: dst.at[entry + (pl.ds(start, count),)], ORDERS[k % 3])

    return [item(k) for k in range(len(shares))]


ROW_CUTS = tuple((pl.ds(start, count), slice(None)) for start, count in SHARES)


class CubeSum:
    def __init__(self, source, part, cuts, scratch, base=0):
        self.source, self.part, self.cuts = source, part, cuts
        self.kept = tuple((pl.ds(row.start - base, row.size) if base else row, lane) for row, lane in cuts)
        *self.got, self.held0, self.got1, self.held1, self.got2, self.send, self.recv = scratch
        self.bits = my_bits()
        self.orders = [ORDERS[k % 3] for k in range(len(cuts))]

    def copy(self, step, k):
        order, cut, kept = self.orders[k], self.cuts[k], self.kept[k]
        other = 1 - self.bits[order[step]]
        if step == 0:
            src = self.source.at[cube_entry({order[0]: other}) + cut]
            dst = self.got[k]
        elif step == 1:
            src = self.held0.at[(other, slice(None)) + kept]
            dst = self.got1.at[(slice(None),) + kept]
        else:
            src = self.held1.at[(other,) + kept]
            dst = self.got2.at[kept]
        return remote(src, dst, self.send.at[step, k], self.recv.at[step, k], neighbour(order[step]))

    def start(self):
        for k in range(len(self.cuts)):
            self.copy(0, k).start()

    def middle(self):
        for k, order in enumerate(self.orders):
            self.copy(0, k).wait_recv()
            cut, kept = self.cuts[k], self.kept[k]

            def add(w, carry, k=k, order=order, cut=cut, kept=kept):
                u, v = w // 2, lax.rem(w, 2)
                mine = {order[0]: self.bits[order[0]], order[1]: u, order[2]: v}
                there = {order[0]: 0, order[1]: u, order[2]: v}
                landed = self.got[k][there[2], there[1], there[0]].astype(f32)
                here = self.part[(mine[2], mine[1], mine[0]) + cut].astype(f32)
                self.held0[(u, v) + kept] = (here + landed).astype(bf16)
                return carry

            lax.fori_loop(0, 4, add, 0)
            self.copy(1, k).start()

    def last(self):
        for k, order in enumerate(self.orders):
            self.copy(1, k).wait_recv()
            kept = self.kept[k]

            def add(v, carry, order=order, kept=kept):
                here = self.held0[(self.bits[order[1]], v) + kept].astype(f32)
                self.held1[(v,) + kept] = (here + self.got1[(v,) + kept].astype(f32)).astype(bf16)
                return carry

            lax.fori_loop(0, 2, add, 0)
            self.copy(2, k).start()

    def finish(self, store):
        for k, order in enumerate(self.orders):
            self.copy(2, k).wait_recv()
            kept = self.kept[k]
            store(
                self.cuts[k], self.held1[(self.bits[order[2]],) + kept].astype(f32) + self.got2[kept].astype(f32)
            )

    def sent(self):
        for step in range(3):
            for k in range(len(self.cuts)):
                self.copy(step, k).wait_send()


def cube_sum_scratch(rows, width, cuts):
    def share(k):
        row, lane = cuts[k]
        shape = [2, 2, 2, rows if row == slice(None) else row.size, width if lane == slice(None) else lane.size]
        shape[2 - ORDERS[k % 3][0]] = 1
        return pltpu.VMEM(tuple(shape), bf16)

    return [
        *(share(k) for k in range(len(cuts))),
        pltpu.VMEM((2, 2, rows, width), bf16),
        pltpu.VMEM((2, rows, width), bf16),
        pltpu.VMEM((2, rows, width), bf16),
        pltpu.VMEM((rows, width), bf16),
        pltpu.SemaphoreType.DMA((3, len(cuts))),
        pltpu.SemaphoreType.DMA((3, len(cuts))),
    ]


class Spread:
    def __init__(self, src, dst, send, recv):
        self.src, self.dst, self.send, self.recv = src, dst, send, recv

    def copy(self, step):
        place, target = peer(step)
        return remote(self.src(place), self.dst(my_place()), self.send.at[step], self.recv.at[step], target)

    def start(self):
        for step in range(1, 8):
            self.copy(step).start()

    def wait(self):
        for step in range(1, 8):
            self.copy(step).wait()


def rope_tables():
    frequency = 10000.0 ** (-(np.arange(128) % 32) * 2.0 / 64)
    near = np.arange(128)[:, None] * frequency[None, :]
    far = np.arange(8)[:, None] * 128.0 * frequency[None, :]
    return tuple(np.asarray(t, np.float32) for t in (np.cos(near), np.sin(near), np.cos(far), np.sin(far)))


def fill_rope(near_cos, near_sin, far_cos, far_sin, cosine, sine):
    for j in range(8):
        rows = pl.ds(j * 128, 128)
        fc, fs = far_cos[pl.ds(j, 1)], far_sin[pl.ds(j, 1)]
        cosine[rows] = fc * near_cos[...] - fs * near_sin[...]
        sine[rows] = fs * near_cos[...] + fc * near_sin[...]


THIRDS = ((0, 384), (384, 384), (768, 256))


def fill_docs(segs, docs):
    for s in range(2):
        for j in range(8):
            row = segs[pl.ds(s, 1), pl.ds(j * 128, 128)].astype(f32)
            docs[s, pl.ds(j * 128, 128)] = jnp.broadcast_to(row, (128, 128)).T[:, 0:1]


def fill_upper(upper):
    row = lax.broadcasted_iota(jnp.int32, upper.shape, 0)
    upper[...] = jnp.where(row < lanes(upper.shape), 1.0, 0.0).astype(bf16)


def forward_kernel(
    tok, cot, wq, wk, wv, wo, attn_gain, moe_gain, router, routes, segs, near_cos, near_sin, far_cos, far_sin,
    attn_hbm, q_out, kv_out, amix, residual_out, moe_in_out, weights_out, wo_hbm, gains_all, router_all, routes_all,
    cot_hbm, cot_mirror, routes_mirror, wkv,
    tok_all, attn_all, cot_all, wo_all, w_all, mix, cosine, sine, docs, gains,
    tok_send, tok_recv, cot_send, cot_recv, small_send, small_recv, mix_send, mix_recv, wo_send, wo_recv,
    pair_send, pair_recv, own_sem, out_sem,
):
    me, core = my_place(), my_core()
    half = pl.ds(pl.multiple_of(core * 64, 64), 64)
    own_entry = (me // 4, lax.rem(me // 2, 2), lax.rem(me, 2))
    first_row = lax.broadcasted_iota(jnp.int32, (16, 128), 0)
    both_gains = jnp.where(first_row == 1, moe_gain[...].astype(f32), 0.0)
    gains[...] = jnp.where(first_row == 0, attn_gain[...].astype(f32), both_gains).astype(bf16)
    for j in range(4):
        low = lanes((128, 128)) < 64
        k_two, v_two = (w[:, j * 128 : (j + 1) * 128].astype(f32) for w in (wk, wv))
        wkv[:, j * 256 : j * 256 + 128] = jnp.where(low, k_two, pltpu.roll(v_two, 64, 1)).astype(bf16)
        wkv[:, j * 256 + 128 : j * 256 + 256] = jnp.where(low, pltpu.roll(k_two, 64, 1), v_two).astype(bf16)
    meet(peers() + [sibling(), mirror()])
    tok_gather = Gather(row_items(tok, tok_all), tok_send, tok_recv)
    tok_gather.start(0)
    pairs = (
        (lambda j: wq.at[half, pl.ds(j * 128, 128)], lambda i: w_all.at[i, half, pl.ds(0, 128)]),
        (lambda j: wkv.at[half, pl.ds(j * 128, 128)], lambda i: w_all.at[i, half, pl.ds(128, 128)]),
        (lambda j: gains, lambda i: gains_all.at[:, pl.ds(i * 128, 128)]),
        (lambda j: router, lambda i: router_all.at[:, pl.ds(i * 128, 128)]),
        (lambda j: routes.at[:, pl.ds(0, 128)], lambda i: routes_all.at[:, pl.ds(i * 128, 128)]),
        (lambda j: routes.at[:, pl.ds(128, 128)], lambda i: routes_all.at[:, pl.ds(1024 + i * 128, 128)]),
    )
    smalls = [Spread(src, dst, small_send.at[k], small_recv.at[k]) for k, (src, dst) in enumerate(pairs)]
    own = [pltpu.make_async_copy(src(me), dst(me), own_sem.at[k]) for k, (src, dst) in enumerate(pairs)]
    own += [
        pltpu.make_async_copy(tok, tok_all.at[own_entry], own_sem.at[6]),
        pltpu.make_async_copy(cot, cot_all.at[own_entry], own_sem.at[7]),
        pltpu.make_async_copy(wo.at[half], wo_all.at[own_entry + (half,)], own_sem.at[8]),
    ]
    for copy in own:
        copy.start()
    for small in smalls:
        small.start()
    fill_rope(near_cos, near_sin, far_cos, far_sin, cosine, sine)
    for copy in own:
        copy.wait()
    tok_gather.advance(1)
    fill_docs(segs, docs)
    tok_gather.advance(2)
    for small in smalls:
        small.wait()
    w_pair = remote(w_all.at[:, half], w_all.at[:, half], pair_send.at[3], pair_recv.at[3], sibling())
    w_pair.start()
    tok_gather.wait(2)
    w_pair.wait()

    def wo_item(k):
        where = (half, pl.ds(*THIRDS[k]))
        return (wo.at[where], lambda entry: wo_all.at[entry + where], ORDERS[k])

    wo_gather = Gather([wo_item(k) for k in range(3)], wo_send, wo_recv)
    wo_gather.start(0)
    cot_gather = Gather(row_items(cot, cot_all), cot_send, cot_recv)
    cot_gather.start(0)
    cot_copy = remote(cot, cot_mirror, pair_send.at[1], pair_recv.at[1], mirror())
    cot_copy.start()
    routes_copy = remote(routes_all, routes_mirror, pair_send.at[0], pair_recv.at[0], mirror())
    routes_copy.start()

    gain_row = gains_all[0:1].astype(f32)

    def project(j, carry):
        rows = pl.ds(pl.multiple_of(j * 128, 128), 128)
        x = tok_all[j // 4, lax.rem(j // 2, 2), lax.rem(j, 2)].astype(f32)
        scale = lax.rsqrt(jnp.mean(x * x, -1, keepdims=True) + epsilon)
        attn_in = (x * scale * gain_row).astype(bf16)
        attn_all[j] = attn_in
        both = dot(attn_in, w_all[...].reshape(1024, 256))
        c = cosine[rows]
        n = sine[rows]
        c2 = jnp.concatenate([c, c], 0)
        n2 = jnp.concatenate([n, n], 0)
        q = both[:, :128]
        kv = both[:, 128:]
        q = (q * c2 + turned(q) * n2).astype(bf16)
        kv = jnp.where(lanes(kv.shape) < 64, kv * c2 + turned(kv) * n2, kv).astype(bf16)
        for s in range(2):
            q_out[s, rows] = q[s * 128 : (s + 1) * 128]
            kv_out[s, rows] = kv[s * 128 : (s + 1) * 128]
        return carry

    lax.fori_loop(0, 8, project, 0)
    attn_copy = pltpu.make_async_copy(attn_all, attn_hbm, out_sem.at[0])
    attn_copy.start()
    wo_gather.advance(1)
    cot_gather.advance(1)
    wo_pair = remote(
        wo_all.at[:, :, :, half], wo_all.at[:, :, :, half], pair_send.at[2], pair_recv.at[2], sibling()
    )

    def mix_copy(i):
        return remote(
            mix.at[i],
            amix.at[:, :, pl.ds(pl.multiple_of(me * 128, 128), 128)],
            mix_send.at[i],
            mix_recv.at[me],
            {"blk": i // 2, "head": lax.rem(i, 2)},
        )

    def send_mix(i):
        @pl.when(me != i)
        def _():
            mix_copy(i).start()

    def attend_block(i):
        def attend(s, carry):
            first, count, q2, kv, probability = block_probability(q_out, kv_out, docs, segs, s, i)
            mixed = dot(probability.astype(bf16), kv)
            low = lanes((128, 128)) < 64
            mix[i, s] = jnp.where(low, pltpu.roll(mixed[:128], 64, 1), mixed[128:]).astype(bf16)
            return carry

        lax.fori_loop(0, 2, attend, 0)

    for i in range(4):
        attend_block(i)
        if i > 0:
            send_mix(i - 1)
        if i == 2:
            wo_gather.advance(2)

    def attend_long(i, carry):
        attend_block(i)
        send_mix(i - 1)

        @pl.when(i == 4)
        def _():
            cot_gather.advance(2)

        return carry

    lax.fori_loop(4, 8, attend_long, 0)
    send_mix(7)
    wo_gather.wait(2)
    wo_pair.start()
    mine = pltpu.make_async_copy(
        mix.at[me], amix.at[:, :, pl.ds(pl.multiple_of(me * 128, 128), 128)], own_sem.at[0]
    )
    mine.start()
    wo_pair.wait()
    wo_copy = pltpu.make_async_copy(wo_all, wo_hbm, out_sem.at[1])
    wo_copy.start()
    for step in range(1, 8):
        place, target = peer(step)
        remote(
            mix.at[place],
            amix.at[:, :, pl.ds(pl.multiple_of(place * 128, 128), 128)],
            mix_send.at[place],
            mix_recv.at[place],
            target,
        ).wait()
    mine.wait()
    width = tok.shape[-1]
    residual = tok[...].astype(f32) + dot(amix[...].reshape(256, width), wo_all[...].reshape(width, width))
    residual_out[...] = residual
    scale = lax.rsqrt(jnp.mean(residual * residual, -1, keepdims=True) + epsilon)
    moe_in = (residual * scale * gains_all[1:2].astype(f32)).astype(bf16)
    moe_in_out[...] = moe_in
    logits = dot_last(router_all[...], moe_in)
    experts = lax.broadcasted_iota(jnp.int32, logits.shape, 0)
    picked = [
        jnp.sum(jnp.where(experts == routes[pl.ds(k, 1)], logits, 0.0), 0, keepdims=True) for k in range(TOP)
    ]
    picked = jnp.concatenate(picked, 0)
    weight = jnp.exp(picked - jnp.max(picked, 0, keepdims=True))
    weights_out[...] = weight / jnp.sum(weight, 0, keepdims=True)
    cot_gather.wait(2)
    cot_out = pltpu.make_async_copy(cot_all, cot_hbm, out_sem.at[2])
    cot_out.start()
    routes_copy.wait()
    cot_copy.wait()
    tok_gather.sent()
    cot_gather.sent()
    wo_gather.sent()
    attn_copy.wait()
    wo_copy.wait()
    cot_out.wait()


def forward(*values):
    tok = values[0]
    width = tok.shape[-1]
    tables = tuple(jnp.asarray(t) for t in rope_tables())
    return pl.pallas_call(
        forward_kernel,
        out_shape=(
            jax.ShapeDtypeStruct((8, 256, width), bf16),
            jax.ShapeDtypeStruct((2, 1024, 128), bf16),
            jax.ShapeDtypeStruct((2, 1024, 128), bf16),
            jax.ShapeDtypeStruct((2, 128, width), bf16),
            jax.ShapeDtypeStruct((256, width), f32),
            jax.ShapeDtypeStruct((256, width), bf16),
            jax.ShapeDtypeStruct((8, 256), f32),
            jax.ShapeDtypeStruct((2, 2, 2, 128, width), bf16),
            jax.ShapeDtypeStruct((16, width), bf16),
            jax.ShapeDtypeStruct((32, width), bf16),
            jax.ShapeDtypeStruct((8, 2048), jnp.int32),
            jax.ShapeDtypeStruct((2, 2, 2, 256, width), bf16),
            jax.ShapeDtypeStruct((256, width), bf16),
            jax.ShapeDtypeStruct((8, 2048), jnp.int32),
            jax.ShapeDtypeStruct((128, 1024), bf16),
        ),
        in_specs=[vmem()] * 15,
        out_specs=(
            anywhere(), vmem(), vmem(), vmem(), vmem(), vmem(), vmem(), anywhere(), vmem(), vmem(), vmem(),
            anywhere(), vmem(), vmem(), vmem(),
        ),
        scratch_shapes=[
            pltpu.VMEM((2, 2, 2, 256, width), bf16),
            pltpu.VMEM((8, 256, width), bf16),
            pltpu.VMEM((2, 2, 2, 256, width), bf16),
            pltpu.VMEM((2, 2, 2, 128, width), bf16),
            pltpu.VMEM((8, 128, 256), bf16),
            pltpu.VMEM((8, 2, 128, 128), bf16),
            pltpu.VMEM((1024, 128), f32),
            pltpu.VMEM((1024, 128), f32),
            pltpu.VMEM((2, 1024, 1), f32),
            pltpu.VMEM((16, 128), bf16),
            pltpu.SemaphoreType.DMA((3, 6)),
            pltpu.SemaphoreType.DMA((3, 6)),
            pltpu.SemaphoreType.DMA((3, 6)),
            pltpu.SemaphoreType.DMA((3, 6)),
            pltpu.SemaphoreType.DMA((6, 8)),
            pltpu.SemaphoreType.DMA((6, 8)),
            pltpu.SemaphoreType.DMA((8,)),
            pltpu.SemaphoreType.DMA((8,)),
            pltpu.SemaphoreType.DMA((3, 3)),
            pltpu.SemaphoreType.DMA((3, 3)),
            pltpu.SemaphoreType.DMA((4,)),
            pltpu.SemaphoreType.DMA((4,)),
            pltpu.SemaphoreType.DMA((9,)),
            pltpu.SemaphoreType.DMA((3,)),
        ],
        compiler_params=pltpu.CompilerParams(
            collective_id=0, has_side_effects=True, vmem_limit_bytes=VMEM_LIMIT
        ),
        name="forward",
    )(*values, *tables)


SLOT = 4 * CAPH
SPAN = 512
TAKEN = 4 * SLOT


def build_rows(routes, upper, plain, first_expert, block):
    columns = pl.ds(pl.multiple_of(block * SPAN, SPAN), SPAN)
    chosen = routes[:, columns]
    masks = [jnp.max((chosen == first_expert + e).astype(f32), 0, keepdims=True) for e in range(4)]
    mask = jnp.concatenate(masks + [jnp.zeros((4, SPAN), f32)], 0)
    rank = dot(mask.astype(bf16), upper[...])
    slots = lax.broadcasted_iota(jnp.int32, (SLOT, SPAN), 0).astype(f32)
    for e in range(4):
        hit = (slots == rank[e : e + 1]) & (mask[e : e + 1] > 0.0)
        plain[block, e * SLOT : (e + 1) * SLOT] = jnp.where(hit, 1.0, 0.0).astype(bf16)


def slot_weights(routes, weights, plain, column, first_expert, block):
    columns = pl.ds(pl.multiple_of(block * SPAN, SPAN), SPAN)
    chosen = routes[:, columns]
    weight = weights[:, columns]
    for e in range(4):
        share = jnp.sum(jnp.where(chosen == first_expert + e, weight, 0.0), 0, keepdims=True)
        mine = pl.ds(e * SLOT, SLOT)
        column[block, mine] = jnp.sum(plain[block, mine].astype(f32) * share, -1, keepdims=True)


def place_rows(source, block):
    width = source.shape[-1]
    rows = pl.ds(pl.multiple_of((block // 2) * 128, 128), 128)
    return source[lax.rem(block, 2), :, :, rows].reshape(SPAN, width)


def expert_rows(e):
    return pl.ds(pl.multiple_of(e * SLOT, 16), SLOT)


def experts_kernel(
    moe_in, my_weights, cot_mirror, cot_hbm, routes, routes_mirror, gate_hbm, up_hbm, down_hbm,
    out_part, in_sum, p_all, rows_out, pair_out, hidden_out, gate_out, up_out, plain_mirror, pair_mirror, moe_mirror,
    weights_other,
    x, c, cm, upper, plain, rows, pair_grad, pair_in, column, p_col, weights, p_part,
    gate, up, down, hid_buf, gg_buf, ug_buf, part_buf,
    row_send, row_recv, cm_send, cm_recv, w_send, w_recv, p_send, p_recv, pair_send, pair_recv,
    sem_c, sem_w, sem_rows, sem_h, sem_part, own_sem, *sums,
):
    me = my_place()
    first = me * 4
    width = x.shape[-1]
    count = 2 * SLOT
    own_entry = (me // 4, lax.rem(me // 2, 2), lax.rem(me, 2))
    meet(peers() + [mirror()])
    gathers = [
        Gather(row_items(moe_in, x, HALF_SHARES[s]), row_send.at[s], row_recv.at[s]) for s in range(2)
    ]
    gathers[0].start(0)

    def weight_lanes(s, i):
        return weights.at[:, pl.ds(pl.multiple_of(s * 1024 + i * 128, 128), 128)]

    own = [
        pltpu.make_async_copy(moe_in, x.at[own_entry], own_sem.at[0]),
        pltpu.make_async_copy(my_weights.at[:, pl.ds(0, 128)], weight_lanes(0, me), own_sem.at[1]),
        pltpu.make_async_copy(my_weights.at[:, pl.ds(128, 128)], weight_lanes(1, me), own_sem.at[2]),
        pltpu.make_async_copy(cot_mirror, cm.at[own_entry], own_sem.at[3]),
    ]
    for copy in own:
        copy.start()
    weight_spreads = [
        Spread(
            lambda j, s=s: my_weights.at[:, pl.ds(s * 128, 128)],
            lambda i, s=s: weight_lanes(s, i),
            w_send.at[s],
            w_recv.at[s],
        )
        for s in range(2)
    ]
    for spread in weight_spreads:
        spread.start()
    load_c = pltpu.make_async_copy(cot_hbm, c, sem_c)
    load_c.start()

    def fetch(e, slot):
        return [
            pltpu.make_async_copy(gate_hbm.at[e], gate.at[slot], sem_w.at[slot, 0]),
            pltpu.make_async_copy(up_hbm.at[e], up.at[slot], sem_w.at[slot, 1]),
            pltpu.make_async_copy(down_hbm.at[e], down.at[slot], sem_w.at[slot, 2]),
        ]

    for copy in fetch(0, 0):
        copy.start()
    fill_upper(upper)

    def build(block, carry):
        build_rows(routes, upper, plain, first, block)
        return carry

    lax.fori_loop(0, 2, build, 0)
    for copy in own:
        copy.wait()
    gathers[0].advance(1)
    lax.fori_loop(2, 4, build, 0)
    load_c.wait()

    def take_c(block, carry):
        pair_grad[block] = dot(plain[block], place_rows(c, block)).astype(bf16)
        return carry

    gathers[0].advance(2)
    gathers[1].start(0)
    lax.fori_loop(0, 4, take_c, 0)
    for spread in weight_spreads:
        spread.wait()
    weights_copy = remote(weights, weights_other, pair_send.at[0], pair_recv.at[0], mirror())
    weights_copy.start()

    def weigh(block, carry):
        slot_weights(routes, weights, plain, column, first, block)
        return carry

    lax.fori_loop(0, 4, weigh, 0)
    cm_gather = Gather(row_items(cot_mirror, cm), cm_send, cm_recv)
    moe_copy = remote(moe_in, moe_mirror, pair_send.at[1], pair_recv.at[1], mirror())
    p_part[...] = jnp.zeros_like(p_part)

    def take_x(block, carry):
        rows[block] = dot(plain[block], place_rows(x, block)).astype(bf16)
        return carry

    def keep_rows(s):
        pair = pl.ds(2 * s, 2)
        return pltpu.make_async_copy(rows.at[pair], rows_out.at[pair], sem_rows.at[s])

    def keep(s, e, slot):
        where = pl.ds(pl.multiple_of(s * count, 16), count)
        return [
            pltpu.make_async_copy(hid_buf.at[slot], hidden_out.at[e, where], sem_h.at[slot, 0]),
            pltpu.make_async_copy(gg_buf.at[slot], gate_out.at[e, where], sem_h.at[slot, 1]),
            pltpu.make_async_copy(ug_buf.at[slot], up_out.at[e, where], sem_h.at[slot, 2]),
        ]

    def total_of(s):
        cuts = tuple((pl.ds(*cut), slice(None)) for cut in HALF_SHARES[s])
        return CubeSum(x, x, cuts, sums[12 * s : 12 * s + 12], s * 128)

    totals = [total_of(s) for s in range(2)]

    def store(cut, value):
        in_sum[cut] = value

    def one_half(s, carry):
        for t in range(2):

            @pl.when(s == t)
            def _(t=t):
                gathers[t].wait(2)
                if t == 0:
                    gathers[1].advance(1)

        lax.fori_loop(2 * s, 2 * s + 2, take_x, 0)
        keep_rows(s).start()

        @pl.when(s == 0)
        def _():
            gathers[1].advance(2)
            cm_gather.start(0)
            moe_copy.start()

        def expert(e, inner):
            slot = lax.rem(e, 2)
            mine = expert_rows(e)
            pair = pl.ds(2 * s, 2)
            for copy in fetch(e, slot):
                copy.wait()

            @pl.when(4 * s + e < 7)
            def _():
                for copy in fetch(lax.rem(e + 1, 4), 1 - slot):
                    copy.start()

            rows_e = rows[pair, mine].reshape(count, width)
            weight_e = column[pair, mine].reshape(count, 1)
            pair_e = (pair_grad[pair, mine].reshape(count, width).astype(f32) * weight_e).astype(bf16)
            pair_grad[pair, mine] = pair_e.reshape(2, SLOT, width)
            hidden, gate_grad, up_grad = expert_inner(rows_e, pair_e, gate[slot], up[slot], down[slot])

            @pl.when(e >= 2)
            def _():
                for copy in keep(s, e - 2, slot):
                    copy.wait()

            hid_buf[slot] = hidden
            gg_buf[slot] = gate_grad
            ug_buf[slot] = up_grad
            for copy in keep(s, e, slot):
                copy.start()

            @pl.when(e == 0)
            def _():
                keep_rows(s).wait()

            out_e = dot(hidden, down[slot]).astype(bf16).astype(f32)
            p = jnp.sum(out_e * pair_e.astype(f32), -1, keepdims=True)
            p_col[pair, mine] = p.reshape(2, SLOT, 1)
            rows[pair, mine] = (out_e * weight_e).astype(bf16).reshape(2, SLOT, width)
            back = dot_last(gate_grad, gate[slot]) + dot_last(up_grad, up[slot])
            pair_in[pair, mine] = back.astype(bf16).reshape(2, SLOT, width)

            @pl.when(4 * s + e == 3)
            def _():
                cm_gather.advance(1)

            @pl.when(4 * s + e == 5)
            def _():
                cm_gather.advance(2)

            @pl.when(4 * s + e == 6)
            def _():
                totals[0].middle()

            return inner

        lax.fori_loop(0, 4, expert, 0)
        for copy in keep(s, 2, 0) + keep(s, 3, 1):
            copy.wait()
        for t in range(2):

            @pl.when(s == t)
            def _(t=t):
                gathers[t].sent()

        def combine_in(block, inner):
            y = lax.rem(block, 2)
            back = dot_first(plain[block], pair_in[block]).astype(bf16)
            mine = pl.ds(pl.multiple_of(s * 128, 128), 128)
            x[y, :, :, mine] = back.reshape(2, 2, 128, width)
            for e in range(4):
                slots = pl.ds(e * SLOT, SLOT)
                p = jnp.sum(plain[block, slots].astype(f32) * p_col[block, slots], 0, keepdims=True)
                for d in range(4):
                    p_part[y * 4 + d, pl.ds(e, 1), mine] = p[:, d * 128 : (d + 1) * 128]
            return inner

        lax.fori_loop(2 * s, 2 * s + 2, combine_in, 0)
        for t in range(2):

            @pl.when(s == t)
            def _(t=t):
                totals[t].start()
                if t == 1:
                    totals[0].last()

        return carry

    lax.fori_loop(0, 2, one_half, 0)
    keep_pair = pltpu.make_async_copy(pair_grad, pair_out, sem_rows.at[0])
    keep_pair.start()
    p_spread = Spread(lambda j: p_part.at[j], lambda i: p_all.at[i], p_send, p_recv)
    p_spread.start()
    p_own = pltpu.make_async_copy(p_part.at[me], p_all.at[me], own_sem.at[0])
    p_own.start()

    def part_copy(block):
        slot = lax.rem(block, 2)
        rows_of = pl.ds(pl.multiple_of((block // 2) * 128, 128), 128)
        return pltpu.make_async_copy(
            part_buf.at[slot], out_part.at[lax.rem(block, 2), :, :, rows_of], sem_part.at[slot]
        )

    def combine_out(block, carry):
        slot = lax.rem(block, 2)

        @pl.when(block >= 2)
        def _():
            part_copy(block - 2).wait()

        out = dot_first(plain[block], rows[block]).astype(bf16)
        part_buf[slot] = out.reshape(2, 2, 128, width)
        part_copy(block).start()
        return carry

    lax.fori_loop(0, 4, combine_out, 0)
    totals[0].finish(store)
    keep_pair.wait()

    def build_mirror(block, carry):
        build_rows(routes_mirror, upper, plain, first, block)
        return carry

    lax.fori_loop(0, 2, build_mirror, 0)
    totals[1].middle()
    lax.fori_loop(2, 4, build_mirror, 0)
    keep_plain = pltpu.make_async_copy(plain, plain_mirror, sem_rows.at[0])
    keep_plain.start()
    cm_gather.wait(2)

    def take_mirror(block, carry):
        pair_grad[block] = dot(plain[block], place_rows(cm, block)).astype(bf16)
        return carry

    lax.fori_loop(0, 2, take_mirror, 0)
    totals[1].last()
    lax.fori_loop(2, 4, take_mirror, 0)
    keep_mirror = pltpu.make_async_copy(pair_grad, pair_mirror, sem_rows.at[1])
    keep_mirror.start()
    p_spread.wait()
    p_own.wait()
    part_copy(2).wait()
    part_copy(3).wait()
    totals[1].finish(store)
    for total in totals:
        total.sent()
    keep_plain.wait()
    keep_mirror.wait()
    cm_gather.sent()
    weights_copy.wait()
    moe_copy.wait()


def half_cuts(s):
    return tuple((pl.ds(*cut), slice(None)) for cut in HALF_SHARES[s])


def experts(moe_in, my_weights, cot_mirror, cot_all, routes, routes_mirror, gate_w, up_w, down_w):
    width = moe_in.shape[-1]
    ff = gate_w.shape[-1]
    return pl.pallas_call(
        experts_kernel,
        out_shape=(
            jax.ShapeDtypeStruct((2, 2, 2, 256, width), bf16),
            jax.ShapeDtypeStruct((256, width), f32),
            jax.ShapeDtypeStruct((8, 8, 256), f32),
            jax.ShapeDtypeStruct((4, TAKEN, width), bf16),
            jax.ShapeDtypeStruct((4, TAKEN, width), bf16),
            jax.ShapeDtypeStruct((4, TAKEN, ff), bf16),
            jax.ShapeDtypeStruct((4, TAKEN, ff), bf16),
            jax.ShapeDtypeStruct((4, TAKEN, ff), bf16),
            jax.ShapeDtypeStruct((4, TAKEN, SPAN), bf16),
            jax.ShapeDtypeStruct((4, TAKEN, width), bf16),
            jax.ShapeDtypeStruct((256, width), bf16),
            jax.ShapeDtypeStruct((8, 2048), f32),
        ),
        in_specs=[vmem(), vmem(), vmem(), anywhere(), vmem(), vmem(), anywhere(), anywhere(), anywhere()],
        out_specs=(anywhere(), vmem(), vmem()) + (anywhere(),) * 7 + (vmem(), vmem()),
        scratch_shapes=[
            pltpu.VMEM((2, 2, 2, 256, width), bf16),
            pltpu.VMEM((2, 2, 2, 256, width), bf16),
            pltpu.VMEM((2, 2, 2, 256, width), bf16),
            pltpu.VMEM((SPAN, SPAN), bf16),
            pltpu.VMEM((4, TAKEN, SPAN), bf16),
            pltpu.VMEM((4, TAKEN, width), bf16),
            pltpu.VMEM((4, TAKEN, width), bf16),
            pltpu.VMEM((4, TAKEN, width), bf16),
            pltpu.VMEM((4, TAKEN, 1), f32),
            pltpu.VMEM((4, TAKEN, 1), f32),
            pltpu.VMEM((8, 2048), f32),
            pltpu.VMEM((8, 8, 256), f32),
            pltpu.VMEM((2, width, ff), bf16),
            pltpu.VMEM((2, width, ff), bf16),
            pltpu.VMEM((2, ff, width), bf16),
            pltpu.VMEM((2, 2 * SLOT, ff), bf16),
            pltpu.VMEM((2, 2 * SLOT, ff), bf16),
            pltpu.VMEM((2, 2 * SLOT, ff), bf16),
            pltpu.VMEM((2, 2, 2, 128, width), bf16),
            pltpu.SemaphoreType.DMA((2, 3, 6)),
            pltpu.SemaphoreType.DMA((2, 3, 6)),
            pltpu.SemaphoreType.DMA((3, 6)),
            pltpu.SemaphoreType.DMA((3, 6)),
            pltpu.SemaphoreType.DMA((2, 8)),
            pltpu.SemaphoreType.DMA((2, 8)),
            pltpu.SemaphoreType.DMA((8,)),
            pltpu.SemaphoreType.DMA((8,)),
            pltpu.SemaphoreType.DMA((2,)),
            pltpu.SemaphoreType.DMA((2,)),
            pltpu.SemaphoreType.DMA,
            pltpu.SemaphoreType.DMA((2, 3)),
            pltpu.SemaphoreType.DMA((2,)),
            pltpu.SemaphoreType.DMA((2, 3)),
            pltpu.SemaphoreType.DMA((2,)),
            pltpu.SemaphoreType.DMA((4,)),
            *cube_sum_scratch(128, width, half_cuts(0)),
            *cube_sum_scratch(128, width, half_cuts(1)),
        ],
        compiler_params=pltpu.CompilerParams(
            collective_id=1, has_side_effects=True, vmem_limit_bytes=VMEM_LIMIT
        ),
        name="experts",
    )(moe_in, my_weights, cot_mirror, cot_all, routes, routes_mirror, gate_w, up_w, down_w)


LANE_SHARE = 128


def backward_kernel(
    cot, residual, in_sum, p_all, routes, weights, router, moe_in, gains_all, wo_hbm, amix, attn_hbm, q_in, kv_in,
    segs, near_cos, near_sin, far_cos, far_sin, tok, wq, wkv, moe_mirror,
    token_grad, grads, mirror_hbm,
    wo_all, attn_all, wq_all, wkv_all, mm, mix_grad, mg, gq, gkv, gq_rows, gkv_rows, g_all, kv_sum, cosine, sine, docs,
    residual_grad, small_grad,
    w_send, w_recv, mm_send, mm_recv, mg_send, mg_recv, g_send, g_recv, pair_send, pair_recv, own_sem, load_sem,
):
    me, core = my_place(), my_core()
    width = tok.shape[-1]
    meet(peers() + [sibling()])
    half = pl.ds(pl.multiple_of(core * 64, 64), 64)
    own_entry = (me // 4, lax.rem(me // 2, 2), lax.rem(me, 2))
    own = [
        pltpu.make_async_copy(wq.at[half], wq_all.at[own_entry + (half,)], own_sem.at[0]),
        pltpu.make_async_copy(wkv.at[half], wkv_all.at[own_entry + (half,)], own_sem.at[1]),
        pltpu.make_async_copy(moe_mirror, mm.at[own_entry], own_sem.at[2]),
    ]
    loads = [
        pltpu.make_async_copy(wo_hbm, wo_all, load_sem.at[0]),
        pltpu.make_async_copy(attn_hbm, attn_all, load_sem.at[1]),
    ]
    for copy in own + loads:
        copy.start()

    def weight_item(src, dst, start, count, order):
        rows = pl.ds(pl.multiple_of(core * 64 + start, 16), count)
        return (src.at[rows], lambda entry: dst.at[entry + (rows,)], order)

    w_gather = Gather(
        [
            weight_item(wq, wq_all, 0, 48, ORDERS[0]),
            weight_item(wq, wq_all, 48, 16, ORDERS[1]),
            weight_item(wkv, wkv_all, 0, 32, ORDERS[1]),
            weight_item(wkv, wkv_all, 32, 32, ORDERS[2]),
        ],
        w_send,
        w_recv,
    )
    w_gather.start(0)
    mm_gather = Gather(row_items(moe_mirror, mm), mm_send, mm_recv)
    mm_gather.start(0)
    ids = lax.broadcasted_iota(jnp.int32, (32, 256), 0)
    dense = jnp.zeros((32, 256), f32)
    for k in range(TOP):
        dense = dense + jnp.where(ids == routes[pl.ds(k, 1)], weights[pl.ds(k, 1)], 0.0)
    p = jnp.concatenate([p_all[i, 0:4] for i in range(8)], 0)
    logit_grad = (p - dense * jnp.sum(p, 0, keepdims=True)).astype(bf16)
    moe_in_grad = in_sum[...] + dot_first(logit_grad, router[...])
    part, moe_gain_grad = norm_back(residual[...], gains_all[1:2].astype(f32), moe_in_grad)
    total = cot[...].astype(f32) + part
    residual_grad[...] = total
    low_grad = total.astype(bf16)
    for copy in loads[:1]:
        copy.wait()
    back = dot_last(low_grad, wo_all[...].reshape(width, width)).astype(bf16)
    for j in range(8):
        mix_grad[j] = back[:, j * 128 : (j + 1) * 128].reshape(2, 128, 128)
    mix_spread = Spread(lambda j: mix_grad.at[j], lambda i: mg.at[i], mg_send, mg_recv)
    mix_spread.start()
    mix_own = pltpu.make_async_copy(mix_grad.at[me], mg.at[me], own_sem.at[3])
    mix_own.start()
    for copy in own:
        copy.wait()
    w_gather.advance(1)
    fill_rope(near_cos, near_sin, far_cos, far_sin, cosine, sine)
    fill_docs(segs, docs)
    wo_grad = dot_first(amix[...].reshape(256, width), low_grad)
    grads[:, :, 0:width] = wo_grad.astype(bf16).reshape(8, 128, width)
    padded = jnp.concatenate([logit_grad, jnp.zeros((LANE_SHARE - 32, 256), bf16)], 0)
    small_grad[...] = lax.dot_general(moe_in[...], padded, (((0,), (1,)), ((), ())), preferred_element_type=f32)
    mix_spread.wait()
    mix_own.wait()
    mm_gather.advance(1)

    def lane_block(i):
        return pl.ds(pl.multiple_of(i * 128, 128), 128)

    def spread_of(s):
        return [
            Spread(lambda j: gq.at[j, s], lambda i: gq_rows.at[s, :, lane_block(i)], g_send.at[2 * s], g_recv.at[2 * s]),
            Spread(
                lambda j: gkv.at[j, s],
                lambda i: gkv_rows.at[s, :, lane_block(i)],
                g_send.at[2 * s + 1],
                g_recv.at[2 * s + 1],
            ),
        ]

    def own_blocks(s):
        return [
            pltpu.make_async_copy(gq.at[me, s], gq_rows.at[s, :, lane_block(me)], own_sem.at[4 + 2 * s]),
            pltpu.make_async_copy(gkv.at[me, s], gkv_rows.at[s, :, lane_block(me)], own_sem.at[5 + 2 * s]),
        ]

    def attend(s, carry):
        kv_sum[...] = jnp.zeros_like(kv_sum)

        def back_block(i):
            first, count, q2, kv, probability = block_probability(q_in, kv_in, docs, segs, s, i)
            g2 = two_heads_high(mg[i, s].astype(f32)).astype(bf16)
            prob_grad = dot_last(g2, kv)
            delta = jnp.sum(probability * prob_grad, -1, keepdims=True)
            score_grad = (probability * (prob_grad - delta) * 0.125).astype(bf16)
            dq = dot(score_grad, kv)
            keys = pl.ds(first, count)
            kv_sum[keys] += dot_first(score_grad, q2.astype(bf16)) + dot_first(probability.astype(bf16), g2)
            low = lanes((128, 128)) < 64
            dq = jnp.where(low, dq[:128], pltpu.roll(dq[128:], 64, 1))
            rows = pl.ds(i * 128 if isinstance(i, int) else pl.multiple_of(i * 128, 128), 128)
            dq = (dq * cosine[rows] - turned(dq) * sine[rows]).astype(bf16)
            gq[i, s] = dq
            g_all[i, s, :, 0:128] = dq

        for i in range(4):
            back_block(i)
            if i == 2:

                @pl.when(s == 0)
                def _():
                    w_gather.advance(2)

        def back_long(i, inner):
            back_block(i)

            @pl.when(s * 8 + i == 6)
            def _():
                mm_gather.advance(2)

            return inner

        lax.fori_loop(4, 8, back_long, 0)

        def keys_back(i, inner):
            rows = pl.ds(pl.multiple_of(i * 128, 128), 128)
            dkv = kv_sum[rows]
            low = lanes((128, 128)) < 64
            dkv = jnp.where(low, dkv * cosine[rows] - turned(dkv) * sine[rows], dkv).astype(bf16)
            gkv[i, s] = dkv
            g_all[i, s, :, 128:256] = dkv
            return inner

        lax.fori_loop(0, 8, keys_back, 0)
        for spread in spread_of(s):
            spread.start()
        for copy in own_blocks(s):
            copy.start()
        return carry

    lax.fori_loop(0, 2, attend, 0)
    keep_own = own_blocks(0) + own_blocks(1)
    w_gather.wait(2)
    shared = [
        remote(w.at[:, :, :, half], w.at[:, :, :, half], pair_send.at[k], pair_recv.at[k], sibling())
        for k, w in enumerate((wq_all, wkv_all))
    ]
    for copy in shared:
        copy.start()
    loads[1].wait()
    w_grad = dot_first(attn_all[...].reshape(2048, width), g_all[...].reshape(2048, 256))
    grads[:, :, width + LANE_SHARE :] = w_grad.astype(bf16).reshape(8, 128, 256)
    for copy in shared + keep_own:
        copy.wait()
    for s in range(2):
        for spread in spread_of(s):
            spread.wait()
    back = dot_last(gq_rows[...].reshape(256, 1024), wq_all[...].reshape(width, 1024))
    back = back + dot_last(gkv_rows[...].reshape(256, 1024), wkv_all[...].reshape(width, 1024))
    part, attn_gain_grad = norm_back(tok[...].astype(f32), gains_all[0:1].astype(f32), back)
    token_grad[...] = residual_grad[...] + part
    row = lax.broadcasted_iota(jnp.int32, (LANE_SHARE, width), 0)
    gain_rows = jnp.where(row == 32, moe_gain_grad, jnp.where(row == 33, attn_gain_grad, 0.0))
    grads[:, :, width : width + LANE_SHARE] = (small_grad[...] + gain_rows.T).astype(bf16).reshape(8, 128, LANE_SHARE)
    mm_gather.wait(2)
    mm_out = pltpu.make_async_copy(mm, mirror_hbm, load_sem.at[0])
    mm_out.start()
    w_gather.sent()
    mm_gather.sent()
    mm_out.wait()


def backward(*values):
    tok = values[15]
    width = tok.shape[-1]
    tables = tuple(jnp.asarray(t) for t in rope_tables())
    values = values[:15] + tables + values[15:]
    specs = [vmem()] * 23
    specs[9] = specs[11] = anywhere()
    return pl.pallas_call(
        backward_kernel,
        out_shape=(
            jax.ShapeDtypeStruct((256, width), f32),
            jax.ShapeDtypeStruct((8, 128, width + 256 + LANE_SHARE), bf16),
            jax.ShapeDtypeStruct((2, 2, 2, 256, width), bf16),
        ),
        in_specs=specs,
        out_specs=(vmem(), vmem(), anywhere()),
        scratch_shapes=[
            pltpu.VMEM((2, 2, 2, 128, width), bf16),
            pltpu.VMEM((8, 256, width), bf16),
            pltpu.VMEM((2, 2, 2, 128, width), bf16),
            pltpu.VMEM((2, 2, 2, 128, width), bf16),
            pltpu.VMEM((2, 2, 2, 256, width), bf16),
            pltpu.VMEM((8, 2, 128, 128), bf16),
            pltpu.VMEM((8, 2, 128, 128), bf16),
            pltpu.VMEM((8, 2, 128, 128), bf16),
            pltpu.VMEM((8, 2, 128, 128), bf16),
            pltpu.VMEM((2, 128, 1024), bf16),
            pltpu.VMEM((2, 128, 1024), bf16),
            pltpu.VMEM((8, 2, 128, 256), bf16),
            pltpu.VMEM((1024, 128), f32),
            pltpu.VMEM((1024, 128), f32),
            pltpu.VMEM((1024, 128), f32),
            pltpu.VMEM((2, 1024, 1), f32),
            pltpu.VMEM((256, width), f32),
            pltpu.VMEM((width, LANE_SHARE), f32),
            pltpu.SemaphoreType.DMA((3, 4)),
            pltpu.SemaphoreType.DMA((3, 4)),
            pltpu.SemaphoreType.DMA((3, 6)),
            pltpu.SemaphoreType.DMA((3, 6)),
            pltpu.SemaphoreType.DMA((8,)),
            pltpu.SemaphoreType.DMA((8,)),
            pltpu.SemaphoreType.DMA((4, 8)),
            pltpu.SemaphoreType.DMA((4, 8)),
            pltpu.SemaphoreType.DMA((2,)),
            pltpu.SemaphoreType.DMA((2,)),
            pltpu.SemaphoreType.DMA((8,)),
            pltpu.SemaphoreType.DMA((2,)),
        ],
        compiler_params=pltpu.CompilerParams(
            collective_id=2, has_side_effects=True, vmem_limit_bytes=VMEM_LIMIT
        ),
        name="backward",
    )(*values)


SUM_CUTS = tuple((slice(None), pl.ds(k * 384, 384)) for k in range(3))


def expert_weights_kernel(
    x_hbm, plain_hbm, pair_raw, routes, weights, gate_hbm, up_hbm, down_hbm, rows_hbm, pair_hbm, hidden_hbm, gg_hbm, ug_hbm,
    out_part, residual, grads,
    gate_own, up_own, down_own, gate_other, up_other, down_other, mixed, shares,
    x, c, plain, rows, pair_grad, column, gate, up, down,
    both_rows, both_pair, both_hidden, both_gate, gate_buf, up_buf, down_buf,
    g0, g1, g2, g3, g4, g5, got1, got2, sum_send, sum_recv,
    s0, s1, s2, sheld0, sgot1, sheld1, sgot2, ssend, srecv,
    core_got, core_sum, core_qkv, all_got, side_sum, side_got,
    grad_send, grad_recv, core_send, core_recv, part_send, part_recv,
    sem_x, sem_w, sem_own, sem_out, own_sem,
):
    me, core = my_place(), my_core()
    first = me * 4
    side = lax.axis_index("group") // 2
    other = 1 - side
    width = x.shape[-1]
    ff = gate.shape[-1]
    half = pl.ds(pl.multiple_of(core * 64, 64), 64)
    other_half = pl.ds(pl.multiple_of((1 - core) * 64, 64), 64)
    meet(peers() + [sibling(), mirror()])
    core_copy = remote(grads.at[:, other_half], core_got, core_send.at[0], core_recv.at[0], sibling())
    core_copy.start()
    total = CubeSum(
        out_part, x, ROW_CUTS, (g0, g1, g2, g3, g4, g5, c.at[pl.ds(0, 2)], got1, c.at[2], got2, sum_send, sum_recv)
    )
    total.start()
    loads = [
        pltpu.make_async_copy(plain_hbm, plain, sem_x.at[1]),
        pltpu.make_async_copy(pair_raw, pair_grad, sem_x.at[2]),
        pltpu.make_async_copy(x_hbm, x, sem_x.at[0]),
    ]
    for copy in loads:
        copy.start()

    def fetch(e, slot):
        return [
            pltpu.make_async_copy(gate_hbm.at[e], gate.at[slot], sem_w.at[slot, 0]),
            pltpu.make_async_copy(up_hbm.at[e], up.at[slot], sem_w.at[slot, 1]),
            pltpu.make_async_copy(down_hbm.at[e], down.at[slot], sem_w.at[slot, 2]),
        ]

    for copy in fetch(0, 0):
        copy.start()
    loads[0].wait()

    def weigh(block, carry):
        slot_weights(routes, weights, plain, column, first, block)
        return carry

    lax.fori_loop(0, 4, weigh, 0)
    core_copy.wait()
    summed = width + LANE_SHARE
    for j in range(8):
        both = (grads[j, half].astype(f32) + core_got[j].astype(f32)).astype(bf16)
        core_sum[j // 4, j // 2 % 2, j % 2] = both[:, :summed]
        core_qkv[j] = both[:, summed:]
    spread = Spread(lambda j: core_qkv.at[j], lambda i: all_got.at[i], grad_send, grad_recv)
    spread.start()
    spread_own = pltpu.make_async_copy(core_qkv.at[me], all_got.at[me], own_sem)
    spread_own.start()
    small_total = CubeSum(
        core_sum, core_sum, SUM_CUTS, (s0, s1, s2, sheld0, sgot1, sheld1, sgot2, ssend, srecv)
    )
    small_total.start()
    for copy in loads[1:]:
        copy.wait()

    def take(block, carry):
        rows[block] = dot(plain[block], place_rows(x, block)).astype(bf16)
        pair_grad[block] = (pair_grad[block].astype(f32) * column[block]).astype(bf16)
        return carry

    lax.fori_loop(0, 4, take, 0)
    load_part = pltpu.make_async_copy(out_part, x, sem_x.at[0])
    load_part.start()
    side_copy = remote(side_sum, side_got, core_send.at[1], core_recv.at[1], mirror())
    last_copy = remote(shares.at[half], shares.at[half], core_send.at[2], core_recv.at[2], sibling())

    def part_copies(e):
        return [
            pltpu.make_async_copy(gate_buf, gate_own.at[e], sem_out.at[0]),
            pltpu.make_async_copy(up_buf, up_own.at[e], sem_out.at[1]),
            pltpu.make_async_copy(down_buf, down_own.at[e], sem_out.at[2]),
            remote(gate_buf, gate_other.at[e], part_send.at[0], part_recv.at[e, 0], sibling()),
            remote(up_buf, up_other.at[e], part_send.at[1], part_recv.at[e, 1], sibling()),
            remote(down_buf, down_other.at[e], part_send.at[2], part_recv.at[e, 2], sibling()),
        ]

    def sent(e):
        made = part_copies(e)
        for copy in made[:3]:
            copy.wait()
        for copy in made[3:]:
            copy.wait_send()

    def expert(e, carry):
        slot = lax.rem(e, 2)
        mine = expert_rows(e)
        own = [
            pltpu.make_async_copy(rows_hbm.at[:, mine], both_rows.at[side], sem_own.at[0]),
            pltpu.make_async_copy(pair_hbm.at[:, mine], both_pair.at[side], sem_own.at[1]),
            pltpu.make_async_copy(hidden_hbm.at[e], both_hidden.at[side], sem_own.at[2]),
            pltpu.make_async_copy(gg_hbm.at[e], both_gate.at[side, :, pl.ds(0, ff)], sem_own.at[3]),
            pltpu.make_async_copy(ug_hbm.at[e], both_gate.at[side, :, pl.ds(ff, ff)], sem_own.at[4]),
        ]
        for copy in own:
            copy.start()
        for copy in fetch(e, slot):
            copy.wait()

        @pl.when(e < 3)
        def _():
            for copy in fetch(e + 1, 1 - slot):
                copy.start()

        rows_e = rows[:, mine].reshape(TAKEN, width)
        pair_e = pair_grad[:, mine].reshape(TAKEN, width)
        hidden, gate_grad, up_grad = expert_inner(rows_e, pair_e, gate[slot], up[slot], down[slot])
        both_rows[other] = rows_e.reshape(4, SLOT, width)
        both_pair[other] = pair_e.reshape(4, SLOT, width)
        both_hidden[other] = hidden
        both_gate[other, :, 0:ff] = gate_grad
        both_gate[other, :, ff : 2 * ff] = up_grad

        for copy in own:
            copy.wait()

        @pl.when(e >= 1)
        def _():
            sent(e - 1)

        sums = dot_first(both_rows[...].reshape(2 * TAKEN, width), both_gate[...].reshape(2 * TAKEN, 2 * ff))
        gate_buf[...] = sums[:, :ff].astype(bf16)
        up_buf[...] = sums[:, ff:].astype(bf16)
        down_buf[...] = dot_first(
            both_hidden[...].reshape(2 * TAKEN, ff), both_pair[...].reshape(2 * TAKEN, width)
        ).astype(bf16)
        for copy in part_copies(e):
            copy.start()

        @pl.when(e == 0)
        def _():
            small_total.middle()
            load_part.wait()
            total.middle()

        @pl.when(e == 1)
        def _():
            small_total.last()
            total.last()

            def keep_sum(cut, value):
                side_sum[cut] = value.astype(bf16)

            small_total.finish(keep_sum)
            spread.wait()
            spread_own.wait()
            for i in range(8):
                side_sum[:, summed + i * 256 : summed + (i + 1) * 256] = all_got[i]
            side_copy.start()

        @pl.when(e == 2)
        def _():
            def store(cut, value):
                mixed[cut] = (residual[cut] + value).astype(bf16)

            total.finish(store)

        return carry

    lax.fori_loop(0, 4, expert, 0)
    side_copy.wait()
    shares[half] = (side_sum[...].astype(f32) + side_got[...].astype(f32)).astype(bf16)
    last_copy.start()
    total.sent()
    small_total.sent()
    last_copy.wait()
    sent(3)
    for e in range(4):
        for copy in part_copies(e)[3:]:
            copy.wait_recv()


def expert_weights(x, plain, pair, routes, weights, gate_w, up_w, down_w, kept, out_part, residual, grads):
    width = gate_w.shape[1]
    ff = gate_w.shape[-1]
    wide = grads.shape[-1]
    out = [jax.ShapeDtypeStruct(w.shape, bf16) for w in (gate_w, up_w, down_w)]
    sums = cube_sum_scratch(256, width, ROW_CUTS)
    return pl.pallas_call(
        expert_weights_kernel,
        out_shape=(
            *out,
            *out,
            jax.ShapeDtypeStruct((256, width), bf16),
            jax.ShapeDtypeStruct((128, width + LANE_SHARE + 2048), bf16),
        ),
        in_specs=[anywhere()] * 3 + [vmem()] * 2 + [anywhere()] * 9 + [vmem()] * 2,
        out_specs=(anywhere(),) * 6 + (vmem(),) * 2,
        scratch_shapes=[
            pltpu.VMEM((2, 2, 2, 256, width), bf16),
            pltpu.VMEM((3, 2, 256, width), bf16),
            pltpu.VMEM((4, TAKEN, SPAN), bf16),
            pltpu.VMEM((4, TAKEN, width), bf16),
            pltpu.VMEM((4, TAKEN, width), bf16),
            pltpu.VMEM((4, TAKEN, 1), f32),
            pltpu.VMEM((2, width, ff), bf16),
            pltpu.VMEM((2, width, ff), bf16),
            pltpu.VMEM((2, ff, width), bf16),
            pltpu.VMEM((2, 4, SLOT, width), bf16),
            pltpu.VMEM((2, 4, SLOT, width), bf16),
            pltpu.VMEM((2, TAKEN, ff), bf16),
            pltpu.VMEM((2, TAKEN, 2 * ff), bf16),
            pltpu.VMEM((width, ff), bf16),
            pltpu.VMEM((width, ff), bf16),
            pltpu.VMEM((ff, width), bf16),
            *sums[:6],
            sums[7],
            sums[9],
            *sums[10:],
            *cube_sum_scratch(64, width + LANE_SHARE, SUM_CUTS),
            pltpu.VMEM((8, 64, wide), bf16),
            pltpu.VMEM((2, 2, 2, 64, width + LANE_SHARE), bf16),
            pltpu.VMEM((8, 64, 256), bf16),
            pltpu.VMEM((8, 64, 256), bf16),
            pltpu.VMEM((64, width + LANE_SHARE + 2048), bf16),
            pltpu.VMEM((64, width + LANE_SHARE + 2048), bf16),
            pltpu.SemaphoreType.DMA((8,)),
            pltpu.SemaphoreType.DMA((8,)),
            pltpu.SemaphoreType.DMA((3,)),
            pltpu.SemaphoreType.DMA((3,)),
            pltpu.SemaphoreType.DMA((3,)),
            pltpu.SemaphoreType.DMA((4, 3)),
            pltpu.SemaphoreType.DMA((3,)),
            pltpu.SemaphoreType.DMA((2, 3)),
            pltpu.SemaphoreType.DMA((5,)),
            pltpu.SemaphoreType.DMA((3,)),
            pltpu.SemaphoreType.DMA,
        ],
        compiler_params=pltpu.CompilerParams(
            collective_id=3, has_side_effects=True, vmem_limit_bytes=VMEM_LIMIT
        ),
        name="expert_weights",
    )(x, plain, pair, routes, weights, gate_w, up_w, down_w, *kept, out_part, residual, grads)


def finish_kernel(
    gate_own, up_own, down_own, gate_other, up_other, down_other, shares, mixed, token_grad,
    gate_out, up_out, down_out, query_out, key_out, value_out, wo_out, router_out, moe_gain_out, attn_gain_out,
    mixed_out, token_out,
):
    for own, other, out in ((gate_own, gate_other, gate_out), (up_own, up_other, up_out), (down_own, down_other, down_out)):
        out[...] = own[...].astype(f32) + other[...].astype(f32)
    mixed_out[...] = mixed[...]
    token_out[...] = token_grad[...]

    @pl.when(pl.program_id(0) == 0)
    def _():
        width = wo_out.shape[-1]
        wo_out[...] = shares[:, 0:width].astype(f32)
        small = shares[:, width : width + LANE_SHARE].astype(f32).T
        router_out[...] = small[0:32]
        moe_gain_out[...] = small[32:33]
        attn_gain_out[...] = small[33:34]
        low = lanes((128, 128)) < 64
        base = width + LANE_SHARE
        for j in range(8):
            query_out[:, j * 128 : (j + 1) * 128] = shares[:, base + j * 256 : base + j * 256 + 128].astype(f32)
        for j in range(4):
            left = shares[:, base + j * 512 + 128 : base + j * 512 + 256].astype(f32)
            right = shares[:, base + j * 512 + 384 : base + j * 512 + 512].astype(f32)
            where = slice(j * 128, (j + 1) * 128)
            key_out[:, where] = jnp.where(low, left, pltpu.roll(right, 64, 1))
            value_out[:, where] = jnp.where(low, pltpu.roll(left, 64, 1), right)


def finish(parts, shares, mixed, token_grad):
    width = parts[0].shape[1]
    steps = parts[0].shape[0]

    def block(shape):
        return pl.BlockSpec((1,) + shape[1:], lambda e: (e, 0, 0))

    def rows(shape):
        return pl.BlockSpec((shape[0] // steps,) + shape[1:], lambda e: (e, 0))

    def whole(shape):
        return pl.BlockSpec(shape, lambda e: (0,) * len(shape))

    small = [(128, 1024), (128, 512), (128, 512), (128, width), (32, LANE_SHARE), (1, LANE_SHARE), (1, LANE_SHARE)]
    return pl.pallas_call(
        finish_kernel,
        grid=(steps,),
        out_shape=tuple(jax.ShapeDtypeStruct(p.shape, f32) for p in parts[:3])
        + tuple(jax.ShapeDtypeStruct(shape, f32) for shape in small)
        + (jax.ShapeDtypeStruct(mixed.shape, bf16), jax.ShapeDtypeStruct(token_grad.shape, f32)),
        in_specs=[block(p.shape) for p in parts] + [whole(shares.shape), rows(mixed.shape), rows(token_grad.shape)],
        out_specs=tuple(block(p.shape) for p in parts[:3])
        + tuple(whole(shape) for shape in small)
        + (rows(mixed.shape), rows(token_grad.shape)),
        compiler_params=pltpu.CompilerParams(vmem_limit_bytes=VMEM_LIMIT),
        name="finish",
    )(*parts, shares, mixed, token_grad)


def fast_on_device(
    tokens, segments, routes, cotangent, attn_gain, moe_gain, query_weight, key_projection_matrix,
    value_projection_matrix, out_weight, router_weight, gate_weight, up_weight, down_weight,
):
    width = tokens.shape[-1]
    tok = tokens.reshape(256, width)
    cot = cotangent.reshape(256, width)
    my_routes = routes.reshape(256, TOP).T
    (
        attn_in, q, kv, amix, residual, moe_in, weights, wo_all, gains_all, router_all, routes_all,
        cot_all, cot_mirror, routes_mirror, wkv,
    ) = forward(
        tok, cot, query_weight, key_projection_matrix, value_projection_matrix, out_weight,
        attn_gain.reshape(1, 128), moe_gain.reshape(1, 128), router_weight.T, my_routes, segments,
    )
    out_part, in_sum, p_all, *kept, plain_mirror, pair_mirror, moe_mirror, weights_mirror = experts(
        moe_in, weights, cot_mirror, cot_all, routes_all, routes_mirror, gate_weight, up_weight, down_weight
    )
    token_grad, grads, moe_mirror_all = backward(
        cot, residual, in_sum, p_all, my_routes, weights, router_all, moe_in, gains_all, wo_all, amix, attn_in,
        q, kv, segments, tok, query_weight, wkv, moe_mirror,
    )
    *parts, mixed, shares = expert_weights(
        moe_mirror_all, plain_mirror, pair_mirror, routes_mirror, weights_mirror, gate_weight, up_weight, down_weight,
        kept, out_part, residual, grads,
    )
    (
        gate_grad, up_grad, down_grad, query_grad, key_grad, value_grad, wo_grad, router_grad, moe_gain_grad,
        attn_gain_grad, mixed, token_grad,
    ) = finish(parts, shares, mixed, token_grad)
    return (
        mixed.reshape(tokens.shape), token_grad.reshape(tokens.shape), attn_gain_grad.reshape(128),
        moe_gain_grad.reshape(128), query_grad, key_grad, value_grad, wo_grad, router_grad.T,
        gate_grad, up_grad, down_grad,
    )


def fits(mesh):
    return dict(mesh.shape) == {"group": 4, "blk": 4, "head": 2}


def solution(mesh):
    placed = (
        P("group", ("blk", "head"), None),
        P("group", None),
        P("group", ("blk", "head"), None),
        P("group", ("blk", "head"), None),
        P(("blk", "head")),
        P(("blk", "head")),
        P(("blk", "head"), None),
        P(("blk", "head"), None),
        P(("blk", "head"), None),
        P(("blk", "head"), None),
        P(("blk", "head"), None),
        P(("blk", "head"), None, None),
        P(("blk", "head"), None, None),
        P(("blk", "head"), None, None),
    )
    return jax.shard_map(
        fast_on_device if fits(mesh) else on_device,
        mesh=mesh,
        in_specs=placed,
        out_specs=(
            P("group", ("blk", "head"), None),
            P("group", ("blk", "head"), None),
            P(("blk", "head")),
            P(("blk", "head")),
            P(("blk", "head"), None),
            P(("blk", "head"), None),
            P(("blk", "head"), None),
            P(("blk", "head"), None),
            P(("blk", "head"), None),
            P(("blk", "head"), None, None),
            P(("blk", "head"), None, None),
            P(("blk", "head"), None, None),
        ),
        check_vma=False,
    )
```

```python
import functools

import jax
import jax.numpy as jnp
import numpy as np
from jax import lax
from jax.experimental import pallas as pl
from jax.experimental.pallas import tpu as pltpu
from jax.sharding import PartitionSpec as P

QUERY_HEADS = 16
KEY_VALUE_HEADS = 8
HEAD_SIZE = 64
TOP = 8
CAPH = 36


epsilon = 1e-05
rope_base = 10000.0
masked_out = -1e30
key_block = 512


def rms_norm(values, gain_vec):
    return values * lax.rsqrt(jnp.mean(values * values, -1, keepdims=True) + epsilon) * gain_vec


def rotary_embedding(field_vals, places, turn_sign):
    half_dim = field_vals.shape[-1] // 2
    frequency = rope_base ** (-jnp.arange(half_dim, dtype=jnp.float32) * 2.0 / field_vals.shape[-1])
    angles = places.astype(jnp.float32)[:, None] * frequency[None, :]
    cosine = jnp.cos(angles)[:, None, :]
    sine_vals = turn_sign * jnp.sin(angles)[:, None, :]
    first_half = field_vals[..., :half_dim]
    second = field_vals[..., half_dim:]
    return jnp.concatenate(
        [first_half * cosine - second * sine_vals, second * cosine + first_half * sine_vals], -1
    )


def add_rows(running, addend, row_start):
    current = lax.dynamic_slice_in_dim(running, row_start, addend.shape[1], 1)
    return lax.dynamic_update_slice_in_dim(running, current + addend, row_start, 1)


def on_device(
    tokens,
    segments,
    routes,
    cotangent,
    attn_gain,
    moe_gain,
    query_weight,
    key_projection_matrix,
    value_projection_matrix,
    out_weight,
    router_weight,
    gate_weight,
    up_weight,
    down_weight,
):
    head_groups, number_of_rows, width_dim = tokens.shape
    query_per_key_head = QUERY_HEADS // KEY_VALUE_HEADS
    shared_head_count = lax.axis_size("head")
    query_rows = number_of_rows * shared_head_count
    grouped_keys = KEY_VALUE_HEADS // shared_head_count
    scale_val = HEAD_SIZE ** (-0.5)
    number_of_tokens = head_groups * number_of_rows
    seq_length = lax.axis_size("blk") * query_rows
    cycle_index = lax.axis_index("blk")
    local_placement = (
        cycle_index * shared_head_count + lax.axis_index("head")
    ) * number_of_rows + jnp.arange(number_of_rows, dtype=jnp.int32)
    own_start = cycle_index * query_rows
    query_place = own_start + jnp.arange(query_rows, dtype=jnp.int32)
    query_doc = lax.dynamic_slice_in_dim(segments, own_start, query_rows, 1)
    query_full, key_full, value_full, out_full, router_full, gain_attn, gain_moe = (
        lax.all_gather(query_weight, ("blk", "head"), axis=0, tiled=True),
        lax.all_gather(key_projection_matrix, ("blk", "head"), axis=0, tiled=True),
        lax.all_gather(value_projection_matrix, ("blk", "head"), axis=0, tiled=True),
        lax.all_gather(out_weight, ("blk", "head"), axis=0, tiled=True),
        lax.all_gather(router_weight, ("blk", "head"), axis=0, tiled=True),
        lax.all_gather(attn_gain, ("blk", "head"), axis=0, tiled=True),
        lax.all_gather(moe_gain, ("blk", "head"), axis=0, tiled=True),
    )
    flat_rows = tokens.reshape(number_of_tokens, width_dim).astype(jnp.float32)
    attn_normed, attn_pull = jax.vjp(rms_norm, flat_rows, gain_attn.astype(jnp.float32))
    attn_in = attn_normed.astype(jnp.bfloat16)
    query_pre = jnp.dot(attn_in, query_full, preferred_element_type=jnp.float32)
    key_before_rotary = jnp.dot(attn_in, key_full, preferred_element_type=jnp.float32)
    value_low = (
        jnp.dot(attn_in, value_full, preferred_element_type=jnp.float32)
        .astype(jnp.bfloat16)
        .reshape(head_groups, number_of_rows, KEY_VALUE_HEADS * HEAD_SIZE)
    )
    query_low = (
        rotary_embedding(
            query_pre.reshape(head_groups, number_of_rows, QUERY_HEADS, HEAD_SIZE),
            local_placement,
            1.0,
        )
        .astype(jnp.bfloat16)
        .reshape(head_groups, number_of_rows, QUERY_HEADS * HEAD_SIZE)
    )
    key_low = (
        rotary_embedding(
            key_before_rotary.reshape(head_groups, number_of_rows, KEY_VALUE_HEADS, HEAD_SIZE),
            local_placement,
            1.0,
        )
        .astype(jnp.bfloat16)
        .reshape(head_groups, number_of_rows, KEY_VALUE_HEADS * HEAD_SIZE)
    )
    query_split, key_split, value_split = (
        lax.all_to_all(query_low, "head", split_axis=2, concat_axis=1, tiled=True),
        lax.all_to_all(key_low, "head", split_axis=2, concat_axis=1, tiled=True),
        lax.all_to_all(value_low, "head", split_axis=2, concat_axis=1, tiled=True),
    )
    query_vectors = query_split.reshape(
        head_groups, query_rows, grouped_keys, query_per_key_head, HEAD_SIZE
    )

    def key_view(source, offset, sub_rows):
        return lax.dynamic_slice_in_dim(source, offset, sub_rows, 1).reshape(
            head_groups, sub_rows, grouped_keys, HEAD_SIZE
        )

    def scored_at(query_part, key_row_block, q_place, q_doc, key_start, sub_rows):
        raw_scores = (
            jnp.einsum(
                "bqgrd,bkgd->bqgrk", query_part, key_row_block, preferred_element_type=jnp.float32
            )
            * scale_val
        )
        key_place = key_start + jnp.arange(sub_rows, dtype=jnp.int32)
        key_doc = lax.dynamic_slice_in_dim(segments, key_start, sub_rows, 1)
        allowed = (q_place[None, :, None] >= key_place[None, None, :]) & (
            q_doc[:, :, None] == key_doc[:, None, :]
        )
        return (raw_scores, allowed[:, :, None, None, :])

    def scored(key_row_block, key_start, sub_rows):
        return scored_at(query_vectors, key_row_block, query_place, query_doc, key_start, sub_rows)

    stats_shape = (head_groups, query_rows, grouped_keys, query_per_key_head)
    init_state = (
        jnp.full(stats_shape, masked_out, jnp.float32),
        jnp.zeros(stats_shape, jnp.float32),
        jnp.zeros(stats_shape + (HEAD_SIZE,), jnp.float32),
    )
    key_all, value_all = (
        lax.all_gather(key_split, "blk", axis=1, tiled=True),
        lax.all_gather(value_split, "blk", axis=1, tiled=True),
    )
    fold_state = init_state
    total_rows = key_all.shape[1]
    sub_rows = key_block

    def forward_one_block(block_state, block_index):
        offset = block_index * sub_rows
        key_row_block = key_view(key_all, offset, sub_rows)
        value_row_block = key_view(value_all, offset, sub_rows)
        raw_scores, allowed = scored(key_row_block, 0 + offset, sub_rows)
        running_max, running_sum, running_acc = block_state
        masked = jnp.where(allowed, raw_scores, masked_out)
        new_max = jnp.maximum(running_max, jnp.max(masked, -1))
        shrink = jnp.exp(running_max - new_max)
        weights_soft = jnp.where(allowed, jnp.exp(masked - new_max[..., None]), 0.0)
        new_sum = running_sum * shrink + jnp.sum(weights_soft, -1)
        new_acc = running_acc * shrink[..., None] + jnp.einsum(
            "bqgrk,bkgd->bqgrd",
            weights_soft.astype(jnp.bfloat16),
            value_row_block,
            preferred_element_type=jnp.float32,
        )
        return ((new_max, new_sum, new_acc), None)

    fold_state, unused = lax.scan(
        forward_one_block, fold_state, jnp.arange(total_rows // sub_rows, dtype=jnp.int32)
    )
    running_max, running_sum, running_acc = fold_state
    mix_heads = running_acc / running_sum[..., None]
    log_total = running_max + jnp.log(running_sum)
    mix_low = mix_heads.astype(jnp.bfloat16).reshape(
        head_groups, query_rows, grouped_keys * query_per_key_head * HEAD_SIZE
    )
    mix_tokens = lax.all_to_all(mix_low, "head", split_axis=1, concat_axis=2, tiled=True)
    attn_mix = mix_tokens.reshape(number_of_tokens, QUERY_HEADS * HEAD_SIZE)
    residual = flat_rows + jnp.dot(attn_mix, out_full, preferred_element_type=jnp.float32)
    moe_normed, moe_pull = jax.vjp(rms_norm, residual, gain_moe.astype(jnp.float32))
    moe_in = moe_normed.astype(jnp.bfloat16)
    logits = jnp.dot(moe_in, router_full, preferred_element_type=jnp.float32)
    route_flat = routes.reshape(number_of_tokens, TOP)
    experts_all = router_full.shape[1]
    choose = route_flat[:, :, None] == jnp.arange(experts_all, dtype=jnp.int32)[None, None, :]
    choose_float = choose.astype(jnp.float32)
    picked_logits = jnp.einsum("nke,ne->nk", choose_float, logits)
    route_weights = jax.nn.softmax(picked_logits, axis=-1)
    choose_whole = choose.astype(jnp.int32).reshape(head_groups, number_of_rows * TOP, experts_all)
    slot_rank = jnp.sum(jnp.cumsum(choose_whole, 1) * choose_whole, -1) - 1
    slot_index = (slot_rank + jnp.arange(head_groups, dtype=jnp.int32)[:, None] * CAPH).reshape(-1)
    targets = route_flat.reshape(-1)
    lane_count = head_groups * CAPH
    outgoing = (
        jnp.zeros((experts_all, lane_count, width_dim), jnp.bfloat16)
        .at[targets, slot_index]
        .set(jnp.repeat(moe_in, TOP, axis=0))
    )
    arrived = lax.all_to_all(outgoing, ("blk", "head"), split_axis=0, concat_axis=1, tiled=True)
    gate_val = jnp.einsum("end,edf->enf", arrived, gate_weight, preferred_element_type=jnp.float32)
    up_val = jnp.einsum("end,edf->enf", arrived, up_weight, preferred_element_type=jnp.float32)
    hidden_low = (jax.nn.silu(gate_val) * up_val).astype(jnp.bfloat16)
    expert_out = jnp.einsum(
        "enf,efd->end", hidden_low, down_weight, preferred_element_type=jnp.float32
    ).astype(jnp.bfloat16)
    returned = lax.all_to_all(expert_out, ("blk", "head"), split_axis=1, concat_axis=0, tiled=True)
    picked_rows = returned[targets, slot_index].reshape(number_of_tokens, TOP, width_dim)
    moe_out = jnp.einsum(
        "nk,nkd->nd", route_weights, picked_rows, preferred_element_type=jnp.float32
    )
    mixed = (
        (residual + moe_out).astype(jnp.bfloat16).reshape(head_groups, number_of_rows, width_dim)
    )
    grad_full = cotangent.reshape(number_of_tokens, width_dim).astype(jnp.float32)
    weight_grad = jnp.einsum(
        "nkd,nd->nk", picked_rows, grad_full, preferred_element_type=jnp.float32
    )
    pair_grad = (
        (route_weights[:, :, None] * grad_full[:, None, :])
        .astype(jnp.bfloat16)
        .reshape(number_of_tokens * TOP, width_dim)
    )
    grad_outgoing = jnp.zeros_like(outgoing).at[targets, slot_index].set(pair_grad)
    grad_arrived = lax.all_to_all(
        grad_outgoing, ("blk", "head"), split_axis=0, concat_axis=1, tiled=True
    )
    grad_hidden = jnp.einsum(
        "end,efd->enf", grad_arrived, down_weight, preferred_element_type=jnp.float32
    )
    sigmoid_val = jax.nn.sigmoid(gate_val)
    grad_gate = (
        grad_hidden * up_val * sigmoid_val * (1.0 + gate_val * (1.0 - sigmoid_val))
    ).astype(jnp.bfloat16)
    grad_up = (grad_hidden * gate_val * sigmoid_val).astype(jnp.bfloat16)
    down_weight_grad = jnp.einsum(
        "enf,end->efd", hidden_low, grad_arrived, preferred_element_type=jnp.float32
    )
    gate_weight_grad = jnp.einsum(
        "end,enf->edf", arrived, grad_gate, preferred_element_type=jnp.float32
    )
    up_weight_grad = jnp.einsum(
        "end,enf->edf", arrived, grad_up, preferred_element_type=jnp.float32
    )
    pair_back = (
        jnp.einsum("enf,edf->end", grad_gate, gate_weight, preferred_element_type=jnp.float32)
        + jnp.einsum("enf,edf->end", grad_up, up_weight, preferred_element_type=jnp.float32)
    ).astype(jnp.bfloat16)
    grad_returned = lax.all_to_all(
        pair_back, ("blk", "head"), split_axis=1, concat_axis=0, tiled=True
    )
    moe_in_grad = jnp.sum(
        grad_returned[targets, slot_index].reshape(number_of_tokens, TOP, width_dim),
        axis=1,
        dtype=jnp.float32,
    )
    mean_term = jnp.sum(route_weights * weight_grad, -1, keepdims=True)
    logit_grad = jnp.einsum("nk,nke->ne", route_weights * (weight_grad - mean_term), choose_float)
    router_grad = jnp.dot(moe_in.T, logit_grad, preferred_element_type=jnp.float32)
    moe_in_grad = moe_in_grad + jnp.dot(
        logit_grad, router_full.T, preferred_element_type=jnp.float32
    )
    residual_part, moe_gain_grad = moe_pull(moe_in_grad)
    residual_grad = grad_full + residual_part
    out_grad_low = residual_grad.astype(jnp.bfloat16)
    out_weight_grad = jnp.dot(attn_mix.T, out_grad_low, preferred_element_type=jnp.float32)
    mix_grad = (
        jnp.dot(out_grad_low, out_full.T, preferred_element_type=jnp.float32)
        .astype(jnp.bfloat16)
        .reshape(head_groups, number_of_rows, QUERY_HEADS * HEAD_SIZE)
    )
    mix_grad_heads = lax.all_to_all(
        mix_grad, "head", split_axis=2, concat_axis=1, tiled=True
    ).reshape(head_groups, query_rows, grouped_keys, query_per_key_head, HEAD_SIZE)
    delta_term = jnp.sum(mix_grad_heads.astype(jnp.float32) * mix_heads, -1)
    query_zero = jnp.zeros(stats_shape + (HEAD_SIZE,), jnp.float32)
    back_init = (
        query_zero,
        jnp.zeros((head_groups, seq_length, grouped_keys, HEAD_SIZE), jnp.float32),
        jnp.zeros((head_groups, seq_length, grouped_keys, HEAD_SIZE), jnp.float32),
    )
    fold_state = back_init
    total_rows = key_all.shape[1]

    def backward_one_block(block_state, block_index):
        offset = block_index * key_block
        key_start = 0 + offset
        key_row_block = key_view(key_all, offset, key_block)
        value_row_block = key_view(value_all, offset, key_block)
        raw_scores, allowed = scored(key_row_block, key_start, key_block)
        masked = jnp.where(allowed, raw_scores, masked_out)
        probability = jnp.where(allowed, jnp.exp(masked - log_total[..., None]), 0.0)
        prob_grad = jnp.einsum(
            "bqgrd,bkgd->bqgrk", mix_grad_heads, value_row_block, preferred_element_type=jnp.float32
        )
        score_grad = (probability * (prob_grad - delta_term[..., None]) * scale_val).astype(
            jnp.bfloat16
        )
        grad_query = block_state[0] + jnp.einsum(
            "bqgrk,bkgd->bqgrd", score_grad, key_row_block, preferred_element_type=jnp.float32
        )
        value_part_grad = jnp.einsum(
            "bqgrk,bqgrd->bkgd",
            probability.astype(jnp.bfloat16),
            mix_grad_heads,
            preferred_element_type=jnp.float32,
        )
        key_part_grad = jnp.einsum(
            "bqgrk,bqgrd->bkgd", score_grad, query_vectors, preferred_element_type=jnp.float32
        )
        grad_keys = add_rows(block_state[1], key_part_grad, key_start)
        grad_values = add_rows(block_state[2], value_part_grad, key_start)
        return ((grad_query, grad_keys, grad_values), None)

    fold_state, unused = lax.scan(
        backward_one_block, fold_state, jnp.arange(total_rows // key_block, dtype=jnp.int32)
    )
    grad_query, grad_keys, grad_values = fold_state
    key_own, value_own = (
        lax.psum_scatter(
            grad_keys.reshape(head_groups, seq_length, grouped_keys * HEAD_SIZE).astype(
                jnp.bfloat16
            ),
            "blk",
            scatter_dimension=1,
            tiled=True,
        ).astype(jnp.float32),
        lax.psum_scatter(
            grad_values.reshape(head_groups, seq_length, grouped_keys * HEAD_SIZE).astype(
                jnp.bfloat16
            ),
            "blk",
            scatter_dimension=1,
            tiled=True,
        ).astype(jnp.float32),
    )
    query_grad_low = (
        rotary_embedding(
            grad_query.reshape(
                head_groups, query_rows, grouped_keys * query_per_key_head, HEAD_SIZE
            ),
            query_place,
            -1.0,
        )
        .astype(jnp.bfloat16)
        .reshape(head_groups, query_rows, grouped_keys * query_per_key_head * HEAD_SIZE)
    )
    key_grad_low = (
        rotary_embedding(
            key_own.reshape(head_groups, query_rows, grouped_keys, HEAD_SIZE), query_place, -1.0
        )
        .astype(jnp.bfloat16)
        .reshape(head_groups, query_rows, grouped_keys * HEAD_SIZE)
    )
    value_grad_low = value_own.astype(jnp.bfloat16)
    query_back, key_pullback, value_pullback = (
        lax.all_to_all(query_grad_low, "head", split_axis=1, concat_axis=2, tiled=True),
        lax.all_to_all(key_grad_low, "head", split_axis=1, concat_axis=2, tiled=True),
        lax.all_to_all(value_grad_low, "head", split_axis=1, concat_axis=2, tiled=True),
    )
    query_flat = query_back.reshape(number_of_tokens, QUERY_HEADS * HEAD_SIZE)
    flattened_keys = key_pullback.reshape(number_of_tokens, KEY_VALUE_HEADS * HEAD_SIZE)
    flattened_values = value_pullback.reshape(number_of_tokens, KEY_VALUE_HEADS * HEAD_SIZE)
    query_weight_grad = jnp.dot(attn_in.T, query_flat, preferred_element_type=jnp.float32)
    key_weight_grad = jnp.dot(attn_in.T, flattened_keys, preferred_element_type=jnp.float32)
    value_weight_grad = jnp.dot(attn_in.T, flattened_values, preferred_element_type=jnp.float32)
    attn_in_grad = (
        jnp.dot(query_flat, query_full.T, preferred_element_type=jnp.float32)
        + jnp.dot(flattened_keys, key_full.T, preferred_element_type=jnp.float32)
        + jnp.dot(flattened_values, value_full.T, preferred_element_type=jnp.float32)
    )
    input_part, attn_gain_grad = attn_pull(attn_in_grad)
    token_grad = (residual_grad + input_part).reshape(head_groups, number_of_rows, width_dim)
    (
        query_shard,
        key_shard,
        value_shard,
        out_shard,
        router_shard,
        attn_gain_shard,
        moe_gain_shard,
    ) = (
        lax.psum_scatter(
            query_weight_grad.astype(jnp.bfloat16), ("blk", "head"), scatter_dimension=0, tiled=True
        ).astype(jnp.float32),
        lax.psum_scatter(
            key_weight_grad.astype(jnp.bfloat16), ("blk", "head"), scatter_dimension=0, tiled=True
        ).astype(jnp.float32),
        lax.psum_scatter(
            value_weight_grad.astype(jnp.bfloat16), ("blk", "head"), scatter_dimension=0, tiled=True
        ).astype(jnp.float32),
        lax.psum_scatter(
            out_weight_grad.astype(jnp.bfloat16), ("blk", "head"), scatter_dimension=0, tiled=True
        ).astype(jnp.float32),
        lax.psum_scatter(
            router_grad.astype(jnp.bfloat16), ("blk", "head"), scatter_dimension=0, tiled=True
        ).astype(jnp.float32),
        lax.psum_scatter(
            attn_gain_grad.astype(jnp.bfloat16), ("blk", "head"), scatter_dimension=0, tiled=True
        ).astype(jnp.float32),
        lax.psum_scatter(
            moe_gain_grad.astype(jnp.bfloat16), ("blk", "head"), scatter_dimension=0, tiled=True
        ).astype(jnp.float32),
    )
    summed = (
        lax.psum(query_shard.astype(jnp.bfloat16), "group").astype(jnp.float32),
        lax.psum(key_shard.astype(jnp.bfloat16), "group").astype(jnp.float32),
        lax.psum(value_shard.astype(jnp.bfloat16), "group").astype(jnp.float32),
        lax.psum(out_shard.astype(jnp.bfloat16), "group").astype(jnp.float32),
        lax.psum(router_shard.astype(jnp.bfloat16), "group").astype(jnp.float32),
        lax.psum(attn_gain_shard.astype(jnp.bfloat16), "group").astype(jnp.float32),
        lax.psum(moe_gain_shard.astype(jnp.bfloat16), "group").astype(jnp.float32),
        lax.psum(gate_weight_grad.astype(jnp.bfloat16), "group").astype(jnp.float32),
        lax.psum(up_weight_grad.astype(jnp.bfloat16), "group").astype(jnp.float32),
        lax.psum(down_weight_grad.astype(jnp.bfloat16), "group").astype(jnp.float32),
    )
    return (
        mixed,
        token_grad,
        summed[5],
        summed[6],
        summed[0],
        summed[1],
        summed[2],
        summed[3],
        summed[4],
        summed[7],
        summed[8],
        summed[9],
    )


bf16 = jnp.bfloat16
f32 = jnp.float32
MESH_ID = pl.DeviceIdType.MESH
VMEM_LIMIT = 67 * 1000 * 1000
COLOURS = ((0, 96), (96, 80), (176, 80))
LINKS = (("head", 1), ("blk", 1), ("blk", 2), ("group", 2), ("group", 1))
ORDERS = ((0, 1, 2), (1, 2, 0), (2, 0, 1))


def vmem():
    return pl.BlockSpec(memory_space=pltpu.VMEM)


def anywhere():
    return pl.BlockSpec(memory_space=pl.ANY)


def dot_last(left, right):
    return lax.dot_general(left, right, (((1,), (1,)), ((), ())), preferred_element_type=f32)


def dot_first(left, right):
    return lax.dot_general(left, right, (((0,), (0,)), ((), ())), preferred_element_type=f32)


def dot(left, right):
    return jnp.dot(left, right, preferred_element_type=f32)


def my_place():
    return lax.axis_index("blk") * 2 + lax.axis_index("head")


def peer(step):
    place = lax.rem(my_place() + step, 8)
    return place, {"blk": place // 2, "head": lax.rem(place, 2)}


def neighbour(link):
    if link == 0:
        return {"head": 1 - lax.axis_index("head")}
    blk = lax.axis_index("blk")
    if link == 1:
        return {"blk": blk + 1 - 2 * lax.rem(blk, 2)}
    return {"blk": lax.rem(blk + 2, 4)}


def my_bits():
    blk = lax.axis_index("blk")
    return (lax.axis_index("head"), lax.rem(blk, 2), blk // 2)


def meet_all():
    barrier = pltpu.get_barrier_semaphore()
    for step in range(1, 8):
        pl.semaphore_signal(barrier, 1, device_id=peer(step)[1], device_id_type=MESH_ID)
    pl.semaphore_wait(barrier, 7)


def remote(src, dst, send, recv, target):
    return pltpu.make_async_remote_copy(
        src_ref=src, dst_ref=dst, send_sem=send, recv_sem=recv, device_id=target, device_id_type=MESH_ID
    )


def cube_index(bits, fixed, rows):
    entries = [pl.ds(fixed[link], 1) if link in fixed else pl.ds(0, 2) for link in (2, 1, 0)]
    return tuple(entries) + (pl.ds(*rows),)


def lanes(shape):
    return lax.broadcasted_iota(jnp.int32, shape, len(shape) - 1)


def turned(u):
    low = lax.rem(lanes(u.shape), 64) < 32
    return jnp.where(low, -pltpu.roll(u, 96, 1), pltpu.roll(u, 32, 1))


def two_heads(q):
    low = lanes(q.shape) < 64
    return jnp.concatenate([jnp.where(low, q, 0.0), jnp.where(low, pltpu.roll(q, 64, 1), 0.0)], 0)


def two_heads_high(g):
    high = lanes(g.shape) >= 64
    return jnp.concatenate([jnp.where(high, pltpu.roll(g, 64, 1), 0.0), jnp.where(high, g, 0.0)], 0)


def block_probability(q_ref, kv_ref, docs, segs, s, i):
    short = isinstance(i, int)
    first = 0 if short else pl.multiple_of((i - 4) * 128, 128)
    count = (i + 1) * 128 if short else 640
    mine = pl.ds(i * 128 if short else pl.multiple_of(i * 128, 128), 128)
    q2 = two_heads(q_ref[s, mine].astype(f32))
    kv = kv_ref[s, pl.ds(first, count)]
    raw = dot_last((q2 * 0.125).astype(bf16), kv)
    q_place = i * 128 + lax.broadcasted_iota(jnp.int32, (128, count), 0)
    k_place = first + lanes((128, count))
    q_doc = docs[s, mine]
    keys = pl.ds(first, count)
    k_doc = jnp.where(s == 0, segs[0:1, keys], segs[1:2, keys]).astype(f32)
    allowed = (q_place >= k_place) & (q_doc == k_doc)
    allowed = jnp.concatenate([allowed, allowed], 0)
    masked = jnp.where(allowed, raw, masked_out)
    top = jnp.max(masked, -1, keepdims=True)
    weight = jnp.exp(masked - top)
    probability = weight * (1.0 / jnp.sum(weight, -1, keepdims=True))
    return first, count, q2, kv, probability


def norm_back(values, gain, grad):
    scale = lax.rsqrt(jnp.mean(values * values, -1, keepdims=True) + epsilon)
    inner = grad * gain
    along = jnp.mean(values * inner, -1, keepdims=True)
    out = scale * inner - values * (scale * scale * scale * along)
    gain_grad = jnp.sum(grad * values * scale, 0, keepdims=True)
    return out, gain_grad


def expert_inner(rows_e, pair_e, gate_w, up_w, down_w):
    gate_val = dot(rows_e, gate_w)
    up_val = dot(rows_e, up_w)
    sig = 1.0 / (1.0 + jnp.exp(-gate_val))
    silu = gate_val * sig
    hidden = (silu * up_val).astype(bf16)
    hidden_grad = dot_last(pair_e, down_w)
    gate_grad = (hidden_grad * up_val * sig * (1.0 + gate_val * (1.0 - sig))).astype(bf16)
    up_grad = (hidden_grad * silu).astype(bf16)
    return hidden, gate_grad, up_grad


def sibling():
    group = lax.axis_index("group")
    return {"group": group + 1 - 2 * lax.rem(group, 2)}


def mirror():
    return {"group": lax.rem(lax.axis_index("group") + 2, 4)}


def my_core():
    return lax.rem(lax.axis_index("group"), 2)


def meet(targets):
    barrier = pltpu.get_barrier_semaphore()
    for target in targets:
        pl.semaphore_signal(barrier, 1, device_id=target, device_id_type=MESH_ID)
    pl.semaphore_wait(barrier, len(targets))


def peers():
    return [peer(step)[1] for step in range(1, 8)]


def cube_entry(fixed):
    return tuple(pl.ds(fixed[link], 1) if link in fixed else pl.ds(0, 2) for link in (2, 1, 0))


class Gather:
    def __init__(self, items, send, recv):
        self.items, self.send, self.recv, self.bits = items, send, recv, my_bits()

    def copies(self, step):
        made = []
        for k, (src, place, order) in enumerate(self.items):
            fixed = {link: self.bits[link] for link in order[step:]}
            where = place(cube_entry(fixed))
            here = where
            if step == 0:
                here = src
                where = place((self.bits[2], self.bits[1], self.bits[0]))
            made.append(remote(here, where, self.send.at[step, k], self.recv.at[step, k], neighbour(order[step])))
        return made

    def start(self, step):
        for copy in self.copies(step):
            copy.start()

    def wait(self, step):
        for copy in self.copies(step):
            copy.wait_recv()

    def advance(self, step):
        for before, after in zip(self.copies(step - 1), self.copies(step)):
            before.wait_recv()
            after.start()

    def sent(self):
        for step in range(3):
            for copy in self.copies(step):
                copy.wait_send()


SHARES = ((0, 48), (96, 48), (176, 48), (48, 48), (144, 32), (224, 32))
HALF_SHARES = tuple(
    tuple((s * 128 + start, count) for start, count in ((0, 32), (32, 32), (64, 16), (80, 16), (96, 16), (112, 16)))
    for s in range(2)
)


def row_items(src, dst, shares=SHARES):
    def item(k):
        start, count = shares[k]
        return (src.at[pl.ds(start, count)], lambda entry: dst.at[entry + (pl.ds(start, count),)], ORDERS[k % 3])

    return [item(k) for k in range(len(shares))]


ROW_CUTS = tuple((pl.ds(start, count), slice(None)) for start, count in SHARES)


class CubeSum:
    def __init__(self, source, part, cuts, scratch, base=0):
        self.source, self.part, self.cuts = source, part, cuts
        self.kept = tuple((pl.ds(row.start - base, row.size) if base else row, lane) for row, lane in cuts)
        *self.got, self.held0, self.got1, self.held1, self.got2, self.send, self.recv = scratch
        self.bits = my_bits()
        self.orders = [ORDERS[k % 3] for k in range(len(cuts))]

    def copy(self, step, k):
        order, cut, kept = self.orders[k], self.cuts[k], self.kept[k]
        other = 1 - self.bits[order[step]]
        if step == 0:
            src = self.source.at[cube_entry({order[0]: other}) + cut]
            dst = self.got[k]
        elif step == 1:
            src = self.held0.at[(other, slice(None)) + kept]
            dst = self.got1.at[(slice(None),) + kept]
        else:
            src = self.held1.at[(other,) + kept]
            dst = self.got2.at[kept]
        return remote(src, dst, self.send.at[step, k], self.recv.at[step, k], neighbour(order[step]))

    def start(self):
        for k in range(len(self.cuts)):
            self.copy(0, k).start()

    def middle(self):
        for k, order in enumerate(self.orders):
            self.copy(0, k).wait_recv()
            cut, kept = self.cuts[k], self.kept[k]

            def add(w, carry, k=k, order=order, cut=cut, kept=kept):
                u, v = w // 2, lax.rem(w, 2)
                mine = {order[0]: self.bits[order[0]], order[1]: u, order[2]: v}
                there = {order[0]: 0, order[1]: u, order[2]: v}
                landed = self.got[k][there[2], there[1], there[0]].astype(f32)
                here = self.part[(mine[2], mine[1], mine[0]) + cut].astype(f32)
                self.held0[(u, v) + kept] = (here + landed).astype(bf16)
                return carry

            lax.fori_loop(0, 4, add, 0)
            self.copy(1, k).start()

    def last(self):
        for k, order in enumerate(self.orders):
            self.copy(1, k).wait_recv()
            kept = self.kept[k]

            def add(v, carry, order=order, kept=kept):
                here = self.held0[(self.bits[order[1]], v) + kept].astype(f32)
                self.held1[(v,) + kept] = (here + self.got1[(v,) + kept].astype(f32)).astype(bf16)
                return carry

            lax.fori_loop(0, 2, add, 0)
            self.copy(2, k).start()

    def finish(self, store):
        for k, order in enumerate(self.orders):
            self.copy(2, k).wait_recv()
            kept = self.kept[k]
            store(
                self.cuts[k], self.held1[(self.bits[order[2]],) + kept].astype(f32) + self.got2[kept].astype(f32)
            )

    def sent(self):
        for step in range(3):
            for k in range(len(self.cuts)):
                self.copy(step, k).wait_send()


def cube_sum_scratch(rows, width, cuts):
    def share(k):
        row, lane = cuts[k]
        shape = [2, 2, 2, rows if row == slice(None) else row.size, width if lane == slice(None) else lane.size]
        shape[2 - ORDERS[k % 3][0]] = 1
        return pltpu.VMEM(tuple(shape), bf16)

    return [
        *(share(k) for k in range(len(cuts))),
        pltpu.VMEM((2, 2, rows, width), bf16),
        pltpu.VMEM((2, rows, width), bf16),
        pltpu.VMEM((2, rows, width), bf16),
        pltpu.VMEM((rows, width), bf16),
        pltpu.SemaphoreType.DMA((3, len(cuts))),
        pltpu.SemaphoreType.DMA((3, len(cuts))),
    ]


class Spread:
    def __init__(self, src, dst, send, recv):
        self.src, self.dst, self.send, self.recv = src, dst, send, recv

    def copy(self, step):
        place, target = peer(step)
        return remote(self.src(place), self.dst(my_place()), self.send.at[step], self.recv.at[step], target)

    def start(self):
        for step in range(1, 8):
            self.copy(step).start()

    def wait(self):
        for step in range(1, 8):
            self.copy(step).wait()


def rope_tables():
    frequency = 10000.0 ** (-(np.arange(128) % 32) * 2.0 / 64)
    near = np.arange(128)[:, None] * frequency[None, :]
    far = np.arange(8)[:, None] * 128.0 * frequency[None, :]
    return tuple(np.asarray(t, np.float32) for t in (np.cos(near), np.sin(near), np.cos(far), np.sin(far)))


def fill_rope(near_cos, near_sin, far_cos, far_sin, cosine, sine):
    for j in range(8):
        rows = pl.ds(j * 128, 128)
        fc, fs = far_cos[pl.ds(j, 1)], far_sin[pl.ds(j, 1)]
        cosine[rows] = fc * near_cos[...] - fs * near_sin[...]
        sine[rows] = fs * near_cos[...] + fc * near_sin[...]


THIRDS = ((0, 384), (384, 384), (768, 256))


def fill_docs(segs, docs):
    for s in range(2):
        for j in range(8):
            row = segs[pl.ds(s, 1), pl.ds(j * 128, 128)].astype(f32)
            docs[s, pl.ds(j * 128, 128)] = jnp.broadcast_to(row, (128, 128)).T[:, 0:1]


def fill_upper(upper):
    row = lax.broadcasted_iota(jnp.int32, upper.shape, 0)
    upper[...] = jnp.where(row < lanes(upper.shape), 1.0, 0.0).astype(bf16)


def forward_kernel(
    tok, cot, wq, wk, wv, wo, attn_gain, moe_gain, router, routes, segs, near_cos, near_sin, far_cos, far_sin,
    attn_hbm, q_out, kv_out, amix, residual_out, moe_in_out, weights_out, wo_hbm, gains_all, router_all, routes_all,
    cot_hbm, cot_mirror, routes_mirror, wkv,
    tok_all, attn_all, cot_all, wo_all, w_all, mix, cosine, sine, docs, gains,
    tok_send, tok_recv, cot_send, cot_recv, small_send, small_recv, mix_send, mix_recv, wo_send, wo_recv,
    pair_send, pair_recv, own_sem, out_sem,
):
    me, core = my_place(), my_core()
    half = pl.ds(pl.multiple_of(core * 64, 64), 64)
    own_entry = (me // 4, lax.rem(me // 2, 2), lax.rem(me, 2))
    first_row = lax.broadcasted_iota(jnp.int32, (16, 128), 0)
    both_gains = jnp.where(first_row == 1, moe_gain[...].astype(f32), 0.0)
    gains[...] = jnp.where(first_row == 0, attn_gain[...].astype(f32), both_gains).astype(bf16)
    for j in range(4):
        low = lanes((128, 128)) < 64
        k_two, v_two = (w[:, j * 128 : (j + 1) * 128].astype(f32) for w in (wk, wv))
        wkv[:, j * 256 : j * 256 + 128] = jnp.where(low, k_two, pltpu.roll(v_two, 64, 1)).astype(bf16)
        wkv[:, j * 256 + 128 : j * 256 + 256] = jnp.where(low, pltpu.roll(k_two, 64, 1), v_two).astype(bf16)
    meet(peers() + [sibling(), mirror()])
    tok_gather = Gather(row_items(tok, tok_all), tok_send, tok_recv)
    tok_gather.start(0)
    pairs = (
        (lambda j: wq.at[half, pl.ds(j * 128, 128)], lambda i: w_all.at[i, half, pl.ds(0, 128)]),
        (lambda j: wkv.at[half, pl.ds(j * 128, 128)], lambda i: w_all.at[i, half, pl.ds(128, 128)]),
        (lambda j: gains, lambda i: gains_all.at[:, pl.ds(i * 128, 128)]),
        (lambda j: router, lambda i: router_all.at[:, pl.ds(i * 128, 128)]),
        (lambda j: routes.at[:, pl.ds(0, 128)], lambda i: routes_all.at[:, pl.ds(i * 128, 128)]),
        (lambda j: routes.at[:, pl.ds(128, 128)], lambda i: routes_all.at[:, pl.ds(1024 + i * 128, 128)]),
    )
    smalls = [Spread(src, dst, small_send.at[k], small_recv.at[k]) for k, (src, dst) in enumerate(pairs)]
    own = [pltpu.make_async_copy(src(me), dst(me), own_sem.at[k]) for k, (src, dst) in enumerate(pairs)]
    own += [
        pltpu.make_async_copy(tok, tok_all.at[own_entry], own_sem.at[6]),
        pltpu.make_async_copy(cot, cot_all.at[own_entry], own_sem.at[7]),
        pltpu.make_async_copy(wo.at[half], wo_all.at[own_entry + (half,)], own_sem.at[8]),
    ]
    for copy in own:
        copy.start()
    for small in smalls:
        small.start()
    fill_rope(near_cos, near_sin, far_cos, far_sin, cosine, sine)
    for copy in own:
        copy.wait()
    tok_gather.advance(1)
    cot_copy = remote(cot, cot_mirror, pair_send.at[1], pair_recv.at[1], mirror())
    cot_copy.start()
    fill_docs(segs, docs)
    tok_gather.advance(2)
    for small in smalls:
        small.wait()
    w_pair = remote(w_all.at[:, half], w_all.at[:, half], pair_send.at[3], pair_recv.at[3], sibling())
    w_pair.start()
    tok_gather.wait(2)
    w_pair.wait()

    def wo_item(k):
        where = (half, pl.ds(*THIRDS[k]))
        return (wo.at[where], lambda entry: wo_all.at[entry + where], ORDERS[k])

    wo_gather = Gather([wo_item(k) for k in range(3)], wo_send, wo_recv)
    wo_gather.start(0)
    cot_gather = Gather(row_items(cot, cot_all), cot_send, cot_recv)
    cot_gather.start(0)
    routes_copy = remote(routes_all, routes_mirror, pair_send.at[0], pair_recv.at[0], mirror())
    routes_copy.start()

    gain_row = gains_all[0:1].astype(f32)

    def project(j, carry):
        rows = pl.ds(pl.multiple_of(j * 128, 128), 128)
        x = tok_all[j // 4, lax.rem(j // 2, 2), lax.rem(j, 2)].astype(f32)
        scale = lax.rsqrt(jnp.mean(x * x, -1, keepdims=True) + epsilon)
        attn_in = (x * scale * gain_row).astype(bf16)
        attn_all[j] = attn_in
        both = dot(attn_in, w_all[...].reshape(1024, 256))
        c = cosine[rows]
        n = sine[rows]
        c2 = jnp.concatenate([c, c], 0)
        n2 = jnp.concatenate([n, n], 0)
        q = both[:, :128]
        kv = both[:, 128:]
        q = (q * c2 + turned(q) * n2).astype(bf16)
        kv = jnp.where(lanes(kv.shape) < 64, kv * c2 + turned(kv) * n2, kv).astype(bf16)
        for s in range(2):
            q_out[s, rows] = q[s * 128 : (s + 1) * 128]
            kv_out[s, rows] = kv[s * 128 : (s + 1) * 128]
        return carry

    lax.fori_loop(0, 8, project, 0)
    attn_copy = pltpu.make_async_copy(attn_all, attn_hbm, out_sem.at[0])
    attn_copy.start()
    wo_gather.advance(1)
    cot_gather.advance(1)
    wo_pair = remote(
        wo_all.at[:, :, :, half], wo_all.at[:, :, :, half], pair_send.at[2], pair_recv.at[2], sibling()
    )

    def mix_copy(i):
        return remote(
            mix.at[i],
            amix.at[:, :, pl.ds(pl.multiple_of(me * 128, 128), 128)],
            mix_send.at[i],
            mix_recv.at[me],
            {"blk": i // 2, "head": lax.rem(i, 2)},
        )

    def send_mix(i):
        @pl.when(me != i)
        def _():
            mix_copy(i).start()

    def attend_block(i):
        def attend(s, carry):
            first, count, q2, kv, probability = block_probability(q_out, kv_out, docs, segs, s, i)
            mixed = dot(probability.astype(bf16), kv)
            low = lanes((128, 128)) < 64
            mix[i, s] = jnp.where(low, pltpu.roll(mixed[:128], 64, 1), mixed[128:]).astype(bf16)
            return carry

        lax.fori_loop(0, 2, attend, 0)

    for i in range(4):
        attend_block(i)
        if i > 0:
            send_mix(i - 1)
        if i == 2:
            wo_gather.advance(2)

    def attend_long(i, carry):
        attend_block(i)
        send_mix(i - 1)

        @pl.when(i == 4)
        def _():
            cot_gather.advance(2)

        return carry

    lax.fori_loop(4, 8, attend_long, 0)
    send_mix(7)
    wo_gather.wait(2)
    wo_pair.start()
    mine = pltpu.make_async_copy(
        mix.at[me], amix.at[:, :, pl.ds(pl.multiple_of(me * 128, 128), 128)], own_sem.at[0]
    )
    mine.start()
    wo_pair.wait()
    wo_copy = pltpu.make_async_copy(wo_all, wo_hbm, out_sem.at[1])
    wo_copy.start()
    for step in range(1, 8):
        place, target = peer(step)
        remote(
            mix.at[place],
            amix.at[:, :, pl.ds(pl.multiple_of(place * 128, 128), 128)],
            mix_send.at[place],
            mix_recv.at[place],
            target,
        ).wait()
    mine.wait()
    width = tok.shape[-1]
    residual = tok[...].astype(f32) + dot(amix[...].reshape(256, width), wo_all[...].reshape(width, width))
    residual_out[...] = residual
    scale = lax.rsqrt(jnp.mean(residual * residual, -1, keepdims=True) + epsilon)
    moe_in = (residual * scale * gains_all[1:2].astype(f32)).astype(bf16)
    moe_in_out[...] = moe_in
    logits = dot_last(router_all[...], moe_in)
    experts = lax.broadcasted_iota(jnp.int32, logits.shape, 0)
    picked = [
        jnp.sum(jnp.where(experts == routes[pl.ds(k, 1)], logits, 0.0), 0, keepdims=True) for k in range(TOP)
    ]
    picked = jnp.concatenate(picked, 0)
    weight = jnp.exp(picked - jnp.max(picked, 0, keepdims=True))
    weights_out[...] = weight / jnp.sum(weight, 0, keepdims=True)
    cot_gather.wait(2)
    cot_out = pltpu.make_async_copy(cot_all, cot_hbm, out_sem.at[2])
    cot_out.start()
    routes_copy.wait()
    cot_copy.wait()
    tok_gather.sent()
    cot_gather.sent()
    wo_gather.sent()
    attn_copy.wait()
    wo_copy.wait()
    cot_out.wait()


def forward(*values):
    tok = values[0]
    width = tok.shape[-1]
    tables = tuple(jnp.asarray(t) for t in rope_tables())
    return pl.pallas_call(
        forward_kernel,
        out_shape=(
            jax.ShapeDtypeStruct((8, 256, width), bf16),
            jax.ShapeDtypeStruct((2, 1024, 128), bf16),
            jax.ShapeDtypeStruct((2, 1024, 128), bf16),
            jax.ShapeDtypeStruct((2, 128, width), bf16),
            jax.ShapeDtypeStruct((256, width), f32),
            jax.ShapeDtypeStruct((256, width), bf16),
            jax.ShapeDtypeStruct((8, 256), f32),
            jax.ShapeDtypeStruct((2, 2, 2, 128, width), bf16),
            jax.ShapeDtypeStruct((16, width), bf16),
            jax.ShapeDtypeStruct((32, width), bf16),
            jax.ShapeDtypeStruct((8, 2048), jnp.int32),
            jax.ShapeDtypeStruct((2, 2, 2, 256, width), bf16),
            jax.ShapeDtypeStruct((256, width), bf16),
            jax.ShapeDtypeStruct((8, 2048), jnp.int32),
            jax.ShapeDtypeStruct((128, 1024), bf16),
        ),
        in_specs=[vmem()] * 15,
        out_specs=(
            anywhere(), vmem(), vmem(), vmem(), vmem(), vmem(), vmem(), anywhere(), vmem(), vmem(), vmem(),
            anywhere(), vmem(), vmem(), vmem(),
        ),
        scratch_shapes=[
            pltpu.VMEM((2, 2, 2, 256, width), bf16),
            pltpu.VMEM((8, 256, width), bf16),
            pltpu.VMEM((2, 2, 2, 256, width), bf16),
            pltpu.VMEM((2, 2, 2, 128, width), bf16),
            pltpu.VMEM((8, 128, 256), bf16),
            pltpu.VMEM((8, 2, 128, 128), bf16),
            pltpu.VMEM((1024, 128), f32),
            pltpu.VMEM((1024, 128), f32),
            pltpu.VMEM((2, 1024, 1), f32),
            pltpu.VMEM((16, 128), bf16),
            pltpu.SemaphoreType.DMA((3, 6)),
            pltpu.SemaphoreType.DMA((3, 6)),
            pltpu.SemaphoreType.DMA((3, 6)),
            pltpu.SemaphoreType.DMA((3, 6)),
            pltpu.SemaphoreType.DMA((6, 8)),
            pltpu.SemaphoreType.DMA((6, 8)),
            pltpu.SemaphoreType.DMA((8,)),
            pltpu.SemaphoreType.DMA((8,)),
            pltpu.SemaphoreType.DMA((3, 3)),
            pltpu.SemaphoreType.DMA((3, 3)),
            pltpu.SemaphoreType.DMA((4,)),
            pltpu.SemaphoreType.DMA((4,)),
            pltpu.SemaphoreType.DMA((9,)),
            pltpu.SemaphoreType.DMA((3,)),
        ],
        compiler_params=pltpu.CompilerParams(
            collective_id=0, has_side_effects=True, vmem_limit_bytes=VMEM_LIMIT
        ),
        name="forward",
    )(*values, *tables)


SLOT = 4 * CAPH
SPAN = 512
TAKEN = 4 * SLOT


def build_rows(routes, upper, plain, first_expert, block):
    columns = pl.ds(pl.multiple_of(block * SPAN, SPAN), SPAN)
    chosen = routes[:, columns]
    masks = [jnp.max((chosen == first_expert + e).astype(f32), 0, keepdims=True) for e in range(4)]
    mask = jnp.concatenate(masks + [jnp.zeros((4, SPAN), f32)], 0)
    rank = dot(mask.astype(bf16), upper[...])
    slots = lax.broadcasted_iota(jnp.int32, (SLOT, SPAN), 0).astype(f32)
    for e in range(4):
        hit = (slots == rank[e : e + 1]) & (mask[e : e + 1] > 0.0)
        plain[block, e * SLOT : (e + 1) * SLOT] = jnp.where(hit, 1.0, 0.0).astype(bf16)


def slot_weights(routes, weights, plain, column, first_expert, block):
    columns = pl.ds(pl.multiple_of(block * SPAN, SPAN), SPAN)
    chosen = routes[:, columns]
    weight = weights[:, columns]
    for e in range(4):
        share = jnp.sum(jnp.where(chosen == first_expert + e, weight, 0.0), 0, keepdims=True)
        mine = pl.ds(e * SLOT, SLOT)
        column[block, mine] = jnp.sum(plain[block, mine].astype(f32) * share, -1, keepdims=True)


def place_rows(source, block):
    width = source.shape[-1]
    rows = pl.ds(pl.multiple_of((block // 2) * 128, 128), 128)
    return source[lax.rem(block, 2), :, :, rows].reshape(SPAN, width)


def expert_rows(e):
    return pl.ds(pl.multiple_of(e * SLOT, 16), SLOT)


def experts_kernel(
    moe_in, my_weights, cot_mirror, cot_hbm, routes, routes_mirror, gate_hbm, up_hbm, down_hbm,
    out_part, in_sum, p_all, rows_out, pair_out, hidden_out, gate_out, up_out, plain_mirror, pair_mirror, moe_mirror,
    weights_other,
    x, c, cm, upper, plain, rows, pair_grad, pair_in, column, p_col, weights, p_part,
    gate, up, down, hid_buf, gg_buf, ug_buf, part_buf,
    row_send, row_recv, cm_send, cm_recv, w_send, w_recv, p_send, p_recv, pair_send, pair_recv,
    sem_c, sem_w, sem_rows, sem_h, sem_part, own_sem, *sums,
):
    me = my_place()
    first = me * 4
    width = x.shape[-1]
    count = 2 * SLOT
    own_entry = (me // 4, lax.rem(me // 2, 2), lax.rem(me, 2))
    meet(peers() + [mirror()])
    gathers = [
        Gather(row_items(moe_in, x, HALF_SHARES[s]), row_send.at[s], row_recv.at[s]) for s in range(2)
    ]
    gathers[0].start(0)

    def weight_lanes(s, i):
        return weights.at[:, pl.ds(pl.multiple_of(s * 1024 + i * 128, 128), 128)]

    own = [
        pltpu.make_async_copy(moe_in, x.at[own_entry], own_sem.at[0]),
        pltpu.make_async_copy(my_weights.at[:, pl.ds(0, 128)], weight_lanes(0, me), own_sem.at[1]),
        pltpu.make_async_copy(my_weights.at[:, pl.ds(128, 128)], weight_lanes(1, me), own_sem.at[2]),
        pltpu.make_async_copy(cot_mirror, cm.at[own_entry], own_sem.at[3]),
    ]
    for copy in own:
        copy.start()
    weight_spreads = [
        Spread(
            lambda j, s=s: my_weights.at[:, pl.ds(s * 128, 128)],
            lambda i, s=s: weight_lanes(s, i),
            w_send.at[s],
            w_recv.at[s],
        )
        for s in range(2)
    ]
    for spread in weight_spreads:
        spread.start()
    load_c = pltpu.make_async_copy(cot_hbm, c, sem_c)
    load_c.start()

    def fetch(e, slot):
        return [
            pltpu.make_async_copy(gate_hbm.at[e], gate.at[slot], sem_w.at[slot, 0]),
            pltpu.make_async_copy(up_hbm.at[e], up.at[slot], sem_w.at[slot, 1]),
            pltpu.make_async_copy(down_hbm.at[e], down.at[slot], sem_w.at[slot, 2]),
        ]

    for copy in fetch(0, 0):
        copy.start()
    fill_upper(upper)

    def build(block, carry):
        build_rows(routes, upper, plain, first, block)
        return carry

    lax.fori_loop(0, 2, build, 0)
    for copy in own:
        copy.wait()
    gathers[0].advance(1)
    lax.fori_loop(2, 4, build, 0)
    load_c.wait()

    def take_c(block, carry):
        pair_grad[block] = dot(plain[block], place_rows(c, block)).astype(bf16)
        return carry

    gathers[0].advance(2)
    gathers[1].start(0)
    lax.fori_loop(0, 4, take_c, 0)
    for spread in weight_spreads:
        spread.wait()
    weights_copy = remote(weights, weights_other, pair_send.at[0], pair_recv.at[0], mirror())
    weights_copy.start()

    def weigh(block, carry):
        slot_weights(routes, weights, plain, column, first, block)
        return carry

    lax.fori_loop(0, 4, weigh, 0)
    cm_gather = Gather(row_items(cot_mirror, cm), cm_send, cm_recv)
    moe_copy = remote(moe_in, moe_mirror, pair_send.at[1], pair_recv.at[1], mirror())
    p_part[...] = jnp.zeros_like(p_part)

    def take_x(block, carry):
        rows[block] = dot(plain[block], place_rows(x, block)).astype(bf16)
        return carry

    def keep_rows(s):
        pair = pl.ds(2 * s, 2)
        return pltpu.make_async_copy(rows.at[pair], rows_out.at[pair], sem_rows.at[s])

    def keep(s, e, slot):
        where = pl.ds(pl.multiple_of(s * count, 16), count)
        return [
            pltpu.make_async_copy(hid_buf.at[slot], hidden_out.at[e, where], sem_h.at[slot, 0]),
            pltpu.make_async_copy(gg_buf.at[slot], gate_out.at[e, where], sem_h.at[slot, 1]),
            pltpu.make_async_copy(ug_buf.at[slot], up_out.at[e, where], sem_h.at[slot, 2]),
        ]

    def total_of(s):
        cuts = tuple((pl.ds(*cut), slice(None)) for cut in HALF_SHARES[s])
        return CubeSum(x, x, cuts, sums[12 * s : 12 * s + 12], s * 128)

    totals = [total_of(s) for s in range(2)]

    def store(cut, value):
        in_sum[cut] = value

    def one_half(s, carry):
        for t in range(2):

            @pl.when(s == t)
            def _(t=t):
                gathers[t].wait(2)
                if t == 0:
                    gathers[1].advance(1)

        lax.fori_loop(2 * s, 2 * s + 2, take_x, 0)
        keep_rows(s).start()

        @pl.when(s == 0)
        def _():
            gathers[1].advance(2)
            cm_gather.start(0)
            moe_copy.start()

        def expert(e, inner):
            slot = lax.rem(e, 2)
            mine = expert_rows(e)
            pair = pl.ds(2 * s, 2)
            for copy in fetch(e, slot):
                copy.wait()

            @pl.when(4 * s + e < 7)
            def _():
                for copy in fetch(lax.rem(e + 1, 4), 1 - slot):
                    copy.start()

            rows_e = rows[pair, mine].reshape(count, width)
            weight_e = column[pair, mine].reshape(count, 1)
            pair_e = (pair_grad[pair, mine].reshape(count, width).astype(f32) * weight_e).astype(bf16)
            pair_grad[pair, mine] = pair_e.reshape(2, SLOT, width)
            hidden, gate_grad, up_grad = expert_inner(rows_e, pair_e, gate[slot], up[slot], down[slot])

            @pl.when(e >= 2)
            def _():
                for copy in keep(s, e - 2, slot):
                    copy.wait()

            hid_buf[slot] = hidden
            gg_buf[slot] = gate_grad
            ug_buf[slot] = up_grad
            for copy in keep(s, e, slot):
                copy.start()

            @pl.when(e == 0)
            def _():
                keep_rows(s).wait()

            out_e = dot(hidden, down[slot]).astype(bf16).astype(f32)
            p = jnp.sum(out_e * pair_e.astype(f32), -1, keepdims=True)
            p_col[pair, mine] = p.reshape(2, SLOT, 1)
            rows[pair, mine] = (out_e * weight_e).astype(bf16).reshape(2, SLOT, width)
            back = dot_last(gate_grad, gate[slot]) + dot_last(up_grad, up[slot])
            pair_in[pair, mine] = back.astype(bf16).reshape(2, SLOT, width)

            @pl.when(4 * s + e == 3)
            def _():
                cm_gather.advance(1)

            @pl.when(4 * s + e == 5)
            def _():
                cm_gather.advance(2)

            @pl.when(4 * s + e == 6)
            def _():
                totals[0].middle()

            return inner

        lax.fori_loop(0, 4, expert, 0)
        for copy in keep(s, 2, 0) + keep(s, 3, 1):
            copy.wait()
        for t in range(2):

            @pl.when(s == t)
            def _(t=t):
                gathers[t].sent()

        def combine_in(block, inner):
            y = lax.rem(block, 2)
            back = dot_first(plain[block], pair_in[block]).astype(bf16)
            mine = pl.ds(pl.multiple_of(s * 128, 128), 128)
            x[y, :, :, mine] = back.reshape(2, 2, 128, width)
            for e in range(4):
                slots = pl.ds(e * SLOT, SLOT)
                p = jnp.sum(plain[block, slots].astype(f32) * p_col[block, slots], 0, keepdims=True)
                for d in range(4):
                    p_part[y * 4 + d, pl.ds(e, 1), mine] = p[:, d * 128 : (d + 1) * 128]
            return inner

        lax.fori_loop(2 * s, 2 * s + 2, combine_in, 0)
        for t in range(2):

            @pl.when(s == t)
            def _(t=t):
                totals[t].start()
                if t == 1:
                    totals[0].last()

        return carry

    lax.fori_loop(0, 2, one_half, 0)
    keep_pair = pltpu.make_async_copy(pair_grad, pair_out, sem_rows.at[0])
    keep_pair.start()
    p_spread = Spread(lambda j: p_part.at[j], lambda i: p_all.at[i], p_send, p_recv)
    p_spread.start()
    p_own = pltpu.make_async_copy(p_part.at[me], p_all.at[me], own_sem.at[0])
    p_own.start()

    def part_copy(block):
        slot = lax.rem(block, 2)
        rows_of = pl.ds(pl.multiple_of((block // 2) * 128, 128), 128)
        return pltpu.make_async_copy(
            part_buf.at[slot], out_part.at[lax.rem(block, 2), :, :, rows_of], sem_part.at[slot]
        )

    def combine_out(block, carry):
        slot = lax.rem(block, 2)

        @pl.when(block >= 2)
        def _():
            part_copy(block - 2).wait()

        out = dot_first(plain[block], rows[block]).astype(bf16)
        part_buf[slot] = out.reshape(2, 2, 128, width)
        part_copy(block).start()
        return carry

    lax.fori_loop(0, 4, combine_out, 0)
    totals[0].finish(store)
    keep_pair.wait()

    def build_mirror(block, carry):
        build_rows(routes_mirror, upper, plain, first, block)
        return carry

    lax.fori_loop(0, 2, build_mirror, 0)
    totals[1].middle()
    lax.fori_loop(2, 4, build_mirror, 0)
    keep_plain = pltpu.make_async_copy(plain, plain_mirror, sem_rows.at[0])
    keep_plain.start()
    cm_gather.wait(2)

    def take_mirror(block, carry):
        pair_grad[block] = dot(plain[block], place_rows(cm, block)).astype(bf16)
        return carry

    lax.fori_loop(0, 2, take_mirror, 0)
    totals[1].last()
    lax.fori_loop(2, 4, take_mirror, 0)
    keep_mirror = pltpu.make_async_copy(pair_grad, pair_mirror, sem_rows.at[1])
    keep_mirror.start()
    p_spread.wait()
    p_own.wait()
    part_copy(2).wait()
    part_copy(3).wait()
    totals[1].finish(store)
    for total in totals:
        total.sent()
    keep_plain.wait()
    keep_mirror.wait()
    cm_gather.sent()
    weights_copy.wait()
    moe_copy.wait()


def half_cuts(s):
    return tuple((pl.ds(*cut), slice(None)) for cut in HALF_SHARES[s])


def experts(moe_in, my_weights, cot_mirror, cot_all, routes, routes_mirror, gate_w, up_w, down_w):
    width = moe_in.shape[-1]
    ff = gate_w.shape[-1]
    return pl.pallas_call(
        experts_kernel,
        out_shape=(
            jax.ShapeDtypeStruct((2, 2, 2, 256, width), bf16),
            jax.ShapeDtypeStruct((256, width), f32),
            jax.ShapeDtypeStruct((8, 8, 256), f32),
            jax.ShapeDtypeStruct((4, TAKEN, width), bf16),
            jax.ShapeDtypeStruct((4, TAKEN, width), bf16),
            jax.ShapeDtypeStruct((4, TAKEN, ff), bf16),
            jax.ShapeDtypeStruct((4, TAKEN, ff), bf16),
            jax.ShapeDtypeStruct((4, TAKEN, ff), bf16),
            jax.ShapeDtypeStruct((4, TAKEN, SPAN), bf16),
            jax.ShapeDtypeStruct((4, TAKEN, width), bf16),
            jax.ShapeDtypeStruct((256, width), bf16),
            jax.ShapeDtypeStruct((8, 2048), f32),
        ),
        in_specs=[vmem(), vmem(), vmem(), anywhere(), vmem(), vmem(), anywhere(), anywhere(), anywhere()],
        out_specs=(anywhere(), vmem(), vmem()) + (anywhere(),) * 7 + (vmem(), vmem()),
        scratch_shapes=[
            pltpu.VMEM((2, 2, 2, 256, width), bf16),
            pltpu.VMEM((2, 2, 2, 256, width), bf16),
            pltpu.VMEM((2, 2, 2, 256, width), bf16),
            pltpu.VMEM((SPAN, SPAN), bf16),
            pltpu.VMEM((4, TAKEN, SPAN), bf16),
            pltpu.VMEM((4, TAKEN, width), bf16),
            pltpu.VMEM((4, TAKEN, width), bf16),
            pltpu.VMEM((4, TAKEN, width), bf16),
            pltpu.VMEM((4, TAKEN, 1), f32),
            pltpu.VMEM((4, TAKEN, 1), f32),
            pltpu.VMEM((8, 2048), f32),
            pltpu.VMEM((8, 8, 256), f32),
            pltpu.VMEM((2, width, ff), bf16),
            pltpu.VMEM((2, width, ff), bf16),
            pltpu.VMEM((2, ff, width), bf16),
            pltpu.VMEM((2, 2 * SLOT, ff), bf16),
            pltpu.VMEM((2, 2 * SLOT, ff), bf16),
            pltpu.VMEM((2, 2 * SLOT, ff), bf16),
            pltpu.VMEM((2, 2, 2, 128, width), bf16),
            pltpu.SemaphoreType.DMA((2, 3, 6)),
            pltpu.SemaphoreType.DMA((2, 3, 6)),
            pltpu.SemaphoreType.DMA((3, 6)),
            pltpu.SemaphoreType.DMA((3, 6)),
            pltpu.SemaphoreType.DMA((2, 8)),
            pltpu.SemaphoreType.DMA((2, 8)),
            pltpu.SemaphoreType.DMA((8,)),
            pltpu.SemaphoreType.DMA((8,)),
            pltpu.SemaphoreType.DMA((2,)),
            pltpu.SemaphoreType.DMA((2,)),
            pltpu.SemaphoreType.DMA,
            pltpu.SemaphoreType.DMA((2, 3)),
            pltpu.SemaphoreType.DMA((2,)),
            pltpu.SemaphoreType.DMA((2, 3)),
            pltpu.SemaphoreType.DMA((2,)),
            pltpu.SemaphoreType.DMA((4,)),
            *cube_sum_scratch(128, width, half_cuts(0)),
            *cube_sum_scratch(128, width, half_cuts(1)),
        ],
        compiler_params=pltpu.CompilerParams(
            collective_id=1, has_side_effects=True, vmem_limit_bytes=VMEM_LIMIT
        ),
        name="experts",
    )(moe_in, my_weights, cot_mirror, cot_all, routes, routes_mirror, gate_w, up_w, down_w)


LANE_SHARE = 128


def backward_kernel(
    cot, residual, in_sum, p_all, routes, weights, router, moe_in, gains_all, wo_hbm, amix, attn_hbm, q_in, kv_in,
    segs, near_cos, near_sin, far_cos, far_sin, tok, wq, wkv, moe_mirror,
    token_grad, grads, mirror_hbm,
    wo_all, attn_all, wq_all, wkv_all, mm, mix_grad, mg, gq, gkv, gq_rows, gkv_rows, g_all, kv_sum, cosine, sine, docs,
    residual_grad, small_grad,
    w_send, w_recv, mm_send, mm_recv, mg_send, mg_recv, g_send, g_recv, pair_send, pair_recv, own_sem, load_sem,
):
    me, core = my_place(), my_core()
    width = tok.shape[-1]
    meet(peers() + [sibling()])
    half = pl.ds(pl.multiple_of(core * 64, 64), 64)
    own_entry = (me // 4, lax.rem(me // 2, 2), lax.rem(me, 2))
    own = [
        pltpu.make_async_copy(wq.at[half], wq_all.at[own_entry + (half,)], own_sem.at[0]),
        pltpu.make_async_copy(wkv.at[half], wkv_all.at[own_entry + (half,)], own_sem.at[1]),
        pltpu.make_async_copy(moe_mirror, mm.at[own_entry], own_sem.at[2]),
    ]
    loads = [
        pltpu.make_async_copy(wo_hbm, wo_all, load_sem.at[0]),
        pltpu.make_async_copy(attn_hbm, attn_all, load_sem.at[1]),
    ]
    for copy in own + loads:
        copy.start()

    def weight_item(src, dst, start, count, order):
        rows = pl.ds(pl.multiple_of(core * 64 + start, 16), count)
        return (src.at[rows], lambda entry: dst.at[entry + (rows,)], order)

    w_gather = Gather(
        [
            weight_item(wq, wq_all, 0, 48, ORDERS[0]),
            weight_item(wq, wq_all, 48, 16, ORDERS[1]),
            weight_item(wkv, wkv_all, 0, 32, ORDERS[1]),
            weight_item(wkv, wkv_all, 32, 32, ORDERS[2]),
        ],
        w_send,
        w_recv,
    )
    w_gather.start(0)
    mm_gather = Gather(row_items(moe_mirror, mm), mm_send, mm_recv)
    mm_gather.start(0)
    ids = lax.broadcasted_iota(jnp.int32, (32, 256), 0)
    dense = jnp.zeros((32, 256), f32)
    for k in range(TOP):
        dense = dense + jnp.where(ids == routes[pl.ds(k, 1)], weights[pl.ds(k, 1)], 0.0)
    p = jnp.concatenate([p_all[i, 0:4] for i in range(8)], 0)
    logit_grad = (p - dense * jnp.sum(p, 0, keepdims=True)).astype(bf16)
    moe_in_grad = in_sum[...] + dot_first(logit_grad, router[...])
    part, moe_gain_grad = norm_back(residual[...], gains_all[1:2].astype(f32), moe_in_grad)
    total = cot[...].astype(f32) + part
    residual_grad[...] = total
    low_grad = total.astype(bf16)
    for copy in loads[:1]:
        copy.wait()
    back = dot_last(low_grad, wo_all[...].reshape(width, width)).astype(bf16)
    for j in range(8):
        mix_grad[j] = back[:, j * 128 : (j + 1) * 128].reshape(2, 128, 128)
    mix_spread = Spread(lambda j: mix_grad.at[j], lambda i: mg.at[i], mg_send, mg_recv)
    mix_spread.start()
    mix_own = pltpu.make_async_copy(mix_grad.at[me], mg.at[me], own_sem.at[3])
    mix_own.start()
    for copy in own:
        copy.wait()
    w_gather.advance(1)
    fill_rope(near_cos, near_sin, far_cos, far_sin, cosine, sine)
    fill_docs(segs, docs)
    wo_grad = dot_first(amix[...].reshape(256, width), low_grad)
    grads[:, :, 0:width] = wo_grad.astype(bf16).reshape(8, 128, width)
    padded = jnp.concatenate([logit_grad, jnp.zeros((LANE_SHARE - 32, 256), bf16)], 0)
    small_grad[...] = lax.dot_general(moe_in[...], padded, (((0,), (1,)), ((), ())), preferred_element_type=f32)
    mix_spread.wait()
    mix_own.wait()
    mm_gather.advance(1)

    def lane_block(i):
        return pl.ds(pl.multiple_of(i * 128, 128), 128)

    def spread_of(s):
        return [
            Spread(lambda j: gq.at[j, s], lambda i: gq_rows.at[s, :, lane_block(i)], g_send.at[2 * s], g_recv.at[2 * s]),
            Spread(
                lambda j: gkv.at[j, s],
                lambda i: gkv_rows.at[s, :, lane_block(i)],
                g_send.at[2 * s + 1],
                g_recv.at[2 * s + 1],
            ),
        ]

    def own_blocks(s):
        return [
            pltpu.make_async_copy(gq.at[me, s], gq_rows.at[s, :, lane_block(me)], own_sem.at[4 + 2 * s]),
            pltpu.make_async_copy(gkv.at[me, s], gkv_rows.at[s, :, lane_block(me)], own_sem.at[5 + 2 * s]),
        ]

    def attend(s, carry):
        kv_sum[...] = jnp.zeros_like(kv_sum)

        def back_block(i):
            first, count, q2, kv, probability = block_probability(q_in, kv_in, docs, segs, s, i)
            g2 = two_heads_high(mg[i, s].astype(f32)).astype(bf16)
            prob_grad = dot_last(g2, kv)
            delta = jnp.sum(probability * prob_grad, -1, keepdims=True)
            score_grad = (probability * (prob_grad - delta) * 0.125).astype(bf16)
            dq = dot(score_grad, kv)
            keys = pl.ds(first, count)
            kv_sum[keys] += dot_first(score_grad, q2.astype(bf16)) + dot_first(probability.astype(bf16), g2)
            low = lanes((128, 128)) < 64
            dq = jnp.where(low, dq[:128], pltpu.roll(dq[128:], 64, 1))
            rows = pl.ds(i * 128 if isinstance(i, int) else pl.multiple_of(i * 128, 128), 128)
            dq = (dq * cosine[rows] - turned(dq) * sine[rows]).astype(bf16)
            gq[i, s] = dq
            g_all[i, s, :, 0:128] = dq

        for i in range(4):
            back_block(i)
            if i == 2:

                @pl.when(s == 0)
                def _():
                    w_gather.advance(2)

        def back_long(i, inner):
            back_block(i)

            @pl.when(s * 8 + i == 6)
            def _():
                mm_gather.advance(2)

            return inner

        lax.fori_loop(4, 8, back_long, 0)

        def keys_back(i, inner):
            rows = pl.ds(pl.multiple_of(i * 128, 128), 128)
            dkv = kv_sum[rows]
            low = lanes((128, 128)) < 64
            dkv = jnp.where(low, dkv * cosine[rows] - turned(dkv) * sine[rows], dkv).astype(bf16)
            gkv[i, s] = dkv
            g_all[i, s, :, 128:256] = dkv
            return inner

        lax.fori_loop(0, 8, keys_back, 0)
        for spread in spread_of(s):
            spread.start()
        for copy in own_blocks(s):
            copy.start()
        return carry

    lax.fori_loop(0, 2, attend, 0)
    keep_own = own_blocks(0) + own_blocks(1)
    w_gather.wait(2)
    shared = [
        remote(w.at[:, :, :, half], w.at[:, :, :, half], pair_send.at[k], pair_recv.at[k], sibling())
        for k, w in enumerate((wq_all, wkv_all))
    ]
    for copy in shared:
        copy.start()
    loads[1].wait()
    w_grad = dot_first(attn_all[...].reshape(2048, width), g_all[...].reshape(2048, 256))
    grads[:, :, width + LANE_SHARE :] = w_grad.astype(bf16).reshape(8, 128, 256)
    for copy in shared + keep_own:
        copy.wait()
    for s in range(2):
        for spread in spread_of(s):
            spread.wait()
    back = dot_last(gq_rows[...].reshape(256, 1024), wq_all[...].reshape(width, 1024))
    back = back + dot_last(gkv_rows[...].reshape(256, 1024), wkv_all[...].reshape(width, 1024))
    part, attn_gain_grad = norm_back(tok[...].astype(f32), gains_all[0:1].astype(f32), back)
    token_grad[...] = residual_grad[...] + part
    row = lax.broadcasted_iota(jnp.int32, (LANE_SHARE, width), 0)
    gain_rows = jnp.where(row == 32, moe_gain_grad, jnp.where(row == 33, attn_gain_grad, 0.0))
    grads[:, :, width : width + LANE_SHARE] = (small_grad[...] + gain_rows.T).astype(bf16).reshape(8, 128, LANE_SHARE)
    mm_gather.wait(2)
    mm_out = pltpu.make_async_copy(mm, mirror_hbm, load_sem.at[0])
    mm_out.start()
    w_gather.sent()
    mm_gather.sent()
    mm_out.wait()


def backward(*values):
    tok = values[15]
    width = tok.shape[-1]
    tables = tuple(jnp.asarray(t) for t in rope_tables())
    values = values[:15] + tables + values[15:]
    specs = [vmem()] * 23
    specs[9] = specs[11] = anywhere()
    return pl.pallas_call(
        backward_kernel,
        out_shape=(
            jax.ShapeDtypeStruct((256, width), f32),
            jax.ShapeDtypeStruct((8, 128, width + 256 + LANE_SHARE), bf16),
            jax.ShapeDtypeStruct((2, 2, 2, 256, width), bf16),
        ),
        in_specs=specs,
        out_specs=(vmem(), vmem(), anywhere()),
        scratch_shapes=[
            pltpu.VMEM((2, 2, 2, 128, width), bf16),
            pltpu.VMEM((8, 256, width), bf16),
            pltpu.VMEM((2, 2, 2, 128, width), bf16),
            pltpu.VMEM((2, 2, 2, 128, width), bf16),
            pltpu.VMEM((2, 2, 2, 256, width), bf16),
            pltpu.VMEM((8, 2, 128, 128), bf16),
            pltpu.VMEM((8, 2, 128, 128), bf16),
            pltpu.VMEM((8, 2, 128, 128), bf16),
            pltpu.VMEM((8, 2, 128, 128), bf16),
            pltpu.VMEM((2, 128, 1024), bf16),
            pltpu.VMEM((2, 128, 1024), bf16),
            pltpu.VMEM((8, 2, 128, 256), bf16),
            pltpu.VMEM((1024, 128), f32),
            pltpu.VMEM((1024, 128), f32),
            pltpu.VMEM((1024, 128), f32),
            pltpu.VMEM((2, 1024, 1), f32),
            pltpu.VMEM((256, width), f32),
            pltpu.VMEM((width, LANE_SHARE), f32),
            pltpu.SemaphoreType.DMA((3, 4)),
            pltpu.SemaphoreType.DMA((3, 4)),
            pltpu.SemaphoreType.DMA((3, 6)),
            pltpu.SemaphoreType.DMA((3, 6)),
            pltpu.SemaphoreType.DMA((8,)),
            pltpu.SemaphoreType.DMA((8,)),
            pltpu.SemaphoreType.DMA((4, 8)),
            pltpu.SemaphoreType.DMA((4, 8)),
            pltpu.SemaphoreType.DMA((2,)),
            pltpu.SemaphoreType.DMA((2,)),
            pltpu.SemaphoreType.DMA((8,)),
            pltpu.SemaphoreType.DMA((2,)),
        ],
        compiler_params=pltpu.CompilerParams(
            collective_id=2, has_side_effects=True, vmem_limit_bytes=VMEM_LIMIT
        ),
        name="backward",
    )(*values)


SUM_CUTS = tuple((slice(None), pl.ds(k * 384, 384)) for k in range(3))


def expert_weights_kernel(
    x_hbm, plain_hbm, pair_raw, routes, weights, gate_hbm, up_hbm, down_hbm, rows_hbm, pair_hbm, hidden_hbm, gg_hbm, ug_hbm,
    out_part, residual, grads,
    gate_own, up_own, down_own, gate_other, up_other, down_other, mixed, shares,
    x, c, plain, rows, pair_grad, column, gate, up, down,
    both_rows, both_pair, both_hidden, both_gate, gate_buf, up_buf, down_buf,
    g0, g1, g2, g3, g4, g5, got1, got2, sum_send, sum_recv,
    s0, s1, s2, sheld0, sgot1, sheld1, sgot2, ssend, srecv,
    core_got, core_sum, core_qkv, all_got, side_sum, side_got,
    grad_send, grad_recv, core_send, core_recv, part_send, part_recv,
    sem_x, sem_w, sem_own, sem_out, own_sem,
):
    me, core = my_place(), my_core()
    first = me * 4
    side = lax.axis_index("group") // 2
    other = 1 - side
    width = x.shape[-1]
    ff = gate.shape[-1]
    half = pl.ds(pl.multiple_of(core * 64, 64), 64)
    other_half = pl.ds(pl.multiple_of((1 - core) * 64, 64), 64)
    meet(peers() + [sibling(), mirror()])
    core_copy = remote(grads.at[:, other_half], core_got, core_send.at[0], core_recv.at[0], sibling())
    core_copy.start()
    total = CubeSum(
        out_part, x, ROW_CUTS, (g0, g1, g2, g3, g4, g5, c.at[pl.ds(0, 2)], got1, c.at[2], got2, sum_send, sum_recv)
    )
    total.start()
    loads = [
        pltpu.make_async_copy(plain_hbm, plain, sem_x.at[1]),
        pltpu.make_async_copy(pair_raw, pair_grad, sem_x.at[2]),
        pltpu.make_async_copy(x_hbm, x, sem_x.at[0]),
    ]
    for copy in loads:
        copy.start()

    def fetch(e, slot):
        return [
            pltpu.make_async_copy(gate_hbm.at[e], gate.at[slot], sem_w.at[slot, 0]),
            pltpu.make_async_copy(up_hbm.at[e], up.at[slot], sem_w.at[slot, 1]),
            pltpu.make_async_copy(down_hbm.at[e], down.at[slot], sem_w.at[slot, 2]),
        ]

    for copy in fetch(0, 0):
        copy.start()
    loads[0].wait()

    def weigh(block, carry):
        slot_weights(routes, weights, plain, column, first, block)
        return carry

    lax.fori_loop(0, 4, weigh, 0)
    core_copy.wait()
    summed = width + LANE_SHARE
    for j in range(8):
        both = (grads[j, half].astype(f32) + core_got[j].astype(f32)).astype(bf16)
        core_sum[j // 4, j // 2 % 2, j % 2] = both[:, :summed]
        core_qkv[j] = both[:, summed:]
    spread = Spread(lambda j: core_qkv.at[j], lambda i: all_got.at[i], grad_send, grad_recv)
    spread.start()
    spread_own = pltpu.make_async_copy(core_qkv.at[me], all_got.at[me], own_sem)
    spread_own.start()
    small_total = CubeSum(
        core_sum, core_sum, SUM_CUTS, (s0, s1, s2, sheld0, sgot1, sheld1, sgot2, ssend, srecv)
    )
    small_total.start()
    for copy in loads[1:]:
        copy.wait()

    def take(block, carry):
        rows[block] = dot(plain[block], place_rows(x, block)).astype(bf16)
        pair_grad[block] = (pair_grad[block].astype(f32) * column[block]).astype(bf16)
        return carry

    lax.fori_loop(0, 4, take, 0)
    load_part = pltpu.make_async_copy(out_part, x, sem_x.at[0])
    load_part.start()
    side_copy = remote(side_sum, side_got, core_send.at[1], core_recv.at[1], mirror())
    last_copy = remote(shares.at[half], shares.at[half], core_send.at[2], core_recv.at[2], sibling())

    def part_copies(e):
        return [
            pltpu.make_async_copy(gate_buf, gate_own.at[e], sem_out.at[0]),
            pltpu.make_async_copy(up_buf, up_own.at[e], sem_out.at[1]),
            pltpu.make_async_copy(down_buf, down_own.at[e], sem_out.at[2]),
            remote(gate_buf, gate_other.at[e], part_send.at[0], part_recv.at[e, 0], sibling()),
            remote(up_buf, up_other.at[e], part_send.at[1], part_recv.at[e, 1], sibling()),
            remote(down_buf, down_other.at[e], part_send.at[2], part_recv.at[e, 2], sibling()),
        ]

    def sent(e):
        made = part_copies(e)
        for copy in made[:3]:
            copy.wait()
        for copy in made[3:]:
            copy.wait_send()

    def expert(e, carry):
        slot = lax.rem(e, 2)
        mine = expert_rows(e)
        own = [
            pltpu.make_async_copy(rows_hbm.at[:, mine], both_rows.at[side], sem_own.at[0]),
            pltpu.make_async_copy(pair_hbm.at[:, mine], both_pair.at[side], sem_own.at[1]),
            pltpu.make_async_copy(hidden_hbm.at[e], both_hidden.at[side], sem_own.at[2]),
            pltpu.make_async_copy(gg_hbm.at[e], both_gate.at[side, :, pl.ds(0, ff)], sem_own.at[3]),
            pltpu.make_async_copy(ug_hbm.at[e], both_gate.at[side, :, pl.ds(ff, ff)], sem_own.at[4]),
        ]
        for copy in own:
            copy.start()
        for copy in fetch(e, slot):
            copy.wait()

        @pl.when(e < 3)
        def _():
            for copy in fetch(e + 1, 1 - slot):
                copy.start()

        rows_e = rows[:, mine].reshape(TAKEN, width)
        pair_e = pair_grad[:, mine].reshape(TAKEN, width)
        hidden, gate_grad, up_grad = expert_inner(rows_e, pair_e, gate[slot], up[slot], down[slot])
        both_rows[other] = rows_e.reshape(4, SLOT, width)
        both_pair[other] = pair_e.reshape(4, SLOT, width)
        both_hidden[other] = hidden
        both_gate[other, :, 0:ff] = gate_grad
        both_gate[other, :, ff : 2 * ff] = up_grad

        for copy in own:
            copy.wait()

        @pl.when(e >= 1)
        def _():
            sent(e - 1)

        sums = dot_first(both_rows[...].reshape(2 * TAKEN, width), both_gate[...].reshape(2 * TAKEN, 2 * ff))
        gate_buf[...] = sums[:, :ff].astype(bf16)
        up_buf[...] = sums[:, ff:].astype(bf16)
        down_buf[...] = dot_first(
            both_hidden[...].reshape(2 * TAKEN, ff), both_pair[...].reshape(2 * TAKEN, width)
        ).astype(bf16)
        for copy in part_copies(e):
            copy.start()

        @pl.when(e == 0)
        def _():
            small_total.middle()
            load_part.wait()
            total.middle()

        @pl.when(e == 1)
        def _():
            small_total.last()
            total.last()

            def keep_sum(cut, value):
                side_sum[cut] = value.astype(bf16)

            small_total.finish(keep_sum)
            spread.wait()
            spread_own.wait()
            for i in range(8):
                side_sum[:, summed + i * 256 : summed + (i + 1) * 256] = all_got[i]
            side_copy.start()

        @pl.when(e == 2)
        def _():
            def store(cut, value):
                mixed[cut] = (residual[cut] + value).astype(bf16)

            total.finish(store)

        return carry

    lax.fori_loop(0, 4, expert, 0)
    side_copy.wait()
    shares[half] = (side_sum[...].astype(f32) + side_got[...].astype(f32)).astype(bf16)
    last_copy.start()
    total.sent()
    small_total.sent()
    last_copy.wait()
    sent(3)
    for e in range(4):
        for copy in part_copies(e)[3:]:
            copy.wait_recv()


def expert_weights(x, plain, pair, routes, weights, gate_w, up_w, down_w, kept, out_part, residual, grads):
    width = gate_w.shape[1]
    ff = gate_w.shape[-1]
    wide = grads.shape[-1]
    out = [jax.ShapeDtypeStruct(w.shape, bf16) for w in (gate_w, up_w, down_w)]
    sums = cube_sum_scratch(256, width, ROW_CUTS)
    return pl.pallas_call(
        expert_weights_kernel,
        out_shape=(
            *out,
            *out,
            jax.ShapeDtypeStruct((256, width), bf16),
            jax.ShapeDtypeStruct((128, width + LANE_SHARE + 2048), bf16),
        ),
        in_specs=[anywhere()] * 3 + [vmem()] * 2 + [anywhere()] * 9 + [vmem()] * 2,
        out_specs=(anywhere(),) * 6 + (vmem(),) * 2,
        scratch_shapes=[
            pltpu.VMEM((2, 2, 2, 256, width), bf16),
            pltpu.VMEM((3, 2, 256, width), bf16),
            pltpu.VMEM((4, TAKEN, SPAN), bf16),
            pltpu.VMEM((4, TAKEN, width), bf16),
            pltpu.VMEM((4, TAKEN, width), bf16),
            pltpu.VMEM((4, TAKEN, 1), f32),
            pltpu.VMEM((2, width, ff), bf16),
            pltpu.VMEM((2, width, ff), bf16),
            pltpu.VMEM((2, ff, width), bf16),
            pltpu.VMEM((2, 4, SLOT, width), bf16),
            pltpu.VMEM((2, 4, SLOT, width), bf16),
            pltpu.VMEM((2, TAKEN, ff), bf16),
            pltpu.VMEM((2, TAKEN, 2 * ff), bf16),
            pltpu.VMEM((width, ff), bf16),
            pltpu.VMEM((width, ff), bf16),
            pltpu.VMEM((ff, width), bf16),
            *sums[:6],
            sums[7],
            sums[9],
            *sums[10:],
            *cube_sum_scratch(64, width + LANE_SHARE, SUM_CUTS),
            pltpu.VMEM((8, 64, wide), bf16),
            pltpu.VMEM((2, 2, 2, 64, width + LANE_SHARE), bf16),
            pltpu.VMEM((8, 64, 256), bf16),
            pltpu.VMEM((8, 64, 256), bf16),
            pltpu.VMEM((64, width + LANE_SHARE + 2048), bf16),
            pltpu.VMEM((64, width + LANE_SHARE + 2048), bf16),
            pltpu.SemaphoreType.DMA((8,)),
            pltpu.SemaphoreType.DMA((8,)),
            pltpu.SemaphoreType.DMA((3,)),
            pltpu.SemaphoreType.DMA((3,)),
            pltpu.SemaphoreType.DMA((3,)),
            pltpu.SemaphoreType.DMA((4, 3)),
            pltpu.SemaphoreType.DMA((3,)),
            pltpu.SemaphoreType.DMA((2, 3)),
            pltpu.SemaphoreType.DMA((5,)),
            pltpu.SemaphoreType.DMA((3,)),
            pltpu.SemaphoreType.DMA,
        ],
        compiler_params=pltpu.CompilerParams(
            collective_id=3, has_side_effects=True, vmem_limit_bytes=VMEM_LIMIT
        ),
        name="expert_weights",
    )(x, plain, pair, routes, weights, gate_w, up_w, down_w, *kept, out_part, residual, grads)


def finish_kernel(
    gate_own, up_own, down_own, gate_other, up_other, down_other, shares, mixed, token_grad,
    gate_out, up_out, down_out, query_out, key_out, value_out, wo_out, router_out, moe_gain_out, attn_gain_out,
    mixed_out, token_out,
):
    for own, other, out in ((gate_own, gate_other, gate_out), (up_own, up_other, up_out), (down_own, down_other, down_out)):
        out[...] = own[...].astype(f32) + other[...].astype(f32)
    mixed_out[...] = mixed[...]
    token_out[...] = token_grad[...]

    @pl.when(pl.program_id(0) == 0)
    def _():
        width = wo_out.shape[-1]
        wo_out[...] = shares[:, 0:width].astype(f32)
        small = shares[:, width : width + LANE_SHARE].astype(f32).T
        router_out[...] = small[0:32]
        moe_gain_out[...] = small[32:33]
        attn_gain_out[...] = small[33:34]
        low = lanes((128, 128)) < 64
        base = width + LANE_SHARE
        for j in range(8):
            query_out[:, j * 128 : (j + 1) * 128] = shares[:, base + j * 256 : base + j * 256 + 128].astype(f32)
        for j in range(4):
            left = shares[:, base + j * 512 + 128 : base + j * 512 + 256].astype(f32)
            right = shares[:, base + j * 512 + 384 : base + j * 512 + 512].astype(f32)
            where = slice(j * 128, (j + 1) * 128)
            key_out[:, where] = jnp.where(low, left, pltpu.roll(right, 64, 1))
            value_out[:, where] = jnp.where(low, pltpu.roll(left, 64, 1), right)


def finish(parts, shares, mixed, token_grad):
    width = parts[0].shape[1]
    steps = parts[0].shape[0]

    def block(shape):
        return pl.BlockSpec((1,) + shape[1:], lambda e: (e, 0, 0))

    def rows(shape):
        return pl.BlockSpec((shape[0] // steps,) + shape[1:], lambda e: (e, 0))

    def whole(shape):
        return pl.BlockSpec(shape, lambda e: (0,) * len(shape))

    small = [(128, 1024), (128, 512), (128, 512), (128, width), (32, LANE_SHARE), (1, LANE_SHARE), (1, LANE_SHARE)]
    return pl.pallas_call(
        finish_kernel,
        grid=(steps,),
        out_shape=tuple(jax.ShapeDtypeStruct(p.shape, f32) for p in parts[:3])
        + tuple(jax.ShapeDtypeStruct(shape, f32) for shape in small)
        + (jax.ShapeDtypeStruct(mixed.shape, bf16), jax.ShapeDtypeStruct(token_grad.shape, f32)),
        in_specs=[block(p.shape) for p in parts] + [whole(shares.shape), rows(mixed.shape), rows(token_grad.shape)],
        out_specs=tuple(block(p.shape) for p in parts[:3])
        + tuple(whole(shape) for shape in small)
        + (rows(mixed.shape), rows(token_grad.shape)),
        compiler_params=pltpu.CompilerParams(vmem_limit_bytes=VMEM_LIMIT),
        name="finish",
    )(*parts, shares, mixed, token_grad)


def fast_on_device(
    tokens, segments, routes, cotangent, attn_gain, moe_gain, query_weight, key_projection_matrix,
    value_projection_matrix, out_weight, router_weight, gate_weight, up_weight, down_weight,
):
    width = tokens.shape[-1]
    tok = tokens.reshape(256, width)
    cot = cotangent.reshape(256, width)
    my_routes = routes.reshape(256, TOP).T
    (
        attn_in, q, kv, amix, residual, moe_in, weights, wo_all, gains_all, router_all, routes_all,
        cot_all, cot_mirror, routes_mirror, wkv,
    ) = forward(
        tok, cot, query_weight, key_projection_matrix, value_projection_matrix, out_weight,
        attn_gain.reshape(1, 128), moe_gain.reshape(1, 128), router_weight.T, my_routes, segments,
    )
    out_part, in_sum, p_all, *kept, plain_mirror, pair_mirror, moe_mirror, weights_mirror = experts(
        moe_in, weights, cot_mirror, cot_all, routes_all, routes_mirror, gate_weight, up_weight, down_weight
    )
    token_grad, grads, moe_mirror_all = backward(
        cot, residual, in_sum, p_all, my_routes, weights, router_all, moe_in, gains_all, wo_all, amix, attn_in,
        q, kv, segments, tok, query_weight, wkv, moe_mirror,
    )
    *parts, mixed, shares = expert_weights(
        moe_mirror_all, plain_mirror, pair_mirror, routes_mirror, weights_mirror, gate_weight, up_weight, down_weight,
        kept, out_part, residual, grads,
    )
    (
        gate_grad, up_grad, down_grad, query_grad, key_grad, value_grad, wo_grad, router_grad, moe_gain_grad,
        attn_gain_grad, mixed, token_grad,
    ) = finish(parts, shares, mixed, token_grad)
    return (
        mixed.reshape(tokens.shape), token_grad.reshape(tokens.shape), attn_gain_grad.reshape(128),
        moe_gain_grad.reshape(128), query_grad, key_grad, value_grad, wo_grad, router_grad.T,
        gate_grad, up_grad, down_grad,
    )


def fits(mesh):
    return dict(mesh.shape) == {"group": 4, "blk": 4, "head": 2}


def solution(mesh):
    placed = (
        P("group", ("blk", "head"), None),
        P("group", None),
        P("group", ("blk", "head"), None),
        P("group", ("blk", "head"), None),
        P(("blk", "head")),
        P(("blk", "head")),
        P(("blk", "head"), None),
        P(("blk", "head"), None),
        P(("blk", "head"), None),
        P(("blk", "head"), None),
        P(("blk", "head"), None),
        P(("blk", "head"), None, None),
        P(("blk", "head"), None, None),
        P(("blk", "head"), None, None),
    )
    return jax.shard_map(
        fast_on_device if fits(mesh) else on_device,
        mesh=mesh,
        in_specs=placed,
        out_specs=(
            P("group", ("blk", "head"), None),
            P("group", ("blk", "head"), None),
            P(("blk", "head")),
            P(("blk", "head")),
            P(("blk", "head"), None),
            P(("blk", "head"), None),
            P(("blk", "head"), None),
            P(("blk", "head"), None),
            P(("blk", "head"), None),
            P(("blk", "head"), None, None),
            P(("blk", "head"), None, None),
            P(("blk", "head"), None, None),
        ),
        check_vma=False,
    )
```
